32 devices in a mesh: dp: 16 (over z, y, x), seq: 2 (over core).
Axes of the slice: x: 2, y: 2, z: 4, core: 2. Of those that a mesh axis runs over, the one named last changes fastest.
Arguments:
- tokens: bfloat16 [16, 2048, 1120], P('dp', 'seq'), may hold values from -6 to 6
- cotangent: bfloat16 [16, 2048, 1120], P('dp', 'seq'), may hold values from -6 to 6
- pad_mask: int32 [16, 2048], P('dp', 'seq'), may hold values from 0 to 1, as said below
- prefix_len: int32 [16], P('dp'), may hold values from 1 to 128
- norm_gains: float32 [2, 1120], replicated, may hold values from 0.5 to 1.5
- norm_shifts: float32 [2, 1120], replicated, may hold values from -1.8 to 1.8
- owner_map: int32 [192], replicated, may hold values from 0 to 191, as said below
- weight_copy: bfloat16 [192, 280, 280], P('dp'), may hold values from -1.8090681 to 1.8090681
- master: float32 [192, 280, 280], P('dp'), may hold values from -1.8090681 to 1.8090681
- average_weights: float32 [192, 280, 280], P('dp'), may hold values from -1.8090681 to 1.8090681
- stat_left: float32 [192, 280, 280], P('dp'), may hold values from -16.290909 to 36.654545, as said below
- stat_right: float32 [192, 280, 280], P('dp'), may hold values from -16.290909 to 36.654545, as said below
- root_left: float32 [192, 280, 280], P('dp'), may hold values from -3 to 5, as said below
- root_right: float32 [192, 280, 280], P('dp'), may hold values from -3 to 5, as said below
Outputs:
- block_out: bfloat16 [16, 2048, 1120], P('dp', 'seq')
- grad_input: float32 [16, 2048, 1120], P('dp', 'seq')
- norm_grad: float32 [4, 1120], replicated
- new_norms: float32 [4, 1120], replicated
- slot_grad: float32 [192, 280, 280], P('dp')
- new_left: float32 [192, 280, 280], P('dp')
- new_right: float32 [192, 280, 280], P('dp')
- new_master: float32 [192, 280, 280], P('dp')
- new_copy: bfloat16 [192, 280, 280], P('dp')
- new_average: float32 [192, 280, 280], P('dp')
The draws below stay inside these ranges and needn't reach their ends.
Inputs may be any that keep to these rules, and one draw needn't show every extreme that they name: `pad_mask`: in each cell the ones come first, 512 or more of them; some cell has no zeros. `owner_map`: each block number appears once. `stat_left`: Symmetric. `stat_right`: Symmetric. `root_left`: Symmetric. `root_right`: Symmetric.
All inputs are finite; a program needn't handle non-finite values.
Results may differ from the reference program's by a relative error of at most 0.0085.
Values may be sent and summed in bfloat16 or wider, within the bound.
A program may use at most 448 MiB of HBM per device.

```python
import math
import jax
import jax.numpy as jnp
from jax import lax

D = 1120
HEADS = 20
FF = 4480
BS = 280
LEN = 2048
GB = 256
PREFIX = 128
CELLS = 16
TOKENS = 32768
NB = 192


def slot_blocks(key):
    return jax.random.permutation(jax.random.fold_in(key, 11), NB).astype(jnp.int32)


def slot_spread(key):
    blocks = slot_blocks(key)
    square = D // BS * (D // BS)
    up_end = 4 * square + D // BS * (FF // BS)
    out_fan = max(D // 100, 1)
    spread = jnp.where(blocks < 3 * square, D ** (-0.5), jnp.where(blocks < 4 * square, out_fan ** (-0.5), jnp.where(blocks < up_end, D ** (-0.5), FF ** (-0.5))))
    return spread.astype(jnp.float32)


def stat_scale(key):
    blocks = slot_blocks(key)
    square = D // BS * (D // BS)
    up_end = 4 * square + D // BS * (FF // BS)
    out_fan = max(D // 100, 1)
    scale = jnp.where(blocks < 3 * square, 0.05 * D / out_fan, jnp.where(blocks < 4 * square, 0.1, jnp.where(blocks < up_end, 0.12, 0.4)))
    return scale.astype(jnp.float32)


def base_noise(key, offset):
    inner_key = jax.random.fold_in(key, offset)
    return jnp.clip(jax.random.normal(inner_key, (NB, BS, BS), jnp.float32), -6.0, 6.0)


def weight_like(key, offset):
    return base_noise(key, offset) * slot_spread(key)[:, None, None]


def symmetric_draw(key, offset, low_end, high_end, slot_scale):
    noise_base = base_noise(key, offset)
    symmetric = (noise_base + jnp.swapaxes(noise_base, 1, 2)) * (0.25 / math.sqrt(2.0 * BS))
    levels = jnp.exp(jax.random.uniform(jax.random.fold_in(key, offset + 100), (NB,), jnp.float32, math.log(low_end), math.log(high_end)))
    levels = levels * slot_scale
    return levels[:, None, None] * (jnp.eye(BS, dtype=jnp.float32)[None] + symmetric)


def draw_pad_mask(key, part):
    first_key, second_key = jax.random.split(jax.random.fold_in(key, 31))
    lengths = jax.random.randint(first_key, (CELLS,), LEN // 4, LEN + 1)
    longest = jax.random.randint(second_key, (), 0, CELLS)
    lengths = jnp.where(jnp.arange(CELLS) == longest, LEN, lengths)
    return (jnp.arange(LEN)[None, :] < lengths[:, None]).astype(jnp.int32)


def draw_owner_map(key, part):
    return slot_blocks(key)


def draw_weight_copy(key, part):
    return weight_like(key, 21).astype(jnp.bfloat16)


def draw_master(key, part):
    return weight_like(key, 22)


def draw_average_weights(key, part):
    return weight_like(key, 23)


def draw_stat_left(key, part):
    return symmetric_draw(key, 41, 1.0, 4.0, stat_scale(key))


def draw_stat_right(key, part):
    return symmetric_draw(key, 42, 1.0, 4.0, stat_scale(key))


def draw_root_left(key, part):
    return symmetric_draw(key, 43, 1.0, 2.0, jnp.ones((NB,), jnp.float32))


def draw_root_right(key, part):
    return symmetric_draw(key, 44, 1.0, 2.0, jnp.ones((NB,), jnp.float32))


def touch_ends(drawn, own_key, low, top_value):
    place = [jax.random.randint(jax.random.fold_in(own_key, axis), (), 0, length) for axis, length in enumerate(drawn.shape)]
    main_axis = drawn.shape.index(max(drawn.shape))
    beside = place[:main_axis] + [(place[main_axis] + 1) % drawn.shape[main_axis]] + place[main_axis + 1:]
    return drawn.at[tuple(place)].set(low).at[tuple(beside)].set(top_value)


def level_of(stream_key, dims, cuts, smallest, high):
    gain, own = 1.0, jax.random.fold_in(stream_key, 6)
    for dim, parts in cuts:
        draws = jnp.exp(jax.random.uniform(jax.random.fold_in(own, dim), (parts,), jnp.float32, smallest / len(cuts), high / len(cuts)))
        gain = gain * jnp.repeat(draws, dims[dim] // parts).reshape([-1 if axis == dim else 1 for axis in range(len(dims))])
    return gain


def bell_draw(rng, dims, scale, bound, cuts=(), held_as=jnp.bfloat16):
    drawn = scale * jax.random.normal(rng, dims, jnp.float32)
    if cuts:
        drawn = drawn * level_of(rng, dims, cuts, -0.22, 0.18)
    return jnp.clip(drawn, -bound, bound).astype(held_as)


def setup_inputs(seed: int = 0) -> dict:
    arg_keys = jax.random.split(jax.random.key(seed), 15)
    return {
        "tokens": bell_draw(arg_keys[0], (CELLS, LEN, D), 1.0, 6.0, ((0, 16), (1, 2))),
        "cotangent": bell_draw(arg_keys[1], (CELLS, LEN, D), 1.0, 6.0, ((0, 16), (1, 2))),
        "pad_mask": draw_pad_mask(jax.random.fold_in(arg_keys[14], 71), 0),
        "prefix_len": touch_ends(jax.random.randint(arg_keys[3], (CELLS,), 1, PREFIX + 1), jax.random.fold_in(arg_keys[3], 1), 1, PREFIX).astype(jnp.int32),
        "norm_gains": jnp.clip(1.0 + 0.1 * jax.random.normal(arg_keys[4], (2, D), jnp.float32), 0.5, 1.5),
        "norm_shifts": bell_draw(arg_keys[5], (2, D), 0.3, 1.8, (), jnp.float32),
        "owner_map": draw_owner_map(jax.random.fold_in(arg_keys[14], 71), 0),
        "weight_copy": draw_weight_copy(jax.random.fold_in(arg_keys[14], 71), 0),
        "master": draw_master(jax.random.fold_in(arg_keys[14], 71), 0),
        "average_weights": draw_average_weights(jax.random.fold_in(arg_keys[14], 71), 0),
        "stat_left": draw_stat_left(jax.random.fold_in(arg_keys[14], 71), 0),
        "stat_right": draw_stat_right(jax.random.fold_in(arg_keys[14], 71), 0),
        "root_left": draw_root_left(jax.random.fold_in(arg_keys[14], 71), 0),
        "root_right": draw_root_right(jax.random.fold_in(arg_keys[14], 71), 0),
    }


@jax.custom_vjp
def low(v):
    return lax.optimization_barrier(v.astype(jnp.bfloat16)).astype(jnp.float32)

@jax.custom_vjp
def low_back(v):
    return v

def low_keep(v):
    return (low(v), None)

def low_pass(kept, grad):
    return (grad,)

def back_keep(v):
    return (v, None)

def back_low(kept, grad):
    return (low(grad),)
low.defvjp(low_keep, low_pass)
low_back.defvjp(back_keep, back_low)
highest = lax.Precision.HIGHEST

def both_round(values):
    return low(low_back(values))

def layer_norm(values, gain_row, shift_row):
    average = lax.optimization_barrier(jnp.mean(values, axis=-1, keepdims=True))
    centred = values - average
    variance = lax.optimization_barrier(jnp.mean(centred * centred, axis=-1, keepdims=True))
    return centred * lax.rsqrt(variance + 1e-05) * gain_row + shift_row

def assemble(pieces, row_blocks, col_blocks):
    block_size = pieces.shape[-1]
    return pieces.reshape(row_blocks, col_blocks, block_size, block_size).transpose(0, 2, 1, 3).reshape(row_blocks * block_size, col_blocks * block_size)

def split_blocks(matrix, block_size):
    row_count, col_count = matrix.shape
    return matrix.reshape(row_count // block_size, block_size, col_count // block_size, block_size).transpose(0, 2, 1, 3).reshape(-1, block_size, block_size)

def cell_layer(inputs, alive_keys, w_query, w_key, w_value, w_out, w_up, w_down, gains, shifts):
    length, features = inputs.shape
    per_cell = length // GB
    head_size = features // HEADS
    normed_in = low(layer_norm(inputs, gains[0], shifts[0]))
    queries = both_round(jnp.dot(normed_in, w_query, precision=highest))
    key_rows = both_round(jnp.dot(normed_in, w_key, precision=highest))
    value_rows = both_round(jnp.dot(normed_in, w_value, precision=highest))
    query_blocks = queries.reshape(per_cell, GB, HEADS, head_size)
    key_blocks = key_rows.reshape(per_cell, GB, HEADS, head_size)
    value_blocks = value_rows.reshape(per_cell, GB, HEADS, head_size)
    prefix_keys = key_rows[:PREFIX].reshape(PREFIX, HEADS, head_size)
    prefix_values = value_rows[:PREFIX].reshape(PREFIX, HEADS, head_size)
    raw_prefix = low_back(jnp.einsum('nqhd,khd->nhqk', query_blocks, prefix_keys, precision=highest))
    raw_local = low_back(jnp.einsum('nqhd,nkhd->nhqk', query_blocks, key_blocks, precision=highest))
    offsets = jnp.arange(GB)
    local_seen = alive_keys.reshape(per_cell, 1, 1, GB) & (offsets[:, None] >= offsets[None, :])[None, None]
    prefix_seen = alive_keys[:PREFIX].reshape(1, 1, 1, PREFIX) & (jnp.arange(per_cell) > 0).reshape(per_cell, 1, 1, 1)
    visible = jnp.concatenate([jnp.broadcast_to(prefix_seen, (per_cell, 1, GB, PREFIX)), jnp.broadcast_to(local_seen, (per_cell, 1, GB, GB))], axis=-1)
    scores = jnp.where(visible, jnp.concatenate([raw_prefix, raw_local], axis=-1) * head_size ** (-0.5), -1e+30)
    row_max = lax.optimization_barrier(jnp.max(scores, axis=-1, keepdims=True))
    exponent = jnp.exp(scores - row_max)
    key_weights = exponent / lax.optimization_barrier(jnp.sum(exponent, axis=-1, keepdims=True))
    weights_low = low(key_weights)
    attended = jnp.einsum('nhqk,khd->nqhd', weights_low[..., :PREFIX], prefix_values, precision=highest)
    attended = attended + jnp.einsum('nhqk,nkhd->nqhd', weights_low[..., PREFIX:], value_blocks, precision=highest)
    attended = both_round(attended.reshape(length, features))
    middle = inputs + low_back(jnp.dot(attended, w_out, precision=highest))
    normed_mid = low(layer_norm(middle, gains[1], shifts[1]))
    up_pre = low_back(jnp.dot(normed_mid, w_up, precision=highest))
    activated = low(jax.nn.gelu(up_pre, approximate=True))
    return middle + low_back(jnp.dot(activated, w_down, precision=highest))

def reference(tokens, cotangent, pad_mask, prefix_len, norm_gains, norm_shifts, owner_map, weight_copy, master, average_weights, stat_left, stat_right, root_left, root_right):
    block_count = owner_map.shape[0]
    row_blocks = D // BS
    col_blocks = FF // BS
    square = row_blocks * row_blocks
    inverse = jnp.zeros((block_count,), jnp.int32).at[owner_map].set(jnp.arange(block_count, dtype=jnp.int32))
    blocks = weight_copy.astype(jnp.float32)[inverse]
    w_query = assemble(blocks[0:square], row_blocks, row_blocks)
    w_key = assemble(blocks[square:2 * square], row_blocks, row_blocks)
    w_value = assemble(blocks[2 * square:3 * square], row_blocks, row_blocks)
    w_out = assemble(blocks[3 * square:4 * square], row_blocks, row_blocks)
    w_up = assemble(blocks[4 * square:4 * square + row_blocks * col_blocks], row_blocks, col_blocks)
    w_down = assemble(blocks[4 * square + row_blocks * col_blocks:], col_blocks, row_blocks)
    position = jnp.arange(LEN, dtype=jnp.int32)
    alive_keys = jnp.where(position[None, :] < PREFIX, position[None, :] < prefix_len[:, None], pad_mask == 1)

    def forward(inputs, m_query, m_key, m_value, m_out, m_up, m_down, gains, shifts):

        def one_cell(cell_pair):
            return cell_layer(cell_pair[0], cell_pair[1], m_query, m_key, m_value, m_out, m_up, m_down, gains, shifts)
        return lax.map(jax.checkpoint(one_cell), (inputs, alive_keys))
    result, backward = jax.vjp(forward, tokens.astype(jnp.float32), w_query, w_key, w_value, w_out, w_up, w_down, norm_gains, norm_shifts)
    grads = backward(cotangent.astype(jnp.float32))
    grad_scale = 1.0 / math.sqrt(TOKENS)
    grad_blocks = jnp.concatenate([split_blocks(matrix, BS) for matrix in grads[1:7]], axis=0) * grad_scale
    slot_grad = grad_blocks[owner_map]
    norm_grad = jnp.stack([grads[7][0], grads[8][0], grads[7][1], grads[8][1]]) * grad_scale
    params = jnp.stack([norm_gains[0], norm_shifts[0], norm_gains[1], norm_shifts[1]])
    new_norms = params - 0.1 * norm_grad * lax.rsqrt(jnp.mean(norm_grad * norm_grad) + 1e-06)
    new_left = 0.5 * stat_left + 0.5 * jnp.einsum('sij,skj->sik', slot_grad, slot_grad, precision=highest) / BS
    new_right = 0.5 * stat_right + 0.5 * jnp.einsum('sji,sjk->sik', slot_grad, slot_grad, precision=highest) / BS
    right_part = jnp.einsum('sij,sjk->sik', slot_grad, root_right, precision=highest)
    precond = jnp.einsum('sij,sjk->sik', root_left, right_part, precision=highest)
    new_master = master - 0.03 * precond
    new_copy = new_master.astype(jnp.bfloat16)
    new_average = 0.8 * average_weights + 0.2 * new_master
    return (result.astype(jnp.bfloat16), grads[0], norm_grad, new_norms, slot_grad, new_left, new_right, new_master, new_copy, new_average)
```

```python
import functools
import math

import jax
import jax.numpy as jnp
from jax import lax
from jax.experimental import pallas as pl
from jax.experimental.pallas import tpu as pltpu
from jax.sharding import PartitionSpec as P

HEADS = 20
GB = 256
PREFIX = 128
HALF = GB // 2
MESH = pl.DeviceIdType.MESH
BF16 = jnp.bfloat16
F32 = jnp.float32

MAIN = 256
RUN = 32


def runs(size):
    rest, per_tile = size - MAIN, 128 // (size - MAIN)
    places = []
    for index in range(-(-size // RUN)):
        lane = 128 * (index // per_tile) + rest * (index % per_tile)
        places.append((RUN * index, min(RUN, size - RUN * index), lane))
    assert places[-1][2] + rest <= MAIN
    return places


def pack_tail(block):
    size = block.shape[0]
    rest = size - MAIN
    pieces, lane = [], 0
    for row, count, start in runs(size):
        if start > lane:
            pieces.append(jnp.zeros((RUN, start - lane), block.dtype))
        piece = block[row : row + count, MAIN:]
        if count < RUN:
            piece = jnp.concatenate([piece, jnp.zeros((RUN - count, rest), block.dtype)], axis=0)
        pieces.append(piece)
        lane = start + rest
    if lane < MAIN:
        pieces.append(jnp.zeros((RUN, MAIN - lane), block.dtype))
    return jnp.concatenate(pieces, axis=1)


def unpack(packed):
    size = packed.shape[0] - RUN
    rest = size - MAIN
    low = packed[size:]
    tail = [low[:count, lane : lane + rest] for _, count, lane in runs(size)]
    return jnp.concatenate([packed[:size], jnp.concatenate(tail, axis=0)], axis=1)


def tn(left, right):
    return lax.dot_general(left, right, (((0,), (0,)), ((), ())), preferred_element_type=F32)


def nn(left, right):
    return lax.dot_general(left, right, (((1,), (0,)), ((), ())), preferred_element_type=F32)


def nt(left, right):
    return lax.dot_general(left, right, (((1,), (1,)), ((), ())), preferred_element_type=F32)


def cost(flops, moved, exps=0):
    return pl.CostEstimate(flops=int(flops), bytes_accessed=int(moved), transcendentals=int(exps))


def pack_kernel(chip, block, packed):
    del chip
    size = block.shape[1]
    values = block[0].astype(F32)
    packed[0, :size] = values[:, :MAIN].astype(BF16)
    packed[0, size:] = pack_tail(values).astype(BF16)


def pack_slots(blocks, chip, slot_count):
    count, size, _ = blocks.shape
    return pl.pallas_call(
        pack_kernel,
        grid_spec=pltpu.PrefetchScalarGridSpec(
            num_scalar_prefetch=1,
            grid=(count,),
            in_specs=[pl.BlockSpec((1, size, size), lambda i, chip: (i, 0, 0))],
            out_specs=pl.BlockSpec((1, size + RUN, MAIN), lambda i, chip: (chip[0] * count + i, 0, 0)),
        ),
        out_shape=jax.ShapeDtypeStruct((slot_count, size + RUN, MAIN), BF16),
        name="pack_slots",
    )(chip, blocks)


def place():
    me, core = lax.axis_index("dp"), lax.axis_index("seq")
    x, y, z = me % 2, (me // 2) % 2, me // 4
    step_x, step_y = 1 - 2 * x, 2 * (1 - 2 * y)
    first = step_y * (1 - core) + step_x * core
    second = step_x * (1 - core) + step_y * core
    return me, core, z, first, second


def greet(partners):
    barrier = pltpu.get_barrier_semaphore()
    for chip, core in partners:
        pl.semaphore_signal(barrier, inc=1, device_id=(chip, core), device_id_type=MESH)
    pl.semaphore_wait(barrier, len(partners))


UP, DOWN, FIRST, SECOND, TWIN, GATHER_LABELS = 0, 4, 8, 12, 20, 36


def gather_kernel(slots, placed, out, send, recv):
    del placed
    me, core, z, first, second = place()
    half = slots // 2
    line = [(me + 4 * ((z + r) % 4 - z), core) for r in range(1, 4)]
    greet([(me + first, core), (me + second, core), (me, 1 - core)] + line)

    def copy(label, chip, dp, c):
        ref = out.at[pl.ds(chip * slots + core * half, half)]
        return pltpu.make_async_remote_copy(
            src_ref=ref,
            dst_ref=ref,
            send_sem=send.at[label],
            recv_sem=recv.at[label],
            device_id=(dp, c),
            device_id_type=MESH,
        )

    def arrival(label):
        ref = out.at[pl.ds(0, half)]
        return pltpu.make_async_remote_copy(
            src_ref=ref,
            dst_ref=ref,
            send_sem=send.at[label],
            recv_sem=recv.at[label],
            device_id=(me, 1 - core),
            device_id_type=MESH,
        )

    def col(zz):
        return me + 4 * (zz - z)

    def up(j):
        return copy(UP + j, me - 4 * (j - 1), me + 4, core)

    def down(j):
        return copy(DOWN + j, me + 4 * (j - 1), me - 4, core)

    def to_first(zz):
        return copy(FIRST + zz, col(zz), me + first, core)

    def to_second(zz, a):
        return copy(SECOND + 2 * zz + a, col(zz) + a * first, me + second, core)

    def to_twin(chip):
        return copy(TWIN + chip, chip, me, 1 - core)

    def spread(zz, own=False):
        to_first(zz).start()
        to_second(zz, 0).start()
        if not own:
            to_twin(col(zz)).start()

    def after_first(zz):
        to_first(zz).wait_recv()
        to_second(zz, 1).start()
        to_twin(col(zz) + first).start()

    def after_second(zz):
        for a in range(2):
            to_second(zz, a).wait_recv()
            to_twin(col(zz) + second + a * first).start()

    @pl.when(z < 3)
    def _():
        up(1).start()

    @pl.when(z > 0)
    def _():
        down(1).start()

    spread(z, own=True)
    for j in range(1, 4):

        @pl.when(z >= j)
        def _():
            up(j).wait_recv()
            if j < 3:

                @pl.when(z < 3)
                def _():
                    up(j + 1).start()

            spread(z - j)

        @pl.when(z + j <= 3)
        def _():
            down(j).wait_recv()
            if j < 3:

                @pl.when(z > 0)
                def _():
                    down(j + 1).start()

            spread(z + j)

        if j == 1:
            after_first(z)
        else:

            @pl.when(z >= j - 1)
            def _():
                after_first(z - (j - 1))

            @pl.when(z + j - 1 <= 3)
            def _():
                after_first(z + j - 1)

    @pl.when(z >= 3)
    def _():
        after_first(z - 3)

    @pl.when(z <= 0)
    def _():
        after_first(z + 3)

    after_second(z)
    for j in range(1, 4):

        @pl.when(z >= j)
        def _():
            after_second(z - j)

        @pl.when(z + j <= 3)
        def _():
            after_second(z + j)

    for zz in range(4):
        for a in range(2):
            for b in range(2):
                chip = col(zz) + a * first + b * second
                if a == 0 and b == 0:

                    @pl.when(zz != z)
                    def _():
                        to_twin(chip).wait_recv()
                        to_twin(chip).wait_send()

                else:
                    to_twin(chip).wait_recv()
                    to_twin(chip).wait_send()
        to_first(zz).wait_send()
        for a in range(2):
            to_second(zz, a).wait_send()

    @pl.when(z < 3)
    def _():
        up(1).wait_send()
        for j in range(1, 3):

            @pl.when(z >= j)
            def _():
                up(j + 1).wait_send()

    @pl.when(z > 0)
    def _():
        down(1).wait_send()
        for j in range(1, 3):

            @pl.when(z + j <= 3)
            def _():
                down(j + 1).wait_send()


def gather_slots(placed, slots):
    return pl.pallas_call(
        functools.partial(gather_kernel, slots),
        out_shape=jax.ShapeDtypeStruct(placed.shape, placed.dtype),
        in_specs=[pl.BlockSpec(memory_space=pl.ANY)],
        out_specs=pl.BlockSpec(memory_space=pl.ANY),
        scratch_shapes=[pltpu.SemaphoreType.DMA((GATHER_LABELS,)), pltpu.SemaphoreType.DMA((GATHER_LABELS,))],
        input_output_aliases={0: 0},
        compiler_params=pltpu.CompilerParams(collective_id=0, has_side_effects=True),
        name="gather_slots",
    )(placed)


R_TWIN, R_SECOND, R_FIRST, R_LINE, R_DONE, REDUCE_LABELS = 0, 16, 24, 28, 32, 33


def reduce_kernel(slots, grads, out, own, r_twin, r_second, r_first, r_line, total, load, send, recv, save):
    me, core, z, first, second = place()
    half = slots // 2
    line = [(me + 4 * ((z + r) % 4 - z), core) for r in range(1, 4)]
    greet([(me + first, core), (me + second, core), (me, 1 - core)] + line)

    def piece(chip, h):
        return grads.at[pl.ds(chip * slots + h * half, half)]

    def chip_at(zz, a, b):
        return me + 4 * (zz - z) + a * first + b * second

    def load_own(zz, a, b):
        chip = chip_at(zz, a, b)
        return pltpu.make_async_copy(piece(chip, core), own.at[chip], load.at[chip])

    def remote(src, dst, label, dp, c):
        return pltpu.make_async_remote_copy(
            src_ref=src,
            dst_ref=dst,
            send_sem=send.at[label],
            recv_sem=recv.at[label],
            device_id=(dp, c),
            device_id_type=MESH,
        )

    def twin(zz, a, b):
        chip = chip_at(zz, a, b)
        return remote(piece(chip, 1 - core), r_twin.at[chip], R_TWIN + chip, me, 1 - core)

    def to_second(zz, a):
        return remote(
            r_twin.at[chip_at(zz, a, 1)], r_second.at[2 * zz + a], R_SECOND + 2 * zz + a, me + second, core
        )

    def to_first(zz):
        return remote(r_twin.at[chip_at(zz, 1, 0)], r_first.at[zz], R_FIRST + zz, me + first, core)

    def to_line(r):
        zz = (z + r) % 4
        return remote(r_twin.at[chip_at(zz, 0, 0)], r_line.at[r - 1], R_LINE + r, chip_at(zz, 0, 0), core)

    def add_up(chip, others):
        def body(s, carry):
            value = own[chip, s].astype(F32) + r_twin[chip, s].astype(F32)
            for ref, index in others:
                value = value + ref[index, s].astype(F32)
            r_twin[chip, s] = value.astype(BF16)
            return carry

        lax.fori_loop(0, half, body, 0)

    def ready(zz, a, b):
        load_own(zz, a, b).wait()
        twin(zz, a, b).wait_recv()

    def send_second(zz, a):
        ready(zz, a, 1)
        add_up(chip_at(zz, a, 1), [])
        to_second(zz, a).start()

    def send_first(zz):
        ready(zz, 1, 0)
        to_second(zz, 1).wait_recv()
        add_up(chip_at(zz, 1, 0), [(r_second, 2 * zz + 1)])
        to_first(zz).start()

    def send_line(r):
        zz = (z + r) % 4
        ready(zz, 0, 0)
        to_second(zz, 0).wait_recv()
        to_first(zz).wait_recv()
        add_up(chip_at(zz, 0, 0), [(r_second, 2 * zz), (r_first, zz)])
        to_line(r).start()

    order = [2, 1, 3, 0]
    where = [(z + r) % 4 for r in order]
    for zz in where:
        for a in (1, 0):
            load_own(zz, a, 1).start()
            twin(zz, 1, a).start()
    for zz in where:
        for a in (1, 0):
            load_own(zz, a, 0).start()
            twin(zz, 0, a).start()

    def send_both(index):
        for a in (1, 0):
            send_second(where[index], a)

    send_both(0)
    send_both(1)
    send_both(2)
    send_first(where[0])
    send_both(3)
    send_first(where[1])
    send_line(order[0])
    send_first(where[2])
    send_line(order[1])
    send_first(where[3])
    send_line(order[2])

    ready(z, 0, 0)
    to_second(z, 0).wait_recv()
    to_first(z).wait_recv()
    for r in range(1, 4):
        to_line(r).wait_recv()

    def body(s, carry):
        value = own[me, s].astype(F32) + r_twin[me, s].astype(F32)
        value = value + r_second[2 * z, s].astype(F32)
        value = value + r_first[z, s].astype(F32)
        for r in range(3):
            value = value + r_line[r, s].astype(F32)
        total[s] = value
        return carry

    lax.fori_loop(0, half, body, 0)
    target = out.at[pl.ds(core * half, half)]
    done = remote(total, target, R_DONE, me, 1 - core)
    done.start()
    saved = pltpu.make_async_copy(total, target, save.at[0])
    saved.start()
    for zz in range(4):
        for a in range(2):
            for b in range(2):
                twin(zz, a, b).wait_send()
            to_second(zz, a).wait_send()
        to_first(zz).wait_send()
    for r in range(1, 4):
        to_line(r).wait_send()
    done.wait()
    saved.wait()


def reduce_slots(grads, slots):
    _, rows, lanes = grads.shape
    half = slots // 2
    pieces = lambda n: pltpu.VMEM((n, half, rows, lanes), BF16)
    return pl.pallas_call(
        functools.partial(reduce_kernel, slots),
        out_shape=jax.ShapeDtypeStruct((slots, rows, lanes), F32),
        in_specs=[pl.BlockSpec(memory_space=pl.ANY)],
        out_specs=pl.BlockSpec(memory_space=pl.ANY),
        scratch_shapes=[
            pieces(16),
            pieces(16),
            pieces(8),
            pieces(4),
            pieces(3),
            pltpu.VMEM((half, rows, lanes), F32),
            pltpu.SemaphoreType.DMA((16,)),
            pltpu.SemaphoreType.DMA((REDUCE_LABELS,)),
            pltpu.SemaphoreType.DMA((REDUCE_LABELS,)),
            pltpu.SemaphoreType.DMA((1,)),
        ],
        compiler_params=pltpu.CompilerParams(collective_id=1, has_side_effects=True, vmem_limit_bytes=60 << 20),
        name="reduce_slots",
    )(grads)


def assemble_kernel(slot_of, *refs):
    del slot_of
    out = refs[-1]
    size = out.shape[0]
    for j, block in enumerate(refs[:-1]):
        out[:, size * j : size * (j + 1)] = unpack(block[0].astype(F32)).astype(BF16)


def assemble(gathered, slot_of, rows, cols, block_of, name):
    packed_rows, lanes = gathered.shape[1:]
    size = packed_rows - RUN
    specs = [
        pl.BlockSpec((1, packed_rows, lanes), functools.partial(lambda j, i, v: (v[block_of(i, j)], 0, 0), j))
        for j in range(cols)
    ]
    return pl.pallas_call(
        assemble_kernel,
        grid_spec=pltpu.PrefetchScalarGridSpec(
            num_scalar_prefetch=1,
            grid=(rows,),
            in_specs=specs,
            out_specs=pl.BlockSpec((size, size * cols), lambda i, v: (i, 0)),
        ),
        out_shape=jax.ShapeDtypeStruct((size * rows, size * cols), BF16),
        name=name,
    )(slot_of, *([gathered] * cols))


def weight_grad_kernel(block_of, deep, size, slot_of, left, right, *refs):
    grads, stage, sem = refs[-3:]
    wide = right.shape[0] // size
    rows, cols = pl.program_id(0), pl.program_id(1)
    step = rows * pl.num_programs(1) + cols
    steps = pl.num_programs(0) * pl.num_programs(1)
    now = step % 2

    def copy(buffer, index, slot):
        return pltpu.make_async_copy(stage.at[buffer, index], grads.at[slot], sem.at[buffer, index])

    @pl.when(step >= 2)
    def _():
        for index in range(deep * wide):
            copy(now, index, 0).wait()

    other = right[...]
    for i in range(deep):
        panel = nt(left[size * i : size * (i + 1), :], other)
        for j in range(wide):
            index = i * wide + j
            block = panel[:, size * j : size * (j + 1)]
            stage[now, index, :size] = block[:, :MAIN].astype(BF16)
            stage[now, index, size:] = pack_tail(block).astype(BF16)
            copy(now, index, slot_of[block_of(rows * deep + i, cols * wide + j)]).start()

    @pl.when(step == steps - 1)
    def _():
        for index in range(deep * wide):
            copy(now, index, 0).wait()

        @pl.when(steps > 1)
        def _():
            for index in range(deep * wide):
                copy(1 - now, index, 0).wait()


def weight_grad(left, right, slot_of, grads, slot_count, size, block_of, name):
    depth = left.shape[1]
    deep = wide = 4
    grid = (left.shape[0] // (size * deep), right.shape[0] // (size * wide))
    anywhere = pl.BlockSpec(memory_space=pl.ANY)
    operands = [slot_of, left, right] + ([] if grads is None else [grads])
    return pl.pallas_call(
        functools.partial(weight_grad_kernel, block_of, deep, size),
        grid_spec=pltpu.PrefetchScalarGridSpec(
            num_scalar_prefetch=1,
            grid=grid,
            in_specs=[
                pl.BlockSpec((size * deep, depth), lambda i, j, v: (i, 0)),
                pl.BlockSpec((size * wide, depth), lambda i, j, v: (j, 0)),
            ]
            + [anywhere] * (len(operands) - 3),
            out_specs=anywhere,
            scratch_shapes=[
                pltpu.VMEM((2, deep * wide, size + RUN, MAIN), BF16),
                pltpu.SemaphoreType.DMA((2, deep * wide)),
            ],
        ),
        out_shape=jax.ShapeDtypeStruct((slot_count, size + RUN, MAIN), BF16),
        input_output_aliases={} if grads is None else {3: 0},
        cost_estimate=cost(
            2 * left.shape[0] * right.shape[0] * depth,
            2 * (left.size + right.size + left.shape[0] * right.shape[0]),
        ),
        name=name,
    )(*operands)


def attention_kernel(scale, qkv, low, high, out, lse):
    for group in range(low.shape[0]):
        base = PREFIX + GB * group
        for h in range(2):
            seen = slice(base, base + HALF * (h + 1))
            keys = jnp.concatenate([qkv[1, :, :PREFIX], qkv[1, :, seen]], axis=1)
            values = jnp.concatenate([qkv[2, :, :PREFIX], qkv[2, :, seen]], axis=1)
            queries = qkv[0, :, base + HALF * h : base + HALF * (h + 1)]
            scores = tn(keys, queries) * scale + (high if h else low)[group]
            top = jnp.max(scores, axis=0, keepdims=True)
            weights = jnp.exp(scores - top)
            total = jnp.sum(weights, axis=0, keepdims=True)
            mine = slice(GB * group + HALF * h, GB * group + HALF * (h + 1))
            out[:, mine] = (nn(values, weights.astype(BF16)) / total).astype(BF16)
            lse[0, :, mine] = top + jnp.log(total)


def attention_back_kernel(scale, qkv, low, high, out, lse, grad_out, grads):
    prefix_k = jnp.zeros((out.shape[0], PREFIX), F32)
    prefix_v = prefix_k
    for group in range(low.shape[0]):
        base = PREFIX + GB * group
        grad_k, grad_v = [None, None], [None, None]
        for h in range(2):
            seen = slice(base, base + HALF * (h + 1))
            keys = jnp.concatenate([qkv[1, :, :PREFIX], qkv[1, :, seen]], axis=1)
            values = jnp.concatenate([qkv[2, :, :PREFIX], qkv[2, :, seen]], axis=1)
            own = slice(base + HALF * h, base + HALF * (h + 1))
            mine = slice(GB * group + HALF * h, GB * group + HALF * (h + 1))
            queries = qkv[0, :, own]
            grad_o = grad_out[:, mine]
            delta = jnp.sum(grad_o.astype(F32) * out[:, mine].astype(F32), axis=0, keepdims=True)
            weights = jnp.exp(tn(keys, queries) * scale + (high if h else low)[group] - lse[0, :, mine])
            grad_s = weights * (tn(values, grad_o) - delta)
            grad_raw = (grad_s * scale).astype(BF16)
            grads[0, :, own] = nn(keys, grad_raw).astype(BF16)
            all_k = nt(queries, grad_raw)
            all_v = nt(grad_o, weights.astype(BF16))
            prefix_k = prefix_k + all_k[:, :PREFIX]
            prefix_v = prefix_v + all_v[:, :PREFIX]
            for i in range(h + 1):
                part = slice(PREFIX + HALF * i, PREFIX + HALF * (i + 1))
                grad_k[i] = all_k[:, part] if grad_k[i] is None else grad_k[i] + all_k[:, part]
                grad_v[i] = all_v[:, part] if grad_v[i] is None else grad_v[i] + all_v[:, part]
        for i in range(2):
            part = slice(base + HALF * i, base + HALF * (i + 1))
            grads[1, :, part] = grad_k[i].astype(BF16)
            grads[2, :, part] = grad_v[i].astype(BF16)
    grads[0, :, :PREFIX] = jnp.zeros((out.shape[0], PREFIX), BF16)
    grads[1, :, :PREFIX] = prefix_k.astype(BF16)
    grads[2, :, :PREFIX] = prefix_v.astype(BF16)


def attention_specs(qkv, low, high):
    _, features, length = qkv.shape
    head, own = features // HEADS, length - PREFIX
    whole = lambda array: pl.BlockSpec(array.shape, lambda h: (0,) * array.ndim)
    three = pl.BlockSpec((3, head, length), lambda h: (0, h, 0))
    one = pl.BlockSpec((head, own), lambda h: (h, 0))
    row = pl.BlockSpec((1, 1, own), lambda h: (h, 0, 0))
    return features, own, head, [three, whole(low), whole(high)], one, row, three


def attention(qkv, low, high):
    features, own, head, specs, one, row, _ = attention_specs(qkv, low, high)
    return pl.pallas_call(
        functools.partial(attention_kernel, head ** (-0.5)),
        grid=(HEADS,),
        in_specs=specs,
        out_specs=[one, row],
        out_shape=[
            jax.ShapeDtypeStruct((features, own), BF16),
            jax.ShapeDtypeStruct((HEADS, 1, own), F32),
        ],
        cost_estimate=cost(8 * features * own * GB, 2 * qkv.size, HEADS * own * GB),
        name="attention",
    )(qkv, low, high)


def attention_back(qkv, low, high, out, lse, grad_out):
    features, own, head, specs, one, row, three = attention_specs(qkv, low, high)
    return pl.pallas_call(
        functools.partial(attention_back_kernel, head ** (-0.5)),
        grid=(HEADS,),
        in_specs=specs + [one, row, one],
        out_specs=three,
        out_shape=jax.ShapeDtypeStruct(qkv.shape, BF16),
        cost_estimate=cost(20 * features * own * GB, 4 * qkv.size, HEADS * own * GB),
        name="attention_back",
    )(qkv, low, high, out, lse, grad_out)


def score_biases(alive, prefix_alive, later):
    groups = alive.shape[0] // GB
    live = alive.reshape(groups, GB, 1)
    square = (groups, HALF, HALF)
    prefix = jnp.broadcast_to(prefix_alive[None, :, None] & later[:, None, None], (groups, PREFIX, HALF))
    ahead = (jnp.arange(HALF)[:, None] <= jnp.arange(HALF)[None, :])[None]
    low = jnp.concatenate([prefix, live[:, :HALF] & ahead], axis=1)
    high = jnp.concatenate([prefix, jnp.broadcast_to(live[:, :HALF], square), live[:, HALF:] & ahead], axis=1)
    return jnp.where(low, 0.0, -1e30).astype(F32), jnp.where(high, 0.0, -1e30).astype(F32)


def split(values):
    high = values.astype(BF16)
    return high, (values - high.astype(F32)).astype(BF16)


def product(form, left, right):
    (left_high, left_low), (right_high, right_low) = left, right
    return form(left_high, right_high) + (form(left_high, right_low) + form(left_low, right_high))


def optimizer_kernel(scale, packed, master, average, left, right, root_left, root_right, *outs):
    slot_grad, new_left, new_right, new_master, new_copy, new_average = outs
    size = master.shape[1]
    grad = unpack(packed[0]) * scale
    slot_grad[0] = grad
    grad_parts = split(grad)
    new_left[0] = 0.5 * left[0] + (0.5 / size) * product(nt, grad_parts, grad_parts)
    new_right[0] = 0.5 * right[0] + (0.5 / size) * product(tn, grad_parts, grad_parts)
    right_part = product(nn, grad_parts, split(root_right[0]))
    step = product(nn, split(root_left[0]), split(right_part))
    moved = master[0] - 0.03 * step
    new_master[0] = moved
    new_copy[0] = moved.astype(BF16)
    new_average[0] = 0.8 * average[0] + 0.2 * moved


def optimizer(packed, scale, arrays):
    slots, size, _ = arrays[0].shape
    block = pl.BlockSpec((1, size, size), lambda i: (i, 0, 0))
    shape = lambda dtype: jax.ShapeDtypeStruct((slots, size, size), dtype)
    return pl.pallas_call(
        functools.partial(optimizer_kernel, scale),
        grid=(slots,),
        in_specs=[pl.BlockSpec((1,) + packed.shape[1:], lambda i: (i, 0, 0))] + [block] * 6,
        out_specs=[block] * 6,
        out_shape=[shape(F32), shape(F32), shape(F32), shape(F32), shape(BF16), shape(F32)],
        name="optimizer",
    )(packed, *arrays)


def norm_parts(values):
    average = jnp.mean(values, axis=0, keepdims=True)
    centred = values - average
    variance = jnp.mean(centred * centred, axis=0, keepdims=True)
    scale = lax.rsqrt(variance + 1e-05)
    return centred * scale, scale


def norm_back(unit, scale, gain, grad):
    inner = grad * gain
    mean_one = jnp.mean(inner, axis=0, keepdims=True)
    mean_two = jnp.mean(inner * unit, axis=0, keepdims=True)
    return scale * (inner - mean_one - unit * mean_two)


def butterfly(values, shape):
    for bit in (1, 2, 4, 8, 16):
        pairs = [(i, i ^ bit) for i in range(32)]
        values = values + lax.ppermute(values, ("dp", "seq"), pairs)
    return values


def local(
    chips,
    cores,
    tokens,
    cotangent,
    pad_mask,
    prefix_len,
    norm_gains,
    norm_shifts,
    owner_map,
    weight_copy,
    master,
    average_weights,
    stat_left,
    stat_right,
    root_left,
    root_right,
):
    cell_count, length, features = tokens.shape
    assert cell_count == 1
    slots, size, _ = weight_copy.shape
    slot_count = owner_map.shape[0]
    row_blocks = features // size
    square = row_blocks * row_blocks
    col_blocks = (slot_count - 4 * square) // (2 * row_blocks)
    known = chips == 16 and cores == 2
    chip = lax.axis_index("dp").astype(jnp.int32)
    seq_index = lax.axis_index("seq")

    slot_of = jnp.zeros((slot_count,), jnp.int32).at[owner_map].set(jnp.arange(slot_count, dtype=jnp.int32))
    if known:
        gathered = gather_slots(pack_slots(weight_copy, chip.reshape(1), slot_count), slots)
    else:
        packed = pack_slots(weight_copy, jnp.zeros((1,), jnp.int32), slots)
        gathered = lax.all_gather(packed, "dp", axis=0, tiled=True)

    def three_of(i, j):
        return (j // row_blocks) * square + i * row_blocks + j % row_blocks

    def out_of(i, j):
        return 3 * square + i * row_blocks + j

    def up_of(i, j):
        return 4 * square + i * col_blocks + j

    def down_of(i, j):
        return 4 * square + row_blocks * col_blocks + i * row_blocks + j

    w_three = assemble(gathered, slot_of, row_blocks, 3 * row_blocks, three_of, "lay_three")
    w_out = assemble(gathered, slot_of, row_blocks, row_blocks, out_of, "lay_out")
    w_up = assemble(gathered, slot_of, row_blocks, col_blocks, up_of, "lay_up")
    w_down = assemble(gathered, slot_of, col_blocks, row_blocks, down_of, "lay_down")

    own_tokens = tokens.reshape(length, features).T
    prefix_tokens = own_tokens[:, :PREFIX]
    if cores == 2:
        arrived = lax.ppermute(prefix_tokens, "seq", [(0, 1)])
        prefix_tokens = jnp.where(seq_index == 0, prefix_tokens, arrived)
    else:
        prefix_tokens = lax.all_gather(prefix_tokens, "seq")[0]
    inputs = own_tokens.astype(F32)
    gain_one, shift_one = norm_gains[0][:, None], norm_shifts[0][:, None]
    gain_two, shift_two = norm_gains[1][:, None], norm_shifts[1][:, None]
    unit_all, _ = norm_parts(jnp.concatenate([prefix_tokens, own_tokens], axis=1).astype(F32))
    normed_in = (unit_all * gain_one + shift_one).astype(BF16)
    qkv = tn(w_three, normed_in).astype(BF16).reshape(3, features, PREFIX + length)

    position = seq_index * length + jnp.arange(length, dtype=jnp.int32)
    alive = jnp.where(position < PREFIX, position < prefix_len[0], pad_mask[0] == 1)
    prefix_alive = jnp.arange(PREFIX, dtype=jnp.int32) < prefix_len[0]
    groups = length // GB
    later = seq_index * groups + jnp.arange(groups) > 0
    low, high = score_biases(alive, prefix_alive, later)

    attended, log_total = attention(qkv, low, high)
    middle = inputs + tn(w_out, attended)
    unit_two, scale_two = norm_parts(middle)
    normed_mid = (unit_two * gain_two + shift_two).astype(BF16)
    up_pre = tn(w_up, normed_mid)
    activated, gelu_back = jax.vjp(functools.partial(jax.nn.gelu, approximate=True), up_pre)
    activated = activated.astype(BF16)
    block_out = (middle + tn(w_down, activated)).astype(BF16)

    grad_low = cotangent.reshape(length, features).T
    grad_pre = gelu_back(nn(w_down, grad_low))[0].astype(BF16)
    grads = weight_grad(activated, grad_low, slot_of, None, slot_count, size, down_of, "grad_down")
    grads = weight_grad(normed_mid, grad_pre, slot_of, grads, slot_count, size, up_of, "grad_up")
    grad_normed_two = nn(w_up, grad_pre)
    grad_middle = grad_low.astype(F32) + norm_back(unit_two, scale_two, gain_two, grad_normed_two)
    grad_branch = grad_middle.astype(BF16)
    grads = weight_grad(attended, grad_branch, slot_of, grads, slot_count, size, out_of, "grad_out")
    grad_att = nn(w_out, grad_branch).astype(BF16)
    grad_three = attention_back(qkv, low, high, attended, log_total, grad_att)
    grad_three = grad_three.reshape(3 * features, PREFIX + length)
    grads = weight_grad(normed_in, grad_three, slot_of, grads, slot_count, size, three_of, "grad_three")
    grad_all = nn(w_three, grad_three)
    prefix_part = grad_all[:, :PREFIX]
    if cores == 2:
        prefix_part = prefix_part + lax.ppermute(prefix_part, "seq", [(1, 0)])
    else:
        prefix_part = lax.psum(prefix_part, "seq")
    prefix_part = jnp.where(seq_index == 0, prefix_part, 0.0)
    grad_normed = grad_all[:, PREFIX:] + jnp.pad(prefix_part, ((0, 0), (0, length - PREFIX)))
    unit_one, scale_one = norm_parts(inputs)
    grad_input = grad_middle + norm_back(unit_one, scale_one, gain_one, grad_normed)

    grad_scale = 1.0 / math.sqrt(length * chips * cores)
    norm_terms = jnp.stack(
        [
            jnp.sum(grad_normed * unit_one, axis=1),
            jnp.sum(grad_normed, axis=1),
            jnp.sum(grad_normed_two * unit_two, axis=1),
            jnp.sum(grad_normed_two, axis=1),
        ]
    )
    norm_terms = norm_terms * grad_scale
    norm_grad = butterfly(norm_terms, None) if known else lax.psum(norm_terms, ("dp", "seq"))
    params = jnp.stack([norm_gains[0], norm_shifts[0], norm_gains[1], norm_shifts[1]])
    new_norms = params - 0.1 * norm_grad * lax.rsqrt(jnp.mean(norm_grad * norm_grad) + 1e-06)

    if known:
        summed = reduce_slots(grads, slots)
    else:
        part = lax.psum_scatter(grads.astype(F32), "dp", scatter_dimension=0, tiled=True)
        summed = lax.psum(part, "seq")
    stepped = optimizer(
        summed, grad_scale, (master, average_weights, stat_left, stat_right, root_left, root_right)
    )
    token_shape = (cell_count, length, features)
    return (
        block_out.T.reshape(token_shape),
        grad_input.T.reshape(token_shape),
        norm_grad,
        new_norms,
        *stepped,
    )


def solution(mesh):
    tokens, slots = P("dp", "seq", None), P("dp", None, None)
    in_specs = (tokens, tokens, P("dp", "seq"), P("dp"), P(), P(), P()) + (slots,) * 7
    out_specs = (tokens, tokens, P(), P()) + (slots,) * 6
    body = functools.partial(local, mesh.shape["dp"], mesh.shape["seq"])
    return jax.shard_map(body, mesh=mesh, in_specs=in_specs, out_specs=out_specs, check_vma=False)
```

```python
import functools
import math

import jax
import jax.numpy as jnp
from jax import lax
from jax.experimental import pallas as pl
from jax.experimental.pallas import tpu as pltpu
from jax.sharding import PartitionSpec as P

HEADS = 20
GB = 256
PREFIX = 128
HALF = GB // 2
MESH = pl.DeviceIdType.MESH
BF16 = jnp.bfloat16
F32 = jnp.float32

MAIN = 256
RUN = 32


def runs(size):
    rest, per_tile = size - MAIN, 128 // (size - MAIN)
    places = []
    for index in range(-(-size // RUN)):
        lane = 128 * (index // per_tile) + rest * (index % per_tile)
        places.append((RUN * index, min(RUN, size - RUN * index), lane))
    assert places[-1][2] + rest <= MAIN
    return places


def pack_tail(block):
    size = block.shape[0]
    rest = size - MAIN
    pieces, lane = [], 0
    for row, count, start in runs(size):
        if start > lane:
            pieces.append(jnp.zeros((RUN, start - lane), block.dtype))
        piece = block[row : row + count, MAIN:]
        if count < RUN:
            piece = jnp.concatenate([piece, jnp.zeros((RUN - count, rest), block.dtype)], axis=0)
        pieces.append(piece)
        lane = start + rest
    if lane < MAIN:
        pieces.append(jnp.zeros((RUN, MAIN - lane), block.dtype))
    return jnp.concatenate(pieces, axis=1)


def unpack(packed):
    size = packed.shape[0] - RUN
    rest = size - MAIN
    low = packed[size:]
    tail = [low[:count, lane : lane + rest] for _, count, lane in runs(size)]
    return jnp.concatenate([packed[:size], jnp.concatenate(tail, axis=0)], axis=1)


def tn(left, right):
    return lax.dot_general(left, right, (((0,), (0,)), ((), ())), preferred_element_type=F32)


def nn(left, right):
    return lax.dot_general(left, right, (((1,), (0,)), ((), ())), preferred_element_type=F32)


def nt(left, right):
    return lax.dot_general(left, right, (((1,), (1,)), ((), ())), preferred_element_type=F32)


def cost(flops, moved, exps=0):
    return pl.CostEstimate(flops=int(flops), bytes_accessed=int(moved), transcendentals=int(exps))


def pack_kernel(chip, block, packed):
    del chip
    size = block.shape[1]
    values = block[0].astype(F32)
    packed[0, :size] = values[:, :MAIN].astype(BF16)
    packed[0, size:] = pack_tail(values).astype(BF16)


def pack_slots(blocks, chip, slot_count):
    count, size, _ = blocks.shape
    return pl.pallas_call(
        pack_kernel,
        grid_spec=pltpu.PrefetchScalarGridSpec(
            num_scalar_prefetch=1,
            grid=(count,),
            in_specs=[pl.BlockSpec((1, size, size), lambda i, chip: (i, 0, 0))],
            out_specs=pl.BlockSpec((1, size + RUN, MAIN), lambda i, chip: (chip[0] * count + i, 0, 0)),
        ),
        out_shape=jax.ShapeDtypeStruct((slot_count, size + RUN, MAIN), BF16),
        name="pack_slots",
    )(chip, blocks)


def place():
    me, core = lax.axis_index("dp"), lax.axis_index("seq")
    x, y, z = me % 2, (me // 2) % 2, me // 4
    step_x, step_y = 1 - 2 * x, 2 * (1 - 2 * y)
    first = step_y * (1 - core) + step_x * core
    second = step_x * (1 - core) + step_y * core
    return me, core, z, first, second


def greet(partners):
    barrier = pltpu.get_barrier_semaphore()
    for chip, core in partners:
        pl.semaphore_signal(barrier, inc=1, device_id=(chip, core), device_id_type=MESH)
    pl.semaphore_wait(barrier, len(partners))


UP, DOWN, FIRST, SECOND, TWIN, GATHER_LABELS = 0, 4, 8, 12, 20, 36


def gather_kernel(slots, placed, out, send, recv):
    del placed
    me, core, z, first, second = place()
    half = slots // 2
    line = [(me + 4 * ((z + r) % 4 - z), core) for r in range(1, 4)]
    greet([(me + first, core), (me + second, core), (me, 1 - core)] + line)

    def copy(label, chip, dp, c):
        ref = out.at[pl.ds(chip * slots + core * half, half)]
        return pltpu.make_async_remote_copy(
            src_ref=ref,
            dst_ref=ref,
            send_sem=send.at[label],
            recv_sem=recv.at[label],
            device_id=(dp, c),
            device_id_type=MESH,
        )

    def arrival(label):
        ref = out.at[pl.ds(0, half)]
        return pltpu.make_async_remote_copy(
            src_ref=ref,
            dst_ref=ref,
            send_sem=send.at[label],
            recv_sem=recv.at[label],
            device_id=(me, 1 - core),
            device_id_type=MESH,
        )

    def col(zz):
        return me + 4 * (zz - z)

    def up(j):
        return copy(UP + j, me - 4 * (j - 1), me + 4, core)

    def down(j):
        return copy(DOWN + j, me + 4 * (j - 1), me - 4, core)

    def to_first(zz):
        return copy(FIRST + zz, col(zz), me + first, core)

    def to_second(zz, a):
        return copy(SECOND + 2 * zz + a, col(zz) + a * first, me + second, core)

    def to_twin(chip):
        return copy(TWIN + chip, chip, me, 1 - core)

    def spread(zz, own=False):
        to_first(zz).start()
        to_second(zz, 0).start()
        if not own:
            to_twin(col(zz)).start()

    def after_first(zz):
        to_first(zz).wait_recv()
        to_second(zz, 1).start()
        to_twin(col(zz) + first).start()

    def after_second(zz):
        for a in range(2):
            to_second(zz, a).wait_recv()
            to_twin(col(zz) + second + a * first).start()

    @pl.when(z < 3)
    def _():
        up(1).start()

    @pl.when(z > 0)
    def _():
        down(1).start()

    spread(z, own=True)
    for j in range(1, 4):

        @pl.when(z >= j)
        def _():
            up(j).wait_recv()
            if j < 3:

                @pl.when(z < 3)
                def _():
                    up(j + 1).start()

            spread(z - j)

        @pl.when(z + j <= 3)
        def _():
            down(j).wait_recv()
            if j < 3:

                @pl.when(z > 0)
                def _():
                    down(j + 1).start()

            spread(z + j)

        if j == 1:
            after_first(z)
        else:

            @pl.when(z >= j - 1)
            def _():
                after_first(z - (j - 1))

            @pl.when(z + j - 1 <= 3)
            def _():
                after_first(z + j - 1)

    @pl.when(z >= 3)
    def _():
        after_first(z - 3)

    @pl.when(z <= 0)
    def _():
        after_first(z + 3)

    after_second(z)
    for j in range(1, 4):

        @pl.when(z >= j)
        def _():
            after_second(z - j)

        @pl.when(z + j <= 3)
        def _():
            after_second(z + j)

    for zz in range(4):
        for a in range(2):
            for b in range(2):
                chip = col(zz) + a * first + b * second
                if a == 0 and b == 0:

                    @pl.when(zz != z)
                    def _():
                        to_twin(chip).wait_recv()
                        to_twin(chip).wait_send()

                else:
                    to_twin(chip).wait_recv()
                    to_twin(chip).wait_send()
        to_first(zz).wait_send()
        for a in range(2):
            to_second(zz, a).wait_send()

    @pl.when(z < 3)
    def _():
        up(1).wait_send()
        for j in range(1, 3):

            @pl.when(z >= j)
            def _():
                up(j + 1).wait_send()

    @pl.when(z > 0)
    def _():
        down(1).wait_send()
        for j in range(1, 3):

            @pl.when(z + j <= 3)
            def _():
                down(j + 1).wait_send()


def gather_slots(placed, slots):
    return pl.pallas_call(
        functools.partial(gather_kernel, slots),
        out_shape=jax.ShapeDtypeStruct(placed.shape, placed.dtype),
        in_specs=[pl.BlockSpec(memory_space=pl.ANY)],
        out_specs=pl.BlockSpec(memory_space=pl.ANY),
        scratch_shapes=[pltpu.SemaphoreType.DMA((GATHER_LABELS,)), pltpu.SemaphoreType.DMA((GATHER_LABELS,))],
        input_output_aliases={0: 0},
        compiler_params=pltpu.CompilerParams(collective_id=0, has_side_effects=True),
        name="gather_slots",
    )(placed)


R_TWIN, R_SECOND, R_FIRST, R_LINE, R_DONE, REDUCE_LABELS = 0, 16, 24, 28, 32, 33


def reduce_kernel(slots, grads, out, own, r_twin, r_second, r_first, r_line, total, load, send, recv, save):
    me, core, z, first, second = place()
    half = slots // 2
    line = [(me + 4 * ((z + r) % 4 - z), core) for r in range(1, 4)]
    greet([(me + first, core), (me + second, core), (me, 1 - core)] + line)

    def piece(chip, h):
        return grads.at[pl.ds(chip * slots + h * half, half)]

    def chip_at(zz, a, b):
        return me + 4 * (zz - z) + a * first + b * second

    def load_own(zz, a, b):
        chip = chip_at(zz, a, b)
        return pltpu.make_async_copy(piece(chip, core), own.at[chip], load.at[chip])

    def remote(src, dst, label, dp, c):
        return pltpu.make_async_remote_copy(
            src_ref=src,
            dst_ref=dst,
            send_sem=send.at[label],
            recv_sem=recv.at[label],
            device_id=(dp, c),
            device_id_type=MESH,
        )

    def twin(zz, a, b):
        chip = chip_at(zz, a, b)
        return remote(piece(chip, 1 - core), r_twin.at[chip], R_TWIN + chip, me, 1 - core)

    def to_second(zz, a):
        return remote(
            r_twin.at[chip_at(zz, a, 1)], r_second.at[2 * zz + a], R_SECOND + 2 * zz + a, me + second, core
        )

    def to_first(zz):
        return remote(r_twin.at[chip_at(zz, 1, 0)], r_first.at[zz], R_FIRST + zz, me + first, core)

    def to_line(r):
        zz = (z + r) % 4
        return remote(r_twin.at[chip_at(zz, 0, 0)], r_line.at[r - 1], R_LINE + r, chip_at(zz, 0, 0), core)

    def add_up(chip, others):
        def body(s, carry):
            value = own[chip, s].astype(F32) + r_twin[chip, s].astype(F32)
            for ref, index in others:
                value = value + ref[index, s].astype(F32)
            r_twin[chip, s] = value.astype(BF16)
            return carry

        lax.fori_loop(0, half, body, 0)

    def ready(zz, a, b):
        load_own(zz, a, b).wait()
        twin(zz, a, b).wait_recv()

    def send_second(zz, a):
        ready(zz, a, 1)
        add_up(chip_at(zz, a, 1), [])
        to_second(zz, a).start()

    def send_first(zz):
        ready(zz, 1, 0)
        to_second(zz, 1).wait_recv()
        add_up(chip_at(zz, 1, 0), [(r_second, 2 * zz + 1)])
        to_first(zz).start()

    def send_line(r):
        zz = (z + r) % 4
        ready(zz, 0, 0)
        to_second(zz, 0).wait_recv()
        to_first(zz).wait_recv()
        add_up(chip_at(zz, 0, 0), [(r_second, 2 * zz), (r_first, zz)])
        to_line(r).start()

    order = [2, 1, 3, 0]
    where = [(z + r) % 4 for r in order]
    for zz in where:
        for a in (1, 0):
            load_own(zz, a, 1).start()
            twin(zz, 1, a).start()
    for zz in where:
        for a in (1, 0):
            load_own(zz, a, 0).start()
            twin(zz, 0, a).start()

    def send_both(index):
        for a in (1, 0):
            send_second(where[index], a)

    send_both(0)
    send_both(1)
    send_both(2)
    send_first(where[0])
    send_both(3)
    send_first(where[1])
    send_line(order[0])
    send_first(where[2])
    send_line(order[1])
    send_first(where[3])
    send_line(order[2])

    ready(z, 0, 0)
    to_second(z, 0).wait_recv()
    to_first(z).wait_recv()
    for r in range(1, 4):
        to_line(r).wait_recv()

    def body(s, carry):
        value = own[me, s].astype(F32) + r_twin[me, s].astype(F32)
        value = value + r_second[2 * z, s].astype(F32)
        value = value + r_first[z, s].astype(F32)
        for r in range(3):
            value = value + r_line[r, s].astype(F32)
        total[s] = value
        return carry

    lax.fori_loop(0, half, body, 0)
    target = out.at[pl.ds(core * half, half)]
    done = remote(total, target, R_DONE, me, 1 - core)
    done.start()
    saved = pltpu.make_async_copy(total, target, save.at[0])
    saved.start()
    for zz in range(4):
        for a in range(2):
            for b in range(2):
                twin(zz, a, b).wait_send()
            to_second(zz, a).wait_send()
        to_first(zz).wait_send()
    for r in range(1, 4):
        to_line(r).wait_send()
    done.wait()
    saved.wait()


def reduce_slots(grads, slots):
    _, rows, lanes = grads.shape
    half = slots // 2
    pieces = lambda n: pltpu.VMEM((n, half, rows, lanes), BF16)
    return pl.pallas_call(
        functools.partial(reduce_kernel, slots),
        out_shape=jax.ShapeDtypeStruct((slots, rows, lanes), F32),
        in_specs=[pl.BlockSpec(memory_space=pl.ANY)],
        out_specs=pl.BlockSpec(memory_space=pl.ANY),
        scratch_shapes=[
            pieces(16),
            pieces(16),
            pieces(8),
            pieces(4),
            pieces(3),
            pltpu.VMEM((half, rows, lanes), F32),
            pltpu.SemaphoreType.DMA((16,)),
            pltpu.SemaphoreType.DMA((REDUCE_LABELS,)),
            pltpu.SemaphoreType.DMA((REDUCE_LABELS,)),
            pltpu.SemaphoreType.DMA((1,)),
        ],
        compiler_params=pltpu.CompilerParams(collective_id=1, has_side_effects=True, vmem_limit_bytes=60 << 20),
        name="reduce_slots",
    )(grads)


def lay(matrix, row, col, block):
    size = block.shape[0] - RUN
    matrix[size * row : size * (row + 1), size * col : size * col + MAIN] = block[:size]
    for start, count, lane in runs(size):
        piece = block[size : size + count, lane : lane + size - MAIN]
        matrix[size * row + start : size * row + start + count, size * col + MAIN : size * (col + 1)] = piece


def block_specs(gathered, rows, cols, block_of, **mode):
    shape = (1,) + gathered.shape[1:]
    pick = lambda i, j, step, v: (v[block_of(step, i, j)], 0, 0)
    return [
        pl.BlockSpec(shape, functools.partial(pick, i, j), **mode) for i in range(rows) for j in range(cols)
    ]


def token_tiles(length):
    tile = GB if length % GB == 0 else HALF
    return [slice(start, start + tile) for start in range(0, length, tile)]


def feature_parts(features):
    part = -(-features // 256) * 128
    return [slice(start, min(start + part, features)) for start in range(0, features, part)]


def fold(values):
    return sum(values[:, start : start + 128] for start in range(0, values.shape[1], 128))


ONCE = pl.Buffered(1)


def front_kernel(slot_of, gain, shift, tokens, *refs):
    del slot_of
    blocks, (weights, out, normed) = refs[:-3], refs[-3:]
    tiles = token_tiles(tokens.shape[1])

    @pl.when(pl.program_id(0) == 0)
    def _():
        for tile in tiles:
            unit, _ = norm_parts(tokens[:, tile].astype(F32))
            normed[:, tile] = (unit * gain[...] + shift[...]).astype(BF16)

    row_blocks = math.isqrt(len(blocks))
    for index, block in enumerate(blocks):
        lay(weights.at[0], index // row_blocks, index % row_blocks, block.at[0])
    out[0] = tn(weights[0], normed[...]).astype(BF16)


def front(gathered, slot_of, gain, shift, tokens, row_blocks):
    features, length = tokens.shape
    square = row_blocks * row_blocks
    whole = lambda shape: pl.BlockSpec(shape, lambda s, v: (0,) * len(shape), pipeline_mode=ONCE)
    blocks = block_specs(gathered, row_blocks, row_blocks, lambda s, i, j: s * square + i * row_blocks + j)
    return pl.pallas_call(
        front_kernel,
        grid_spec=pltpu.PrefetchScalarGridSpec(
            num_scalar_prefetch=1,
            grid=(3,),
            in_specs=[whole((features, 1))] * 2 + [whole((features, length))] + blocks,
            out_specs=[
                pl.BlockSpec((1, features, features), lambda s, v: (s, 0, 0)),
                pl.BlockSpec((1, features, length), lambda s, v: (s, 0, 0)),
                pl.BlockSpec((features, length), lambda s, v: (0, 0)),
            ],
        ),
        out_shape=[
            jax.ShapeDtypeStruct((3, features, features), BF16),
            jax.ShapeDtypeStruct((3, features, length), BF16),
            jax.ShapeDtypeStruct((features, length), BF16),
        ],
        compiler_params=pltpu.CompilerParams(vmem_limit_bytes=60 << 20),
        name="front",
    )(slot_of, gain, shift, tokens, *([gathered] * square))


def gelu_pair(values):
    square = values * values
    bend = jnp.tanh(values * (0.7978845608028654 + (0.7978845608028654 * 0.044715) * square))
    half = 0.5 * values
    slope = 0.7978845608028654 + (3 * 0.7978845608028654 * 0.044715) * square
    return half + half * bend, 0.5 + 0.5 * bend + half * (1.0 - bend * bend) * slope


def middle_kernel(row_blocks, slot_of, gain, shift, tokens, attended, grad_low, *refs):
    del slot_of
    square = row_blocks * row_blocks
    out_blocks, up_blocks, down_blocks = (refs[square * k : square * (k + 1)] for k in range(3))
    outs, scratch = refs[3 * square : 3 * square + 8], refs[3 * square + 8 :]
    block_out, activated, grad_pre, normed, grad_branch, grad_att, grad_middle, sums = outs
    w_out, w_up, w_down, middle, total, stats, sem = scratch
    tiles, parts = grad_low.shape[1] // GB, feature_parts(normed.shape[0])
    at = lambda index: pl.ds(pl.multiple_of(index * GB, GB), GB)
    step, last = pl.program_id(0), pl.num_programs(0) - 1

    @pl.when(step == 0)
    def _():
        copies = [
            pltpu.make_async_copy(tokens, block_out, sem.at[0]),
            pltpu.make_async_copy(attended, grad_att, sem.at[1]),
        ]
        for copy in copies:
            copy.start()
        for index, block in enumerate(out_blocks):
            lay(w_out, index // row_blocks, index % row_blocks, block.at[0])
        for copy in copies:
            copy.wait()
        def enter(index, carry):
            tile = at(index)
            for part in parts:
                values = block_out[part, tile].astype(F32) + tn(w_out[:, part], grad_att[:, tile])
                middle[part, tile] = values
                total[part, tile] = values
                grad_middle[part, tile] = jnp.zeros_like(values)
            values = middle[:, tile]
            average = jnp.mean(values, axis=0, keepdims=True)
            centred = values - average
            scale = lax.rsqrt(jnp.mean(centred * centred, axis=0, keepdims=True) + 1e-05)
            stats[0:1, tile] = average
            stats[1:2, tile] = scale
            normed[:, tile] = (centred * scale * gain[...] + shift[...]).astype(BF16)
            return carry

        lax.fori_loop(0, tiles, enter, 0)
        sums[...] = jnp.zeros_like(sums)

    for index in range(square):
        lay(w_up, index // row_blocks, index % row_blocks, up_blocks[index].at[0])
        lay(w_down, index // row_blocks, index % row_blocks, down_blocks[index].at[0])

    def advance(index, carry):
        tile = at(index)
        for part in parts:
            value, slope = gelu_pair(tn(w_up[:, part], normed[:, tile]))
            activated[part, tile] = value.astype(BF16)
            grad_pre[part, tile] = (nn(w_down[part, :], grad_low[:, tile]) * slope).astype(BF16)
        for part in parts:
            total[part, tile] += tn(w_down[:, part], activated[:, tile])
            grad_middle[part, tile] += nn(w_up[part, :], grad_pre[:, tile])
        return carry

    lax.fori_loop(0, tiles, advance, 0)

    @pl.when(step == last)
    def _():
        def leave(index, carry):
            tile = at(index)
            block_out[:, tile] = total[:, tile].astype(BF16)
            scale = stats[1:2, tile]
            unit = (middle[:, tile] - stats[0:1, tile]) * scale
            grad = grad_middle[:, tile]
            sums[0] += fold(grad * unit)
            sums[1] += fold(grad)
            values = grad_low[:, tile].astype(F32) + norm_back(unit, scale, gain[...], grad)
            grad_middle[:, tile] = values
            grad_branch[:, tile] = values.astype(BF16)
            for part in parts:
                grad_att[part, tile] = nn(w_out[part, :], grad_branch[:, tile]).astype(BF16)
            return carry

        lax.fori_loop(0, tiles, leave, 0)


def middle_part(gathered, slot_of, gain, shift, tokens, attended, grad_low, row_blocks, col_blocks):
    features, length = tokens.shape
    square = row_blocks * row_blocks
    hidden = features * col_blocks // row_blocks
    up_start, down_start = 4 * square, 4 * square + row_blocks * col_blocks
    whole = lambda *shape: pl.BlockSpec(shape, lambda s, v: (0,) * len(shape), pipeline_mode=ONCE)
    anywhere = pl.BlockSpec(memory_space=pl.ANY)
    part = pl.BlockSpec((features, length), lambda s, v: (s, 0))
    blocks = (
        block_specs(
            gathered, row_blocks, row_blocks, lambda s, i, j: 3 * square + i * row_blocks + j, pipeline_mode=ONCE
        )
        + block_specs(
            gathered, row_blocks, row_blocks, lambda s, i, j: up_start + i * col_blocks + s * row_blocks + j
        )
        + block_specs(
            gathered, row_blocks, row_blocks, lambda s, i, j: down_start + (s * row_blocks + i) * row_blocks + j
        )
    )
    shape = jax.ShapeDtypeStruct
    square_scratch = pltpu.VMEM((features, features), BF16)
    return pl.pallas_call(
        functools.partial(middle_kernel, row_blocks),
        grid_spec=pltpu.PrefetchScalarGridSpec(
            num_scalar_prefetch=1,
            grid=(col_blocks // row_blocks,),
            in_specs=[whole(features, 1)] * 2 + [anywhere] * 2 + [whole(features, length)] + blocks,
            out_specs=[whole(features, length), part, part]
            + [whole(features, length)] * 4
            + [whole(2, features, 128)],
            scratch_shapes=[square_scratch] * 3
            + [pltpu.VMEM((features, length), F32)] * 2
            + [pltpu.VMEM((8, length), F32), pltpu.SemaphoreType.DMA((2,))],
        ),
        out_shape=[
            shape((features, length), BF16),
            shape((hidden, length), BF16),
            shape((hidden, length), BF16),
            shape((features, length), BF16),
            shape((features, length), BF16),
            shape((features, length), BF16),
            shape((features, length), F32),
            shape((2, features, 128), F32),
        ],
        compiler_params=pltpu.CompilerParams(vmem_limit_bytes=63 << 20),
        name="middle_part",
    )(slot_of, gain, shift, tokens, attended, grad_low, *([gathered] * (3 * square)))


def weight_grad_kernel(block_of, deep, size, slot_of, left, right, *refs):
    grads, stage, sem = refs[-3:]
    wide = right.shape[0] // size
    rows, cols = pl.program_id(0), pl.program_id(1)
    step = rows * pl.num_programs(1) + cols
    steps = pl.num_programs(0) * pl.num_programs(1)
    now = step % 2

    def copy(buffer, index, slot):
        return pltpu.make_async_copy(stage.at[buffer, index], grads.at[slot], sem.at[buffer, index])

    @pl.when(step >= 2)
    def _():
        for index in range(deep * wide):
            copy(now, index, 0).wait()

    other = right[...]
    for i in range(deep):
        panel = nt(left[size * i : size * (i + 1), :], other)
        for j in range(wide):
            index = i * wide + j
            block = panel[:, size * j : size * (j + 1)]
            stage[now, index, :size] = block[:, :MAIN].astype(BF16)
            stage[now, index, size:] = pack_tail(block).astype(BF16)
            copy(now, index, slot_of[block_of(rows * deep + i, cols * wide + j)]).start()

    @pl.when(step == steps - 1)
    def _():
        for index in range(deep * wide):
            copy(now, index, 0).wait()

        @pl.when(steps > 1)
        def _():
            for index in range(deep * wide):
                copy(1 - now, index, 0).wait()


def weight_grad(left, right, slot_of, grads, slot_count, size, block_of, name):
    depth = left.shape[1]
    deep = wide = 4
    grid = (left.shape[0] // (size * deep), right.shape[0] // (size * wide))
    anywhere = pl.BlockSpec(memory_space=pl.ANY)
    operands = [slot_of, left, right] + ([] if grads is None else [grads])
    return pl.pallas_call(
        functools.partial(weight_grad_kernel, block_of, deep, size),
        grid_spec=pltpu.PrefetchScalarGridSpec(
            num_scalar_prefetch=1,
            grid=grid,
            in_specs=[
                pl.BlockSpec((size * deep, depth), lambda i, j, v: (i, 0)),
                pl.BlockSpec((size * wide, depth), lambda i, j, v: (j, 0)),
            ]
            + [anywhere] * (len(operands) - 3),
            out_specs=anywhere,
            scratch_shapes=[
                pltpu.VMEM((2, deep * wide, size + RUN, MAIN), BF16),
                pltpu.SemaphoreType.DMA((2, deep * wide)),
            ],
        ),
        out_shape=jax.ShapeDtypeStruct((slot_count, size + RUN, MAIN), BF16),
        input_output_aliases={} if grads is None else {3: 0},
        cost_estimate=cost(
            2 * left.shape[0] * right.shape[0] * depth,
            2 * (left.size + right.size + left.shape[0] * right.shape[0]),
        ),
        name=name,
    )(*operands)


EXTRA = 8
FAR = -1e30


def causal():
    return lax.broadcasted_iota(jnp.int32, (HALF, HALF), 0) <= lax.broadcasted_iota(jnp.int32, (HALF, HALF), 1)


def places(groups):
    found = []
    for group in range(groups):
        base = PREFIX + GB * group
        low, high = slice(base, base + HALF), slice(base + HALF, base + GB)
        found.append((low, high, slice(base, base + GB), slice(GB * group, GB * (group + 1))))
    return found


def side(left, right):
    return jnp.concatenate([left, right], axis=1)


def attention_kernel(scale, qkv, extras, out, lse, queries, keys, values, keys_t):
    head = qkv.shape[1]
    unit = scale * math.log2(math.e)

    @pl.when(pl.program_id(0) == 0)
    def _():
        queries[head:] = extras[0]
        keys[head:] = extras[1]
        values[head:] = extras[2]

    queries[:head] = qkv[0]
    keys[:head] = qkv[1]
    values[:head] = qkv[2]
    keys_t[...] = keys[...].T
    ahead = causal()
    spots = places(out.shape[1] // GB)
    scores = []
    for low, high, both, _ in spots:
        asked = queries[:, both]
        scores.append((nn(keys_t[:PREFIX], asked), nn(keys_t[low], asked), nn(keys_t[high], asked[:, HALF:])))

    def peak(array):
        return jnp.max(array, axis=0, keepdims=True)

    def soft(array, top):
        return jnp.exp2((array - top) * unit).astype(BF16)

    tops, weights = [], []
    for prefix, first, second in scores:
        first = side(jnp.where(ahead, first[:, :HALF], FAR), first[:, HALF:])
        second = jnp.where(ahead, second, FAR)
        top = jnp.maximum(peak(prefix), peak(first))
        top = side(top[:, :HALF], jnp.maximum(top[:, HALF:], peak(second)))
        tops.append(top)
        weights.append((soft(prefix, top), soft(first, top), soft(second, top[:, HALF:])))
    for (low, high, _, mine), top, (prefix, first, second) in zip(spots, tops, weights):
        sums = nn(values[:, :PREFIX], prefix) + nn(values[:, low], first)
        sums = side(sums[:, :HALF], sums[:, HALF:] + nn(values[:, high], second))
        total = sums[head : head + 1]
        out[:, mine] = (sums[:head] / total).astype(BF16)
        lse[0, :, mine] = top + jnp.log(total) * (1.0 / scale)


def thirds(values):
    high = values.astype(BF16).astype(F32)
    rest = values - high
    middle = rest.astype(BF16).astype(F32)
    return high, middle, rest - middle


def with_rows(base, start, rows):
    index = lax.broadcasted_iota(jnp.int32, base.shape, 0)
    for offset, row in enumerate(rows):
        base = jnp.where(index == start + offset, row, base)
    return base.astype(BF16)


def attention_back_kernel(scale, qkv, extras, out, lse, grad_out, grads, queries, keys, values, grad_o, keys_t, values_t):
    head, own = qkv.shape[1], out.shape[1]
    unit = scale * math.log2(math.e)

    @pl.when(pl.program_id(0) == 0)
    def _():
        keys[head:] = extras[1]
        values[head:] = extras[2]

    queries[:head] = qkv[0, :, PREFIX:]
    keys[:head] = qkv[1]
    values[:head] = qkv[2]
    grad_o[:head] = grad_out[...]
    keys_t[...] = keys[...].T
    values_t[...] = values[...].T
    queries[head:] = with_rows(extras[0, :, PREFIX:].astype(F32), 2, thirds(-lse[0]))
    delta = jnp.sum(grad_out[...].astype(F32) * out[...].astype(F32), axis=0, keepdims=True)
    grad_o[head:] = with_rows(jnp.zeros((EXTRA, own), F32), 0, thirds(-delta))
    ahead = causal()
    spots = places(own // GB)

    def weigh(rows, asked, given, mask):
        weights = jnp.exp2(nn(keys_t[rows], asked) * unit)
        if mask == 1:
            weights = side(jnp.where(ahead, weights[:, :HALF], 0.0), weights[:, HALF:])
        if mask == 2:
            weights = jnp.where(ahead, weights, 0.0)
        return weights.astype(BF16), (weights * nn(values_t[rows], given)).astype(BF16)

    found = []
    for low, high, _, mine in spots:
        asked, given = queries[:, mine], grad_o[:, mine]
        found.append(
            (
                weigh(slice(0, PREFIX), asked, given, 0),
                weigh(low, asked, given, 1),
                weigh(high, asked[:, HALF:], given[:, HALF:], 2),
            )
        )
    prefix_k = prefix_v = None
    for (low, high, both, mine), ((p0, d0), (p1, d1), (p2, d2)) in zip(spots, found):
        asked, given = queries[:head, mine], grad_o[:head, mine]
        grad_q = nn(keys[:head, :PREFIX], d0) + nn(keys[:head, low], d1)
        grad_q = side(grad_q[:, :HALF], grad_q[:, HALF:] + nn(keys[:head, high], d2))
        grads[0, :, both] = (grad_q * scale).astype(BF16)
        part_k, part_v = nt(asked, d0), nt(given, p0)
        prefix_k = part_k if prefix_k is None else prefix_k + part_k
        prefix_v = part_v if prefix_v is None else prefix_v + part_v
        grads[1, :, low] = (nt(asked, d1) * scale).astype(BF16)
        grads[2, :, low] = nt(given, p1).astype(BF16)
        grads[1, :, high] = (nt(asked[:, HALF:], d2) * scale).astype(BF16)
        grads[2, :, high] = nt(given[:, HALF:], p2).astype(BF16)
    grads[0, :, :PREFIX] = jnp.zeros((head, PREFIX), BF16)
    grads[1, :, :PREFIX] = (prefix_k * scale).astype(BF16)
    grads[2, :, :PREFIX] = prefix_v.astype(BF16)


def attention_specs(qkv):
    _, features, length = qkv.shape
    head, own = features // HEADS, length - PREFIX
    three = pl.BlockSpec((3, head, length), lambda h: (0, h, 0))
    extra = pl.BlockSpec((3, EXTRA, length), lambda h: (0, 0, 0))
    one = pl.BlockSpec((head, own), lambda h: (h, 0))
    row = pl.BlockSpec((1, 1, own), lambda h: (h, 0, 0))
    wide = lambda columns: pltpu.VMEM((head + EXTRA, columns), BF16)
    tall = pltpu.VMEM((length, head + EXTRA), BF16)
    return features, length, own, head, three, extra, one, row, wide, tall


def attention(qkv, extras):
    features, length, own, head, three, extra, one, row, wide, tall = attention_specs(qkv)
    return pl.pallas_call(
        functools.partial(attention_kernel, head ** (-0.5)),
        grid=(HEADS,),
        in_specs=[three, extra],
        out_specs=[one, row],
        out_shape=[
            jax.ShapeDtypeStruct((features, own), BF16),
            jax.ShapeDtypeStruct((HEADS, 1, own), F32),
        ],
        scratch_shapes=[wide(length), wide(length), wide(length), tall],
        cost_estimate=cost(8 * features * own * GB, 2 * qkv.size, HEADS * own * GB),
        name="attention",
    )(qkv, extras)


def attention_back(qkv, extras, out, lse, grad_out):
    features, length, own, head, three, extra, one, row, wide, tall = attention_specs(qkv)
    return pl.pallas_call(
        functools.partial(attention_back_kernel, head ** (-0.5)),
        grid=(HEADS,),
        in_specs=[three, extra, one, row, one],
        out_specs=three,
        out_shape=jax.ShapeDtypeStruct(qkv.shape, BF16),
        scratch_shapes=[wide(own), wide(length), wide(length), wide(own), tall, tall],
        cost_estimate=cost(20 * features * own * GB, 4 * qkv.size, HEADS * own * GB),
        name="attention_back",
    )(qkv, extras, out, lse, grad_out)


def score_extras(alive, prefix_alive, later):
    length = PREFIX + alive.shape[0]
    dead = jnp.where(jnp.concatenate([prefix_alive, alive]), 0.0, FAR)
    prefix = (jnp.arange(length) < PREFIX).astype(F32)
    barred = jnp.concatenate([jnp.zeros((PREFIX,)), jnp.where(jnp.repeat(later, GB), 0.0, FAR)])
    one, zero = jnp.ones((length,)), jnp.zeros((length,))
    query_rows = jnp.stack([one, barred] + [zero] * 6)
    key_rows = jnp.stack([dead, prefix] + [one] * 3 + [zero] * 3)
    value_rows = jnp.stack([one] * 3 + [zero] * 5)
    return jnp.stack([query_rows, key_rows, value_rows]).astype(BF16)


def split(values):
    high = values.astype(BF16)
    return high, (values - high.astype(F32)).astype(BF16)


def product(form, left, right):
    (left_high, left_low), (right_high, right_low) = left, right
    return form(left_high, right_high) + (form(left_high, right_low) + form(left_low, right_high))


def optimizer_kernel(scale, packed, master, average, left, right, root_left, root_right, *outs):
    slot_grad, new_left, new_right, new_master, new_copy, new_average = outs
    size = master.shape[1]
    grad = unpack(packed[0]) * scale
    slot_grad[0] = grad
    grad_parts = split(grad)
    new_left[0] = 0.5 * left[0] + (0.5 / size) * product(nt, grad_parts, grad_parts)
    new_right[0] = 0.5 * right[0] + (0.5 / size) * product(tn, grad_parts, grad_parts)
    right_part = product(nn, grad_parts, split(root_right[0]))
    step = product(nn, split(root_left[0]), split(right_part))
    moved = master[0] - 0.03 * step
    new_master[0] = moved
    new_copy[0] = moved.astype(BF16)
    new_average[0] = 0.8 * average[0] + 0.2 * moved


def optimizer(packed, scale, arrays):
    slots, size, _ = arrays[0].shape
    block = pl.BlockSpec((1, size, size), lambda i: (i, 0, 0))
    shape = lambda dtype: jax.ShapeDtypeStruct((slots, size, size), dtype)
    return pl.pallas_call(
        functools.partial(optimizer_kernel, scale),
        grid=(slots,),
        in_specs=[pl.BlockSpec((1,) + packed.shape[1:], lambda i: (i, 0, 0))] + [block] * 6,
        out_specs=[block] * 6,
        out_shape=[shape(F32), shape(F32), shape(F32), shape(F32), shape(BF16), shape(F32)],
        name="optimizer",
    )(packed, *arrays)


def norm_parts(values):
    average = jnp.mean(values, axis=0, keepdims=True)
    centred = values - average
    variance = jnp.mean(centred * centred, axis=0, keepdims=True)
    scale = lax.rsqrt(variance + 1e-05)
    return centred * scale, scale


def norm_back(unit, scale, gain, grad):
    inner = grad * gain
    mean_one = jnp.mean(inner, axis=0, keepdims=True)
    mean_two = jnp.mean(inner * unit, axis=0, keepdims=True)
    return scale * (inner - mean_one - unit * mean_two)


def butterfly(values, shape):
    for bit in (1, 2, 4, 8, 16):
        pairs = [(i, i ^ bit) for i in range(32)]
        values = values + lax.ppermute(values, ("dp", "seq"), pairs)
    return values


def local(
    chips,
    cores,
    tokens,
    cotangent,
    pad_mask,
    prefix_len,
    norm_gains,
    norm_shifts,
    owner_map,
    weight_copy,
    master,
    average_weights,
    stat_left,
    stat_right,
    root_left,
    root_right,
):
    cell_count, length, features = tokens.shape
    assert cell_count == 1
    slots, size, _ = weight_copy.shape
    slot_count = owner_map.shape[0]
    row_blocks = features // size
    square = row_blocks * row_blocks
    col_blocks = (slot_count - 4 * square) // (2 * row_blocks)
    known = chips == 16 and cores == 2
    chip = lax.axis_index("dp").astype(jnp.int32)
    seq_index = lax.axis_index("seq")

    slot_of = jnp.zeros((slot_count,), jnp.int32).at[owner_map].set(jnp.arange(slot_count, dtype=jnp.int32))
    if known:
        gathered = gather_slots(pack_slots(weight_copy, chip.reshape(1), slot_count), slots)
    else:
        packed = pack_slots(weight_copy, jnp.zeros((1,), jnp.int32), slots)
        gathered = lax.all_gather(packed, "dp", axis=0, tiled=True)

    def three_of(i, j):
        return (j // row_blocks) * square + i * row_blocks + j % row_blocks

    def out_of(i, j):
        return 3 * square + i * row_blocks + j

    def up_of(i, j):
        return 4 * square + i * col_blocks + j

    def down_of(i, j):
        return 4 * square + row_blocks * col_blocks + i * row_blocks + j

    own_tokens = tokens.reshape(length, features).T
    prefix_tokens = own_tokens[:, :PREFIX]
    if cores == 2:
        arrived = lax.ppermute(prefix_tokens, "seq", [(0, 1)])
        prefix_tokens = jnp.where(seq_index == 0, prefix_tokens, arrived)
    else:
        prefix_tokens = lax.all_gather(prefix_tokens, "seq")[0]
    gain_one, shift_one = norm_gains[0][:, None], norm_shifts[0][:, None]
    gain_two, shift_two = norm_gains[1][:, None], norm_shifts[1][:, None]
    all_tokens = jnp.concatenate([prefix_tokens, own_tokens], axis=1)
    w_three, qkv, normed_in = front(gathered, slot_of, gain_one, shift_one, all_tokens, row_blocks)

    position = seq_index * length + jnp.arange(length, dtype=jnp.int32)
    alive = jnp.where(position < PREFIX, position < prefix_len[0], pad_mask[0] == 1)
    prefix_alive = jnp.arange(PREFIX, dtype=jnp.int32) < prefix_len[0]
    groups = length // GB
    later = seq_index * groups + jnp.arange(groups) > 0
    extras = score_extras(alive, prefix_alive, later)

    grad_low = cotangent.reshape(length, features).T
    attended, log_total = attention(qkv, extras)
    block_out, activated, grad_pre, normed_mid, grad_branch, grad_att, grad_middle, sums = middle_part(
        gathered, slot_of, gain_two, shift_two, own_tokens, attended, grad_low, row_blocks, col_blocks
    )
    grads = weight_grad(activated, grad_low, slot_of, None, slot_count, size, down_of, "grad_down")
    grads = weight_grad(normed_mid, grad_pre, slot_of, grads, slot_count, size, up_of, "grad_up")
    grads = weight_grad(attended, grad_branch, slot_of, grads, slot_count, size, out_of, "grad_out")
    grad_three = attention_back(qkv, extras, attended, log_total, grad_att)
    grad_three = grad_three.reshape(3 * features, PREFIX + length)
    grads = weight_grad(normed_in, grad_three, slot_of, grads, slot_count, size, three_of, "grad_three")
    grad_all = sum(nn(w_three[k], grad_three[features * k : features * (k + 1)]) for k in range(3))
    prefix_part = grad_all[:, :PREFIX]
    if cores == 2:
        prefix_part = prefix_part + lax.ppermute(prefix_part, "seq", [(1, 0)])
    else:
        prefix_part = lax.psum(prefix_part, "seq")
    prefix_part = jnp.where(seq_index == 0, prefix_part, 0.0)
    grad_normed = grad_all[:, PREFIX:] + jnp.pad(prefix_part, ((0, 0), (0, length - PREFIX)))
    unit_one, scale_one = norm_parts(own_tokens.astype(F32))
    grad_input = grad_middle + norm_back(unit_one, scale_one, gain_one, grad_normed)

    grad_scale = 1.0 / math.sqrt(length * chips * cores)
    norm_terms = jnp.stack(
        [
            jnp.sum(grad_normed * unit_one, axis=1),
            jnp.sum(grad_normed, axis=1),
            jnp.sum(sums[0], axis=1),
            jnp.sum(sums[1], axis=1),
        ]
    )
    norm_terms = norm_terms * grad_scale
    norm_grad = butterfly(norm_terms, None) if known else lax.psum(norm_terms, ("dp", "seq"))
    params = jnp.stack([norm_gains[0], norm_shifts[0], norm_gains[1], norm_shifts[1]])
    new_norms = params - 0.1 * norm_grad * lax.rsqrt(jnp.mean(norm_grad * norm_grad) + 1e-06)

    if known:
        summed = reduce_slots(grads, slots)
    else:
        part = lax.psum_scatter(grads.astype(F32), "dp", scatter_dimension=0, tiled=True)
        summed = lax.psum(part, "seq")
    stepped = optimizer(
        summed, grad_scale, (master, average_weights, stat_left, stat_right, root_left, root_right)
    )
    token_shape = (cell_count, length, features)
    return (
        block_out.T.reshape(token_shape),
        grad_input.T.reshape(token_shape),
        norm_grad,
        new_norms,
        *stepped,
    )


def solution(mesh):
    tokens, slots = P("dp", "seq", None), P("dp", None, None)
    in_specs = (tokens, tokens, P("dp", "seq"), P("dp"), P(), P(), P()) + (slots,) * 7
    out_specs = (tokens, tokens, P(), P()) + (slots,) * 6
    body = functools.partial(local, mesh.shape["dp"], mesh.shape["seq"])
    return jax.shard_map(body, mesh=mesh, in_specs=in_specs, out_specs=out_specs, check_vma=False)
```

```python
import functools
import math

import jax
import jax.numpy as jnp
from jax import lax
from jax.experimental import pallas as pl
from jax.experimental.pallas import tpu as pltpu
from jax.sharding import PartitionSpec as P

HEADS = 20
GB = 256
PREFIX = 128
HALF = GB // 2
MESH = pl.DeviceIdType.MESH
BF16 = jnp.bfloat16
F32 = jnp.float32

MAIN = 256
RUN = 32


def runs(size):
    rest, per_tile = size - MAIN, 128 // (size - MAIN)
    places = []
    for index in range(-(-size // RUN)):
        lane = 128 * (index // per_tile) + rest * (index % per_tile)
        places.append((RUN * index, min(RUN, size - RUN * index), lane))
    assert places[-1][2] + rest <= MAIN
    return places


def pack_tail(block):
    size = block.shape[0]
    rest = size - MAIN
    pieces, lane = [], 0
    for row, count, start in runs(size):
        if start > lane:
            pieces.append(jnp.zeros((RUN, start - lane), block.dtype))
        piece = block[row : row + count, MAIN:]
        if count < RUN:
            piece = jnp.concatenate([piece, jnp.zeros((RUN - count, rest), block.dtype)], axis=0)
        pieces.append(piece)
        lane = start + rest
    if lane < MAIN:
        pieces.append(jnp.zeros((RUN, MAIN - lane), block.dtype))
    return jnp.concatenate(pieces, axis=1)


def unpack(packed):
    size = packed.shape[0] - RUN
    rest = size - MAIN
    low = packed[size:]
    tail = [low[:count, lane : lane + rest] for _, count, lane in runs(size)]
    return jnp.concatenate([packed[:size], jnp.concatenate(tail, axis=0)], axis=1)


def tn(left, right):
    return lax.dot_general(left, right, (((0,), (0,)), ((), ())), preferred_element_type=F32)


def nn(left, right):
    return lax.dot_general(left, right, (((1,), (0,)), ((), ())), preferred_element_type=F32)


def nt(left, right):
    return lax.dot_general(left, right, (((1,), (1,)), ((), ())), preferred_element_type=F32)


def cost(flops, moved, exps=0):
    return pl.CostEstimate(flops=int(flops), bytes_accessed=int(moved), transcendentals=int(exps))


def pack_kernel(chip, block, packed):
    del chip
    size = block.shape[1]
    values = block[0].astype(F32)
    packed[0, :size] = values[:, :MAIN].astype(BF16)
    packed[0, size:] = pack_tail(values).astype(BF16)


def pack_slots(blocks, chip, slot_count):
    count, size, _ = blocks.shape
    return pl.pallas_call(
        pack_kernel,
        grid_spec=pltpu.PrefetchScalarGridSpec(
            num_scalar_prefetch=1,
            grid=(count,),
            in_specs=[pl.BlockSpec((1, size, size), lambda i, chip: (i, 0, 0))],
            out_specs=pl.BlockSpec((1, size + RUN, MAIN), lambda i, chip: (chip[0] * count + i, 0, 0)),
        ),
        out_shape=jax.ShapeDtypeStruct((slot_count, size + RUN, MAIN), BF16),
        name="pack_slots",
    )(chip, blocks)


def place():
    me, core = lax.axis_index("dp"), lax.axis_index("seq")
    x, y, z = me % 2, (me // 2) % 2, me // 4
    step_x, step_y = 1 - 2 * x, 2 * (1 - 2 * y)
    first = step_y * (1 - core) + step_x * core
    second = step_x * (1 - core) + step_y * core
    return me, core, z, first, second


def greet(partners):
    barrier = pltpu.get_barrier_semaphore()
    for chip, core in partners:
        pl.semaphore_signal(barrier, inc=1, device_id=(chip, core), device_id_type=MESH)
    pl.semaphore_wait(barrier, len(partners))


UP, DOWN, FIRST, SECOND, TWIN, GATHER_LABELS = 0, 4, 8, 12, 20, 36


def gather_kernel(slots, placed, out, send, recv):
    del placed
    me, core, z, first, second = place()
    half = slots // 2
    line = [(me + 4 * ((z + r) % 4 - z), core) for r in range(1, 4)]
    greet([(me + first, core), (me + second, core), (me, 1 - core)] + line)

    def copy(label, chip, dp, c):
        ref = out.at[pl.ds(chip * slots + core * half, half)]
        return pltpu.make_async_remote_copy(
            src_ref=ref,
            dst_ref=ref,
            send_sem=send.at[label],
            recv_sem=recv.at[label],
            device_id=(dp, c),
            device_id_type=MESH,
        )

    def col(zz):
        return me + 4 * (zz - z)

    def up(j):
        return copy(UP + j, me - 4 * (j - 1), me + 4, core)

    def down(j):
        return copy(DOWN + j, me + 4 * (j - 1), me - 4, core)

    def to_first(zz):
        return copy(FIRST + zz, col(zz), me + first, core)

    def to_second(zz, a):
        return copy(SECOND + 2 * zz + a, col(zz) + a * first, me + second, core)

    def to_twin(chip):
        return copy(TWIN + chip, chip, me, 1 - core)

    def spread(zz, own=False):
        to_first(zz).start()
        to_second(zz, 0).start()
        if not own:
            to_twin(col(zz)).start()

    def after_first(zz):
        to_first(zz).wait_recv()
        to_second(zz, 1).start()
        to_twin(col(zz) + first).start()

    def after_second(zz):
        for a in range(2):
            to_second(zz, a).wait_recv()
            to_twin(col(zz) + second + a * first).start()

    @pl.when(z < 3)
    def _():
        up(1).start()

    @pl.when(z > 0)
    def _():
        down(1).start()

    spread(z, own=True)
    for j in range(1, 4):

        @pl.when(z >= j)
        def _():
            up(j).wait_recv()
            if j < 3:

                @pl.when(z < 3)
                def _():
                    up(j + 1).start()

            spread(z - j)

        @pl.when(z + j <= 3)
        def _():
            down(j).wait_recv()
            if j < 3:

                @pl.when(z > 0)
                def _():
                    down(j + 1).start()

            spread(z + j)

        if j == 1:
            after_first(z)
        else:

            @pl.when(z >= j - 1)
            def _():
                after_first(z - (j - 1))

            @pl.when(z + j - 1 <= 3)
            def _():
                after_first(z + j - 1)

    @pl.when(z >= 3)
    def _():
        after_first(z - 3)

    @pl.when(z <= 0)
    def _():
        after_first(z + 3)

    after_second(z)
    for j in range(1, 4):

        @pl.when(z >= j)
        def _():
            after_second(z - j)

        @pl.when(z + j <= 3)
        def _():
            after_second(z + j)

    for zz in range(4):
        for a in range(2):
            for b in range(2):
                chip = col(zz) + a * first + b * second
                if a == 0 and b == 0:

                    @pl.when(zz != z)
                    def _():
                        to_twin(chip).wait_recv()
                        to_twin(chip).wait_send()

                else:
                    to_twin(chip).wait_recv()
                    to_twin(chip).wait_send()
        to_first(zz).wait_send()
        for a in range(2):
            to_second(zz, a).wait_send()

    @pl.when(z < 3)
    def _():
        up(1).wait_send()
        for j in range(1, 3):

            @pl.when(z >= j)
            def _():
                up(j + 1).wait_send()

    @pl.when(z > 0)
    def _():
        down(1).wait_send()
        for j in range(1, 3):

            @pl.when(z + j <= 3)
            def _():
                down(j + 1).wait_send()


def gather_slots(placed, slots):
    return pl.pallas_call(
        functools.partial(gather_kernel, slots),
        out_shape=jax.ShapeDtypeStruct(placed.shape, placed.dtype),
        in_specs=[pl.BlockSpec(memory_space=pl.ANY)],
        out_specs=pl.BlockSpec(memory_space=pl.ANY),
        scratch_shapes=[pltpu.SemaphoreType.DMA((GATHER_LABELS,)), pltpu.SemaphoreType.DMA((GATHER_LABELS,))],
        input_output_aliases={0: 0},
        compiler_params=pltpu.CompilerParams(collective_id=0, has_side_effects=True),
        name="gather_slots",
    )(placed)


R_TWIN, R_SECOND, R_FIRST, R_LINE, R_DONE, R_PREFIX, R_FLOW, REDUCE_LABELS = 0, 16, 24, 28, 32, 33, 34, 42
RING = 3
PANELS = 5


def reduce_kernel(
    slots,
    grads,
    w_three,
    grad_three,
    tokens,
    grad_middle,
    params,
    sums,
    out,
    grad_input,
    norm_sums,
    ring,
    r_twin,
    r_second,
    r_first,
    r_line,
    total,
    weights,
    inner,
    acc,
    prefix,
    given,
    folds,
    flow,
    arrived,
    load,
    send,
    recv,
    save,
):
    me, core, z, first, second = place()
    half = slots // 2
    features, length = acc.shape
    line = [(me + 4 * ((z + r) % 4 - z), core) for r in range(1, 4)]
    greet([(me + first, core), (me + second, core), (me, 1 - core)] + line)

    def piece(chip, h):
        return grads.at[pl.ds(chip * slots + h * half, half)]

    def chip_at(zz, a, b):
        return me + 4 * (zz - z) + a * first + b * second

    def remote(src, dst, label, dp, c):
        return pltpu.make_async_remote_copy(
            src_ref=src,
            dst_ref=dst,
            send_sem=send.at[label],
            recv_sem=recv.at[label],
            device_id=(dp, c),
            device_id_type=MESH,
        )

    def twin(zz, a, b):
        chip = chip_at(zz, a, b)
        return remote(piece(chip, 1 - core), r_twin.at[chip], R_TWIN + chip, me, 1 - core)

    def to_second(zz, a):
        return remote(
            r_twin.at[chip_at(zz, a, 1)], r_second.at[2 * zz + a], R_SECOND + 2 * zz + a, me + second, core
        )

    def to_first(zz):
        return remote(r_twin.at[chip_at(zz, 1, 0)], r_first.at[zz], R_FIRST + zz, me + first, core)

    def to_line(r):
        zz = (z + r) % 4
        return remote(r_twin.at[chip_at(zz, 0, 0)], r_line.at[r - 1], R_LINE + r, chip_at(zz, 0, 0), core)

    order = [2, 1, 3, 0]
    where = [(z + r) % 4 for r in order]
    turns = []
    for index in range(3):
        turns += [(where[index], 1, 1), (where[index], 0, 1)]
    turns += [(where[0], 1, 0), (where[3], 1, 1), (where[3], 0, 1), (where[0], 0, 0), (where[1], 1, 0)]
    turns += [(where[2], 1, 0), (where[1], 0, 0), (where[3], 1, 0), (where[2], 0, 0), (where[3], 0, 0)]

    def load_own(turn):
        return pltpu.make_async_copy(piece(chip_at(*turns[turn]), core), ring.at[turn % RING], load.at[turn % RING])

    def add_up(turn, others):
        chip = chip_at(*turns[turn])
        load_own(turn).wait()
        twin(*turns[turn]).wait_recv()

        def body(s, carry):
            value = ring[turn % RING, s].astype(F32) + r_twin[chip, s].astype(F32)
            for ref, index in others:
                value = value + ref[index, s].astype(F32)
            if turn < len(turns) - 1:
                r_twin[chip, s] = value.astype(BF16)
            else:
                total[s] = value
            return carry

        lax.fori_loop(0, half, body, 0)
        if turn + RING < len(turns):
            load_own(turn + RING).start()

    def send_second(turn):
        zz, a, _ = turns[turn]
        add_up(turn, [])
        to_second(zz, a).start()

    def send_first(turn):
        zz = turns[turn][0]
        to_second(zz, 1).wait_recv()
        add_up(turn, [(r_second, 2 * zz + 1)])
        to_first(zz).start()

    def send_line(turn, r):
        zz = turns[turn][0]
        to_second(zz, 0).wait_recv()
        to_first(zz).wait_recv()
        add_up(turn, [(r_second, 2 * zz), (r_first, zz)])
        to_line(r).start()

    for turn in range(RING):
        load_own(turn).start()
    for zz in where:
        for a in (1, 0):
            twin(zz, 1, a).start()
    for zz in where:
        for a in (1, 0):
            twin(zz, 0, a).start()
    fetches = [
        pltpu.make_async_copy(w_three, weights, save.at[0]),
        pltpu.make_async_copy(grad_three, inner, save.at[1]),
    ]
    for fetch in fetches:
        fetch.start()
    for turn in range(6):
        send_second(turn)
    send_first(6)
    send_second(7)
    send_second(8)
    for fetch in fetches:
        fetch.wait()

    rows = features // PANELS

    def panel(index, carry):
        mine = pl.ds(pl.multiple_of(index * rows, 16), rows)
        acc[mine, :] = sum(nn(weights[k, mine, :], inner[k]) for k in range(3))
        return carry

    lax.fori_loop(0, PANELS, panel, 0)

    swap = remote(acc.at[:, pl.ds(0, PREFIX)], prefix, R_PREFIX, me, 1 - core)
    swap.start()
    own_tokens = weights.at[0, :, pl.ds(0, length - PREFIX)]
    take = pltpu.make_async_copy(tokens, own_tokens, save.at[0])
    take.start()

    def at(index):
        return pl.ds(pl.multiple_of(index * GB, GB), GB)

    def ahead(index):
        return pl.ds(pl.multiple_of(PREFIX + index * GB, PREFIX), GB)

    def give(index, slot):
        return pltpu.make_async_copy(grad_middle.at[:, at(index)], given.at[slot], save.at[2 + slot])

    def store(index):
        return pltpu.make_async_copy(acc.at[:, ahead(index)], grad_input.at[:, at(index)], save.at[4 + index])

    give(0, 0).start()
    send_line(9, order[0])
    send_first(10)
    take.wait()
    swap.wait()
    here = (1 - core).astype(F32)
    acc[:, PREFIX : 2 * PREFIX] += (acc[:, :PREFIX] + prefix[...]) * here
    folds[...] = jnp.zeros_like(folds)
    groups = (length - PREFIX) // GB
    for index in range(groups):
        if index + 1 < groups:
            give(index + 1, (index + 1) % 2).start()
        give(index, index % 2).wait()
        unit, scale = norm_parts(weights[0, :, GB * index : GB * (index + 1)].astype(F32))
        mine = slice(PREFIX + GB * index, PREFIX + GB * (index + 1))
        grad = acc[:, mine]
        folds[0] += fold(grad * unit)
        folds[1] += fold(grad)
        acc[:, mine] = given[index % 2] + norm_back(unit, scale, params[:, 0:1], grad)
        store(index).start()

    flow[0] = sums[...] + row_sums(folds[0], 0) + row_sums(folds[1], 1)
    pairs = [(me, 1 - core), (me + first, core), (me, 1 - core), (me + first, core), (me, 1 - core)] + line
    sources = [flow.at[0], flow.at[1], flow.at[2], arrived.at[2], flow.at[3]] + [flow.at[4]] * 3

    def pass_on(k):
        return remote(sources[k], arrived.at[k], R_FLOW + k, *pairs[k])

    for k in range(2):
        pass_on(k).start()
        pass_on(k).wait_recv()
        flow[k + 1] = flow[k] + arrived[k]
    pass_on(2).start()
    pass_on(2).wait_recv()
    pass_on(3).start()
    send_first(11)
    pass_on(3).wait_recv()
    flow[3] = arrived[2] + arrived[3]
    pass_on(4).start()
    pass_on(4).wait_recv()
    plane = jnp.where(core == 0, flow[3], arrived[4])
    flow[4] = plane
    arrived[4] = plane
    for k in range(5, 8):
        pass_on(k).start()
    send_line(12, order[1])
    send_first(13)
    send_line(14, order[2])
    for k in range(5, 8):
        pass_on(k).wait_recv()
    norm_sums[...] = sum(arrived[4 + (z - zz + 4) % 4] for zz in range(4))
    to_second(z, 0).wait_recv()
    to_first(z).wait_recv()
    for r in range(1, 4):
        to_line(r).wait_recv()
    add_up(15, [(r_second, 2 * z), (r_first, z), (r_line, 0), (r_line, 1), (r_line, 2)])
    target = out.at[pl.ds(core * half, half)]
    done = remote(total, target, R_DONE, me, 1 - core)
    done.start()
    saved = pltpu.make_async_copy(total, target, save.at[0])
    saved.start()
    for zz in range(4):
        for a in range(2):
            for b in range(2):
                twin(zz, a, b).wait_send()
            to_second(zz, a).wait_send()
        to_first(zz).wait_send()
    for r in range(1, 4):
        to_line(r).wait_send()
    for k in range(len(pairs)):
        pass_on(k).wait_send()
    for index in range(groups):
        store(index).wait()
    done.wait()
    saved.wait()


def reduce_slots(grads, slots, w_three, grad_three, tokens, grad_middle, params, sums):
    _, lines, lanes = grads.shape
    half = slots // 2
    _, features, length = grad_three.shape
    pieces = lambda n: pltpu.VMEM((n, half, lines, lanes), BF16)
    anywhere, inside = pl.BlockSpec(memory_space=pl.ANY), pl.BlockSpec(memory_space=pltpu.VMEM)
    groups = (length - PREFIX) // GB
    return pl.pallas_call(
        functools.partial(reduce_kernel, slots),
        out_shape=[
            jax.ShapeDtypeStruct((slots, lines, lanes), F32),
            jax.ShapeDtypeStruct((features, length - PREFIX), F32),
            jax.ShapeDtypeStruct((8, features), F32),
        ],
        in_specs=[anywhere] * 5 + [inside] * 2,
        out_specs=[anywhere, anywhere, inside],
        scratch_shapes=[
            pieces(RING),
            pieces(16),
            pieces(8),
            pieces(4),
            pieces(3),
            pltpu.VMEM((half, lines, lanes), F32),
            pltpu.VMEM(w_three.shape, BF16),
            pltpu.VMEM(grad_three.shape, BF16),
            pltpu.VMEM((features, length), F32),
            pltpu.VMEM((features, PREFIX), F32),
            pltpu.VMEM((2, features, GB), F32),
            pltpu.VMEM((2, features, 128), F32),
            pltpu.VMEM((5, 8, features), F32),
            pltpu.VMEM((8, 8, features), F32),
            pltpu.SemaphoreType.DMA((RING,)),
            pltpu.SemaphoreType.DMA((REDUCE_LABELS,)),
            pltpu.SemaphoreType.DMA((REDUCE_LABELS,)),
            pltpu.SemaphoreType.DMA((4 + groups,)),
        ],
        compiler_params=pltpu.CompilerParams(collective_id=1, has_side_effects=True, vmem_limit_bytes=63 << 20),
        name="reduce_slots",
    )(grads, w_three, grad_three, tokens, grad_middle, params, sums)


def lay(matrix, row, col, block):
    size = block.shape[0] - RUN
    matrix[size * row : size * (row + 1), size * col : size * col + MAIN] = block[:size]
    for start, count, lane in runs(size):
        piece = block[size : size + count, lane : lane + size - MAIN]
        matrix[size * row + start : size * row + start + count, size * col + MAIN : size * (col + 1)] = piece


def block_specs(gathered, rows, cols, block_of, **mode):
    shape = (1,) + gathered.shape[1:]
    pick = lambda i, j, step, v: (v[block_of(step, i, j)], 0, 0)
    return [
        pl.BlockSpec(shape, functools.partial(pick, i, j), **mode) for i in range(rows) for j in range(cols)
    ]


def token_tiles(length):
    tile = GB if length % GB == 0 else HALF
    return [slice(start, start + tile) for start in range(0, length, tile)]


def feature_parts(features):
    part = -(-features // 256) * 128
    return [slice(start, min(start + part, features)) for start in range(0, features, part)]


def fold(values):
    return sum(values[:, start : start + 128] for start in range(0, values.shape[1], 128))


def row_sums(values, row):
    ones = jnp.ones((8, values.shape[1]), F32)
    summed = lax.dot_general(
        ones, values, (((1,), (1,)), ((), ())), precision=lax.Precision.HIGHEST, preferred_element_type=F32
    )
    return jnp.where(lax.broadcasted_iota(jnp.int32, summed.shape, 0) == row, summed, 0.0)


ONCE = pl.Buffered(1)


def front_kernel(slot_of, params, tokens, *refs):
    del slot_of
    blocks, (weights, out, normed) = refs[:-3], refs[-3:]
    tiles = token_tiles(tokens.shape[1])

    @pl.when(pl.program_id(0) == 0)
    def _():
        for tile in tiles:
            unit, _ = norm_parts(tokens[:, tile].astype(F32))
            normed[:, tile] = (unit * params[:, 0:1] + params[:, 1:2]).astype(BF16)

    row_blocks = math.isqrt(len(blocks))
    for index, block in enumerate(blocks):
        lay(weights.at[0], index // row_blocks, index % row_blocks, block.at[0])
    out[0] = tn(weights[0], normed[...]).astype(BF16)


def front(gathered, slot_of, params, tokens, row_blocks):
    features, length = tokens.shape
    square = row_blocks * row_blocks
    whole = lambda shape: pl.BlockSpec(shape, lambda s, v: (0,) * len(shape), pipeline_mode=ONCE)
    blocks = block_specs(gathered, row_blocks, row_blocks, lambda s, i, j: s * square + i * row_blocks + j)
    return pl.pallas_call(
        front_kernel,
        grid_spec=pltpu.PrefetchScalarGridSpec(
            num_scalar_prefetch=1,
            grid=(3,),
            in_specs=[whole(params.shape), whole((features, length))] + blocks,
            out_specs=[
                pl.BlockSpec((1, features, features), lambda s, v: (s, 0, 0)),
                pl.BlockSpec((1, features, length), lambda s, v: (s, 0, 0)),
                pl.BlockSpec((features, length), lambda s, v: (0, 0)),
            ],
        ),
        out_shape=[
            jax.ShapeDtypeStruct((3, features, features), BF16),
            jax.ShapeDtypeStruct((3, features, length), BF16),
            jax.ShapeDtypeStruct((features, length), BF16),
        ],
        compiler_params=pltpu.CompilerParams(vmem_limit_bytes=60 << 20),
        name="front",
    )(slot_of, params, tokens, *([gathered] * square))


def gelu_pair(values):
    square = values * values
    bend = jnp.tanh(values * (0.7978845608028654 + (0.7978845608028654 * 0.044715) * square))
    half = 0.5 * values
    slope = 0.7978845608028654 + (3 * 0.7978845608028654 * 0.044715) * square
    return half + half * bend, 0.5 + 0.5 * bend + half * (1.0 - bend * bend) * slope


def middle_kernel(row_blocks, slot_of, params, tokens, attended, grad_low, *refs):
    del slot_of
    square = row_blocks * row_blocks
    out_blocks, up_blocks, down_blocks = (refs[square * k : square * (k + 1)] for k in range(3))
    outs, scratch = refs[3 * square : 3 * square + 8], refs[3 * square + 8 :]
    block_out, activated, grad_pre, normed, grad_branch, grad_att, grad_middle, sums = outs
    w_out, w_up, w_down, middle, total, stats, folds, sem = scratch
    tiles, parts = grad_low.shape[1] // GB, feature_parts(normed.shape[0])
    at = lambda index: pl.ds(pl.multiple_of(index * GB, GB), GB)
    step, last = pl.program_id(0), pl.num_programs(0) - 1

    @pl.when(step == 0)
    def _():
        copies = [
            pltpu.make_async_copy(tokens, block_out, sem.at[0]),
            pltpu.make_async_copy(attended, grad_att, sem.at[1]),
        ]
        for copy in copies:
            copy.start()
        for index, block in enumerate(out_blocks):
            lay(w_out, index // row_blocks, index % row_blocks, block.at[0])
        for copy in copies:
            copy.wait()
        def enter(index, carry):
            tile = at(index)
            for part in parts:
                values = block_out[part, tile].astype(F32) + tn(w_out[:, part], grad_att[:, tile])
                middle[part, tile] = values
                total[part, tile] = values
                grad_middle[part, tile] = jnp.zeros_like(values)
            values = middle[:, tile]
            average = jnp.mean(values, axis=0, keepdims=True)
            centred = values - average
            scale = lax.rsqrt(jnp.mean(centred * centred, axis=0, keepdims=True) + 1e-05)
            stats[0:1, tile] = average
            stats[1:2, tile] = scale
            normed[:, tile] = (centred * scale * params[:, 2:3] + params[:, 3:4]).astype(BF16)
            return carry

        lax.fori_loop(0, tiles, enter, 0)
        folds[...] = jnp.zeros_like(folds)

    for index in range(square):
        lay(w_up, index // row_blocks, index % row_blocks, up_blocks[index].at[0])
        lay(w_down, index // row_blocks, index % row_blocks, down_blocks[index].at[0])

    def advance(index, carry):
        tile = at(index)
        for part in parts:
            value, slope = gelu_pair(tn(w_up[:, part], normed[:, tile]))
            activated[part, tile] = value.astype(BF16)
            grad_pre[part, tile] = (nn(w_down[part, :], grad_low[:, tile]) * slope).astype(BF16)
        for part in parts:
            total[part, tile] += tn(w_down[:, part], activated[:, tile])
            grad_middle[part, tile] += nn(w_up[part, :], grad_pre[:, tile])
        return carry

    lax.fori_loop(0, tiles, advance, 0)

    @pl.when(step == last)
    def _():
        def leave(index, carry):
            tile = at(index)
            block_out[:, tile] = total[:, tile].astype(BF16)
            scale = stats[1:2, tile]
            unit = (middle[:, tile] - stats[0:1, tile]) * scale
            grad = grad_middle[:, tile]
            folds[0] += fold(grad * unit)
            folds[1] += fold(grad)
            values = grad_low[:, tile].astype(F32) + norm_back(unit, scale, params[:, 2:3], grad)
            grad_middle[:, tile] = values
            grad_branch[:, tile] = values.astype(BF16)
            for part in parts:
                grad_att[part, tile] = nn(w_out[part, :], grad_branch[:, tile]).astype(BF16)
            return carry

        lax.fori_loop(0, tiles, leave, 0)
        sums[...] = row_sums(folds[0], 2) + row_sums(folds[1], 3)


def middle_part(gathered, slot_of, params, tokens, attended, grad_low, row_blocks, col_blocks):
    features, length = tokens.shape
    square = row_blocks * row_blocks
    hidden = features * col_blocks // row_blocks
    up_start, down_start = 4 * square, 4 * square + row_blocks * col_blocks
    whole = lambda *shape: pl.BlockSpec(shape, lambda s, v: (0,) * len(shape), pipeline_mode=ONCE)
    anywhere = pl.BlockSpec(memory_space=pl.ANY)
    part = pl.BlockSpec((features, length), lambda s, v: (s, 0))
    blocks = (
        block_specs(
            gathered, row_blocks, row_blocks, lambda s, i, j: 3 * square + i * row_blocks + j, pipeline_mode=ONCE
        )
        + block_specs(
            gathered, row_blocks, row_blocks, lambda s, i, j: up_start + i * col_blocks + s * row_blocks + j
        )
        + block_specs(
            gathered, row_blocks, row_blocks, lambda s, i, j: down_start + (s * row_blocks + i) * row_blocks + j
        )
    )
    shape = jax.ShapeDtypeStruct
    square_scratch = pltpu.VMEM((features, features), BF16)
    return pl.pallas_call(
        functools.partial(middle_kernel, row_blocks),
        grid_spec=pltpu.PrefetchScalarGridSpec(
            num_scalar_prefetch=1,
            grid=(col_blocks // row_blocks,),
            in_specs=[whole(*params.shape)] + [anywhere] * 2 + [whole(features, length)] + blocks,
            out_specs=[whole(features, length), part, part]
            + [whole(features, length)] * 4
            + [whole(8, features)],
            scratch_shapes=[square_scratch] * 3
            + [pltpu.VMEM((features, length), F32)] * 2
            + [
                pltpu.VMEM((8, length), F32),
                pltpu.VMEM((2, features, 128), F32),
                pltpu.SemaphoreType.DMA((2,)),
            ],
        ),
        out_shape=[
            shape((features, length), BF16),
            shape((hidden, length), BF16),
            shape((hidden, length), BF16),
            shape((features, length), BF16),
            shape((features, length), BF16),
            shape((features, length), BF16),
            shape((features, length), F32),
            shape((8, features), F32),
        ],
        compiler_params=pltpu.CompilerParams(vmem_limit_bytes=63 << 20),
        name="middle_part",
    )(slot_of, params, tokens, attended, grad_low, *([gathered] * (3 * square)))


def weight_grad_kernel(block_of, deep, size, slot_of, left, right, *refs):
    grads, stage, sem = refs[-3:]
    wide = right.shape[0] // size
    rows, cols = pl.program_id(0), pl.program_id(1)
    step = rows * pl.num_programs(1) + cols
    steps = pl.num_programs(0) * pl.num_programs(1)
    now = step % 2

    def copy(buffer, index, slot):
        return pltpu.make_async_copy(stage.at[buffer, index], grads.at[slot], sem.at[buffer, index])

    @pl.when(step >= 2)
    def _():
        for index in range(deep * wide):
            copy(now, index, 0).wait()

    other = right[...]
    for i in range(deep):
        panel = nt(left[size * i : size * (i + 1), :], other)
        for j in range(wide):
            index = i * wide + j
            block = panel[:, size * j : size * (j + 1)]
            stage[now, index, :size] = block[:, :MAIN].astype(BF16)
            stage[now, index, size:] = pack_tail(block).astype(BF16)
            copy(now, index, slot_of[block_of(rows * deep + i, cols * wide + j)]).start()

    @pl.when(step == steps - 1)
    def _():
        for index in range(deep * wide):
            copy(now, index, 0).wait()

        @pl.when(steps > 1)
        def _():
            for index in range(deep * wide):
                copy(1 - now, index, 0).wait()


def weight_grad(left, right, slot_of, grads, slot_count, size, block_of, name):
    depth = left.shape[1]
    deep = wide = 4
    grid = (left.shape[0] // (size * deep), right.shape[0] // (size * wide))
    anywhere = pl.BlockSpec(memory_space=pl.ANY)
    operands = [slot_of, left, right] + ([] if grads is None else [grads])
    return pl.pallas_call(
        functools.partial(weight_grad_kernel, block_of, deep, size),
        grid_spec=pltpu.PrefetchScalarGridSpec(
            num_scalar_prefetch=1,
            grid=grid,
            in_specs=[
                pl.BlockSpec((size * deep, depth), lambda i, j, v: (i, 0)),
                pl.BlockSpec((size * wide, depth), lambda i, j, v: (j, 0)),
            ]
            + [anywhere] * (len(operands) - 3),
            out_specs=anywhere,
            scratch_shapes=[
                pltpu.VMEM((2, deep * wide, size + RUN, MAIN), BF16),
                pltpu.SemaphoreType.DMA((2, deep * wide)),
            ],
        ),
        out_shape=jax.ShapeDtypeStruct((slot_count, size + RUN, MAIN), BF16),
        input_output_aliases={} if grads is None else {3: 0},
        cost_estimate=cost(
            2 * left.shape[0] * right.shape[0] * depth,
            2 * (left.size + right.size + left.shape[0] * right.shape[0]),
        ),
        name=name,
    )(*operands)


EXTRA = 8
FAR = -1e30


def causal():
    return lax.broadcasted_iota(jnp.int32, (HALF, HALF), 0) <= lax.broadcasted_iota(jnp.int32, (HALF, HALF), 1)


def places(groups):
    found = []
    for group in range(groups):
        base = PREFIX + GB * group
        low, high = slice(base, base + HALF), slice(base + HALF, base + GB)
        found.append((low, high, slice(base, base + GB), slice(GB * group, GB * (group + 1))))
    return found


def side(left, right):
    return jnp.concatenate([left, right], axis=1)


def attention_kernel(scale, qkv, extras, out, lse, queries, keys, values, keys_t):
    head = qkv.shape[1]
    unit = scale * math.log2(math.e)

    @pl.when(pl.program_id(0) == 0)
    def _():
        queries[head:] = extras[0]
        keys[head:] = extras[1]
        values[head:] = extras[2]

    queries[:head] = qkv[0]
    keys[:head] = qkv[1]
    values[:head] = qkv[2]
    keys_t[...] = keys[...].T
    ahead = causal()
    spots = places(out.shape[1] // GB)
    scores = []
    for low, high, both, _ in spots:
        asked = queries[:, both]
        scores.append((nn(keys_t[:PREFIX], asked), nn(keys_t[low], asked), nn(keys_t[high], asked[:, HALF:])))

    def peak(array):
        return jnp.max(array, axis=0, keepdims=True)

    def soft(array, top):
        return jnp.exp2((array - top) * unit).astype(BF16)

    tops, weights = [], []
    for prefix, first, second in scores:
        first = side(jnp.where(ahead, first[:, :HALF], FAR), first[:, HALF:])
        second = jnp.where(ahead, second, FAR)
        top = jnp.maximum(peak(prefix), peak(first))
        top = side(top[:, :HALF], jnp.maximum(top[:, HALF:], peak(second)))
        tops.append(top)
        weights.append((soft(prefix, top), soft(first, top), soft(second, top[:, HALF:])))
    for (low, high, _, mine), top, (prefix, first, second) in zip(spots, tops, weights):
        sums = nn(values[:, :PREFIX], prefix) + nn(values[:, low], first)
        sums = side(sums[:, :HALF], sums[:, HALF:] + nn(values[:, high], second))
        total = sums[head : head + 1]
        out[:, mine] = (sums[:head] / total).astype(BF16)
        lse[0, :, mine] = top + jnp.log(total) * (1.0 / scale)


def thirds(values):
    high = values.astype(BF16).astype(F32)
    rest = values - high
    middle = rest.astype(BF16).astype(F32)
    return high, middle, rest - middle


def with_rows(base, start, rows):
    index = lax.broadcasted_iota(jnp.int32, base.shape, 0)
    for offset, row in enumerate(rows):
        base = jnp.where(index == start + offset, row, base)
    return base.astype(BF16)


def attention_back_kernel(scale, qkv, extras, out, lse, grad_out, grads, queries, keys, values, grad_o, keys_t, values_t):
    head, own = qkv.shape[1], out.shape[1]
    unit = scale * math.log2(math.e)

    @pl.when(pl.program_id(0) == 0)
    def _():
        keys[head:] = extras[1]
        values[head:] = extras[2]

    queries[:head] = qkv[0, :, PREFIX:]
    keys[:head] = qkv[1]
    values[:head] = qkv[2]
    grad_o[:head] = grad_out[...]
    keys_t[...] = keys[...].T
    values_t[...] = values[...].T
    queries[head:] = with_rows(extras[0, :, PREFIX:].astype(F32), 2, thirds(-lse[0]))
    delta = jnp.sum(grad_out[...].astype(F32) * out[...].astype(F32), axis=0, keepdims=True)
    grad_o[head:] = with_rows(jnp.zeros((EXTRA, own), F32), 0, thirds(-delta))
    ahead = causal()
    spots = places(own // GB)

    def weigh(rows, asked, given, mask):
        weights = jnp.exp2(nn(keys_t[rows], asked) * unit)
        if mask == 1:
            weights = side(jnp.where(ahead, weights[:, :HALF], 0.0), weights[:, HALF:])
        if mask == 2:
            weights = jnp.where(ahead, weights, 0.0)
        return weights.astype(BF16), (weights * nn(values_t[rows], given)).astype(BF16)

    found = []
    for low, high, _, mine in spots:
        asked, given = queries[:, mine], grad_o[:, mine]
        found.append(
            (
                weigh(slice(0, PREFIX), asked, given, 0),
                weigh(low, asked, given, 1),
                weigh(high, asked[:, HALF:], given[:, HALF:], 2),
            )
        )
    prefix_k = prefix_v = None
    for (low, high, both, mine), ((p0, d0), (p1, d1), (p2, d2)) in zip(spots, found):
        asked, given = queries[:head, mine], grad_o[:head, mine]
        grad_q = nn(keys[:head, :PREFIX], d0) + nn(keys[:head, low], d1)
        grad_q = side(grad_q[:, :HALF], grad_q[:, HALF:] + nn(keys[:head, high], d2))
        grads[0, :, both] = (grad_q * scale).astype(BF16)
        part_k, part_v = nt(asked, d0), nt(given, p0)
        prefix_k = part_k if prefix_k is None else prefix_k + part_k
        prefix_v = part_v if prefix_v is None else prefix_v + part_v
        grads[1, :, low] = (nt(asked, d1) * scale).astype(BF16)
        grads[2, :, low] = nt(given, p1).astype(BF16)
        grads[1, :, high] = (nt(asked[:, HALF:], d2) * scale).astype(BF16)
        grads[2, :, high] = nt(given[:, HALF:], p2).astype(BF16)
    grads[0, :, :PREFIX] = jnp.zeros((head, PREFIX), BF16)
    grads[1, :, :PREFIX] = (prefix_k * scale).astype(BF16)
    grads[2, :, :PREFIX] = prefix_v.astype(BF16)


def attention_specs(qkv):
    _, features, length = qkv.shape
    head, own = features // HEADS, length - PREFIX
    three = pl.BlockSpec((3, head, length), lambda h: (0, h, 0))
    extra = pl.BlockSpec((3, EXTRA, length), lambda h: (0, 0, 0))
    one = pl.BlockSpec((head, own), lambda h: (h, 0))
    row = pl.BlockSpec((1, 1, own), lambda h: (h, 0, 0))
    wide = lambda columns: pltpu.VMEM((head + EXTRA, columns), BF16)
    tall = pltpu.VMEM((length, head + EXTRA), BF16)
    return features, length, own, head, three, extra, one, row, wide, tall


def attention(qkv, extras):
    features, length, own, head, three, extra, one, row, wide, tall = attention_specs(qkv)
    return pl.pallas_call(
        functools.partial(attention_kernel, head ** (-0.5)),
        grid=(HEADS,),
        in_specs=[three, extra],
        out_specs=[one, row],
        out_shape=[
            jax.ShapeDtypeStruct((features, own), BF16),
            jax.ShapeDtypeStruct((HEADS, 1, own), F32),
        ],
        scratch_shapes=[wide(length), wide(length), wide(length), tall],
        cost_estimate=cost(8 * features * own * GB, 2 * qkv.size, HEADS * own * GB),
        name="attention",
    )(qkv, extras)


def attention_back(qkv, extras, out, lse, grad_out):
    features, length, own, head, three, extra, one, row, wide, tall = attention_specs(qkv)
    return pl.pallas_call(
        functools.partial(attention_back_kernel, head ** (-0.5)),
        grid=(HEADS,),
        in_specs=[three, extra, one, row, one],
        out_specs=three,
        out_shape=jax.ShapeDtypeStruct(qkv.shape, BF16),
        scratch_shapes=[wide(own), wide(length), wide(length), wide(own), tall, tall],
        cost_estimate=cost(20 * features * own * GB, 4 * qkv.size, HEADS * own * GB),
        name="attention_back",
    )(qkv, extras, out, lse, grad_out)


def score_extras(alive, prefix_alive, later):
    length = PREFIX + alive.shape[0]
    dead = jnp.where(jnp.concatenate([prefix_alive, alive]), 0.0, FAR)
    prefix = (jnp.arange(length) < PREFIX).astype(F32)
    barred = jnp.concatenate([jnp.zeros((PREFIX,)), jnp.where(jnp.repeat(later, GB), 0.0, FAR)])
    one, zero = jnp.ones((length,)), jnp.zeros((length,))
    query_rows = jnp.stack([one, barred] + [zero] * 6)
    key_rows = jnp.stack([dead, prefix] + [one] * 3 + [zero] * 3)
    value_rows = jnp.stack([one] * 3 + [zero] * 5)
    return jnp.stack([query_rows, key_rows, value_rows]).astype(BF16)


def split(values):
    high = values.astype(BF16)
    return high, (values - high.astype(F32)).astype(BF16)


def product(form, left, right):
    (left_high, left_low), (right_high, right_low) = left, right
    return form(left_high, right_high) + (form(left_high, right_low) + form(left_low, right_high))


def optimizer_kernel(scale, packed, master, average, left, right, root_left, root_right, *outs):
    slot_grad, new_left, new_right, new_master, new_copy, new_average = outs
    size = master.shape[1]
    grad = unpack(packed[0]) * scale
    slot_grad[0] = grad
    grad_parts = split(grad)
    new_left[0] = 0.5 * left[0] + (0.5 / size) * product(nt, grad_parts, grad_parts)
    new_right[0] = 0.5 * right[0] + (0.5 / size) * product(tn, grad_parts, grad_parts)
    right_part = product(nn, grad_parts, split(root_right[0]))
    step = product(nn, split(root_left[0]), split(right_part))
    moved = master[0] - 0.03 * step
    new_master[0] = moved
    new_copy[0] = moved.astype(BF16)
    new_average[0] = 0.8 * average[0] + 0.2 * moved


def optimizer(packed, scale, arrays):
    slots, size, _ = arrays[0].shape
    block = pl.BlockSpec((1, size, size), lambda i: (i, 0, 0))
    shape = lambda dtype: jax.ShapeDtypeStruct((slots, size, size), dtype)
    return pl.pallas_call(
        functools.partial(optimizer_kernel, scale),
        grid=(slots,),
        in_specs=[pl.BlockSpec((1,) + packed.shape[1:], lambda i: (i, 0, 0))] + [block] * 6,
        out_specs=[block] * 6,
        out_shape=[shape(F32), shape(F32), shape(F32), shape(F32), shape(BF16), shape(F32)],
        name="optimizer",
    )(packed, *arrays)


def norm_parts(values):
    average = jnp.mean(values, axis=0, keepdims=True)
    centred = values - average
    variance = jnp.mean(centred * centred, axis=0, keepdims=True)
    scale = lax.rsqrt(variance + 1e-05)
    return centred * scale, scale


def norm_back(unit, scale, gain, grad):
    inner = grad * gain
    mean_one = jnp.mean(inner, axis=0, keepdims=True)
    mean_two = jnp.mean(inner * unit, axis=0, keepdims=True)
    return scale * (inner - mean_one - unit * mean_two)


def local(
    chips,
    cores,
    tokens,
    cotangent,
    pad_mask,
    prefix_len,
    norm_gains,
    norm_shifts,
    owner_map,
    weight_copy,
    master,
    average_weights,
    stat_left,
    stat_right,
    root_left,
    root_right,
):
    cell_count, length, features = tokens.shape
    assert cell_count == 1
    slots, size, _ = weight_copy.shape
    slot_count = owner_map.shape[0]
    row_blocks = features // size
    square = row_blocks * row_blocks
    col_blocks = (slot_count - 4 * square) // (2 * row_blocks)
    known = chips == 16 and cores == 2
    chip = lax.axis_index("dp").astype(jnp.int32)
    seq_index = lax.axis_index("seq")

    slot_of = jnp.zeros((slot_count,), jnp.int32).at[owner_map].set(jnp.arange(slot_count, dtype=jnp.int32))
    if known:
        gathered = gather_slots(pack_slots(weight_copy, chip.reshape(1), slot_count), slots)
    else:
        packed = pack_slots(weight_copy, jnp.zeros((1,), jnp.int32), slots)
        gathered = lax.all_gather(packed, "dp", axis=0, tiled=True)

    def three_of(i, j):
        return (j // row_blocks) * square + i * row_blocks + j % row_blocks

    def out_of(i, j):
        return 3 * square + i * row_blocks + j

    def up_of(i, j):
        return 4 * square + i * col_blocks + j

    def down_of(i, j):
        return 4 * square + row_blocks * col_blocks + i * row_blocks + j

    own_tokens = tokens.reshape(length, features).T
    prefix_tokens = own_tokens[:, :PREFIX]
    if cores == 2:
        arrived = lax.ppermute(prefix_tokens, "seq", [(0, 1)])
        prefix_tokens = jnp.where(seq_index == 0, prefix_tokens, arrived)
    else:
        prefix_tokens = lax.all_gather(prefix_tokens, "seq")[0]
    norms = jnp.stack([norm_gains[0], norm_shifts[0], norm_gains[1], norm_shifts[1]])
    params = norms.T
    all_tokens = jnp.concatenate([prefix_tokens, own_tokens], axis=1)
    w_three, qkv, normed_in = front(gathered, slot_of, params, all_tokens, row_blocks)

    position = seq_index * length + jnp.arange(length, dtype=jnp.int32)
    alive = jnp.where(position < PREFIX, position < prefix_len[0], pad_mask[0] == 1)
    prefix_alive = jnp.arange(PREFIX, dtype=jnp.int32) < prefix_len[0]
    groups = length // GB
    later = seq_index * groups + jnp.arange(groups) > 0
    extras = score_extras(alive, prefix_alive, later)

    grad_low = cotangent.reshape(length, features).T
    attended, log_total = attention(qkv, extras)
    block_out, activated, grad_pre, normed_mid, grad_branch, grad_att, grad_middle, sums = middle_part(
        gathered, slot_of, params, own_tokens, attended, grad_low, row_blocks, col_blocks
    )
    grads = weight_grad(activated, grad_low, slot_of, None, slot_count, size, down_of, "grad_down")
    grads = weight_grad(normed_mid, grad_pre, slot_of, grads, slot_count, size, up_of, "grad_up")
    grads = weight_grad(attended, grad_branch, slot_of, grads, slot_count, size, out_of, "grad_out")
    grad_three = attention_back(qkv, extras, attended, log_total, grad_att)
    flat_three = grad_three.reshape(3 * features, PREFIX + length)
    grads = weight_grad(normed_in, flat_three, slot_of, grads, slot_count, size, three_of, "grad_three")
    grad_scale = 1.0 / math.sqrt(length * chips * cores)
    if known:
        summed, grad_input, norm_sums = reduce_slots(
            grads, slots, w_three, grad_three, own_tokens, grad_middle, params, sums
        )
    else:
        part = lax.psum_scatter(grads.astype(F32), "dp", scatter_dimension=0, tiled=True)
        summed = lax.psum(part, "seq")
        grad_all = sum(nn(w_three[k], grad_three[k]) for k in range(3))
        prefix_part = jnp.where(seq_index == 0, lax.psum(grad_all[:, :PREFIX], "seq"), 0.0)
        grad_normed = grad_all[:, PREFIX:] + jnp.pad(prefix_part, ((0, 0), (0, length - PREFIX)))
        unit_one, scale_one = norm_parts(own_tokens.astype(F32))
        grad_input = grad_middle + norm_back(unit_one, scale_one, params[:, 0:1], grad_normed)
        first_sums = [jnp.sum(grad_normed * unit_one, axis=1), jnp.sum(grad_normed, axis=1)]
        norm_sums = lax.psum(jnp.stack(first_sums + [sums[2], sums[3]]), ("dp", "seq"))
    norm_grad = norm_sums[:4] * grad_scale
    new_norms = norms - 0.1 * norm_grad * lax.rsqrt(jnp.mean(norm_grad * norm_grad) + 1e-06)
    stepped = optimizer(
        summed, grad_scale, (master, average_weights, stat_left, stat_right, root_left, root_right)
    )
    token_shape = (cell_count, length, features)
    return (
        block_out.T.reshape(token_shape),
        grad_input.T.reshape(token_shape),
        norm_grad,
        new_norms,
        *stepped,
    )


def solution(mesh):
    tokens, slots = P("dp", "seq", None), P("dp", None, None)
    in_specs = (tokens, tokens, P("dp", "seq"), P("dp"), P(), P(), P()) + (slots,) * 7
    out_specs = (tokens, tokens, P(), P()) + (slots,) * 6
    body = functools.partial(local, mesh.shape["dp"], mesh.shape["seq"])
    return jax.shard_map(body, mesh=mesh, in_specs=in_specs, out_specs=out_specs, check_vma=False)
```

```python
import functools
import math

import jax
import jax.numpy as jnp
from jax import lax
from jax.experimental import pallas as pl
from jax.experimental.pallas import tpu as pltpu
from jax.sharding import PartitionSpec as P

HEADS = 20
GB = 256
PREFIX = 128
HALF = GB // 2
MESH = pl.DeviceIdType.MESH
BF16 = jnp.bfloat16
F32 = jnp.float32

MAIN = 256
RUN = 32


def runs(size):
    rest, per_tile = size - MAIN, 128 // (size - MAIN)
    places = []
    for index in range(-(-size // RUN)):
        lane = 128 * (index // per_tile) + rest * (index % per_tile)
        places.append((RUN * index, min(RUN, size - RUN * index), lane))
    assert places[-1][2] + rest <= MAIN
    return places


def pack_tail(block):
    size = block.shape[0]
    rest = size - MAIN
    pieces, lane = [], 0
    for row, count, start in runs(size):
        if start > lane:
            pieces.append(jnp.zeros((RUN, start - lane), block.dtype))
        piece = block[row : row + count, MAIN:]
        if count < RUN:
            piece = jnp.concatenate([piece, jnp.zeros((RUN - count, rest), block.dtype)], axis=0)
        pieces.append(piece)
        lane = start + rest
    if lane < MAIN:
        pieces.append(jnp.zeros((RUN, MAIN - lane), block.dtype))
    return jnp.concatenate(pieces, axis=1)


def unpack(packed):
    size = packed.shape[0] - RUN
    rest = size - MAIN
    low = packed[size:]
    tail = [low[:count, lane : lane + rest] for _, count, lane in runs(size)]
    return jnp.concatenate([packed[:size], jnp.concatenate(tail, axis=0)], axis=1)


def tn(left, right):
    return lax.dot_general(left, right, (((0,), (0,)), ((), ())), preferred_element_type=F32)


def nn(left, right):
    return lax.dot_general(left, right, (((1,), (0,)), ((), ())), preferred_element_type=F32)


def nt(left, right):
    return lax.dot_general(left, right, (((1,), (1,)), ((), ())), preferred_element_type=F32)


def cost(flops, moved, exps=0):
    return pl.CostEstimate(flops=int(flops), bytes_accessed=int(moved), transcendentals=int(exps))


def pack_kernel(start, block, packed):
    del start
    size = block.shape[1]
    rest = size - MAIN
    packed[0, :size] = block[0, :, :MAIN]
    packed[0, size:] = jnp.zeros((RUN, MAIN), BF16)
    for row, count, lane in runs(size):
        packed[0, size : size + count, lane : lane + rest] = block[0, row : row + count, MAIN:]


def pack_slots(blocks, start, count, slot_count):
    size = blocks.shape[1]
    return pl.pallas_call(
        pack_kernel,
        grid_spec=pltpu.PrefetchScalarGridSpec(
            num_scalar_prefetch=1,
            grid=(count,),
            in_specs=[pl.BlockSpec((1, size, size), lambda i, start: (start[0] + i, 0, 0))],
            out_specs=pl.BlockSpec((1, size + RUN, MAIN), lambda i, start: (start[1] + i, 0, 0)),
        ),
        out_shape=jax.ShapeDtypeStruct((slot_count, size + RUN, MAIN), BF16),
        name="pack_slots",
    )(start, blocks)


def place():
    me, core = lax.axis_index("dp"), lax.axis_index("seq")
    x, y, z = me % 2, (me // 2) % 2, me // 4
    step_x, step_y = 1 - 2 * x, 2 * (1 - 2 * y)
    first = step_y * (1 - core) + step_x * core
    second = step_x * (1 - core) + step_y * core
    return me, core, z, first, second


def greet(partners):
    barrier = pltpu.get_barrier_semaphore()
    for chip, core in partners:
        pl.semaphore_signal(barrier, inc=1, device_id=(chip, core), device_id_type=MESH)
    pl.semaphore_wait(barrier, len(partners))


UP, DOWN, FIRST, SECOND, TWIN, HEAD, GATHER_LABELS = 0, 4, 8, 12, 20, 36, 37


def gather_kernel(slots, placed, tokens, params, out, normed, held, send, recv, take):
    del placed
    me, core, z, first, second = place()
    half = slots // 2
    line = [(me + 4 * ((z + r) % 4 - z), core) for r in range(1, 4)]
    greet([(me + first, core), (me + second, core), (me, 1 - core)] + line)

    def copy(label, chip, dp, c):
        ref = out.at[pl.ds(chip * slots + core * half, half)]
        return pltpu.make_async_remote_copy(
            src_ref=ref,
            dst_ref=ref,
            send_sem=send.at[label],
            recv_sem=recv.at[label],
            device_id=(dp, c),
            device_id_type=MESH,
        )

    def col(zz):
        return me + 4 * (zz - z)

    def up(j):
        return copy(UP + j, me - 4 * (j - 1), me + 4, core)

    def down(j):
        return copy(DOWN + j, me + 4 * (j - 1), me - 4, core)

    def to_first(zz):
        return copy(FIRST + zz, col(zz), me + first, core)

    def to_second(zz, a):
        return copy(SECOND + 2 * zz + a, col(zz) + a * first, me + second, core)

    def to_twin(chip):
        return copy(TWIN + chip, chip, me, 1 - core)

    def spread(zz):
        to_first(zz).start()
        to_second(zz, 0).start()
        to_twin(col(zz)).start()

    def after_first(zz):
        to_first(zz).wait_recv()
        to_second(zz, 1).start()
        to_twin(col(zz) + first).start()

    def after_second(zz):
        for a in range(2):
            to_second(zz, a).wait_recv()
            to_twin(col(zz) + second + a * first).start()

    @pl.when(z < 3)
    def _():
        up(1).start()

    @pl.when(z > 0)
    def _():
        down(1).start()

    spread(z)

    prefix, seat = tokens.at[:, pl.ds(0, PREFIX)], held.at[:, pl.ds(0, PREFIX)]
    mine = pltpu.make_async_copy(tokens, held.at[:, pl.ds(PREFIX, tokens.shape[1])], take.at[0])
    near = pltpu.make_async_copy(prefix, seat, take.at[1])
    far = pltpu.make_async_remote_copy(
        src_ref=prefix,
        dst_ref=seat,
        send_sem=send.at[HEAD],
        recv_sem=recv.at[HEAD],
        device_id=(me, 1 - core),
        device_id_type=MESH,
    )
    mine.start()

    @pl.when(core == 0)
    def _():
        far.start()
        near.start()
        near.wait()

    @pl.when(core == 1)
    def _():
        far.wait_recv()

    mine.wait()

    def normalize(index, carry):
        tile = pl.ds(pl.multiple_of(index * PREFIX, PREFIX), PREFIX)
        unit, _ = norm_parts(held[:, tile].astype(F32))
        normed[:, tile] = (unit * params[:, 0:1] + params[:, 1:2]).astype(BF16)
        return carry

    lax.fori_loop(0, held.shape[1] // PREFIX, normalize, 0)
    for j in range(1, 4):

        @pl.when(z >= j)
        def _():
            up(j).wait_recv()
            if j < 3:

                @pl.when(z < 3)
                def _():
                    up(j + 1).start()

            spread(z - j)

        @pl.when(z + j <= 3)
        def _():
            down(j).wait_recv()
            if j < 3:

                @pl.when(z > 0)
                def _():
                    down(j + 1).start()

            spread(z + j)

        if j == 1:
            after_first(z)
        else:

            @pl.when(z >= j - 1)
            def _():
                after_first(z - (j - 1))

            @pl.when(z + j - 1 <= 3)
            def _():
                after_first(z + j - 1)

    @pl.when(z >= 3)
    def _():
        after_first(z - 3)

    @pl.when(z <= 0)
    def _():
        after_first(z + 3)

    after_second(z)
    for j in range(1, 4):

        @pl.when(z >= j)
        def _():
            after_second(z - j)

        @pl.when(z + j <= 3)
        def _():
            after_second(z + j)

    for zz in range(4):
        for a in range(2):
            for b in range(2):
                chip = col(zz) + a * first + b * second
                to_twin(chip).wait_recv()
                to_twin(chip).wait_send()
        to_first(zz).wait_send()
        for a in range(2):
            to_second(zz, a).wait_send()

    @pl.when(z < 3)
    def _():
        up(1).wait_send()
        for j in range(1, 3):

            @pl.when(z >= j)
            def _():
                up(j + 1).wait_send()

    @pl.when(z > 0)
    def _():
        down(1).wait_send()
        for j in range(1, 3):

            @pl.when(z + j <= 3)
            def _():
                down(j + 1).wait_send()

    @pl.when(core == 0)
    def _():
        far.wait_send()


def gather_slots(placed, tokens, params, slots):
    anywhere, inside = pl.BlockSpec(memory_space=pl.ANY), pl.BlockSpec(memory_space=pltpu.VMEM)
    wide = (tokens.shape[0], PREFIX + tokens.shape[1])
    return pl.pallas_call(
        functools.partial(gather_kernel, slots),
        out_shape=[jax.ShapeDtypeStruct(placed.shape, placed.dtype), jax.ShapeDtypeStruct(wide, BF16)],
        in_specs=[anywhere, anywhere, inside],
        out_specs=[anywhere, inside],
        scratch_shapes=[
            pltpu.VMEM(wide, BF16),
            pltpu.SemaphoreType.DMA((GATHER_LABELS,)),
            pltpu.SemaphoreType.DMA((GATHER_LABELS,)),
            pltpu.SemaphoreType.DMA((2,)),
        ],
        input_output_aliases={0: 0},
        compiler_params=pltpu.CompilerParams(collective_id=0, has_side_effects=True),
        name="gather_slots",
    )(placed, tokens, params)


R_TWIN, R_SECOND, R_FIRST, R_LINE, R_DONE, R_PREFIX, R_FLOW, REDUCE_LABELS = 0, 16, 24, 28, 32, 33, 34, 42
RING = 3
PANELS = 5


def reduce_kernel(
    slots,
    grads,
    w_three,
    grad_three,
    tokens,
    grad_middle,
    params,
    sums,
    out,
    grad_input,
    norm_sums,
    ring,
    r_twin,
    r_second,
    r_first,
    r_line,
    total,
    weights,
    inner,
    acc,
    prefix,
    given,
    folds,
    flow,
    arrived,
    load,
    send,
    recv,
    save,
):
    me, core, z, first, second = place()
    half = slots // 2
    features, length = acc.shape
    line = [(me + 4 * ((z + r) % 4 - z), core) for r in range(1, 4)]
    greet([(me + first, core), (me + second, core), (me, 1 - core)] + line)

    def piece(chip, h):
        return grads.at[pl.ds(chip * slots + h * half, half)]

    def chip_at(zz, a, b):
        return me + 4 * (zz - z) + a * first + b * second

    def remote(src, dst, label, dp, c):
        return pltpu.make_async_remote_copy(
            src_ref=src,
            dst_ref=dst,
            send_sem=send.at[label],
            recv_sem=recv.at[label],
            device_id=(dp, c),
            device_id_type=MESH,
        )

    def twin(zz, a, b):
        chip = chip_at(zz, a, b)
        return remote(piece(chip, 1 - core), r_twin.at[chip], R_TWIN + chip, me, 1 - core)

    def to_second(zz, a):
        return remote(
            r_twin.at[chip_at(zz, a, 1)], r_second.at[2 * zz + a], R_SECOND + 2 * zz + a, me + second, core
        )

    def to_first(zz):
        return remote(r_twin.at[chip_at(zz, 1, 0)], r_first.at[zz], R_FIRST + zz, me + first, core)

    def to_line(r):
        zz = (z + r) % 4
        return remote(r_twin.at[chip_at(zz, 0, 0)], r_line.at[r - 1], R_LINE + r, chip_at(zz, 0, 0), core)

    order = [2, 1, 3, 0]
    where = [(z + r) % 4 for r in order]
    turns = []
    for index in range(3):
        turns += [(where[index], 1, 1), (where[index], 0, 1)]
    turns += [(where[0], 1, 0), (where[3], 1, 1), (where[3], 0, 1), (where[0], 0, 0), (where[1], 1, 0)]
    turns += [(where[2], 1, 0), (where[1], 0, 0), (where[3], 1, 0), (where[2], 0, 0), (where[3], 0, 0)]

    def load_own(turn):
        return pltpu.make_async_copy(piece(chip_at(*turns[turn]), core), ring.at[turn % RING], load.at[turn % RING])

    def add_up(turn, others):
        chip = chip_at(*turns[turn])
        load_own(turn).wait()
        twin(*turns[turn]).wait_recv()

        def body(s, carry):
            value = ring[turn % RING, s].astype(F32) + r_twin[chip, s].astype(F32)
            for ref, index in others:
                value = value + ref[index, s].astype(F32)
            if turn < len(turns) - 1:
                r_twin[chip, s] = value.astype(BF16)
            else:
                total[s] = value
            return carry

        lax.fori_loop(0, half, body, 0)
        if turn + RING < len(turns):
            load_own(turn + RING).start()

    def send_second(turn):
        zz, a, _ = turns[turn]
        add_up(turn, [])
        to_second(zz, a).start()

    def send_first(turn):
        zz = turns[turn][0]
        to_second(zz, 1).wait_recv()
        add_up(turn, [(r_second, 2 * zz + 1)])
        to_first(zz).start()

    def send_line(turn, r):
        zz = turns[turn][0]
        to_second(zz, 0).wait_recv()
        to_first(zz).wait_recv()
        add_up(turn, [(r_second, 2 * zz), (r_first, zz)])
        to_line(r).start()

    for turn in range(RING):
        load_own(turn).start()
    for zz in where:
        for a in (1, 0):
            twin(zz, 1, a).start()
    for zz in where:
        for a in (1, 0):
            twin(zz, 0, a).start()
    fetches = [
        pltpu.make_async_copy(w_three, weights, save.at[0]),
        pltpu.make_async_copy(grad_three, inner, save.at[1]),
    ]
    for fetch in fetches:
        fetch.start()
    for turn in range(6):
        send_second(turn)
    send_first(6)
    send_second(7)
    send_second(8)
    for fetch in fetches:
        fetch.wait()

    rows = features // PANELS

    def panel(index, carry):
        mine = pl.ds(pl.multiple_of(index * rows, 16), rows)
        acc[mine, :] = sum(nn(weights[k, mine, :], inner[k]) for k in range(3))
        return carry

    lax.fori_loop(0, PANELS, panel, 0)

    swap = remote(acc.at[:, pl.ds(0, PREFIX)], prefix, R_PREFIX, me, 1 - core)
    swap.start()
    own_tokens = weights.at[0, :, pl.ds(0, length - PREFIX)]
    take = pltpu.make_async_copy(tokens, own_tokens, save.at[0])
    take.start()

    def at(index):
        return pl.ds(pl.multiple_of(index * GB, GB), GB)

    def ahead(index):
        return pl.ds(pl.multiple_of(PREFIX + index * GB, PREFIX), GB)

    def give(index, slot):
        return pltpu.make_async_copy(grad_middle.at[:, at(index)], given.at[slot], save.at[2 + slot])

    def store(index):
        return pltpu.make_async_copy(acc.at[:, ahead(index)], grad_input.at[:, at(index)], save.at[4 + index])

    give(0, 0).start()
    send_line(9, order[0])
    send_first(10)
    take.wait()
    swap.wait()
    here = (1 - core).astype(F32)
    acc[:, PREFIX : 2 * PREFIX] += (acc[:, :PREFIX] + prefix[...]) * here
    folds[...] = jnp.zeros_like(folds)
    groups = (length - PREFIX) // GB

    def back(index, carry):
        @pl.when(index + 1 < groups)
        def _():
            give(index + 1, (index + 1) % 2).start()

        give(index, index % 2).wait()
        unit, scale = norm_parts(weights[0, :, at(index)].astype(F32))
        grad = acc[:, ahead(index)]
        folds[0] += fold(grad * unit)
        folds[1] += fold(grad)
        acc[:, ahead(index)] = given[index % 2] + norm_back(unit, scale, params[:, 0:1], grad)
        store(index).start()
        return carry

    lax.fori_loop(0, groups, back, 0)
    flow[0] = sums[...] + row_sums(folds[0], 0) + row_sums(folds[1], 1)
    pairs = [(me, 1 - core), (me + first, core), (me, 1 - core), (me + first, core), (me, 1 - core)] + line
    sources = [flow.at[0], flow.at[1], flow.at[2], arrived.at[2], flow.at[3]] + [flow.at[4]] * 3

    def pass_on(k):
        return remote(sources[k], arrived.at[k], R_FLOW + k, *pairs[k])

    for k in range(2):
        pass_on(k).start()
        pass_on(k).wait_recv()
        flow[k + 1] = flow[k] + arrived[k]
    pass_on(2).start()
    pass_on(2).wait_recv()
    pass_on(3).start()
    send_first(11)
    pass_on(3).wait_recv()
    flow[3] = arrived[2] + arrived[3]
    pass_on(4).start()
    pass_on(4).wait_recv()
    plane = jnp.where(core == 0, flow[3], arrived[4])
    flow[4] = plane
    arrived[4] = plane
    for k in range(5, 8):
        pass_on(k).start()
    send_line(12, order[1])
    send_first(13)
    send_line(14, order[2])
    for k in range(5, 8):
        pass_on(k).wait_recv()
    norm_sums[...] = sum(arrived[4 + (z - zz + 4) % 4] for zz in range(4))
    to_second(z, 0).wait_recv()
    to_first(z).wait_recv()
    for r in range(1, 4):
        to_line(r).wait_recv()
    add_up(15, [(r_second, 2 * z), (r_first, z), (r_line, 0), (r_line, 1), (r_line, 2)])
    target = out.at[pl.ds(core * half, half)]
    done = remote(total, target, R_DONE, me, 1 - core)
    done.start()
    saved = pltpu.make_async_copy(total, target, save.at[0])
    saved.start()
    for zz in range(4):
        for a in range(2):
            for b in range(2):
                twin(zz, a, b).wait_send()
            to_second(zz, a).wait_send()
        to_first(zz).wait_send()
    for r in range(1, 4):
        to_line(r).wait_send()
    for k in range(len(pairs)):
        pass_on(k).wait_send()
    for index in range(groups):
        store(index).wait()
    done.wait()
    saved.wait()


def reduce_slots(grads, slots, w_three, grad_three, tokens, grad_middle, params, sums):
    _, lines, lanes = grads.shape
    half = slots // 2
    _, features, length = grad_three.shape
    pieces = lambda n: pltpu.VMEM((n, half, lines, lanes), BF16)
    anywhere, inside = pl.BlockSpec(memory_space=pl.ANY), pl.BlockSpec(memory_space=pltpu.VMEM)
    groups = (length - PREFIX) // GB
    return pl.pallas_call(
        functools.partial(reduce_kernel, slots),
        out_shape=[
            jax.ShapeDtypeStruct((slots, lines, lanes), F32),
            jax.ShapeDtypeStruct((features, length - PREFIX), F32),
            jax.ShapeDtypeStruct((8, features), F32),
        ],
        in_specs=[anywhere] * 5 + [inside] * 2,
        out_specs=[anywhere, anywhere, inside],
        scratch_shapes=[
            pieces(RING),
            pieces(16),
            pieces(8),
            pieces(4),
            pieces(3),
            pltpu.VMEM((half, lines, lanes), F32),
            pltpu.VMEM(w_three.shape, BF16),
            pltpu.VMEM(grad_three.shape, BF16),
            pltpu.VMEM((features, length), F32),
            pltpu.VMEM((features, PREFIX), F32),
            pltpu.VMEM((2, features, GB), F32),
            pltpu.VMEM((2, features, 128), F32),
            pltpu.VMEM((5, 8, features), F32),
            pltpu.VMEM((8, 8, features), F32),
            pltpu.SemaphoreType.DMA((RING,)),
            pltpu.SemaphoreType.DMA((REDUCE_LABELS,)),
            pltpu.SemaphoreType.DMA((REDUCE_LABELS,)),
            pltpu.SemaphoreType.DMA((4 + groups,)),
        ],
        compiler_params=pltpu.CompilerParams(collective_id=1, has_side_effects=True, vmem_limit_bytes=63 << 20),
        name="reduce_slots",
    )(grads, w_three, grad_three, tokens, grad_middle, params, sums)


def lay(matrix, row, col, block):
    size = block.shape[0] - RUN
    matrix[size * row : size * (row + 1), size * col : size * col + MAIN] = block[:size]
    for start, count, lane in runs(size):
        piece = block[size : size + count, lane : lane + size - MAIN]
        matrix[size * row + start : size * row + start + count, size * col + MAIN : size * (col + 1)] = piece


def block_specs(gathered, rows, cols, block_of, **mode):
    shape = (1,) + gathered.shape[1:]
    pick = lambda i, j, step, v: (v[block_of(step, i, j)], 0, 0)
    return [
        pl.BlockSpec(shape, functools.partial(pick, i, j), **mode) for i in range(rows) for j in range(cols)
    ]


def feature_parts(features):
    part = -(-features // 256) * 128
    return [slice(start, min(start + part, features)) for start in range(0, features, part)]


def fold(values):
    return sum(values[:, start : start + 128] for start in range(0, values.shape[1], 128))


def row_sums(values, row):
    ones = jnp.ones((8, values.shape[1]), F32)
    summed = lax.dot_general(
        ones, values, (((1,), (1,)), ((), ())), precision=lax.Precision.HIGHEST, preferred_element_type=F32
    )
    return jnp.where(lax.broadcasted_iota(jnp.int32, summed.shape, 0) == row, summed, 0.0)


ONCE = pl.Buffered(1)


def front_kernel(slot_of, normed, *refs):
    del slot_of
    blocks, (weights, out) = refs[:-2], refs[-2:]
    row_blocks = math.isqrt(len(blocks))
    for index, block in enumerate(blocks):
        lay(weights.at[0], index // row_blocks, index % row_blocks, block.at[0])
    out[0] = tn(weights[0], normed[...]).astype(BF16)


def front(gathered, slot_of, normed, row_blocks):
    features, length = normed.shape
    square = row_blocks * row_blocks
    blocks = block_specs(gathered, row_blocks, row_blocks, lambda s, i, j: s * square + i * row_blocks + j)
    return pl.pallas_call(
        front_kernel,
        grid_spec=pltpu.PrefetchScalarGridSpec(
            num_scalar_prefetch=1,
            grid=(3,),
            in_specs=[pl.BlockSpec((features, length), lambda s, v: (0, 0), pipeline_mode=ONCE)] + blocks,
            out_specs=[
                pl.BlockSpec((1, features, features), lambda s, v: (s, 0, 0)),
                pl.BlockSpec((1, features, length), lambda s, v: (s, 0, 0)),
            ],
        ),
        out_shape=[
            jax.ShapeDtypeStruct((3, features, features), BF16),
            jax.ShapeDtypeStruct((3, features, length), BF16),
        ],
        compiler_params=pltpu.CompilerParams(vmem_limit_bytes=60 << 20),
        name="front",
    )(slot_of, normed, *([gathered] * square))


def gelu_pair(values):
    square = values * values
    bend = jnp.tanh(values * (0.7978845608028654 + (0.7978845608028654 * 0.044715) * square))
    half = 0.5 * values
    slope = 0.7978845608028654 + (3 * 0.7978845608028654 * 0.044715) * square
    return half + half * bend, 0.5 + 0.5 * bend + half * (1.0 - bend * bend) * slope


def middle_kernel(row_blocks, slot_of, params, tokens, attended, grad_low, *refs):
    del slot_of
    square = row_blocks * row_blocks
    out_blocks, up_blocks, down_blocks = (refs[square * k : square * (k + 1)] for k in range(3))
    outs, scratch = refs[3 * square : 3 * square + 8], refs[3 * square + 8 :]
    block_out, activated, grad_pre, normed, grad_branch, grad_att, grad_middle, sums = outs
    w_out, w_up, w_down, middle, total, stats, folds, sem = scratch
    tiles, parts = grad_low.shape[1] // GB, feature_parts(normed.shape[0])
    at = lambda index: pl.ds(pl.multiple_of(index * GB, GB), GB)
    step, last = pl.program_id(0), pl.num_programs(0) - 1

    @pl.when(step == 0)
    def _():
        copies = [
            pltpu.make_async_copy(tokens, block_out, sem.at[0]),
            pltpu.make_async_copy(attended, grad_att, sem.at[1]),
        ]
        for copy in copies:
            copy.start()
        for index, block in enumerate(out_blocks):
            lay(w_out, index // row_blocks, index % row_blocks, block.at[0])
        for copy in copies:
            copy.wait()
        def enter(index, carry):
            tile = at(index)
            for part in parts:
                values = block_out[part, tile].astype(F32) + tn(w_out[:, part], grad_att[:, tile])
                middle[part, tile] = values
                total[part, tile] = values
                grad_middle[part, tile] = jnp.zeros_like(values)
            values = middle[:, tile]
            average = jnp.mean(values, axis=0, keepdims=True)
            centred = values - average
            scale = lax.rsqrt(jnp.mean(centred * centred, axis=0, keepdims=True) + 1e-05)
            stats[0:1, tile] = average
            stats[1:2, tile] = scale
            normed[:, tile] = (centred * scale * params[:, 2:3] + params[:, 3:4]).astype(BF16)
            return carry

        lax.fori_loop(0, tiles, enter, 0)
        folds[...] = jnp.zeros_like(folds)

    for index in range(square):
        lay(w_up, index // row_blocks, index % row_blocks, up_blocks[index].at[0])
        lay(w_down, index // row_blocks, index % row_blocks, down_blocks[index].at[0])

    def advance(index, carry):
        tile = pl.ds(pl.multiple_of(index * wide, wide), wide)
        for part in parts:
            value, slope = gelu_pair(tn(w_up[:, part], normed[:, tile]))
            activated[part, tile] = value.astype(BF16)
            grad_pre[part, tile] = (nn(w_down[part, :], grad_low[:, tile]) * slope).astype(BF16)
        for part in parts:
            total[part, tile] += tn(w_down[:, part], activated[:, tile])
            grad_middle[part, tile] += nn(w_up[part, :], grad_pre[:, tile])
        return carry

    wide = 2 * GB if tiles % 2 == 0 else GB
    lax.fori_loop(0, grad_low.shape[1] // wide, advance, 0)

    @pl.when(step == last)
    def _():
        def leave(index, carry):
            tile = at(index)
            block_out[:, tile] = total[:, tile].astype(BF16)
            scale = stats[1:2, tile]
            unit = (middle[:, tile] - stats[0:1, tile]) * scale
            grad = grad_middle[:, tile]
            folds[0] += fold(grad * unit)
            folds[1] += fold(grad)
            values = grad_low[:, tile].astype(F32) + norm_back(unit, scale, params[:, 2:3], grad)
            grad_middle[:, tile] = values
            grad_branch[:, tile] = values.astype(BF16)
            for part in parts:
                grad_att[part, tile] = nn(w_out[part, :], grad_branch[:, tile]).astype(BF16)
            return carry

        lax.fori_loop(0, tiles, leave, 0)
        sums[...] = row_sums(folds[0], 2) + row_sums(folds[1], 3)


def middle_part(gathered, slot_of, params, tokens, attended, grad_low, row_blocks, col_blocks):
    features, length = tokens.shape
    square = row_blocks * row_blocks
    hidden = features * col_blocks // row_blocks
    up_start, down_start = 4 * square, 4 * square + row_blocks * col_blocks
    whole = lambda *shape: pl.BlockSpec(shape, lambda s, v: (0,) * len(shape), pipeline_mode=ONCE)
    anywhere = pl.BlockSpec(memory_space=pl.ANY)
    part = pl.BlockSpec((features, length), lambda s, v: (s, 0))
    blocks = (
        block_specs(
            gathered, row_blocks, row_blocks, lambda s, i, j: 3 * square + i * row_blocks + j, pipeline_mode=ONCE
        )
        + block_specs(
            gathered, row_blocks, row_blocks, lambda s, i, j: up_start + i * col_blocks + s * row_blocks + j
        )
        + block_specs(
            gathered, row_blocks, row_blocks, lambda s, i, j: down_start + (s * row_blocks + i) * row_blocks + j
        )
    )
    shape = jax.ShapeDtypeStruct
    square_scratch = pltpu.VMEM((features, features), BF16)
    return pl.pallas_call(
        functools.partial(middle_kernel, row_blocks),
        grid_spec=pltpu.PrefetchScalarGridSpec(
            num_scalar_prefetch=1,
            grid=(col_blocks // row_blocks,),
            in_specs=[whole(*params.shape)] + [anywhere] * 2 + [whole(features, length)] + blocks,
            out_specs=[whole(features, length), part, part]
            + [whole(features, length)] * 4
            + [whole(8, features)],
            scratch_shapes=[square_scratch] * 3
            + [pltpu.VMEM((features, length), F32)] * 2
            + [
                pltpu.VMEM((8, length), F32),
                pltpu.VMEM((2, features, 128), F32),
                pltpu.SemaphoreType.DMA((2,)),
            ],
        ),
        out_shape=[
            shape((features, length), BF16),
            shape((hidden, length), BF16),
            shape((hidden, length), BF16),
            shape((features, length), BF16),
            shape((features, length), BF16),
            shape((features, length), BF16),
            shape((features, length), F32),
            shape((8, features), F32),
        ],
        compiler_params=pltpu.CompilerParams(vmem_limit_bytes=63 << 20),
        name="middle_part",
    )(slot_of, params, tokens, attended, grad_low, *([gathered] * (3 * square)))


def weight_grad_kernel(block_of, deep, size, slot_of, left, right, *refs):
    grads, stage, sem = refs[-3:]
    wide = right.shape[0] // size
    rows, cols = pl.program_id(0), pl.program_id(1)
    step = rows * pl.num_programs(1) + cols
    steps = pl.num_programs(0) * pl.num_programs(1)
    now = step % 2

    def copy(buffer, index, slot):
        return pltpu.make_async_copy(stage.at[buffer, index], grads.at[slot], sem.at[buffer, index])

    @pl.when(step >= 2)
    def _():
        for index in range(deep * wide):
            copy(now, index, 0).wait()

    other = right[...]
    for i in range(deep):
        panel = nt(left[size * i : size * (i + 1), :], other)
        for j in range(wide):
            index = i * wide + j
            block = panel[:, size * j : size * (j + 1)]
            stage[now, index, :size] = block[:, :MAIN].astype(BF16)
            stage[now, index, size:] = pack_tail(block).astype(BF16)
            copy(now, index, slot_of[block_of(rows * deep + i, cols * wide + j)]).start()

    @pl.when(step == steps - 1)
    def _():
        for index in range(deep * wide):
            copy(now, index, 0).wait()

        @pl.when(steps > 1)
        def _():
            for index in range(deep * wide):
                copy(1 - now, index, 0).wait()


def weight_grad(left, right, slot_of, grads, slot_count, size, block_of, name):
    depth = left.shape[1]
    deep = wide = 4
    grid = (left.shape[0] // (size * deep), right.shape[0] // (size * wide))
    anywhere = pl.BlockSpec(memory_space=pl.ANY)
    operands = [slot_of, left, right] + ([] if grads is None else [grads])
    return pl.pallas_call(
        functools.partial(weight_grad_kernel, block_of, deep, size),
        grid_spec=pltpu.PrefetchScalarGridSpec(
            num_scalar_prefetch=1,
            grid=grid,
            in_specs=[
                pl.BlockSpec((size * deep, depth), lambda i, j, v: (i, 0)),
                pl.BlockSpec((size * wide, depth), lambda i, j, v: (j, 0)),
            ]
            + [anywhere] * (len(operands) - 3),
            out_specs=anywhere,
            scratch_shapes=[
                pltpu.VMEM((2, deep * wide, size + RUN, MAIN), BF16),
                pltpu.SemaphoreType.DMA((2, deep * wide)),
            ],
        ),
        out_shape=jax.ShapeDtypeStruct((slot_count, size + RUN, MAIN), BF16),
        input_output_aliases={} if grads is None else {3: 0},
        cost_estimate=cost(
            2 * left.shape[0] * right.shape[0] * depth,
            2 * (left.size + right.size + left.shape[0] * right.shape[0]),
        ),
        name=name,
    )(*operands)


def weight_grads_kernel(starts, col_blocks, size, slot_of, *refs):
    activated, grad_low, normed, grad_pre, attended, grad_branch, grads, left, right, stage, get, put = refs
    out_start, up_start, down_start = starts
    side_length = left.shape[1]
    row_blocks = side_length // size
    count = row_blocks * row_blocks
    parts = activated.shape[0] // side_length
    step, steps = pl.program_id(0), pl.num_programs(0)
    now = step % 2

    def rows(index):
        return pl.ds(pl.multiple_of(index * side_length, 16), side_length)

    def fetch(index, buffer):
        def start(one, other):
            pltpu.make_async_copy(one, left.at[buffer], get.at[0, buffer]).start()
            pltpu.make_async_copy(other, right.at[buffer], get.at[1, buffer]).start()

        @pl.when(index < parts)
        def _():
            start(activated.at[rows(index)], grad_low)

        @pl.when((index >= parts) & (index < 2 * parts))
        def _():
            start(normed, grad_pre.at[rows(index - parts)])

        @pl.when(index == 2 * parts)
        def _():
            start(attended, grad_branch)

    def copy(buffer, index, slot):
        return pltpu.make_async_copy(stage.at[buffer, index], grads.at[slot], put.at[buffer, index])

    @pl.when(step == 0)
    def _():
        fetch(0, 0)

    @pl.when(step + 1 < steps)
    def _():
        fetch(step + 1, 1 - now)

    pltpu.make_async_copy(normed, left.at[now], get.at[0, now]).wait()
    pltpu.make_async_copy(normed, right.at[now], get.at[1, now]).wait()

    @pl.when(step >= 2)
    def _():
        for index in range(count):
            copy(now, index, 0).wait()

    up = (step >= parts) & (step < 2 * parts)
    start = jnp.where(up, up_start + (step - parts) * row_blocks, out_start)
    start = jnp.where(step < parts, down_start + step * count, start)
    stride = jnp.where(up, col_blocks, row_blocks)
    other = right[now]
    for i in range(row_blocks):
        panel = nt(left[now, size * i : size * (i + 1), :], other)
        for j in range(row_blocks):
            index = i * row_blocks + j
            block = panel[:, size * j : size * (j + 1)]
            stage[now, index, :size] = block[:, :MAIN].astype(BF16)
            stage[now, index, size:] = pack_tail(block).astype(BF16)
            copy(now, index, slot_of[start + i * stride + j]).start()

    @pl.when(step == steps - 1)
    def _():
        for index in range(count):
            copy(now, index, 0).wait()
            copy(1 - now, index, 0).wait()


def weight_grads(slot_of, operands, slot_count, size, starts, col_blocks):
    hidden, length = operands[0].shape
    features = operands[1].shape[0]
    count = (features // size) ** 2
    steps = 2 * (hidden // features) + 1
    anywhere = pl.BlockSpec(memory_space=pl.ANY)
    part = pltpu.VMEM((2, features, length), BF16)
    return pl.pallas_call(
        functools.partial(weight_grads_kernel, starts, col_blocks, size),
        grid_spec=pltpu.PrefetchScalarGridSpec(
            num_scalar_prefetch=1,
            grid=(steps,),
            in_specs=[anywhere] * 6,
            out_specs=anywhere,
            scratch_shapes=[
                part,
                part,
                pltpu.VMEM((2, count, size + RUN, MAIN), BF16),
                pltpu.SemaphoreType.DMA((2, 2)),
                pltpu.SemaphoreType.DMA((2, count)),
            ],
        ),
        out_shape=jax.ShapeDtypeStruct((slot_count, size + RUN, MAIN), BF16),
        cost_estimate=cost(2 * steps * features * features * length, 8 * steps * features * length),
        name="weight_grads",
    )(slot_of, *operands)


EXTRA = 8
FAR = -1e30


def causal():
    return lax.broadcasted_iota(jnp.int32, (HALF, HALF), 0) <= lax.broadcasted_iota(jnp.int32, (HALF, HALF), 1)


def places(groups):
    found = []
    for group in range(groups):
        base = PREFIX + GB * group
        low, high = slice(base, base + HALF), slice(base + HALF, base + GB)
        found.append((low, high, slice(base, base + GB), slice(GB * group, GB * (group + 1))))
    return found


def side(left, right):
    return jnp.concatenate([left, right], axis=1)


def attention_kernel(scale, qkv, extras, out, lse, queries, keys, values, keys_t):
    head = qkv.shape[1]
    unit = scale * math.log2(math.e)

    @pl.when(pl.program_id(0) == 0)
    def _():
        queries[head:] = extras[0]
        keys[head:] = extras[1]
        values[head:] = extras[2]

    queries[:head] = qkv[0]
    keys[:head] = qkv[1]
    values[:head] = qkv[2]
    keys_t[...] = keys[...].T
    ahead = causal()
    spots = places(out.shape[1] // GB)
    scores = []
    for low, high, both, _ in spots:
        asked = queries[:, both]
        scores.append((nn(keys_t[:PREFIX], asked), nn(keys_t[low], asked), nn(keys_t[high], asked[:, HALF:])))

    def peak(array):
        return jnp.max(array, axis=0, keepdims=True)

    def soft(array, top):
        return jnp.exp2((array - top) * unit).astype(BF16)

    tops, weights = [], []
    for prefix, first, second in scores:
        first = side(jnp.where(ahead, first[:, :HALF], FAR), first[:, HALF:])
        second = jnp.where(ahead, second, FAR)
        top = jnp.maximum(peak(prefix), peak(first))
        top = side(top[:, :HALF], jnp.maximum(top[:, HALF:], peak(second)))
        tops.append(top)
        weights.append((soft(prefix, top), soft(first, top), soft(second, top[:, HALF:])))
    for (low, high, _, mine), top, (prefix, first, second) in zip(spots, tops, weights):
        sums = nn(values[:, :PREFIX], prefix) + nn(values[:, low], first)
        sums = side(sums[:, :HALF], sums[:, HALF:] + nn(values[:, high], second))
        total = sums[head : head + 1]
        out[:, mine] = (sums[:head] / total).astype(BF16)
        lse[0, :, mine] = top + jnp.log(total) * (1.0 / scale)


def thirds(values):
    high = values.astype(BF16).astype(F32)
    rest = values - high
    middle = rest.astype(BF16).astype(F32)
    return high, middle, rest - middle


def with_rows(base, start, rows):
    index = lax.broadcasted_iota(jnp.int32, base.shape, 0)
    for offset, row in enumerate(rows):
        base = jnp.where(index == start + offset, row, base)
    return base.astype(BF16)


def attention_back_kernel(scale, qkv, extras, out, lse, grad_out, grads, queries, keys, values, grad_o, keys_t, values_t):
    head, own = qkv.shape[1], out.shape[1]
    unit = scale * math.log2(math.e)

    @pl.when(pl.program_id(0) == 0)
    def _():
        keys[head:] = extras[1]
        values[head:] = extras[2]

    queries[:head] = qkv[0, :, PREFIX:]
    keys[:head] = qkv[1]
    values[:head] = qkv[2]
    grad_o[:head] = grad_out[...]
    keys_t[...] = keys[...].T
    values_t[...] = values[...].T
    queries[head:] = with_rows(extras[0, :, PREFIX:].astype(F32), 2, thirds(-lse[0]))
    delta = jnp.sum(grad_out[...].astype(F32) * out[...].astype(F32), axis=0, keepdims=True)
    grad_o[head:] = with_rows(jnp.zeros((EXTRA, own), F32), 0, thirds(-delta))
    ahead = causal()
    spots = places(own // GB)

    def weigh(rows, asked, given, mask):
        weights = jnp.exp2(nn(keys_t[rows], asked) * unit)
        if mask == 1:
            weights = side(jnp.where(ahead, weights[:, :HALF], 0.0), weights[:, HALF:])
        if mask == 2:
            weights = jnp.where(ahead, weights, 0.0)
        return weights.astype(BF16), (weights * nn(values_t[rows], given)).astype(BF16)

    found = []
    for low, high, _, mine in spots:
        asked, given = queries[:, mine], grad_o[:, mine]
        found.append(
            (
                weigh(slice(0, PREFIX), asked, given, 0),
                weigh(low, asked, given, 1),
                weigh(high, asked[:, HALF:], given[:, HALF:], 2),
            )
        )
    prefix_k = prefix_v = None
    for (low, high, both, mine), ((p0, d0), (p1, d1), (p2, d2)) in zip(spots, found):
        asked, given = queries[:head, mine], grad_o[:head, mine]
        grad_q = nn(keys[:head, :PREFIX], d0) + nn(keys[:head, low], d1)
        grad_q = side(grad_q[:, :HALF], grad_q[:, HALF:] + nn(keys[:head, high], d2))
        grads[0, :, both] = (grad_q * scale).astype(BF16)
        part_k, part_v = nt(asked, d0), nt(given, p0)
        prefix_k = part_k if prefix_k is None else prefix_k + part_k
        prefix_v = part_v if prefix_v is None else prefix_v + part_v
        grads[1, :, low] = (nt(asked, d1) * scale).astype(BF16)
        grads[2, :, low] = nt(given, p1).astype(BF16)
        grads[1, :, high] = (nt(asked[:, HALF:], d2) * scale).astype(BF16)
        grads[2, :, high] = nt(given[:, HALF:], p2).astype(BF16)
    grads[0, :, :PREFIX] = jnp.zeros((head, PREFIX), BF16)
    grads[1, :, :PREFIX] = (prefix_k * scale).astype(BF16)
    grads[2, :, :PREFIX] = prefix_v.astype(BF16)


def attention_specs(qkv):
    _, features, length = qkv.shape
    head, own = features // HEADS, length - PREFIX
    three = pl.BlockSpec((3, head, length), lambda h: (0, h, 0))
    extra = pl.BlockSpec((3, EXTRA, length), lambda h: (0, 0, 0))
    one = pl.BlockSpec((head, own), lambda h: (h, 0))
    row = pl.BlockSpec((1, 1, own), lambda h: (h, 0, 0))
    wide = lambda columns: pltpu.VMEM((head + EXTRA, columns), BF16)
    tall = pltpu.VMEM((length, head + EXTRA), BF16)
    return features, length, own, head, three, extra, one, row, wide, tall


def attention(qkv, extras):
    features, length, own, head, three, extra, one, row, wide, tall = attention_specs(qkv)
    return pl.pallas_call(
        functools.partial(attention_kernel, head ** (-0.5)),
        grid=(HEADS,),
        in_specs=[three, extra],
        out_specs=[one, row],
        out_shape=[
            jax.ShapeDtypeStruct((features, own), BF16),
            jax.ShapeDtypeStruct((HEADS, 1, own), F32),
        ],
        scratch_shapes=[wide(length), wide(length), wide(length), tall],
        cost_estimate=cost(8 * features * own * GB, 2 * qkv.size, HEADS * own * GB),
        name="attention",
    )(qkv, extras)


def attention_back(qkv, extras, out, lse, grad_out):
    features, length, own, head, three, extra, one, row, wide, tall = attention_specs(qkv)
    return pl.pallas_call(
        functools.partial(attention_back_kernel, head ** (-0.5)),
        grid=(HEADS,),
        in_specs=[three, extra, one, row, one],
        out_specs=three,
        out_shape=jax.ShapeDtypeStruct(qkv.shape, BF16),
        scratch_shapes=[wide(own), wide(length), wide(length), wide(own), tall, tall],
        cost_estimate=cost(20 * features * own * GB, 4 * qkv.size, HEADS * own * GB),
        name="attention_back",
    )(qkv, extras, out, lse, grad_out)


def score_extras(alive, prefix_alive, later):
    length = PREFIX + alive.shape[0]
    dead = jnp.where(jnp.concatenate([prefix_alive, alive]), 0.0, FAR)
    prefix = (jnp.arange(length) < PREFIX).astype(F32)
    barred = jnp.concatenate([jnp.zeros((PREFIX,)), jnp.where(jnp.repeat(later, GB), 0.0, FAR)])
    one, zero = jnp.ones((length,)), jnp.zeros((length,))
    query_rows = jnp.stack([one, barred] + [zero] * 6)
    key_rows = jnp.stack([dead, prefix] + [one] * 3 + [zero] * 3)
    value_rows = jnp.stack([one] * 3 + [zero] * 5)
    return jnp.stack([query_rows, key_rows, value_rows]).astype(BF16)


def split(values):
    high = values.astype(BF16)
    return high, (values - high.astype(F32)).astype(BF16)


def product(form, left, right):
    (left_high, left_low), (right_high, right_low) = left, right
    return form(left_high, right_high) + (form(left_high, right_low) + form(left_low, right_high))


def optimizer_kernel(scale, packed, master, average, left, right, root_left, root_right, *outs):
    slot_grad, new_left, new_right, new_master, new_copy, new_average = outs
    size = master.shape[1]
    grad = unpack(packed[0]) * scale
    slot_grad[0] = grad
    grad_parts = split(grad)
    new_left[0] = 0.5 * left[0] + (0.5 / size) * product(nt, grad_parts, grad_parts)
    new_right[0] = 0.5 * right[0] + (0.5 / size) * product(tn, grad_parts, grad_parts)
    right_part = product(nn, grad_parts, split(root_right[0]))
    step = product(nn, split(root_left[0]), split(right_part))
    moved = master[0] - 0.03 * step
    new_master[0] = moved
    new_copy[0] = moved.astype(BF16)
    new_average[0] = 0.8 * average[0] + 0.2 * moved


def optimizer(packed, scale, arrays):
    slots, size, _ = arrays[0].shape
    block = pl.BlockSpec((1, size, size), lambda i: (i, 0, 0))
    shape = lambda dtype: jax.ShapeDtypeStruct((slots, size, size), dtype)
    return pl.pallas_call(
        functools.partial(optimizer_kernel, scale),
        grid=(slots,),
        in_specs=[pl.BlockSpec((1,) + packed.shape[1:], lambda i: (i, 0, 0))] + [block] * 6,
        out_specs=[block] * 6,
        out_shape=[shape(F32), shape(F32), shape(F32), shape(F32), shape(BF16), shape(F32)],
        name="optimizer",
    )(packed, *arrays)


def norm_parts(values):
    average = jnp.mean(values, axis=0, keepdims=True)
    centred = values - average
    variance = jnp.mean(centred * centred, axis=0, keepdims=True)
    scale = lax.rsqrt(variance + 1e-05)
    return centred * scale, scale


def norm_back(unit, scale, gain, grad):
    inner = grad * gain
    mean_one = jnp.mean(inner, axis=0, keepdims=True)
    mean_two = jnp.mean(inner * unit, axis=0, keepdims=True)
    return scale * (inner - mean_one - unit * mean_two)


def local(
    chips,
    cores,
    tokens,
    cotangent,
    pad_mask,
    prefix_len,
    norm_gains,
    norm_shifts,
    owner_map,
    weight_copy,
    master,
    average_weights,
    stat_left,
    stat_right,
    root_left,
    root_right,
):
    cell_count, length, features = tokens.shape
    assert cell_count == 1
    slots, size, _ = weight_copy.shape
    slot_count = owner_map.shape[0]
    row_blocks = features // size
    square = row_blocks * row_blocks
    col_blocks = (slot_count - 4 * square) // (2 * row_blocks)
    known = chips == 16 and cores == 2
    chip = lax.axis_index("dp").astype(jnp.int32)
    seq_index = lax.axis_index("seq")

    slot_of = jnp.zeros((slot_count,), jnp.int32).at[owner_map].set(jnp.arange(slot_count, dtype=jnp.int32))
    own_tokens = tokens.reshape(length, features).T
    norms = jnp.stack([norm_gains[0], norm_shifts[0], norm_gains[1], norm_shifts[1]])
    params = norms.T
    if known:
        half = slots // 2
        begin = seq_index.astype(jnp.int32) * half
        placed = pack_slots(weight_copy, jnp.stack([begin, chip * slots + begin]), half, slot_count)
        gathered, normed_in = gather_slots(placed, own_tokens, params, slots)
    else:
        packed = pack_slots(weight_copy, jnp.zeros((2,), jnp.int32), slots, slots)
        gathered = lax.all_gather(packed, "dp", axis=0, tiled=True)
        prefix_tokens = lax.all_gather(own_tokens[:, :PREFIX], "seq")[0]
        unit_all, _ = norm_parts(jnp.concatenate([prefix_tokens, own_tokens], axis=1).astype(F32))
        normed_in = (unit_all * params[:, 0:1] + params[:, 1:2]).astype(BF16)
    starts = (3 * square, 4 * square, 4 * square + row_blocks * col_blocks)

    def three_of(i, j):
        return (j // row_blocks) * square + i * row_blocks + j % row_blocks

    w_three, qkv = front(gathered, slot_of, normed_in, row_blocks)

    position = seq_index * length + jnp.arange(length, dtype=jnp.int32)
    alive = jnp.where(position < PREFIX, position < prefix_len[0], pad_mask[0] == 1)
    prefix_alive = jnp.arange(PREFIX, dtype=jnp.int32) < prefix_len[0]
    groups = length // GB
    later = seq_index * groups + jnp.arange(groups) > 0
    extras = score_extras(alive, prefix_alive, later)

    grad_low = cotangent.reshape(length, features).T
    attended, log_total = attention(qkv, extras)
    block_out, activated, grad_pre, normed_mid, grad_branch, grad_att, grad_middle, sums = middle_part(
        gathered, slot_of, params, own_tokens, attended, grad_low, row_blocks, col_blocks
    )
    operands = (activated, grad_low, normed_mid, grad_pre, attended, grad_branch)
    grads = weight_grads(slot_of, operands, slot_count, size, starts, col_blocks)
    grad_three = attention_back(qkv, extras, attended, log_total, grad_att)
    flat_three = grad_three.reshape(3 * features, PREFIX + length)
    grads = weight_grad(normed_in, flat_three, slot_of, grads, slot_count, size, three_of, "grad_three")
    grad_scale = 1.0 / math.sqrt(length * chips * cores)
    if known:
        summed, grad_input, norm_sums = reduce_slots(
            grads, slots, w_three, grad_three, own_tokens, grad_middle, params, sums
        )
    else:
        part = lax.psum_scatter(grads.astype(F32), "dp", scatter_dimension=0, tiled=True)
        summed = lax.psum(part, "seq")
        grad_all = sum(nn(w_three[k], grad_three[k]) for k in range(3))
        prefix_part = jnp.where(seq_index == 0, lax.psum(grad_all[:, :PREFIX], "seq"), 0.0)
        grad_normed = grad_all[:, PREFIX:] + jnp.pad(prefix_part, ((0, 0), (0, length - PREFIX)))
        unit_one, scale_one = norm_parts(own_tokens.astype(F32))
        grad_input = grad_middle + norm_back(unit_one, scale_one, params[:, 0:1], grad_normed)
        first_sums = [jnp.sum(grad_normed * unit_one, axis=1), jnp.sum(grad_normed, axis=1)]
        norm_sums = lax.psum(jnp.stack(first_sums + [sums[2], sums[3]]), ("dp", "seq"))
    norm_grad = norm_sums[:4] * grad_scale
    new_norms = norms - 0.1 * norm_grad * lax.rsqrt(jnp.mean(norm_grad * norm_grad) + 1e-06)
    stepped = optimizer(
        summed, grad_scale, (master, average_weights, stat_left, stat_right, root_left, root_right)
    )
    token_shape = (cell_count, length, features)
    return (
        block_out.T.reshape(token_shape),
        grad_input.T.reshape(token_shape),
        norm_grad,
        new_norms,
        *stepped,
    )


def solution(mesh):
    tokens, slots = P("dp", "seq", None), P("dp", None, None)
    in_specs = (tokens, tokens, P("dp", "seq"), P("dp"), P(), P(), P()) + (slots,) * 7
    out_specs = (tokens, tokens, P(), P()) + (slots,) * 6
    body = functools.partial(local, mesh.shape["dp"], mesh.shape["seq"])
    return jax.shard_map(body, mesh=mesh, in_specs=in_specs, out_specs=out_specs, check_vma=False)
```

```python
import functools
import math

import jax
import jax.numpy as jnp
from jax import lax
from jax.experimental import pallas as pl
from jax.experimental.pallas import tpu as pltpu
from jax.sharding import PartitionSpec as P

HEADS = 20
GB = 256
PREFIX = 128
HALF = GB // 2
MESH = pl.DeviceIdType.MESH
BF16 = jnp.bfloat16
F32 = jnp.float32

MAIN = 256
RUN = 32


def runs(size):
    rest, per_tile = size - MAIN, 128 // (size - MAIN)
    places = []
    for index in range(-(-size // RUN)):
        lane = 128 * (index // per_tile) + rest * (index % per_tile)
        places.append((RUN * index, min(RUN, size - RUN * index), lane))
    assert places[-1][2] + rest <= MAIN
    return places


def pack_tail(block):
    size = block.shape[0]
    rest = size - MAIN
    pieces, lane = [], 0
    for row, count, start in runs(size):
        if start > lane:
            pieces.append(jnp.zeros((RUN, start - lane), block.dtype))
        piece = block[row : row + count, MAIN:]
        if count < RUN:
            piece = jnp.concatenate([piece, jnp.zeros((RUN - count, rest), block.dtype)], axis=0)
        pieces.append(piece)
        lane = start + rest
    if lane < MAIN:
        pieces.append(jnp.zeros((RUN, MAIN - lane), block.dtype))
    return jnp.concatenate(pieces, axis=1)


def unpack(packed):
    size = packed.shape[0] - RUN
    rest = size - MAIN
    low = packed[size:]
    tail = [low[:count, lane : lane + rest] for _, count, lane in runs(size)]
    return jnp.concatenate([packed[:size], jnp.concatenate(tail, axis=0)], axis=1)


def tn(left, right):
    return lax.dot_general(left, right, (((0,), (0,)), ((), ())), preferred_element_type=F32)


def nn(left, right):
    return lax.dot_general(left, right, (((1,), (0,)), ((), ())), preferred_element_type=F32)


def nt(left, right):
    return lax.dot_general(left, right, (((1,), (1,)), ((), ())), preferred_element_type=F32)


def cost(flops, moved, exps=0):
    return pl.CostEstimate(flops=int(flops), bytes_accessed=int(moved), transcendentals=int(exps))


def pack_kernel(start, block, packed):
    del start
    size = block.shape[1]
    rest = size - MAIN
    packed[0, :size] = block[0, :, :MAIN]
    packed[0, size:] = jnp.zeros((RUN, MAIN), BF16)
    for row, count, lane in runs(size):
        packed[0, size : size + count, lane : lane + rest] = block[0, row : row + count, MAIN:]


def pack_slots(blocks, start, count, slot_count):
    size = blocks.shape[1]
    return pl.pallas_call(
        pack_kernel,
        grid_spec=pltpu.PrefetchScalarGridSpec(
            num_scalar_prefetch=1,
            grid=(count,),
            in_specs=[pl.BlockSpec((1, size, size), lambda i, start: (start[0] + i, 0, 0))],
            out_specs=pl.BlockSpec((1, size + RUN, MAIN), lambda i, start: (start[1] + i, 0, 0)),
        ),
        out_shape=jax.ShapeDtypeStruct((slot_count, size + RUN, MAIN), BF16),
        name="pack_slots",
    )(start, blocks)


def place():
    me, core = lax.axis_index("dp"), lax.axis_index("seq")
    x, y, z = me % 2, (me // 2) % 2, me // 4
    step_x, step_y = 1 - 2 * x, 2 * (1 - 2 * y)
    first = step_y * (1 - core) + step_x * core
    second = step_x * (1 - core) + step_y * core
    return me, core, z, first, second


def greet(partners):
    barrier = pltpu.get_barrier_semaphore()
    for chip, core in partners:
        pl.semaphore_signal(barrier, inc=1, device_id=(chip, core), device_id_type=MESH)
    pl.semaphore_wait(barrier, len(partners))


UP, DOWN, FIRST, SECOND, TWIN, HEAD, GATHER_LABELS = 0, 4, 8, 12, 20, 36, 37


def gather_kernel(slots, placed, tokens, params, out, normed, held, send, recv, take):
    del placed
    me, core, z, first, second = place()
    half = slots // 2
    line = [(me + 4 * ((z + r) % 4 - z), core) for r in range(1, 4)]
    greet([(me + first, core), (me + second, core), (me, 1 - core)] + line)

    def copy(label, chip, dp, c):
        ref = out.at[pl.ds(chip * slots + core * half, half)]
        return pltpu.make_async_remote_copy(
            src_ref=ref,
            dst_ref=ref,
            send_sem=send.at[label],
            recv_sem=recv.at[label],
            device_id=(dp, c),
            device_id_type=MESH,
        )

    def col(zz):
        return me + 4 * (zz - z)

    def up(j):
        return copy(UP + j, me - 4 * (j - 1), me + 4, core)

    def down(j):
        return copy(DOWN + j, me + 4 * (j - 1), me - 4, core)

    def to_first(zz):
        return copy(FIRST + zz, col(zz), me + first, core)

    def to_second(zz, a):
        return copy(SECOND + 2 * zz + a, col(zz) + a * first, me + second, core)

    def to_twin(chip):
        return copy(TWIN + chip, chip, me, 1 - core)

    def spread(zz):
        to_first(zz).start()
        to_second(zz, 0).start()
        to_twin(col(zz)).start()

    def after_first(zz):
        to_first(zz).wait_recv()
        to_second(zz, 1).start()
        to_twin(col(zz) + first).start()

    def after_second(zz):
        for a in range(2):
            to_second(zz, a).wait_recv()
            to_twin(col(zz) + second + a * first).start()

    @pl.when(z < 3)
    def _():
        up(1).start()

    @pl.when(z > 0)
    def _():
        down(1).start()

    spread(z)

    prefix, seat = tokens.at[:, pl.ds(0, PREFIX)], held.at[:, pl.ds(0, PREFIX)]
    mine = pltpu.make_async_copy(tokens, held.at[:, pl.ds(PREFIX, tokens.shape[1])], take.at[0])
    near = pltpu.make_async_copy(prefix, seat, take.at[1])
    far = pltpu.make_async_remote_copy(
        src_ref=prefix,
        dst_ref=seat,
        send_sem=send.at[HEAD],
        recv_sem=recv.at[HEAD],
        device_id=(me, 1 - core),
        device_id_type=MESH,
    )
    mine.start()

    @pl.when(core == 0)
    def _():
        far.start()
        near.start()
        near.wait()

    @pl.when(core == 1)
    def _():
        far.wait_recv()

    mine.wait()

    def normalize(index, carry):
        tile = pl.ds(pl.multiple_of(index * PREFIX, PREFIX), PREFIX)
        unit, _ = norm_parts(held[:, tile].astype(F32))
        normed[:, tile] = (unit * params[:, 0:1] + params[:, 1:2]).astype(BF16)
        return carry

    lax.fori_loop(0, held.shape[1] // PREFIX, normalize, 0)
    for j in range(1, 4):

        @pl.when(z >= j)
        def _():
            up(j).wait_recv()
            if j < 3:

                @pl.when(z < 3)
                def _():
                    up(j + 1).start()

            spread(z - j)

        @pl.when(z + j <= 3)
        def _():
            down(j).wait_recv()
            if j < 3:

                @pl.when(z > 0)
                def _():
                    down(j + 1).start()

            spread(z + j)

        if j == 1:
            after_first(z)
        else:

            @pl.when(z >= j - 1)
            def _():
                after_first(z - (j - 1))

            @pl.when(z + j - 1 <= 3)
            def _():
                after_first(z + j - 1)

    @pl.when(z >= 3)
    def _():
        after_first(z - 3)

    @pl.when(z <= 0)
    def _():
        after_first(z + 3)

    after_second(z)
    for j in range(1, 4):

        @pl.when(z >= j)
        def _():
            after_second(z - j)

        @pl.when(z + j <= 3)
        def _():
            after_second(z + j)

    for zz in range(4):
        for a in range(2):
            for b in range(2):
                chip = col(zz) + a * first + b * second
                to_twin(chip).wait_recv()
                to_twin(chip).wait_send()
        to_first(zz).wait_send()
        for a in range(2):
            to_second(zz, a).wait_send()

    @pl.when(z < 3)
    def _():
        up(1).wait_send()
        for j in range(1, 3):

            @pl.when(z >= j)
            def _():
                up(j + 1).wait_send()

    @pl.when(z > 0)
    def _():
        down(1).wait_send()
        for j in range(1, 3):

            @pl.when(z + j <= 3)
            def _():
                down(j + 1).wait_send()

    @pl.when(core == 0)
    def _():
        far.wait_send()


def gather_slots(placed, tokens, params, slots):
    anywhere, inside = pl.BlockSpec(memory_space=pl.ANY), pl.BlockSpec(memory_space=pltpu.VMEM)
    wide = (tokens.shape[0], PREFIX + tokens.shape[1])
    return pl.pallas_call(
        functools.partial(gather_kernel, slots),
        out_shape=[jax.ShapeDtypeStruct(placed.shape, placed.dtype), jax.ShapeDtypeStruct(wide, BF16)],
        in_specs=[anywhere, anywhere, inside],
        out_specs=[anywhere, inside],
        scratch_shapes=[
            pltpu.VMEM(wide, BF16),
            pltpu.SemaphoreType.DMA((GATHER_LABELS,)),
            pltpu.SemaphoreType.DMA((GATHER_LABELS,)),
            pltpu.SemaphoreType.DMA((2,)),
        ],
        input_output_aliases={0: 0},
        compiler_params=pltpu.CompilerParams(collective_id=0, has_side_effects=True),
        name="gather_slots",
    )(placed, tokens, params)


R_TWIN, R_SECOND, R_FIRST, R_LINE, R_DONE, R_PREFIX, R_FLOW, REDUCE_LABELS = 0, 16, 24, 28, 32, 33, 34, 42
RING = 3
PANELS = 5


def reduce_kernel(
    slots,
    grads,
    w_three,
    grad_three,
    tokens,
    grad_middle,
    params,
    sums,
    out,
    grad_input,
    norm_sums,
    ring,
    r_twin,
    r_second,
    r_first,
    r_line,
    total,
    weights,
    inner,
    acc,
    prefix,
    given,
    folds,
    flow,
    arrived,
    load,
    send,
    recv,
    save,
):
    me, core, z, first, second = place()
    half = slots // 2
    features, length = acc.shape
    line = [(me + 4 * ((z + r) % 4 - z), core) for r in range(1, 4)]
    greet([(me + first, core), (me + second, core), (me, 1 - core)] + line)

    def piece(chip, h):
        return grads.at[pl.ds(chip * slots + h * half, half)]

    def chip_at(zz, a, b):
        return me + 4 * (zz - z) + a * first + b * second

    def remote(src, dst, label, dp, c):
        return pltpu.make_async_remote_copy(
            src_ref=src,
            dst_ref=dst,
            send_sem=send.at[label],
            recv_sem=recv.at[label],
            device_id=(dp, c),
            device_id_type=MESH,
        )

    def twin(zz, a, b):
        chip = chip_at(zz, a, b)
        return remote(piece(chip, 1 - core), r_twin.at[chip], R_TWIN + chip, me, 1 - core)

    def to_second(zz, a):
        return remote(
            r_twin.at[chip_at(zz, a, 1)], r_second.at[2 * zz + a], R_SECOND + 2 * zz + a, me + second, core
        )

    def to_first(zz):
        return remote(r_twin.at[chip_at(zz, 1, 0)], r_first.at[zz], R_FIRST + zz, me + first, core)

    def to_line(r):
        zz = (z + r) % 4
        return remote(r_twin.at[chip_at(zz, 0, 0)], r_line.at[r - 1], R_LINE + r, chip_at(zz, 0, 0), core)

    order = [2, 1, 3, 0]
    where = [(z + r) % 4 for r in order]
    turns = []
    for index in range(3):
        turns += [(where[index], 1, 1), (where[index], 0, 1)]
    turns += [(where[0], 1, 0), (where[3], 1, 1), (where[3], 0, 1), (where[0], 0, 0), (where[1], 1, 0)]
    turns += [(where[2], 1, 0), (where[1], 0, 0), (where[3], 1, 0), (where[2], 0, 0), (where[3], 0, 0)]

    def load_piece(chip, slot):
        return pltpu.make_async_copy(piece(chip, core), ring.at[slot], load.at[slot])

    def load_own(turn):
        return load_piece(chip_at(*turns[turn]), turn % RING)

    def add_up(turn, others):
        chip = chip_at(*turns[turn])
        load_own(turn).wait()
        twin(*turns[turn]).wait_recv()

        def body(s, carry):
            value = ring[turn % RING, s].astype(F32) + r_twin[chip, s].astype(F32)
            for ref, index in others:
                value = value + ref[index, s].astype(F32)
            if turn < len(turns) - 1:
                r_twin[chip, s] = value.astype(BF16)
            else:
                total[s] = value
            return carry

        lax.fori_loop(0, half, body, 0)
        if turn + RING < len(turns):
            load_own(turn + RING).start()

    def send_second(turn):
        zz, a, _ = turns[turn]
        add_up(turn, [])
        to_second(zz, a).start()

    def send_first(turn):
        zz = turns[turn][0]
        to_second(zz, 1).wait_recv()
        add_up(turn, [(r_second, 2 * zz + 1)])
        to_first(zz).start()

    def send_line(turn, r):
        zz = turns[turn][0]
        to_second(zz, 0).wait_recv()
        to_first(zz).wait_recv()
        add_up(turn, [(r_second, 2 * zz), (r_first, zz)])
        to_line(r).start()

    for turn in range(RING):
        load_own(turn).start()
    for zz in where:
        for a in (1, 0):
            twin(zz, 1, a).start()
    for zz in where:
        for a in (1, 0):
            twin(zz, 0, a).start()
    fetches = [
        pltpu.make_async_copy(w_three, weights, save.at[0]),
        pltpu.make_async_copy(grad_three, inner, save.at[1]),
    ]
    for fetch in fetches:
        fetch.start()
    def early(turn, carry):
        def pick(values):
            return sum(jnp.where(turn == index, value, 0) for index, value in enumerate(values))

        zz, a, slot = pick([t[0] for t in turns[:6]]), 1 - turn % 2, turn % RING
        chip, after = chip_at(zz, a, 1), pick([chip_at(*t) for t in turns[RING : RING + 6]])
        load_piece(chip, slot).wait()
        twin(zz, a, 1).wait_recv()

        def body(s, inner_carry):
            r_twin[chip, s] = (ring[slot, s].astype(F32) + r_twin[chip, s].astype(F32)).astype(BF16)
            return inner_carry

        lax.fori_loop(0, half, body, 0)
        load_piece(after, slot).start()
        to_second(zz, a).start()
        return carry

    lax.fori_loop(0, 6, early, 0)
    send_first(6)
    send_second(7)
    send_second(8)
    for fetch in fetches:
        fetch.wait()

    rows = features // PANELS

    def panel(index, carry):
        mine = pl.ds(pl.multiple_of(index * rows, 16), rows)
        acc[mine, :] = sum(nn(weights[k, mine, :], inner[k]) for k in range(3))
        return carry

    lax.fori_loop(0, PANELS, panel, 0)

    swap = remote(acc.at[:, pl.ds(0, PREFIX)], prefix, R_PREFIX, me, 1 - core)
    swap.start()
    own_tokens = weights.at[0, :, pl.ds(0, length - PREFIX)]
    take = pltpu.make_async_copy(tokens, own_tokens, save.at[0])
    take.start()

    def at(index):
        return pl.ds(pl.multiple_of(index * GB, GB), GB)

    def ahead(index):
        return pl.ds(pl.multiple_of(PREFIX + index * GB, PREFIX), GB)

    def give(index, slot):
        return pltpu.make_async_copy(grad_middle.at[:, at(index)], given.at[slot], save.at[2 + slot])

    def store(index):
        return pltpu.make_async_copy(acc.at[:, ahead(index)], grad_input.at[:, at(index)], save.at[4 + index])

    give(0, 0).start()
    send_line(9, order[0])
    send_first(10)
    take.wait()
    swap.wait()
    here = (1 - core).astype(F32)
    acc[:, PREFIX : 2 * PREFIX] += (acc[:, :PREFIX] + prefix[...]) * here
    folds[...] = jnp.zeros_like(folds)
    groups = (length - PREFIX) // GB

    def back(index, carry):
        @pl.when(index + 1 < groups)
        def _():
            give(index + 1, (index + 1) % 2).start()

        give(index, index % 2).wait()
        unit, scale = norm_parts(weights[0, :, at(index)].astype(F32))
        grad = acc[:, ahead(index)]
        folds[0] += fold(grad * unit)
        folds[1] += fold(grad)
        acc[:, ahead(index)] = given[index % 2] + norm_back(unit, scale, params[:, 0:1], grad)
        store(index).start()
        return carry

    lax.fori_loop(0, groups, back, 0)
    flow[0] = sums[...] + row_sums(folds[0], 0) + row_sums(folds[1], 1)
    pairs = [(me, 1 - core), (me + first, core), (me, 1 - core), (me + first, core), (me, 1 - core)] + line
    sources = [flow.at[0], flow.at[1], flow.at[2], arrived.at[2], flow.at[3]] + [flow.at[4]] * 3

    def pass_on(k):
        return remote(sources[k], arrived.at[k], R_FLOW + k, *pairs[k])

    for k in range(2):
        pass_on(k).start()
        pass_on(k).wait_recv()
        flow[k + 1] = flow[k] + arrived[k]
    pass_on(2).start()
    pass_on(2).wait_recv()
    pass_on(3).start()
    send_first(11)
    pass_on(3).wait_recv()
    flow[3] = arrived[2] + arrived[3]
    pass_on(4).start()
    pass_on(4).wait_recv()
    plane = jnp.where(core == 0, flow[3], arrived[4])
    flow[4] = plane
    arrived[4] = plane
    for k in range(5, 8):
        pass_on(k).start()
    send_line(12, order[1])
    send_first(13)
    send_line(14, order[2])
    for k in range(5, 8):
        pass_on(k).wait_recv()
    norm_sums[...] = sum(arrived[4 + (z - zz + 4) % 4] for zz in range(4))
    to_second(z, 0).wait_recv()
    to_first(z).wait_recv()
    for r in range(1, 4):
        to_line(r).wait_recv()
    add_up(15, [(r_second, 2 * z), (r_first, z), (r_line, 0), (r_line, 1), (r_line, 2)])
    target = out.at[pl.ds(core * half, half)]
    done = remote(total, target, R_DONE, me, 1 - core)
    done.start()
    saved = pltpu.make_async_copy(total, target, save.at[0])
    saved.start()
    for zz in range(4):
        for a in range(2):
            for b in range(2):
                twin(zz, a, b).wait_send()
            to_second(zz, a).wait_send()
        to_first(zz).wait_send()
    for r in range(1, 4):
        to_line(r).wait_send()
    for k in range(len(pairs)):
        pass_on(k).wait_send()
    for index in range(groups):
        store(index).wait()
    done.wait()
    saved.wait()


def reduce_slots(grads, slots, w_three, grad_three, tokens, grad_middle, params, sums):
    _, lines, lanes = grads.shape
    half = slots // 2
    _, features, length = grad_three.shape
    pieces = lambda n: pltpu.VMEM((n, half, lines, lanes), BF16)
    anywhere, inside = pl.BlockSpec(memory_space=pl.ANY), pl.BlockSpec(memory_space=pltpu.VMEM)
    groups = (length - PREFIX) // GB
    return pl.pallas_call(
        functools.partial(reduce_kernel, slots),
        out_shape=[
            jax.ShapeDtypeStruct((slots, lines, lanes), F32),
            jax.ShapeDtypeStruct((features, length - PREFIX), F32),
            jax.ShapeDtypeStruct((8, features), F32),
        ],
        in_specs=[anywhere] * 5 + [inside] * 2,
        out_specs=[anywhere, anywhere, inside],
        scratch_shapes=[
            pieces(RING),
            pieces(16),
            pieces(8),
            pieces(4),
            pieces(3),
            pltpu.VMEM((half, lines, lanes), F32),
            pltpu.VMEM(w_three.shape, BF16),
            pltpu.VMEM(grad_three.shape, BF16),
            pltpu.VMEM((features, length), F32),
            pltpu.VMEM((features, PREFIX), F32),
            pltpu.VMEM((2, features, GB), F32),
            pltpu.VMEM((2, features, 128), F32),
            pltpu.VMEM((5, 8, features), F32),
            pltpu.VMEM((8, 8, features), F32),
            pltpu.SemaphoreType.DMA((RING,)),
            pltpu.SemaphoreType.DMA((REDUCE_LABELS,)),
            pltpu.SemaphoreType.DMA((REDUCE_LABELS,)),
            pltpu.SemaphoreType.DMA((4 + groups,)),
        ],
        compiler_params=pltpu.CompilerParams(collective_id=1, has_side_effects=True, vmem_limit_bytes=63 << 20),
        name="reduce_slots",
    )(grads, w_three, grad_three, tokens, grad_middle, params, sums)


def lay(matrix, row, col, block):
    size = block.shape[0] - RUN
    matrix[size * row : size * (row + 1), size * col : size * col + MAIN] = block[:size]
    for start, count, lane in runs(size):
        piece = block[size : size + count, lane : lane + size - MAIN]
        matrix[size * row + start : size * row + start + count, size * col + MAIN : size * (col + 1)] = piece


def block_specs(gathered, rows, cols, block_of, **mode):
    shape = (1,) + gathered.shape[1:]
    pick = lambda i, j, step, v: (v[block_of(step, i, j)], 0, 0)
    return [
        pl.BlockSpec(shape, functools.partial(pick, i, j), **mode) for i in range(rows) for j in range(cols)
    ]


def feature_parts(features):
    part = -(-features // 256) * 128
    return [slice(start, min(start + part, features)) for start in range(0, features, part)]


def fold(values):
    return sum(values[:, start : start + 128] for start in range(0, values.shape[1], 128))


def row_sums(values, row):
    ones = jnp.ones((8, values.shape[1]), F32)
    summed = lax.dot_general(
        ones, values, (((1,), (1,)), ((), ())), precision=lax.Precision.HIGHEST, preferred_element_type=F32
    )
    return jnp.where(lax.broadcasted_iota(jnp.int32, summed.shape, 0) == row, summed, 0.0)


ONCE = pl.Buffered(1)


def front_kernel(slot_of, normed, *refs):
    del slot_of
    blocks, (weights, out) = refs[:-2], refs[-2:]
    row_blocks = math.isqrt(len(blocks))
    for index, block in enumerate(blocks):
        lay(weights.at[0], index // row_blocks, index % row_blocks, block.at[0])
    out[0] = tn(weights[0], normed[...]).astype(BF16)


def front(gathered, slot_of, normed, row_blocks):
    features, length = normed.shape
    square = row_blocks * row_blocks
    blocks = block_specs(gathered, row_blocks, row_blocks, lambda s, i, j: s * square + i * row_blocks + j)
    return pl.pallas_call(
        front_kernel,
        grid_spec=pltpu.PrefetchScalarGridSpec(
            num_scalar_prefetch=1,
            grid=(3,),
            in_specs=[pl.BlockSpec((features, length), lambda s, v: (0, 0), pipeline_mode=ONCE)] + blocks,
            out_specs=[
                pl.BlockSpec((1, features, features), lambda s, v: (s, 0, 0)),
                pl.BlockSpec((1, features, length), lambda s, v: (s, 0, 0)),
            ],
        ),
        out_shape=[
            jax.ShapeDtypeStruct((3, features, features), BF16),
            jax.ShapeDtypeStruct((3, features, length), BF16),
        ],
        compiler_params=pltpu.CompilerParams(vmem_limit_bytes=60 << 20),
        name="front",
    )(slot_of, normed, *([gathered] * square))


def gelu_pair(values):
    square = values * values
    bend = jnp.tanh(values * (0.7978845608028654 + (0.7978845608028654 * 0.044715) * square))
    half = 0.5 * values
    slope = 0.7978845608028654 + (3 * 0.7978845608028654 * 0.044715) * square
    return half + half * bend, 0.5 + 0.5 * bend + half * (1.0 - bend * bend) * slope


def middle_kernel(row_blocks, slot_of, params, tokens, attended, grad_low, *refs):
    del slot_of
    square = row_blocks * row_blocks
    out_blocks, up_blocks, down_blocks = (refs[square * k : square * (k + 1)] for k in range(3))
    outs, scratch = refs[3 * square : 3 * square + 8], refs[3 * square + 8 :]
    block_out, activated, grad_pre, normed, grad_branch, grad_att, grad_middle, sums = outs
    w_out, w_up, w_down, middle, total, stats, folds, sem = scratch
    tiles, parts = grad_low.shape[1] // GB, feature_parts(normed.shape[0])
    at = lambda index: pl.ds(pl.multiple_of(index * GB, GB), GB)
    step, last = pl.program_id(0), pl.num_programs(0) - 1

    @pl.when(step == 0)
    def _():
        copies = [
            pltpu.make_async_copy(tokens, block_out, sem.at[0]),
            pltpu.make_async_copy(attended, grad_att, sem.at[1]),
        ]
        for copy in copies:
            copy.start()
        for index, block in enumerate(out_blocks):
            lay(w_out, index // row_blocks, index % row_blocks, block.at[0])
        for copy in copies:
            copy.wait()
        def enter(index, carry):
            tile = at(index)
            for part in parts:
                values = block_out[part, tile].astype(F32) + tn(w_out[:, part], grad_att[:, tile])
                middle[part, tile] = values
                total[part, tile] = values
                grad_middle[part, tile] = jnp.zeros_like(values)
            values = middle[:, tile]
            average = jnp.mean(values, axis=0, keepdims=True)
            centred = values - average
            scale = lax.rsqrt(jnp.mean(centred * centred, axis=0, keepdims=True) + 1e-05)
            stats[0:1, tile] = average
            stats[1:2, tile] = scale
            normed[:, tile] = (centred * scale * params[:, 2:3] + params[:, 3:4]).astype(BF16)
            return carry

        lax.fori_loop(0, tiles, enter, 0)
        folds[...] = jnp.zeros_like(folds)

    for index in range(square):
        lay(w_up, index // row_blocks, index % row_blocks, up_blocks[index].at[0])
        lay(w_down, index // row_blocks, index % row_blocks, down_blocks[index].at[0])

    def advance(index, carry):
        tile = pl.ds(pl.multiple_of(index * wide, wide), wide)
        for part in parts:
            value, slope = gelu_pair(tn(w_up[:, part], normed[:, tile]))
            activated[part, tile] = value.astype(BF16)
            grad_pre[part, tile] = (nn(w_down[part, :], grad_low[:, tile]) * slope).astype(BF16)
        for part in parts:
            total[part, tile] += tn(w_down[:, part], activated[:, tile])
            grad_middle[part, tile] += nn(w_up[part, :], grad_pre[:, tile])
        return carry

    wide = 2 * GB if tiles % 2 == 0 else GB
    lax.fori_loop(0, grad_low.shape[1] // wide, advance, 0)

    @pl.when(step == last)
    def _():
        def leave(index, carry):
            tile = at(index)
            block_out[:, tile] = total[:, tile].astype(BF16)
            scale = stats[1:2, tile]
            unit = (middle[:, tile] - stats[0:1, tile]) * scale
            grad = grad_middle[:, tile]
            folds[0] += fold(grad * unit)
            folds[1] += fold(grad)
            values = grad_low[:, tile].astype(F32) + norm_back(unit, scale, params[:, 2:3], grad)
            grad_middle[:, tile] = values
            grad_branch[:, tile] = values.astype(BF16)
            for part in parts:
                grad_att[part, tile] = nn(w_out[part, :], grad_branch[:, tile]).astype(BF16)
            return carry

        lax.fori_loop(0, tiles, leave, 0)
        sums[...] = row_sums(folds[0], 2) + row_sums(folds[1], 3)


def middle_part(gathered, slot_of, params, tokens, attended, grad_low, row_blocks, col_blocks):
    features, length = tokens.shape
    square = row_blocks * row_blocks
    hidden = features * col_blocks // row_blocks
    up_start, down_start = 4 * square, 4 * square + row_blocks * col_blocks
    whole = lambda *shape: pl.BlockSpec(shape, lambda s, v: (0,) * len(shape), pipeline_mode=ONCE)
    anywhere = pl.BlockSpec(memory_space=pl.ANY)
    part = pl.BlockSpec((features, length), lambda s, v: (s, 0))
    blocks = (
        block_specs(
            gathered, row_blocks, row_blocks, lambda s, i, j: 3 * square + i * row_blocks + j, pipeline_mode=ONCE
        )
        + block_specs(
            gathered, row_blocks, row_blocks, lambda s, i, j: up_start + i * col_blocks + s * row_blocks + j
        )
        + block_specs(
            gathered, row_blocks, row_blocks, lambda s, i, j: down_start + (s * row_blocks + i) * row_blocks + j
        )
    )
    shape = jax.ShapeDtypeStruct
    square_scratch = pltpu.VMEM((features, features), BF16)
    return pl.pallas_call(
        functools.partial(middle_kernel, row_blocks),
        grid_spec=pltpu.PrefetchScalarGridSpec(
            num_scalar_prefetch=1,
            grid=(col_blocks // row_blocks,),
            in_specs=[whole(*params.shape)] + [anywhere] * 2 + [whole(features, length)] + blocks,
            out_specs=[whole(features, length), part, part]
            + [whole(features, length)] * 4
            + [whole(8, features)],
            scratch_shapes=[square_scratch] * 3
            + [pltpu.VMEM((features, length), F32)] * 2
            + [
                pltpu.VMEM((8, length), F32),
                pltpu.VMEM((2, features, 128), F32),
                pltpu.SemaphoreType.DMA((2,)),
            ],
        ),
        out_shape=[
            shape((features, length), BF16),
            shape((hidden, length), BF16),
            shape((hidden, length), BF16),
            shape((features, length), BF16),
            shape((features, length), BF16),
            shape((features, length), BF16),
            shape((features, length), F32),
            shape((8, features), F32),
        ],
        compiler_params=pltpu.CompilerParams(vmem_limit_bytes=63 << 20),
        name="middle_part",
    )(slot_of, params, tokens, attended, grad_low, *([gathered] * (3 * square)))


def weight_grad_kernel(block_of, deep, size, slot_of, left, right, *refs):
    grads, stage, sem = refs[-3:]
    wide = right.shape[0] // size
    rows, cols = pl.program_id(0), pl.program_id(1)
    step = rows * pl.num_programs(1) + cols
    steps = pl.num_programs(0) * pl.num_programs(1)
    now = step % 2

    def copy(buffer, index, slot):
        return pltpu.make_async_copy(stage.at[buffer, index], grads.at[slot], sem.at[buffer, index])

    @pl.when(step >= 2)
    def _():
        for index in range(deep * wide):
            copy(now, index, 0).wait()

    other = right[...]
    for i in range(deep):
        panel = nt(left[size * i : size * (i + 1), :], other)
        for j in range(wide):
            index = i * wide + j
            block = panel[:, size * j : size * (j + 1)]
            stage[now, index, :size] = block[:, :MAIN].astype(BF16)
            stage[now, index, size:] = pack_tail(block).astype(BF16)
            copy(now, index, slot_of[block_of(rows * deep + i, cols * wide + j)]).start()

    @pl.when(step == steps - 1)
    def _():
        for index in range(deep * wide):
            copy(now, index, 0).wait()

        @pl.when(steps > 1)
        def _():
            for index in range(deep * wide):
                copy(1 - now, index, 0).wait()


def weight_grad(left, right, slot_of, grads, slot_count, size, block_of, name):
    depth = left.shape[1]
    deep = wide = 4
    grid = (left.shape[0] // (size * deep), right.shape[0] // (size * wide))
    anywhere = pl.BlockSpec(memory_space=pl.ANY)
    operands = [slot_of, left, right] + ([] if grads is None else [grads])
    return pl.pallas_call(
        functools.partial(weight_grad_kernel, block_of, deep, size),
        grid_spec=pltpu.PrefetchScalarGridSpec(
            num_scalar_prefetch=1,
            grid=grid,
            in_specs=[
                pl.BlockSpec((size * deep, depth), lambda i, j, v: (i, 0)),
                pl.BlockSpec((size * wide, depth), lambda i, j, v: (j, 0)),
            ]
            + [anywhere] * (len(operands) - 3),
            out_specs=anywhere,
            scratch_shapes=[
                pltpu.VMEM((2, deep * wide, size + RUN, MAIN), BF16),
                pltpu.SemaphoreType.DMA((2, deep * wide)),
            ],
        ),
        out_shape=jax.ShapeDtypeStruct((slot_count, size + RUN, MAIN), BF16),
        input_output_aliases={} if grads is None else {3: 0},
        cost_estimate=cost(
            2 * left.shape[0] * right.shape[0] * depth,
            2 * (left.size + right.size + left.shape[0] * right.shape[0]),
        ),
        name=name,
    )(*operands)


def weight_grads_kernel(starts, col_blocks, size, slot_of, *refs):
    activated, grad_low, normed, grad_pre, attended, grad_branch, grads, left, right, stage, get, put = refs
    out_start, up_start, down_start = starts
    side_length = left.shape[1]
    row_blocks = side_length // size
    count = row_blocks * row_blocks
    parts = activated.shape[0] // side_length
    step, steps = pl.program_id(0), pl.num_programs(0)
    now = step % 2

    def rows(index):
        return pl.ds(pl.multiple_of(index * side_length, 16), side_length)

    def fetch(index, buffer):
        def start(one, other):
            pltpu.make_async_copy(one, left.at[buffer], get.at[0, buffer]).start()
            pltpu.make_async_copy(other, right.at[buffer], get.at[1, buffer]).start()

        @pl.when(index < parts)
        def _():
            start(activated.at[rows(index)], grad_low)

        @pl.when((index >= parts) & (index < 2 * parts))
        def _():
            start(normed, grad_pre.at[rows(index - parts)])

        @pl.when(index == 2 * parts)
        def _():
            start(attended, grad_branch)

    def copy(buffer, index, slot):
        return pltpu.make_async_copy(stage.at[buffer, index], grads.at[slot], put.at[buffer, index])

    @pl.when(step == 0)
    def _():
        fetch(0, 0)

    @pl.when(step + 1 < steps)
    def _():
        fetch(step + 1, 1 - now)

    pltpu.make_async_copy(normed, left.at[now], get.at[0, now]).wait()
    pltpu.make_async_copy(normed, right.at[now], get.at[1, now]).wait()

    @pl.when(step >= 2)
    def _():
        for index in range(count):
            copy(now, index, 0).wait()

    up = (step >= parts) & (step < 2 * parts)
    start = jnp.where(up, up_start + (step - parts) * row_blocks, out_start)
    start = jnp.where(step < parts, down_start + step * count, start)
    stride = jnp.where(up, col_blocks, row_blocks)
    other = right[now]
    for i in range(row_blocks):
        panel = nt(left[now, size * i : size * (i + 1), :], other)
        for j in range(row_blocks):
            index = i * row_blocks + j
            block = panel[:, size * j : size * (j + 1)]
            stage[now, index, :size] = block[:, :MAIN].astype(BF16)
            stage[now, index, size:] = pack_tail(block).astype(BF16)
            copy(now, index, slot_of[start + i * stride + j]).start()

    @pl.when(step == steps - 1)
    def _():
        for index in range(count):
            copy(now, index, 0).wait()
            copy(1 - now, index, 0).wait()


def weight_grads(slot_of, operands, slot_count, size, starts, col_blocks):
    hidden, length = operands[0].shape
    features = operands[1].shape[0]
    count = (features // size) ** 2
    steps = 2 * (hidden // features) + 1
    anywhere = pl.BlockSpec(memory_space=pl.ANY)
    part = pltpu.VMEM((2, features, length), BF16)
    return pl.pallas_call(
        functools.partial(weight_grads_kernel, starts, col_blocks, size),
        grid_spec=pltpu.PrefetchScalarGridSpec(
            num_scalar_prefetch=1,
            grid=(steps,),
            in_specs=[anywhere] * 6,
            out_specs=anywhere,
            scratch_shapes=[
                part,
                part,
                pltpu.VMEM((2, count, size + RUN, MAIN), BF16),
                pltpu.SemaphoreType.DMA((2, 2)),
                pltpu.SemaphoreType.DMA((2, count)),
            ],
        ),
        out_shape=jax.ShapeDtypeStruct((slot_count, size + RUN, MAIN), BF16),
        cost_estimate=cost(2 * steps * features * features * length, 8 * steps * features * length),
        name="weight_grads",
    )(slot_of, *operands)


EXTRA = 8
TOGETHER = 2
FAR = -1e30


def causal():
    return lax.broadcasted_iota(jnp.int32, (HALF, HALF), 0) <= lax.broadcasted_iota(jnp.int32, (HALF, HALF), 1)


def places(groups):
    found = []
    for group in range(groups):
        base = PREFIX + GB * group
        low, high = slice(base, base + HALF), slice(base + HALF, base + GB)
        found.append((low, high, slice(base, base + GB), slice(GB * group, GB * (group + 1))))
    return found


def side(left, right):
    return jnp.concatenate([left, right], axis=1)


def attention_kernel(scale, head, qkv, extras, out, lse, queries, keys, values, keys_t):
    unit = scale * math.log2(math.e)
    heads = range(queries.shape[0])

    @pl.when(pl.program_id(0) == 0)
    def _():
        for k in heads:
            queries[k, head:] = extras[0]
            keys[k, head:] = extras[1]
            values[k, head:] = extras[2]

    for k in heads:
        rows = slice(head * k, head * (k + 1))
        queries[k, :head] = qkv[0, rows]
        keys[k, :head] = qkv[1, rows]
        values[k, :head] = qkv[2, rows]
    for k in heads:
        keys_t[k] = keys[k].T
    ahead = causal()
    spots = [(k,) + spot for k in heads for spot in places(out.shape[1] // GB)]
    scores = []
    for k, low, high, both, _ in spots:
        asked = queries[k, :, both]
        scores.append((nn(keys_t[k, :PREFIX], asked), nn(keys_t[k, low], asked), nn(keys_t[k, high], asked[:, HALF:])))

    def peak(array):
        return jnp.max(array, axis=0, keepdims=True)

    def soft(array, top):
        return jnp.exp2((array - top) * unit).astype(BF16)

    tops, weights = [], []
    for prefix, first, second in scores:
        first = side(jnp.where(ahead, first[:, :HALF], FAR), first[:, HALF:])
        second = jnp.where(ahead, second, FAR)
        top = jnp.maximum(peak(prefix), peak(first))
        top = side(top[:, :HALF], jnp.maximum(top[:, HALF:], peak(second)))
        tops.append(top)
        weights.append((soft(prefix, top), soft(first, top), soft(second, top[:, HALF:])))
    for (k, low, high, _, mine), top, (prefix, first, second) in zip(spots, tops, weights):
        sums = nn(values[k, :, :PREFIX], prefix) + nn(values[k, :, low], first)
        sums = side(sums[:, :HALF], sums[:, HALF:] + nn(values[k, :, high], second))
        total = sums[head : head + 1]
        out[head * k : head * (k + 1), mine] = (sums[:head] / total).astype(BF16)
        lse[k, :, mine] = top + jnp.log(total) * (1.0 / scale)


def thirds(values):
    high = values.astype(BF16).astype(F32)
    rest = values - high
    middle = rest.astype(BF16).astype(F32)
    return high, middle, rest - middle


def with_rows(base, start, rows):
    index = lax.broadcasted_iota(jnp.int32, base.shape, 0)
    for offset, row in enumerate(rows):
        base = jnp.where(index == start + offset, row, base)
    return base.astype(BF16)


def attention_back_kernel(
    scale, head, qkv, extras, out, lse, grad_out, grads, queries, keys, values, grad_o, keys_t, values_t
):
    own = out.shape[1]
    unit = scale * math.log2(math.e)
    heads = range(queries.shape[0])

    @pl.when(pl.program_id(0) == 0)
    def _():
        for k in heads:
            keys[k, head:] = extras[1]
            values[k, head:] = extras[2]

    for k in heads:
        rows = slice(head * k, head * (k + 1))
        queries[k, :head] = qkv[0, rows, PREFIX:]
        keys[k, :head] = qkv[1, rows]
        values[k, :head] = qkv[2, rows]
        given = grad_out[rows]
        grad_o[k, :head] = given
        queries[k, head:] = with_rows(extras[0, :, PREFIX:].astype(F32), 2, thirds(-lse[k]))
        delta = jnp.sum(given.astype(F32) * out[rows].astype(F32), axis=0, keepdims=True)
        grad_o[k, head:] = with_rows(jnp.zeros((EXTRA, own), F32), 0, thirds(-delta))
    for k in heads:
        keys_t[k] = keys[k].T
        values_t[k] = values[k].T
    ahead = causal()
    spots = [(k,) + spot for k in heads for spot in places(own // GB)]

    def weigh(k, rows, asked, given, mask):
        weights = jnp.exp2(nn(keys_t[k, rows], asked) * unit)
        if mask == 1:
            weights = side(jnp.where(ahead, weights[:, :HALF], 0.0), weights[:, HALF:])
        if mask == 2:
            weights = jnp.where(ahead, weights, 0.0)
        return weights.astype(BF16), (weights * nn(values_t[k, rows], given)).astype(BF16)

    found = []
    for k, low, high, _, mine in spots:
        asked, given = queries[k, :, mine], grad_o[k, :, mine]
        found.append(
            (
                weigh(k, slice(0, PREFIX), asked, given, 0),
                weigh(k, low, asked, given, 1),
                weigh(k, high, asked[:, HALF:], given[:, HALF:], 2),
            )
        )
    prefix_k, prefix_v = {}, {}
    for (k, low, high, both, mine), ((p0, d0), (p1, d1), (p2, d2)) in zip(spots, found):
        rows = slice(head * k, head * (k + 1))
        asked, given = queries[k, :head, mine], grad_o[k, :head, mine]
        grad_q = nn(keys[k, :head, :PREFIX], d0) + nn(keys[k, :head, low], d1)
        grad_q = side(grad_q[:, :HALF], grad_q[:, HALF:] + nn(keys[k, :head, high], d2))
        grads[0, rows, both] = (grad_q * scale).astype(BF16)
        part_k, part_v = nt(asked, d0), nt(given, p0)
        prefix_k[k] = prefix_k[k] + part_k if k in prefix_k else part_k
        prefix_v[k] = prefix_v[k] + part_v if k in prefix_v else part_v
        grads[1, rows, low] = (nt(asked, d1) * scale).astype(BF16)
        grads[2, rows, low] = nt(given, p1).astype(BF16)
        grads[1, rows, high] = (nt(asked[:, HALF:], d2) * scale).astype(BF16)
        grads[2, rows, high] = nt(given[:, HALF:], p2).astype(BF16)
    for k in heads:
        rows = slice(head * k, head * (k + 1))
        grads[0, rows, :PREFIX] = jnp.zeros((head, PREFIX), BF16)
        grads[1, rows, :PREFIX] = (prefix_k[k] * scale).astype(BF16)
        grads[2, rows, :PREFIX] = prefix_v[k].astype(BF16)


def attention_specs(qkv):
    _, features, length = qkv.shape
    head, own = features // HEADS, length - PREFIX
    three = pl.BlockSpec((3, TOGETHER * head, length), lambda h: (0, h, 0))
    extra = pl.BlockSpec((3, EXTRA, length), lambda h: (0, 0, 0))
    one = pl.BlockSpec((TOGETHER * head, own), lambda h: (h, 0))
    row = pl.BlockSpec((TOGETHER, 1, own), lambda h: (h, 0, 0))
    wide = lambda columns: pltpu.VMEM((TOGETHER, head + EXTRA, columns), BF16)
    tall = pltpu.VMEM((TOGETHER, length, head + EXTRA), BF16)
    return features, length, own, head, three, extra, one, row, wide, tall


def attention(qkv, extras):
    features, length, own, head, three, extra, one, row, wide, tall = attention_specs(qkv)
    return pl.pallas_call(
        functools.partial(attention_kernel, head ** (-0.5), head),
        grid=(HEADS // TOGETHER,),
        in_specs=[three, extra],
        out_specs=[one, row],
        out_shape=[
            jax.ShapeDtypeStruct((features, own), BF16),
            jax.ShapeDtypeStruct((HEADS, 1, own), F32),
        ],
        scratch_shapes=[wide(length), wide(length), wide(length), tall],
        cost_estimate=cost(8 * features * own * GB, 2 * qkv.size, HEADS * own * GB),
        name="attention",
    )(qkv, extras)


def attention_back(qkv, extras, out, lse, grad_out):
    features, length, own, head, three, extra, one, row, wide, tall = attention_specs(qkv)
    return pl.pallas_call(
        functools.partial(attention_back_kernel, head ** (-0.5), head),
        grid=(HEADS // TOGETHER,),
        in_specs=[three, extra, one, row, one],
        out_specs=three,
        out_shape=jax.ShapeDtypeStruct(qkv.shape, BF16),
        scratch_shapes=[wide(own), wide(length), wide(length), wide(own), tall, tall],
        cost_estimate=cost(20 * features * own * GB, 4 * qkv.size, HEADS * own * GB),
        name="attention_back",
    )(qkv, extras, out, lse, grad_out)


def score_extras(alive, prefix_alive, later):
    length = PREFIX + alive.shape[0]
    dead = jnp.where(jnp.concatenate([prefix_alive, alive]), 0.0, FAR)
    prefix = (jnp.arange(length) < PREFIX).astype(F32)
    barred = jnp.concatenate([jnp.zeros((PREFIX,)), jnp.where(jnp.repeat(later, GB), 0.0, FAR)])
    one, zero = jnp.ones((length,)), jnp.zeros((length,))
    query_rows = jnp.stack([one, barred] + [zero] * 6)
    key_rows = jnp.stack([dead, prefix] + [one] * 3 + [zero] * 3)
    value_rows = jnp.stack([one] * 3 + [zero] * 5)
    return jnp.stack([query_rows, key_rows, value_rows]).astype(BF16)


def split(values):
    high = values.astype(BF16)
    return high, (values - high.astype(F32)).astype(BF16)


def product(form, left, right):
    (left_high, left_low), (right_high, right_low) = left, right
    return form(left_high, right_high) + (form(left_high, right_low) + form(left_low, right_high))


def optimizer_kernel(scale, packed, master, average, left, right, root_left, root_right, passed, sums, norms, *outs):
    slot_grad, new_left, new_right, new_master, new_copy, new_average, passed_on, norm_grad, new_norms = outs
    size = master.shape[1]
    passed_on[...] = passed[...]

    @pl.when(pl.program_id(0) == 0)
    def _():
        count = norms.shape[0]
        scaled = sums[:count] * scale
        norm_grad[...] = scaled
        square = jnp.sum(jnp.sum(scaled * scaled, axis=1, keepdims=True), axis=0, keepdims=True)
        new_norms[...] = norms[...] - 0.1 * scaled * lax.rsqrt(square * (1.0 / norms.size) + 1e-06)

    grad = unpack(packed[0]) * scale
    slot_grad[0] = grad
    grad_parts = split(grad)
    new_left[0] = 0.5 * left[0] + (0.5 / size) * nt(grad_parts[0], grad_parts[0])
    new_right[0] = 0.5 * right[0] + (0.5 / size) * tn(grad_parts[0], grad_parts[0])
    right_part = product(nn, grad_parts, split(root_right[0]))
    step = product(nn, split(root_left[0]), split(right_part))
    moved = master[0] - 0.03 * step
    new_master[0] = moved
    new_copy[0] = moved.astype(BF16)
    new_average[0] = 0.8 * average[0] + 0.2 * moved


def optimizer(packed, scale, arrays, passed, sums, norms):
    slots, size, _ = arrays[0].shape
    block = pl.BlockSpec((1, size, size), lambda i: (i, 0, 0))
    whole = lambda array: pl.BlockSpec(array.shape, lambda i: (0, 0))
    shape = lambda dtype: jax.ShapeDtypeStruct((slots, size, size), dtype)
    width = 128 * -(-passed.shape[1] // (128 * slots))
    last = passed.shape[1] // width - 1
    strip = pl.BlockSpec((passed.shape[0], width), lambda i: (0, jnp.minimum(i, last)))
    same = lambda array: jax.ShapeDtypeStruct(array.shape, F32)
    return pl.pallas_call(
        functools.partial(optimizer_kernel, scale),
        grid=(slots,),
        in_specs=[pl.BlockSpec((1,) + packed.shape[1:], lambda i: (i, 0, 0))]
        + [block] * 6
        + [strip, whole(sums), whole(norms)],
        out_specs=[block] * 6 + [strip, whole(norms), whole(norms)],
        out_shape=[shape(F32)] * 4 + [shape(BF16), shape(F32), same(passed), same(norms), same(norms)],
        name="optimizer",
    )(packed, *arrays, passed, sums, norms)


def norm_parts(values):
    average = jnp.mean(values, axis=0, keepdims=True)
    centred = values - average
    variance = jnp.mean(centred * centred, axis=0, keepdims=True)
    scale = lax.rsqrt(variance + 1e-05)
    return centred * scale, scale


def norm_back(unit, scale, gain, grad):
    inner = grad * gain
    mean_one = jnp.mean(inner, axis=0, keepdims=True)
    mean_two = jnp.mean(inner * unit, axis=0, keepdims=True)
    return scale * (inner - mean_one - unit * mean_two)


def local(
    chips,
    cores,
    tokens,
    cotangent,
    pad_mask,
    prefix_len,
    norm_gains,
    norm_shifts,
    owner_map,
    weight_copy,
    master,
    average_weights,
    stat_left,
    stat_right,
    root_left,
    root_right,
):
    cell_count, length, features = tokens.shape
    assert cell_count == 1
    slots, size, _ = weight_copy.shape
    slot_count = owner_map.shape[0]
    row_blocks = features // size
    square = row_blocks * row_blocks
    col_blocks = (slot_count - 4 * square) // (2 * row_blocks)
    known = chips == 16 and cores == 2
    chip = lax.axis_index("dp").astype(jnp.int32)
    seq_index = lax.axis_index("seq")

    slot_of = jnp.zeros((slot_count,), jnp.int32).at[owner_map].set(jnp.arange(slot_count, dtype=jnp.int32))
    own_tokens = tokens.reshape(length, features).T
    norms = jnp.stack([norm_gains[0], norm_shifts[0], norm_gains[1], norm_shifts[1]])
    params = norms.T
    if known:
        half = slots // 2
        begin = seq_index.astype(jnp.int32) * half
        placed = pack_slots(weight_copy, jnp.stack([begin, chip * slots + begin]), half, slot_count)
        gathered, normed_in = gather_slots(placed, own_tokens, params, slots)
    else:
        packed = pack_slots(weight_copy, jnp.zeros((2,), jnp.int32), slots, slots)
        gathered = lax.all_gather(packed, "dp", axis=0, tiled=True)
        prefix_tokens = lax.all_gather(own_tokens[:, :PREFIX], "seq")[0]
        unit_all, _ = norm_parts(jnp.concatenate([prefix_tokens, own_tokens], axis=1).astype(F32))
        normed_in = (unit_all * params[:, 0:1] + params[:, 1:2]).astype(BF16)
    starts = (3 * square, 4 * square, 4 * square + row_blocks * col_blocks)

    def three_of(i, j):
        return (j // row_blocks) * square + i * row_blocks + j % row_blocks

    w_three, qkv = front(gathered, slot_of, normed_in, row_blocks)

    position = seq_index * length + jnp.arange(length, dtype=jnp.int32)
    alive = jnp.where(position < PREFIX, position < prefix_len[0], pad_mask[0] == 1)
    prefix_alive = jnp.arange(PREFIX, dtype=jnp.int32) < prefix_len[0]
    groups = length // GB
    later = seq_index * groups + jnp.arange(groups) > 0
    extras = score_extras(alive, prefix_alive, later)

    grad_low = cotangent.reshape(length, features).T
    attended, log_total = attention(qkv, extras)
    block_out, activated, grad_pre, normed_mid, grad_branch, grad_att, grad_middle, sums = middle_part(
        gathered, slot_of, params, own_tokens, attended, grad_low, row_blocks, col_blocks
    )
    operands = (activated, grad_low, normed_mid, grad_pre, attended, grad_branch)
    grads = weight_grads(slot_of, operands, slot_count, size, starts, col_blocks)
    grad_three = attention_back(qkv, extras, attended, log_total, grad_att)
    flat_three = grad_three.reshape(3 * features, PREFIX + length)
    grads = weight_grad(normed_in, flat_three, slot_of, grads, slot_count, size, three_of, "grad_three")
    grad_scale = 1.0 / math.sqrt(length * chips * cores)
    if known:
        summed, grad_input, norm_sums = reduce_slots(
            grads, slots, w_three, grad_three, own_tokens, grad_middle, params, sums
        )
    else:
        part = lax.psum_scatter(grads.astype(F32), "dp", scatter_dimension=0, tiled=True)
        summed = lax.psum(part, "seq")
        grad_all = sum(nn(w_three[k], grad_three[k]) for k in range(3))
        prefix_part = jnp.where(seq_index == 0, lax.psum(grad_all[:, :PREFIX], "seq"), 0.0)
        grad_normed = grad_all[:, PREFIX:] + jnp.pad(prefix_part, ((0, 0), (0, length - PREFIX)))
        unit_one, scale_one = norm_parts(own_tokens.astype(F32))
        grad_input = grad_middle + norm_back(unit_one, scale_one, params[:, 0:1], grad_normed)
        first_sums = [jnp.sum(grad_normed * unit_one, axis=1), jnp.sum(grad_normed, axis=1)]
        norm_sums = lax.psum(jnp.stack(first_sums + [sums[2], sums[3]]), ("dp", "seq"))
    arrays = (master, average_weights, stat_left, stat_right, root_left, root_right)
    *stepped, grad_input, norm_grad, new_norms = optimizer(summed, grad_scale, arrays, grad_input, norm_sums, norms)
    token_shape = (cell_count, length, features)
    return (
        block_out.T.reshape(token_shape),
        grad_input.T.reshape(token_shape),
        norm_grad,
        new_norms,
        *stepped,
    )


def solution(mesh):
    tokens, slots = P("dp", "seq", None), P("dp", None, None)
    in_specs = (tokens, tokens, P("dp", "seq"), P("dp"), P(), P(), P()) + (slots,) * 7
    out_specs = (tokens, tokens, P(), P()) + (slots,) * 6
    body = functools.partial(local, mesh.shape["dp"], mesh.shape["seq"])
    return jax.shard_map(body, mesh=mesh, in_specs=in_specs, out_specs=out_specs, check_vma=False)
```

```python
import functools
import math

import jax
import jax.numpy as jnp
from jax import lax
from jax.experimental import pallas as pl
from jax.experimental.pallas import tpu as pltpu
from jax.sharding import PartitionSpec as P

HEADS = 20
GB = 256
PREFIX = 128
HALF = GB // 2
MESH = pl.DeviceIdType.MESH
BF16 = jnp.bfloat16
F32 = jnp.float32

MAIN = 256
RUN = 32


def runs(size):
    rest, per_tile = size - MAIN, 128 // (size - MAIN)
    places = []
    for index in range(-(-size // RUN)):
        lane = 128 * (index // per_tile) + rest * (index % per_tile)
        places.append((RUN * index, min(RUN, size - RUN * index), lane))
    assert places[-1][2] + rest <= MAIN
    return places


def pack_tail(block):
    size = block.shape[0]
    rest = size - MAIN
    pieces, lane = [], 0
    for row, count, start in runs(size):
        if start > lane:
            pieces.append(jnp.zeros((RUN, start - lane), block.dtype))
        piece = block[row : row + count, MAIN:]
        if count < RUN:
            piece = jnp.concatenate([piece, jnp.zeros((RUN - count, rest), block.dtype)], axis=0)
        pieces.append(piece)
        lane = start + rest
    if lane < MAIN:
        pieces.append(jnp.zeros((RUN, MAIN - lane), block.dtype))
    return jnp.concatenate(pieces, axis=1)


def unpack(packed):
    size = packed.shape[0] - RUN
    rest = size - MAIN
    low = packed[size:]
    tail = [low[:count, lane : lane + rest] for _, count, lane in runs(size)]
    return jnp.concatenate([packed[:size], jnp.concatenate(tail, axis=0)], axis=1)


def tn(left, right):
    return lax.dot_general(left, right, (((0,), (0,)), ((), ())), preferred_element_type=F32)


def nn(left, right):
    return lax.dot_general(left, right, (((1,), (0,)), ((), ())), preferred_element_type=F32)


def nt(left, right):
    return lax.dot_general(left, right, (((1,), (1,)), ((), ())), preferred_element_type=F32)


def cost(flops, moved, exps=0):
    return pl.CostEstimate(flops=int(flops), bytes_accessed=int(moved), transcendentals=int(exps))


def pack_kernel(start, block, packed):
    del start
    size = block.shape[1]
    rest = size - MAIN
    packed[0, :size] = block[0, :, :MAIN]
    packed[0, size:] = jnp.zeros((RUN, MAIN), BF16)
    for row, count, lane in runs(size):
        packed[0, size : size + count, lane : lane + rest] = block[0, row : row + count, MAIN:]


def pack_slots(blocks, start, count, slot_count):
    size = blocks.shape[1]
    return pl.pallas_call(
        pack_kernel,
        grid_spec=pltpu.PrefetchScalarGridSpec(
            num_scalar_prefetch=1,
            grid=(count,),
            in_specs=[pl.BlockSpec((1, size, size), lambda i, start: (start[0] + i, 0, 0))],
            out_specs=pl.BlockSpec((1, size + RUN, MAIN), lambda i, start: (start[1] + i, 0, 0)),
        ),
        out_shape=jax.ShapeDtypeStruct((slot_count, size + RUN, MAIN), BF16),
        name="pack_slots",
    )(start, blocks)


def place():
    me, core = lax.axis_index("dp"), lax.axis_index("seq")
    x, y, z = me % 2, (me // 2) % 2, me // 4
    step_x, step_y = 1 - 2 * x, 2 * (1 - 2 * y)
    first = step_y * (1 - core) + step_x * core
    second = step_x * (1 - core) + step_y * core
    return me, core, z, first, second


def greet(partners):
    barrier = pltpu.get_barrier_semaphore()
    for chip, core in partners:
        pl.semaphore_signal(barrier, inc=1, device_id=(chip, core), device_id_type=MESH)
    pl.semaphore_wait(barrier, len(partners))


UP, DOWN, FIRST, SECOND, TWIN, HEAD = 0, 4, 8, 12, 20, 36
LAST_FIRST, LAST_SECOND, LAST_UP, LAST_DOWN, LAST_TWIN, GATHER_LABELS = 37, 38, 40, 52, 64, 80


def gather_kernel(slots, placed, tokens, params, out, normed, held, send, recv, take):
    del placed
    me, core, z, first, second = place()
    half = slots // 2
    line = [(me + 4 * ((z + r) % 4 - z), core) for r in range(1, 4)]
    greet([(me + first, core), (me + second, core), (me, 1 - core)] + line)

    def copy(label, chip, dp, c, many=True):
        start = chip * slots + core * half
        ref = out.at[pl.ds(start, half - 1)] if many else out.at[pl.ds(start + half - 1, 1)]
        return pltpu.make_async_remote_copy(
            src_ref=ref,
            dst_ref=ref,
            send_sem=send.at[label],
            recv_sem=recv.at[label],
            device_id=(dp, c),
            device_id_type=MESH,
        )

    def col(zz):
        return me + 4 * (zz - z)

    def up(j):
        return copy(UP + j, me - 4 * (j - 1), me + 4, core)

    def down(j):
        return copy(DOWN + j, me + 4 * (j - 1), me - 4, core)

    def to_first(zz):
        return copy(FIRST + zz, col(zz), me + first, core)

    def to_second(zz, a):
        return copy(SECOND + 2 * zz + a, col(zz) + a * first, me + second, core)

    def to_twin(chip):
        return copy(TWIN + chip, chip, me, 1 - core)

    def spread(zz):
        to_first(zz).start()
        to_second(zz, 0).start()
        to_twin(col(zz)).start()

    def after_first(zz):
        to_first(zz).wait_recv()
        to_second(zz, 1).start()
        to_twin(col(zz) + first).start()

    def after_second(zz):
        for a in range(2):
            to_second(zz, a).wait_recv()
            to_twin(col(zz) + second + a * first).start()

    def off(q):
        return (q % 2) * first + (q // 2) * second

    def last_first():
        return copy(LAST_FIRST, me, me + first, core, False)

    def last_second(a):
        return copy(LAST_SECOND + a, me + a * first, me + second, core, False)

    def last_up(j, q):
        return copy(LAST_UP + 4 * (j - 1) + q, me - 4 * (j - 1) + off(q), me + 4, core, False)

    def last_down(j, q):
        return copy(LAST_DOWN + 4 * (j - 1) + q, me + 4 * (j - 1) + off(q), me - 4, core, False)

    def last_twin(chip):
        return copy(LAST_TWIN + chip, chip, me, 1 - core, False)

    def leave_plane(q):
        last_twin(me + off(q)).start()

        @pl.when(z < 3)
        def _():
            last_up(1, q).start()

        @pl.when(z > 0)
        def _():
            last_down(1, q).start()

    last_first().start()
    last_second(0).start()

    @pl.when(z < 3)
    def _():
        up(1).start()

    @pl.when(z > 0)
    def _():
        down(1).start()

    leave_plane(0)
    spread(z)

    prefix, seat = tokens.at[:, pl.ds(0, PREFIX)], held.at[:, pl.ds(0, PREFIX)]
    mine = pltpu.make_async_copy(tokens, held.at[:, pl.ds(PREFIX, tokens.shape[1])], take.at[0])
    near = pltpu.make_async_copy(prefix, seat, take.at[1])
    far = pltpu.make_async_remote_copy(
        src_ref=prefix,
        dst_ref=seat,
        send_sem=send.at[HEAD],
        recv_sem=recv.at[HEAD],
        device_id=(me, 1 - core),
        device_id_type=MESH,
    )
    mine.start()

    @pl.when(core == 0)
    def _():
        far.start()
        near.start()
        near.wait()

    @pl.when(core == 1)
    def _():
        far.wait_recv()

    mine.wait()

    def normalize(index, carry):
        tile = pl.ds(pl.multiple_of(index * PREFIX, PREFIX), PREFIX)
        unit, _ = norm_parts(held[:, tile].astype(F32))
        normed[:, tile] = (unit * params[:, 0:1] + params[:, 1:2]).astype(BF16)
        return carry

    lax.fori_loop(0, held.shape[1] // PREFIX, normalize, 0)
    last_first().wait_recv()
    last_second(1).start()
    leave_plane(1)
    last_second(0).wait_recv()
    leave_plane(2)
    for j in range(1, 4):

        @pl.when(z >= j)
        def _():
            up(j).wait_recv()
            if j < 3:

                @pl.when(z < 3)
                def _():
                    up(j + 1).start()

            spread(z - j)

        @pl.when(z + j <= 3)
        def _():
            down(j).wait_recv()
            if j < 3:

                @pl.when(z > 0)
                def _():
                    down(j + 1).start()

            spread(z + j)

        if j == 1:
            after_first(z)
        else:

            @pl.when(z >= j - 1)
            def _():
                after_first(z - (j - 1))

            @pl.when(z + j - 1 <= 3)
            def _():
                after_first(z + j - 1)

        if j == 1:
            last_second(1).wait_recv()
            leave_plane(3)
        for q in range(4):

            @pl.when(z >= j)
            def _():
                last_up(j, q).wait_recv()
                last_twin(me - 4 * j + off(q)).start()
                if j < 3:

                    @pl.when(z < 3)
                    def _():
                        last_up(j + 1, q).start()

            @pl.when(z + j <= 3)
            def _():
                last_down(j, q).wait_recv()
                last_twin(me + 4 * j + off(q)).start()
                if j < 3:

                    @pl.when(z > 0)
                    def _():
                        last_down(j + 1, q).start()

    @pl.when(z >= 3)
    def _():
        after_first(z - 3)

    @pl.when(z <= 0)
    def _():
        after_first(z + 3)

    after_second(z)
    for j in range(1, 4):

        @pl.when(z >= j)
        def _():
            after_second(z - j)

        @pl.when(z + j <= 3)
        def _():
            after_second(z + j)

    for zz in range(4):
        for a in range(2):
            for b in range(2):
                chip = col(zz) + a * first + b * second
                to_twin(chip).wait_recv()
                to_twin(chip).wait_send()
                last_twin(chip).wait_recv()
                last_twin(chip).wait_send()
        to_first(zz).wait_send()
        for a in range(2):
            to_second(zz, a).wait_send()

    last_first().wait_send()
    for a in range(2):
        last_second(a).wait_send()

    @pl.when(z < 3)
    def _():
        up(1).wait_send()
        for q in range(4):
            last_up(1, q).wait_send()
        for j in range(1, 3):

            @pl.when(z >= j)
            def _():
                up(j + 1).wait_send()
                for q in range(4):
                    last_up(j + 1, q).wait_send()

    @pl.when(z > 0)
    def _():
        down(1).wait_send()
        for q in range(4):
            last_down(1, q).wait_send()
        for j in range(1, 3):

            @pl.when(z + j <= 3)
            def _():
                down(j + 1).wait_send()
                for q in range(4):
                    last_down(j + 1, q).wait_send()

    @pl.when(core == 0)
    def _():
        far.wait_send()


def gather_slots(placed, tokens, params, slots):
    anywhere, inside = pl.BlockSpec(memory_space=pl.ANY), pl.BlockSpec(memory_space=pltpu.VMEM)
    wide = (tokens.shape[0], PREFIX + tokens.shape[1])
    return pl.pallas_call(
        functools.partial(gather_kernel, slots),
        out_shape=[jax.ShapeDtypeStruct(placed.shape, placed.dtype), jax.ShapeDtypeStruct(wide, BF16)],
        in_specs=[anywhere, anywhere, inside],
        out_specs=[anywhere, inside],
        scratch_shapes=[
            pltpu.VMEM(wide, BF16),
            pltpu.SemaphoreType.DMA((GATHER_LABELS,)),
            pltpu.SemaphoreType.DMA((GATHER_LABELS,)),
            pltpu.SemaphoreType.DMA((2,)),
        ],
        input_output_aliases={0: 0},
        compiler_params=pltpu.CompilerParams(collective_id=0, has_side_effects=True),
        name="gather_slots",
    )(placed, tokens, params)


R_TWIN, R_SECOND, R_FIRST, R_LINE, R_DONE, R_PREFIX, R_FLOW, REDUCE_LABELS = 0, 16, 24, 28, 32, 33, 34, 42
RING = 3
PANELS = 5


def reduce_kernel(
    slots,
    grads,
    w_three,
    grad_three,
    tokens,
    grad_middle,
    params,
    sums,
    out,
    grad_input,
    norm_sums,
    ring,
    r_twin,
    r_second,
    r_first,
    r_line,
    total,
    weights,
    inner,
    acc,
    prefix,
    given,
    folds,
    flow,
    arrived,
    load,
    send,
    recv,
    save,
):
    me, core, z, first, second = place()
    half = slots // 2
    features, length = acc.shape
    line = [(me + 4 * ((z + r) % 4 - z), core) for r in range(1, 4)]
    greet([(me + first, core), (me + second, core), (me, 1 - core)] + line)

    def piece(chip, h):
        return grads.at[pl.ds(chip * slots + h * half, half)]

    def chip_at(zz, a, b):
        return me + 4 * (zz - z) + a * first + b * second

    def remote(src, dst, label, dp, c):
        return pltpu.make_async_remote_copy(
            src_ref=src,
            dst_ref=dst,
            send_sem=send.at[label],
            recv_sem=recv.at[label],
            device_id=(dp, c),
            device_id_type=MESH,
        )

    def twin(zz, a, b):
        chip = chip_at(zz, a, b)
        return remote(piece(chip, 1 - core), r_twin.at[chip], R_TWIN + chip, me, 1 - core)

    def to_second(zz, a):
        return remote(
            r_twin.at[chip_at(zz, a, 1)], r_second.at[2 * zz + a], R_SECOND + 2 * zz + a, me + second, core
        )

    def to_first(zz):
        return remote(r_twin.at[chip_at(zz, 1, 0)], r_first.at[zz], R_FIRST + zz, me + first, core)

    def to_line(r):
        zz = (z + r) % 4
        return remote(r_twin.at[chip_at(zz, 0, 0)], r_line.at[r - 1], R_LINE + r, chip_at(zz, 0, 0), core)

    order = [2, 1, 3, 0]
    where = [(z + r) % 4 for r in order]
    turns = []
    for index in range(3):
        turns += [(where[index], 1, 1), (where[index], 0, 1)]
    turns += [(where[0], 1, 0), (where[3], 1, 1), (where[3], 0, 1), (where[0], 0, 0), (where[1], 1, 0)]
    turns += [(where[2], 1, 0), (where[1], 0, 0), (where[3], 1, 0), (where[2], 0, 0), (where[3], 0, 0)]

    def load_piece(chip, slot):
        return pltpu.make_async_copy(piece(chip, core), ring.at[slot], load.at[slot])

    def load_own(turn):
        return load_piece(chip_at(*turns[turn]), turn % RING)

    def add_up(turn, others):
        chip = chip_at(*turns[turn])
        load_own(turn).wait()
        twin(*turns[turn]).wait_recv()

        def body(s, carry):
            value = ring[turn % RING, s].astype(F32) + r_twin[chip, s].astype(F32)
            for ref, index in others:
                value = value + ref[index, s].astype(F32)
            if turn < len(turns) - 1:
                r_twin[chip, s] = value.astype(BF16)
            else:
                total[s] = value
            return carry

        lax.fori_loop(0, half, body, 0)
        if turn + RING < len(turns):
            load_own(turn + RING).start()

    def send_second(turn):
        zz, a, _ = turns[turn]
        add_up(turn, [])
        to_second(zz, a).start()

    def send_first(turn):
        zz = turns[turn][0]
        to_second(zz, 1).wait_recv()
        add_up(turn, [(r_second, 2 * zz + 1)])
        to_first(zz).start()

    def send_line(turn, r):
        zz = turns[turn][0]
        to_second(zz, 0).wait_recv()
        to_first(zz).wait_recv()
        add_up(turn, [(r_second, 2 * zz), (r_first, zz)])
        to_line(r).start()

    for turn in range(RING):
        load_own(turn).start()
    for zz in where:
        for a in (1, 0):
            twin(zz, 1, a).start()
    for zz in where:
        for a in (1, 0):
            twin(zz, 0, a).start()
    fetches = [
        pltpu.make_async_copy(w_three, weights, save.at[0]),
        pltpu.make_async_copy(grad_three, inner, save.at[1]),
    ]
    for fetch in fetches:
        fetch.start()
    def early(turn, carry):
        def pick(values):
            return sum(jnp.where(turn == index, value, 0) for index, value in enumerate(values))

        zz, a, slot = pick([t[0] for t in turns[:6]]), 1 - turn % 2, turn % RING
        chip, after = chip_at(zz, a, 1), pick([chip_at(*t) for t in turns[RING : RING + 6]])
        load_piece(chip, slot).wait()
        twin(zz, a, 1).wait_recv()

        def body(s, inner_carry):
            r_twin[chip, s] = (ring[slot, s].astype(F32) + r_twin[chip, s].astype(F32)).astype(BF16)
            return inner_carry

        lax.fori_loop(0, half, body, 0)
        load_piece(after, slot).start()
        to_second(zz, a).start()
        return carry

    lax.fori_loop(0, 6, early, 0)
    send_first(6)
    send_second(7)
    send_second(8)
    for fetch in fetches:
        fetch.wait()

    rows = features // PANELS

    def panel(index, carry):
        mine = pl.ds(pl.multiple_of(index * rows, 16), rows)
        acc[mine, :] = sum(nn(weights[k, mine, :], inner[k]) for k in range(3))
        return carry

    lax.fori_loop(0, PANELS, panel, 0)

    swap = remote(acc.at[:, pl.ds(0, PREFIX)], prefix, R_PREFIX, me, 1 - core)
    swap.start()
    own_tokens = weights.at[0, :, pl.ds(0, length - PREFIX)]
    take = pltpu.make_async_copy(tokens, own_tokens, save.at[0])
    take.start()

    def at(index):
        return pl.ds(pl.multiple_of(index * GB, GB), GB)

    def ahead(index):
        return pl.ds(pl.multiple_of(PREFIX + index * GB, PREFIX), GB)

    def give(index, slot):
        return pltpu.make_async_copy(grad_middle.at[:, at(index)], given.at[slot], save.at[2 + slot])

    def store(index):
        return pltpu.make_async_copy(acc.at[:, ahead(index)], grad_input.at[:, at(index)], save.at[4 + index])

    give(0, 0).start()
    send_line(9, order[0])
    send_first(10)
    take.wait()
    swap.wait()
    here = (1 - core).astype(F32)
    acc[:, PREFIX : 2 * PREFIX] += (acc[:, :PREFIX] + prefix[...]) * here
    folds[...] = jnp.zeros_like(folds)
    groups = (length - PREFIX) // GB

    def back(index, carry):
        @pl.when(index + 1 < groups)
        def _():
            give(index + 1, (index + 1) % 2).start()

        give(index, index % 2).wait()
        unit, scale = norm_parts(weights[0, :, at(index)].astype(F32))
        grad = acc[:, ahead(index)]
        folds[0] += fold(grad * unit)
        folds[1] += fold(grad)
        acc[:, ahead(index)] = given[index % 2] + norm_back(unit, scale, params[:, 0:1], grad)
        store(index).start()
        return carry

    lax.fori_loop(0, groups, back, 0)
    flow[0] = sums[...] + row_sums(folds[0], 0) + row_sums(folds[1], 1)
    pairs = [(me, 1 - core), (me + first, core), (me, 1 - core), (me + first, core), (me, 1 - core)] + line
    sources = [flow.at[0], flow.at[1], flow.at[2], arrived.at[2], flow.at[3]] + [flow.at[4]] * 3

    def pass_on(k):
        return remote(sources[k], arrived.at[k], R_FLOW + k, *pairs[k])

    for k in range(2):
        pass_on(k).start()
        pass_on(k).wait_recv()
        flow[k + 1] = flow[k] + arrived[k]
    pass_on(2).start()
    pass_on(2).wait_recv()
    pass_on(3).start()
    send_first(11)
    pass_on(3).wait_recv()
    flow[3] = arrived[2] + arrived[3]
    pass_on(4).start()
    pass_on(4).wait_recv()
    plane = jnp.where(core == 0, flow[3], arrived[4])
    flow[4] = plane
    arrived[4] = plane
    for k in range(5, 8):
        pass_on(k).start()
    send_line(12, order[1])
    send_first(13)
    send_line(14, order[2])
    for k in range(5, 8):
        pass_on(k).wait_recv()
    norm_sums[...] = sum(arrived[4 + (z - zz + 4) % 4] for zz in range(4))
    to_second(z, 0).wait_recv()
    to_first(z).wait_recv()
    for r in range(1, 4):
        to_line(r).wait_recv()
    add_up(15, [(r_second, 2 * z), (r_first, z), (r_line, 0), (r_line, 1), (r_line, 2)])
    target = out.at[pl.ds(core * half, half)]
    done = remote(total, target, R_DONE, me, 1 - core)
    done.start()
    saved = pltpu.make_async_copy(total, target, save.at[0])
    saved.start()
    for zz in range(4):
        for a in range(2):
            for b in range(2):
                twin(zz, a, b).wait_send()
            to_second(zz, a).wait_send()
        to_first(zz).wait_send()
    for r in range(1, 4):
        to_line(r).wait_send()
    for k in range(len(pairs)):
        pass_on(k).wait_send()
    for index in range(groups):
        store(index).wait()
    done.wait()
    saved.wait()


def reduce_slots(grads, slots, w_three, grad_three, tokens, grad_middle, params, sums):
    _, lines, lanes = grads.shape
    half = slots // 2
    _, features, length = grad_three.shape
    pieces = lambda n: pltpu.VMEM((n, half, lines, lanes), BF16)
    anywhere, inside = pl.BlockSpec(memory_space=pl.ANY), pl.BlockSpec(memory_space=pltpu.VMEM)
    groups = (length - PREFIX) // GB
    return pl.pallas_call(
        functools.partial(reduce_kernel, slots),
        out_shape=[
            jax.ShapeDtypeStruct((slots, lines, lanes), F32),
            jax.ShapeDtypeStruct((features, length - PREFIX), F32),
            jax.ShapeDtypeStruct((8, features), F32),
        ],
        in_specs=[anywhere] * 5 + [inside] * 2,
        out_specs=[anywhere, anywhere, inside],
        scratch_shapes=[
            pieces(RING),
            pieces(16),
            pieces(8),
            pieces(4),
            pieces(3),
            pltpu.VMEM((half, lines, lanes), F32),
            pltpu.VMEM(w_three.shape, BF16),
            pltpu.VMEM(grad_three.shape, BF16),
            pltpu.VMEM((features, length), F32),
            pltpu.VMEM((features, PREFIX), F32),
            pltpu.VMEM((2, features, GB), F32),
            pltpu.VMEM((2, features, 128), F32),
            pltpu.VMEM((5, 8, features), F32),
            pltpu.VMEM((8, 8, features), F32),
            pltpu.SemaphoreType.DMA((RING,)),
            pltpu.SemaphoreType.DMA((REDUCE_LABELS,)),
            pltpu.SemaphoreType.DMA((REDUCE_LABELS,)),
            pltpu.SemaphoreType.DMA((4 + groups,)),
        ],
        compiler_params=pltpu.CompilerParams(collective_id=1, has_side_effects=True, vmem_limit_bytes=63 << 20),
        name="reduce_slots",
    )(grads, w_three, grad_three, tokens, grad_middle, params, sums)


def lay(matrix, row, col, block):
    size = block.shape[0] - RUN
    matrix[size * row : size * (row + 1), size * col : size * col + MAIN] = block[:size]
    for start, count, lane in runs(size):
        piece = block[size : size + count, lane : lane + size - MAIN]
        matrix[size * row + start : size * row + start + count, size * col + MAIN : size * (col + 1)] = piece


def block_specs(gathered, rows, cols, block_of, **mode):
    shape = (1,) + gathered.shape[1:]
    pick = lambda i, j, step, v: (v[block_of(step, i, j)], 0, 0)
    return [
        pl.BlockSpec(shape, functools.partial(pick, i, j), **mode) for i in range(rows) for j in range(cols)
    ]


def feature_parts(features):
    part = -(-features // 256) * 128
    return [slice(start, min(start + part, features)) for start in range(0, features, part)]


def fold(values):
    return sum(values[:, start : start + 128] for start in range(0, values.shape[1], 128))


def row_sums(values, row):
    ones = jnp.ones((8, values.shape[1]), F32)
    summed = lax.dot_general(
        ones, values, (((1,), (1,)), ((), ())), precision=lax.Precision.HIGHEST, preferred_element_type=F32
    )
    return jnp.where(lax.broadcasted_iota(jnp.int32, summed.shape, 0) == row, summed, 0.0)


ONCE = pl.Buffered(1)


def front_kernel(slot_of, normed, *refs):
    del slot_of
    blocks, (weights, out) = refs[:-2], refs[-2:]
    row_blocks = math.isqrt(len(blocks))
    for index, block in enumerate(blocks):
        lay(weights.at[0], index // row_blocks, index % row_blocks, block.at[0])
    out[0] = tn(weights[0], normed[...]).astype(BF16)


def front(gathered, slot_of, normed, row_blocks):
    features, length = normed.shape
    square = row_blocks * row_blocks
    blocks = block_specs(gathered, row_blocks, row_blocks, lambda s, i, j: s * square + i * row_blocks + j)
    return pl.pallas_call(
        front_kernel,
        grid_spec=pltpu.PrefetchScalarGridSpec(
            num_scalar_prefetch=1,
            grid=(3,),
            in_specs=[pl.BlockSpec((features, length), lambda s, v: (0, 0), pipeline_mode=ONCE)] + blocks,
            out_specs=[
                pl.BlockSpec((1, features, features), lambda s, v: (s, 0, 0)),
                pl.BlockSpec((1, features, length), lambda s, v: (s, 0, 0)),
            ],
        ),
        out_shape=[
            jax.ShapeDtypeStruct((3, features, features), BF16),
            jax.ShapeDtypeStruct((3, features, length), BF16),
        ],
        compiler_params=pltpu.CompilerParams(vmem_limit_bytes=60 << 20),
        name="front",
    )(slot_of, normed, *([gathered] * square))


def gelu_pair(values):
    square = values * values
    bend = jnp.tanh(values * (0.7978845608028654 + (0.7978845608028654 * 0.044715) * square))
    half = 0.5 * values
    slope = 0.7978845608028654 + (3 * 0.7978845608028654 * 0.044715) * square
    return half + half * bend, 0.5 + 0.5 * bend + half * (1.0 - bend * bend) * slope


def middle_kernel(row_blocks, slot_of, params, tokens, attended, grad_low, *refs):
    del slot_of
    square = row_blocks * row_blocks
    out_blocks, up_blocks, down_blocks = (refs[square * k : square * (k + 1)] for k in range(3))
    outs, scratch = refs[3 * square : 3 * square + 8], refs[3 * square + 8 :]
    block_out, activated, grad_pre, normed, grad_branch, grad_att, grad_middle, sums = outs
    w_out, w_up, w_down, middle, total, stats, folds, sem = scratch
    tiles, parts = grad_low.shape[1] // GB, feature_parts(normed.shape[0])
    at = lambda index: pl.ds(pl.multiple_of(index * GB, GB), GB)
    step, last = pl.program_id(0), pl.num_programs(0) - 1

    @pl.when(step == 0)
    def _():
        copies = [
            pltpu.make_async_copy(tokens, block_out, sem.at[0]),
            pltpu.make_async_copy(attended, grad_att, sem.at[1]),
        ]
        for copy in copies:
            copy.start()
        for index, block in enumerate(out_blocks):
            lay(w_out, index // row_blocks, index % row_blocks, block.at[0])
        for copy in copies:
            copy.wait()
        def enter(index, carry):
            tile = at(index)
            for part in parts:
                values = block_out[part, tile].astype(F32) + tn(w_out[:, part], grad_att[:, tile])
                middle[part, tile] = values
                total[part, tile] = values
                grad_middle[part, tile] = jnp.zeros_like(values)
            values = middle[:, tile]
            average = jnp.mean(values, axis=0, keepdims=True)
            centred = values - average
            scale = lax.rsqrt(jnp.mean(centred * centred, axis=0, keepdims=True) + 1e-05)
            stats[0:1, tile] = average
            stats[1:2, tile] = scale
            normed[:, tile] = (centred * scale * params[:, 2:3] + params[:, 3:4]).astype(BF16)
            return carry

        lax.fori_loop(0, tiles, enter, 0)
        folds[...] = jnp.zeros_like(folds)

    for index in range(square):
        lay(w_up, index // row_blocks, index % row_blocks, up_blocks[index].at[0])
        lay(w_down, index // row_blocks, index % row_blocks, down_blocks[index].at[0])

    def advance(index, carry):
        tile = pl.ds(pl.multiple_of(index * wide, wide), wide)
        for part in parts:
            value, slope = gelu_pair(tn(w_up[:, part], normed[:, tile]))
            activated[part, tile] = value.astype(BF16)
            grad_pre[part, tile] = (nn(w_down[part, :], grad_low[:, tile]) * slope).astype(BF16)
        for part in parts:
            total[part, tile] += tn(w_down[:, part], activated[:, tile])
            grad_middle[part, tile] += nn(w_up[part, :], grad_pre[:, tile])
        return carry

    wide = 2 * GB if tiles % 2 == 0 else GB
    lax.fori_loop(0, grad_low.shape[1] // wide, advance, 0)

    @pl.when(step == last)
    def _():
        def leave(index, carry):
            tile = at(index)
            block_out[:, tile] = total[:, tile].astype(BF16)
            scale = stats[1:2, tile]
            unit = (middle[:, tile] - stats[0:1, tile]) * scale
            grad = grad_middle[:, tile]
            folds[0] += fold(grad * unit)
            folds[1] += fold(grad)
            values = grad_low[:, tile].astype(F32) + norm_back(unit, scale, params[:, 2:3], grad)
            grad_middle[:, tile] = values
            grad_branch[:, tile] = values.astype(BF16)
            for part in parts:
                grad_att[part, tile] = nn(w_out[part, :], grad_branch[:, tile]).astype(BF16)
            return carry

        lax.fori_loop(0, tiles, leave, 0)
        sums[...] = row_sums(folds[0], 2) + row_sums(folds[1], 3)


def middle_part(gathered, slot_of, params, tokens, attended, grad_low, row_blocks, col_blocks):
    features, length = tokens.shape
    square = row_blocks * row_blocks
    hidden = features * col_blocks // row_blocks
    up_start, down_start = 4 * square, 4 * square + row_blocks * col_blocks
    whole = lambda *shape: pl.BlockSpec(shape, lambda s, v: (0,) * len(shape), pipeline_mode=ONCE)
    anywhere = pl.BlockSpec(memory_space=pl.ANY)
    part = pl.BlockSpec((features, length), lambda s, v: (s, 0))
    blocks = (
        block_specs(
            gathered, row_blocks, row_blocks, lambda s, i, j: 3 * square + i * row_blocks + j, pipeline_mode=ONCE
        )
        + block_specs(
            gathered, row_blocks, row_blocks, lambda s, i, j: up_start + i * col_blocks + s * row_blocks + j
        )
        + block_specs(
            gathered, row_blocks, row_blocks, lambda s, i, j: down_start + (s * row_blocks + i) * row_blocks + j
        )
    )
    shape = jax.ShapeDtypeStruct
    square_scratch = pltpu.VMEM((features, features), BF16)
    return pl.pallas_call(
        functools.partial(middle_kernel, row_blocks),
        grid_spec=pltpu.PrefetchScalarGridSpec(
            num_scalar_prefetch=1,
            grid=(col_blocks // row_blocks,),
            in_specs=[whole(*params.shape)] + [anywhere] * 2 + [whole(features, length)] + blocks,
            out_specs=[whole(features, length), part, part]
            + [whole(features, length)] * 4
            + [whole(8, features)],
            scratch_shapes=[square_scratch] * 3
            + [pltpu.VMEM((features, length), F32)] * 2
            + [
                pltpu.VMEM((8, length), F32),
                pltpu.VMEM((2, features, 128), F32),
                pltpu.SemaphoreType.DMA((2,)),
            ],
        ),
        out_shape=[
            shape((features, length), BF16),
            shape((hidden, length), BF16),
            shape((hidden, length), BF16),
            shape((features, length), BF16),
            shape((features, length), BF16),
            shape((features, length), BF16),
            shape((features, length), F32),
            shape((8, features), F32),
        ],
        compiler_params=pltpu.CompilerParams(vmem_limit_bytes=63 << 20),
        name="middle_part",
    )(slot_of, params, tokens, attended, grad_low, *([gathered] * (3 * square)))


def weight_grad_kernel(block_of, deep, size, slot_of, left, right, *refs):
    grads, stage, sem = refs[-3:]
    wide = right.shape[0] // size
    rows, cols = pl.program_id(0), pl.program_id(1)
    step = rows * pl.num_programs(1) + cols
    steps = pl.num_programs(0) * pl.num_programs(1)
    now = step % 2

    def copy(buffer, index, slot):
        return pltpu.make_async_copy(stage.at[buffer, index], grads.at[slot], sem.at[buffer, index])

    @pl.when(step >= 2)
    def _():
        for index in range(deep * wide):
            copy(now, index, 0).wait()

    other = right[...]
    for i in range(deep):
        panel = nt(left[size * i : size * (i + 1), :], other)
        for j in range(wide):
            index = i * wide + j
            block = panel[:, size * j : size * (j + 1)]
            stage[now, index, :size] = block[:, :MAIN].astype(BF16)
            stage[now, index, size:] = pack_tail(block).astype(BF16)
            copy(now, index, slot_of[block_of(rows * deep + i, cols * wide + j)]).start()

    @pl.when(step == steps - 1)
    def _():
        for index in range(deep * wide):
            copy(now, index, 0).wait()

        @pl.when(steps > 1)
        def _():
            for index in range(deep * wide):
                copy(1 - now, index, 0).wait()


def weight_grad(left, right, slot_of, grads, slot_count, size, block_of, name):
    depth = left.shape[1]
    deep = wide = 4
    grid = (left.shape[0] // (size * deep), right.shape[0] // (size * wide))
    anywhere = pl.BlockSpec(memory_space=pl.ANY)
    operands = [slot_of, left, right] + ([] if grads is None else [grads])
    return pl.pallas_call(
        functools.partial(weight_grad_kernel, block_of, deep, size),
        grid_spec=pltpu.PrefetchScalarGridSpec(
            num_scalar_prefetch=1,
            grid=grid,
            in_specs=[
                pl.BlockSpec((size * deep, depth), lambda i, j, v: (i, 0)),
                pl.BlockSpec((size * wide, depth), lambda i, j, v: (j, 0)),
            ]
            + [anywhere] * (len(operands) - 3),
            out_specs=anywhere,
            scratch_shapes=[
                pltpu.VMEM((2, deep * wide, size + RUN, MAIN), BF16),
                pltpu.SemaphoreType.DMA((2, deep * wide)),
            ],
        ),
        out_shape=jax.ShapeDtypeStruct((slot_count, size + RUN, MAIN), BF16),
        input_output_aliases={} if grads is None else {3: 0},
        cost_estimate=cost(
            2 * left.shape[0] * right.shape[0] * depth,
            2 * (left.size + right.size + left.shape[0] * right.shape[0]),
        ),
        name=name,
    )(*operands)


def weight_grads_kernel(starts, col_blocks, size, slot_of, *refs):
    activated, grad_low, normed, grad_pre, attended, grad_branch, grads, left, right, stage, get, put = refs
    out_start, up_start, down_start = starts
    side_length = left.shape[1]
    row_blocks = side_length // size
    count = row_blocks * row_blocks
    parts = activated.shape[0] // side_length
    step, steps = pl.program_id(0), pl.num_programs(0)
    now = step % 2

    def rows(index):
        return pl.ds(pl.multiple_of(index * side_length, 16), side_length)

    def fetch(index, buffer):
        def start(one, other):
            pltpu.make_async_copy(one, left.at[buffer], get.at[0, buffer]).start()
            pltpu.make_async_copy(other, right.at[buffer], get.at[1, buffer]).start()

        @pl.when(index < parts)
        def _():
            start(activated.at[rows(index)], grad_low)

        @pl.when((index >= parts) & (index < 2 * parts))
        def _():
            start(normed, grad_pre.at[rows(index - parts)])

        @pl.when(index == 2 * parts)
        def _():
            start(attended, grad_branch)

    def copy(buffer, index, slot):
        return pltpu.make_async_copy(stage.at[buffer, index], grads.at[slot], put.at[buffer, index])

    @pl.when(step == 0)
    def _():
        fetch(0, 0)

    @pl.when(step + 1 < steps)
    def _():
        fetch(step + 1, 1 - now)

    pltpu.make_async_copy(normed, left.at[now], get.at[0, now]).wait()
    pltpu.make_async_copy(normed, right.at[now], get.at[1, now]).wait()

    @pl.when(step >= 2)
    def _():
        for index in range(count):
            copy(now, index, 0).wait()

    up = (step >= parts) & (step < 2 * parts)
    start = jnp.where(up, up_start + (step - parts) * row_blocks, out_start)
    start = jnp.where(step < parts, down_start + step * count, start)
    stride = jnp.where(up, col_blocks, row_blocks)
    other = right[now]
    for i in range(row_blocks):
        panel = nt(left[now, size * i : size * (i + 1), :], other)
        for j in range(row_blocks):
            index = i * row_blocks + j
            block = panel[:, size * j : size * (j + 1)]
            stage[now, index, :size] = block[:, :MAIN].astype(BF16)
            stage[now, index, size:] = pack_tail(block).astype(BF16)
            copy(now, index, slot_of[start + i * stride + j]).start()

    @pl.when(step == steps - 1)
    def _():
        for index in range(count):
            copy(now, index, 0).wait()
            copy(1 - now, index, 0).wait()


def weight_grads(slot_of, operands, slot_count, size, starts, col_blocks):
    hidden, length = operands[0].shape
    features = operands[1].shape[0]
    count = (features // size) ** 2
    steps = 2 * (hidden // features) + 1
    anywhere = pl.BlockSpec(memory_space=pl.ANY)
    part = pltpu.VMEM((2, features, length), BF16)
    return pl.pallas_call(
        functools.partial(weight_grads_kernel, starts, col_blocks, size),
        grid_spec=pltpu.PrefetchScalarGridSpec(
            num_scalar_prefetch=1,
            grid=(steps,),
            in_specs=[anywhere] * 6,
            out_specs=anywhere,
            scratch_shapes=[
                part,
                part,
                pltpu.VMEM((2, count, size + RUN, MAIN), BF16),
                pltpu.SemaphoreType.DMA((2, 2)),
                pltpu.SemaphoreType.DMA((2, count)),
            ],
        ),
        out_shape=jax.ShapeDtypeStruct((slot_count, size + RUN, MAIN), BF16),
        cost_estimate=cost(2 * steps * features * features * length, 8 * steps * features * length),
        name="weight_grads",
    )(slot_of, *operands)


EXTRA = 8
TOGETHER = 2
FAR = -1e30


def causal():
    return lax.broadcasted_iota(jnp.int32, (HALF, HALF), 0) <= lax.broadcasted_iota(jnp.int32, (HALF, HALF), 1)


def places(groups):
    found = []
    for group in range(groups):
        base = PREFIX + GB * group
        low, high = slice(base, base + HALF), slice(base + HALF, base + GB)
        found.append((low, high, slice(base, base + GB), slice(GB * group, GB * (group + 1))))
    return found


def side(left, right):
    return jnp.concatenate([left, right], axis=1)


def attention_kernel(scale, head, qkv, extras, out, lse, queries, keys, values, keys_t):
    unit = scale * math.log2(math.e)
    heads = range(queries.shape[0])

    @pl.when(pl.program_id(0) == 0)
    def _():
        for k in heads:
            queries[k, head:] = extras[0]
            keys[k, head:] = extras[1]
            values[k, head:] = extras[2]

    for k in heads:
        rows = slice(head * k, head * (k + 1))
        queries[k, :head] = qkv[0, rows]
        keys[k, :head] = qkv[1, rows]
        values[k, :head] = qkv[2, rows]
    for k in heads:
        keys_t[k] = keys[k].T
    ahead = causal()
    spots = [(k,) + spot for k in heads for spot in places(out.shape[1] // GB)]
    scores = []
    for k, low, high, both, _ in spots:
        asked = queries[k, :, both]
        scores.append((nn(keys_t[k, :PREFIX], asked), nn(keys_t[k, low], asked), nn(keys_t[k, high], asked[:, HALF:])))

    def peak(array):
        return jnp.max(array, axis=0, keepdims=True)

    def soft(array, top):
        return jnp.exp2((array - top) * unit).astype(BF16)

    tops, weights = [], []
    for prefix, first, second in scores:
        first = side(jnp.where(ahead, first[:, :HALF], FAR), first[:, HALF:])
        second = jnp.where(ahead, second, FAR)
        top = jnp.maximum(peak(prefix), peak(first))
        top = side(top[:, :HALF], jnp.maximum(top[:, HALF:], peak(second)))
        tops.append(top)
        weights.append((soft(prefix, top), soft(first, top), soft(second, top[:, HALF:])))
    for (k, low, high, _, mine), top, (prefix, first, second) in zip(spots, tops, weights):
        sums = nn(values[k, :, :PREFIX], prefix) + nn(values[k, :, low], first)
        sums = side(sums[:, :HALF], sums[:, HALF:] + nn(values[k, :, high], second))
        total = sums[head : head + 1]
        out[head * k : head * (k + 1), mine] = (sums[:head] / total).astype(BF16)
        lse[k, :, mine] = top + jnp.log(total) * (1.0 / scale)


def thirds(values):
    high = values.astype(BF16).astype(F32)
    rest = values - high
    middle = rest.astype(BF16).astype(F32)
    return high, middle, rest - middle


def with_rows(base, start, rows):
    index = lax.broadcasted_iota(jnp.int32, base.shape, 0)
    for offset, row in enumerate(rows):
        base = jnp.where(index == start + offset, row, base)
    return base.astype(BF16)


def attention_back_kernel(
    scale, head, qkv, extras, out, lse, grad_out, grads, queries, keys, values, grad_o, keys_t, values_t
):
    own = out.shape[1]
    unit = scale * math.log2(math.e)
    heads = range(queries.shape[0])

    @pl.when(pl.program_id(0) == 0)
    def _():
        for k in heads:
            keys[k, head:] = extras[1]
            values[k, head:] = extras[2]

    for k in heads:
        rows = slice(head * k, head * (k + 1))
        queries[k, :head] = qkv[0, rows, PREFIX:]
        keys[k, :head] = qkv[1, rows]
        values[k, :head] = qkv[2, rows]
        given = grad_out[rows]
        grad_o[k, :head] = given
        queries[k, head:] = with_rows(extras[0, :, PREFIX:].astype(F32), 2, thirds(-lse[k]))
        delta = jnp.sum(given.astype(F32) * out[rows].astype(F32), axis=0, keepdims=True)
        grad_o[k, head:] = with_rows(jnp.zeros((EXTRA, own), F32), 0, thirds(-delta))
    for k in heads:
        keys_t[k] = keys[k].T
        values_t[k] = values[k].T
    ahead = causal()
    spots = [(k,) + spot for k in heads for spot in places(own // GB)]

    def weigh(k, rows, asked, given, mask):
        weights = jnp.exp2(nn(keys_t[k, rows], asked) * unit)
        if mask == 1:
            weights = side(jnp.where(ahead, weights[:, :HALF], 0.0), weights[:, HALF:])
        if mask == 2:
            weights = jnp.where(ahead, weights, 0.0)
        return weights.astype(BF16), (weights * nn(values_t[k, rows], given)).astype(BF16)

    found = []
    for k, low, high, _, mine in spots:
        asked, given = queries[k, :, mine], grad_o[k, :, mine]
        found.append(
            (
                weigh(k, slice(0, PREFIX), asked, given, 0),
                weigh(k, low, asked, given, 1),
                weigh(k, high, asked[:, HALF:], given[:, HALF:], 2),
            )
        )
    prefix_k, prefix_v = {}, {}
    for (k, low, high, both, mine), ((p0, d0), (p1, d1), (p2, d2)) in zip(spots, found):
        rows = slice(head * k, head * (k + 1))
        asked, given = queries[k, :head, mine], grad_o[k, :head, mine]
        grad_q = nn(keys[k, :head, :PREFIX], d0) + nn(keys[k, :head, low], d1)
        grad_q = side(grad_q[:, :HALF], grad_q[:, HALF:] + nn(keys[k, :head, high], d2))
        grads[0, rows, both] = (grad_q * scale).astype(BF16)
        part_k, part_v = nt(asked, d0), nt(given, p0)
        prefix_k[k] = prefix_k[k] + part_k if k in prefix_k else part_k
        prefix_v[k] = prefix_v[k] + part_v if k in prefix_v else part_v
        grads[1, rows, low] = (nt(asked, d1) * scale).astype(BF16)
        grads[2, rows, low] = nt(given, p1).astype(BF16)
        grads[1, rows, high] = (nt(asked[:, HALF:], d2) * scale).astype(BF16)
        grads[2, rows, high] = nt(given[:, HALF:], p2).astype(BF16)
    for k in heads:
        rows = slice(head * k, head * (k + 1))
        grads[0, rows, :PREFIX] = jnp.zeros((head, PREFIX), BF16)
        grads[1, rows, :PREFIX] = (prefix_k[k] * scale).astype(BF16)
        grads[2, rows, :PREFIX] = prefix_v[k].astype(BF16)


def attention_specs(qkv):
    _, features, length = qkv.shape
    head, own = features // HEADS, length - PREFIX
    three = pl.BlockSpec((3, TOGETHER * head, length), lambda h: (0, h, 0))
    extra = pl.BlockSpec((3, EXTRA, length), lambda h: (0, 0, 0))
    one = pl.BlockSpec((TOGETHER * head, own), lambda h: (h, 0))
    row = pl.BlockSpec((TOGETHER, 1, own), lambda h: (h, 0, 0))
    wide = lambda columns: pltpu.VMEM((TOGETHER, head + EXTRA, columns), BF16)
    tall = pltpu.VMEM((TOGETHER, length, head + EXTRA), BF16)
    return features, length, own, head, three, extra, one, row, wide, tall


def attention(qkv, extras):
    features, length, own, head, three, extra, one, row, wide, tall = attention_specs(qkv)
    return pl.pallas_call(
        functools.partial(attention_kernel, head ** (-0.5), head),
        grid=(HEADS // TOGETHER,),
        in_specs=[three, extra],
        out_specs=[one, row],
        out_shape=[
            jax.ShapeDtypeStruct((features, own), BF16),
            jax.ShapeDtypeStruct((HEADS, 1, own), F32),
        ],
        scratch_shapes=[wide(length), wide(length), wide(length), tall],
        cost_estimate=cost(8 * features * own * GB, 2 * qkv.size, HEADS * own * GB),
        name="attention",
    )(qkv, extras)


def attention_back(qkv, extras, out, lse, grad_out):
    features, length, own, head, three, extra, one, row, wide, tall = attention_specs(qkv)
    return pl.pallas_call(
        functools.partial(attention_back_kernel, head ** (-0.5), head),
        grid=(HEADS // TOGETHER,),
        in_specs=[three, extra, one, row, one],
        out_specs=three,
        out_shape=jax.ShapeDtypeStruct(qkv.shape, BF16),
        scratch_shapes=[wide(own), wide(length), wide(length), wide(own), tall, tall],
        cost_estimate=cost(20 * features * own * GB, 4 * qkv.size, HEADS * own * GB),
        name="attention_back",
    )(qkv, extras, out, lse, grad_out)


def score_extras(alive, prefix_alive, later):
    length = PREFIX + alive.shape[0]
    dead = jnp.where(jnp.concatenate([prefix_alive, alive]), 0.0, FAR)
    prefix = (jnp.arange(length) < PREFIX).astype(F32)
    barred = jnp.concatenate([jnp.zeros((PREFIX,)), jnp.where(jnp.repeat(later, GB), 0.0, FAR)])
    one, zero = jnp.ones((length,)), jnp.zeros((length,))
    query_rows = jnp.stack([one, barred] + [zero] * 6)
    key_rows = jnp.stack([dead, prefix] + [one] * 3 + [zero] * 3)
    value_rows = jnp.stack([one] * 3 + [zero] * 5)
    return jnp.stack([query_rows, key_rows, value_rows]).astype(BF16)


def split(values):
    high = values.astype(BF16)
    return high, (values - high.astype(F32)).astype(BF16)


def product(form, left, right):
    (left_high, left_low), (right_high, right_low) = left, right
    return form(left_high, right_high) + (form(left_high, right_low) + form(left_low, right_high))


def optimizer_kernel(scale, packed, master, average, left, right, root_left, root_right, passed, sums, norms, *outs):
    slot_grad, new_left, new_right, new_master, new_copy, new_average, passed_on, norm_grad, new_norms = outs
    size = master.shape[1]
    passed_on[...] = passed[...]

    @pl.when(pl.program_id(0) == 0)
    def _():
        count = norms.shape[0]
        scaled = sums[:count] * scale
        norm_grad[...] = scaled
        square = jnp.sum(jnp.sum(scaled * scaled, axis=1, keepdims=True), axis=0, keepdims=True)
        new_norms[...] = norms[...] - 0.1 * scaled * lax.rsqrt(square * (1.0 / norms.size) + 1e-06)

    grad = unpack(packed[0]) * scale
    slot_grad[0] = grad
    grad_parts = split(grad)
    new_left[0] = 0.5 * left[0] + (0.5 / size) * nt(grad_parts[0], grad_parts[0])
    new_right[0] = 0.5 * right[0] + (0.5 / size) * tn(grad_parts[0], grad_parts[0])
    right_part = product(nn, grad_parts, split(root_right[0]))
    step = product(nn, split(root_left[0]), split(right_part))
    moved = master[0] - 0.03 * step
    new_master[0] = moved
    new_copy[0] = moved.astype(BF16)
    new_average[0] = 0.8 * average[0] + 0.2 * moved


def optimizer(packed, scale, arrays, passed, sums, norms):
    slots, size, _ = arrays[0].shape
    block = pl.BlockSpec((1, size, size), lambda i: (i, 0, 0))
    whole = lambda array: pl.BlockSpec(array.shape, lambda i: (0, 0))
    shape = lambda dtype: jax.ShapeDtypeStruct((slots, size, size), dtype)
    width = 128 * -(-passed.shape[1] // (128 * slots))
    last = passed.shape[1] // width - 1
    strip = pl.BlockSpec((passed.shape[0], width), lambda i: (0, jnp.minimum(i, last)))
    same = lambda array: jax.ShapeDtypeStruct(array.shape, F32)
    return pl.pallas_call(
        functools.partial(optimizer_kernel, scale),
        grid=(slots,),
        in_specs=[pl.BlockSpec((1,) + packed.shape[1:], lambda i: (i, 0, 0))]
        + [block] * 6
        + [strip, whole(sums), whole(norms)],
        out_specs=[block] * 6 + [strip, whole(norms), whole(norms)],
        out_shape=[shape(F32)] * 4 + [shape(BF16), shape(F32), same(passed), same(norms), same(norms)],
        name="optimizer",
    )(packed, *arrays, passed, sums, norms)


def norm_parts(values):
    average = jnp.mean(values, axis=0, keepdims=True)
    centred = values - average
    variance = jnp.mean(centred * centred, axis=0, keepdims=True)
    scale = lax.rsqrt(variance + 1e-05)
    return centred * scale, scale


def norm_back(unit, scale, gain, grad):
    inner = grad * gain
    mean_one = jnp.mean(inner, axis=0, keepdims=True)
    mean_two = jnp.mean(inner * unit, axis=0, keepdims=True)
    return scale * (inner - mean_one - unit * mean_two)


def local(
    chips,
    cores,
    tokens,
    cotangent,
    pad_mask,
    prefix_len,
    norm_gains,
    norm_shifts,
    owner_map,
    weight_copy,
    master,
    average_weights,
    stat_left,
    stat_right,
    root_left,
    root_right,
):
    cell_count, length, features = tokens.shape
    assert cell_count == 1
    slots, size, _ = weight_copy.shape
    slot_count = owner_map.shape[0]
    row_blocks = features // size
    square = row_blocks * row_blocks
    col_blocks = (slot_count - 4 * square) // (2 * row_blocks)
    known = chips == 16 and cores == 2
    chip = lax.axis_index("dp").astype(jnp.int32)
    seq_index = lax.axis_index("seq")

    slot_of = jnp.zeros((slot_count,), jnp.int32).at[owner_map].set(jnp.arange(slot_count, dtype=jnp.int32))
    own_tokens = tokens.reshape(length, features).T
    norms = jnp.stack([norm_gains[0], norm_shifts[0], norm_gains[1], norm_shifts[1]])
    params = norms.T
    if known:
        half = slots // 2
        begin = seq_index.astype(jnp.int32) * half
        placed = pack_slots(weight_copy, jnp.stack([begin, chip * slots + begin]), half, slot_count)
        gathered, normed_in = gather_slots(placed, own_tokens, params, slots)
    else:
        packed = pack_slots(weight_copy, jnp.zeros((2,), jnp.int32), slots, slots)
        gathered = lax.all_gather(packed, "dp", axis=0, tiled=True)
        prefix_tokens = lax.all_gather(own_tokens[:, :PREFIX], "seq")[0]
        unit_all, _ = norm_parts(jnp.concatenate([prefix_tokens, own_tokens], axis=1).astype(F32))
        normed_in = (unit_all * params[:, 0:1] + params[:, 1:2]).astype(BF16)
    starts = (3 * square, 4 * square, 4 * square + row_blocks * col_blocks)

    def three_of(i, j):
        return (j // row_blocks) * square + i * row_blocks + j % row_blocks

    w_three, qkv = front(gathered, slot_of, normed_in, row_blocks)

    position = seq_index * length + jnp.arange(length, dtype=jnp.int32)
    alive = jnp.where(position < PREFIX, position < prefix_len[0], pad_mask[0] == 1)
    prefix_alive = jnp.arange(PREFIX, dtype=jnp.int32) < prefix_len[0]
    groups = length // GB
    later = seq_index * groups + jnp.arange(groups) > 0
    extras = score_extras(alive, prefix_alive, later)

    grad_low = cotangent.reshape(length, features).T
    attended, log_total = attention(qkv, extras)
    block_out, activated, grad_pre, normed_mid, grad_branch, grad_att, grad_middle, sums = middle_part(
        gathered, slot_of, params, own_tokens, attended, grad_low, row_blocks, col_blocks
    )
    operands = (activated, grad_low, normed_mid, grad_pre, attended, grad_branch)
    grads = weight_grads(slot_of, operands, slot_count, size, starts, col_blocks)
    grad_three = attention_back(qkv, extras, attended, log_total, grad_att)
    flat_three = grad_three.reshape(3 * features, PREFIX + length)
    grads = weight_grad(normed_in, flat_three, slot_of, grads, slot_count, size, three_of, "grad_three")
    grad_scale = 1.0 / math.sqrt(length * chips * cores)
    if known:
        summed, grad_input, norm_sums = reduce_slots(
            grads, slots, w_three, grad_three, own_tokens, grad_middle, params, sums
        )
    else:
        part = lax.psum_scatter(grads.astype(F32), "dp", scatter_dimension=0, tiled=True)
        summed = lax.psum(part, "seq")
        grad_all = sum(nn(w_three[k], grad_three[k]) for k in range(3))
        prefix_part = jnp.where(seq_index == 0, lax.psum(grad_all[:, :PREFIX], "seq"), 0.0)
        grad_normed = grad_all[:, PREFIX:] + jnp.pad(prefix_part, ((0, 0), (0, length - PREFIX)))
        unit_one, scale_one = norm_parts(own_tokens.astype(F32))
        grad_input = grad_middle + norm_back(unit_one, scale_one, params[:, 0:1], grad_normed)
        first_sums = [jnp.sum(grad_normed * unit_one, axis=1), jnp.sum(grad_normed, axis=1)]
        norm_sums = lax.psum(jnp.stack(first_sums + [sums[2], sums[3]]), ("dp", "seq"))
    arrays = (master, average_weights, stat_left, stat_right, root_left, root_right)
    *stepped, grad_input, norm_grad, new_norms = optimizer(summed, grad_scale, arrays, grad_input, norm_sums, norms)
    token_shape = (cell_count, length, features)
    return (
        block_out.T.reshape(token_shape),
        grad_input.T.reshape(token_shape),
        norm_grad,
        new_norms,
        *stepped,
    )


def solution(mesh):
    tokens, slots = P("dp", "seq", None), P("dp", None, None)
    in_specs = (tokens, tokens, P("dp", "seq"), P("dp"), P(), P(), P()) + (slots,) * 7
    out_specs = (tokens, tokens, P(), P()) + (slots,) * 6
    body = functools.partial(local, mesh.shape["dp"], mesh.shape["seq"])
    return jax.shard_map(body, mesh=mesh, in_specs=in_specs, out_specs=out_specs, check_vma=False)
```

```python
import functools
import math

import jax
import jax.numpy as jnp
from jax import lax
from jax.experimental import pallas as pl
from jax.experimental.pallas import tpu as pltpu
from jax.sharding import PartitionSpec as P

HEADS = 20
GB = 256
PREFIX = 128
HALF = GB // 2
MESH = pl.DeviceIdType.MESH
BF16 = jnp.bfloat16
F32 = jnp.float32

MAIN = 256
RUN = 32


def runs(size):
    rest, per_tile = size - MAIN, 128 // (size - MAIN)
    places = []
    for index in range(-(-size // RUN)):
        lane = 128 * (index // per_tile) + rest * (index % per_tile)
        places.append((RUN * index, min(RUN, size - RUN * index), lane))
    assert places[-1][2] + rest <= MAIN
    return places


def pack_tail(block):
    size = block.shape[0]
    rest = size - MAIN
    pieces, lane = [], 0
    for row, count, start in runs(size):
        if start > lane:
            pieces.append(jnp.zeros((RUN, start - lane), block.dtype))
        piece = block[row : row + count, MAIN:]
        if count < RUN:
            piece = jnp.concatenate([piece, jnp.zeros((RUN - count, rest), block.dtype)], axis=0)
        pieces.append(piece)
        lane = start + rest
    if lane < MAIN:
        pieces.append(jnp.zeros((RUN, MAIN - lane), block.dtype))
    return jnp.concatenate(pieces, axis=1)


def unpack(packed):
    size = packed.shape[0] - RUN
    rest = size - MAIN
    low = packed[size:]
    tail = [low[:count, lane : lane + rest] for _, count, lane in runs(size)]
    return jnp.concatenate([packed[:size], jnp.concatenate(tail, axis=0)], axis=1)


def tn(left, right):
    return lax.dot_general(left, right, (((0,), (0,)), ((), ())), preferred_element_type=F32)


def nn(left, right):
    return lax.dot_general(left, right, (((1,), (0,)), ((), ())), preferred_element_type=F32)


def nt(left, right):
    return lax.dot_general(left, right, (((1,), (1,)), ((), ())), preferred_element_type=F32)


def cost(flops, moved, exps=0):
    return pl.CostEstimate(flops=int(flops), bytes_accessed=int(moved), transcendentals=int(exps))


def pack_kernel(start, block, packed):
    del start
    size = block.shape[1]
    rest = size - MAIN
    packed[0, :size] = block[0, :, :MAIN]
    packed[0, size:] = jnp.zeros((RUN, MAIN), BF16)
    for row, count, lane in runs(size):
        packed[0, size : size + count, lane : lane + rest] = block[0, row : row + count, MAIN:]


def pack_slots(blocks, start, count, slot_count):
    size = blocks.shape[1]
    return pl.pallas_call(
        pack_kernel,
        grid_spec=pltpu.PrefetchScalarGridSpec(
            num_scalar_prefetch=1,
            grid=(count,),
            in_specs=[pl.BlockSpec((1, size, size), lambda i, start: (start[0] + i, 0, 0))],
            out_specs=pl.BlockSpec((1, size + RUN, MAIN), lambda i, start: (start[1] + i, 0, 0)),
        ),
        out_shape=jax.ShapeDtypeStruct((slot_count, size + RUN, MAIN), BF16),
        name="pack_slots",
    )(start, blocks)


def place():
    me, core = lax.axis_index("dp"), lax.axis_index("seq")
    x, y, z = me % 2, (me // 2) % 2, me // 4
    step_x, step_y = 1 - 2 * x, 2 * (1 - 2 * y)
    first = step_y * (1 - core) + step_x * core
    second = step_x * (1 - core) + step_y * core
    return me, core, z, first, second


def greet(partners):
    barrier = pltpu.get_barrier_semaphore()
    for chip, core in partners:
        pl.semaphore_signal(barrier, inc=1, device_id=(chip, core), device_id_type=MESH)
    pl.semaphore_wait(barrier, len(partners))


UP, DOWN, FIRST, SECOND, TWIN, HEAD = 0, 4, 8, 12, 20, 36
LAST_FIRST, LAST_SECOND, LAST_UP, LAST_DOWN, LAST_TWIN, GATHER_LABELS = 37, 38, 40, 52, 64, 80


def gather_kernel(slots, placed, tokens, params, out, normed, held, send, recv, take):
    del placed
    me, core, z, first, second = place()
    half = slots // 2
    line = [(me + 4 * ((z + r) % 4 - z), core) for r in range(1, 4)]
    greet([(me + first, core), (me + second, core), (me, 1 - core)] + line)

    def copy(label, chip, dp, c, many=True):
        start = chip * slots + core * half
        ref = out.at[pl.ds(start, half - 1)] if many else out.at[pl.ds(start + half - 1, 1)]
        return pltpu.make_async_remote_copy(
            src_ref=ref,
            dst_ref=ref,
            send_sem=send.at[label],
            recv_sem=recv.at[label],
            device_id=(dp, c),
            device_id_type=MESH,
        )

    def col(zz):
        return me + 4 * (zz - z)

    def up(j):
        return copy(UP + j, me - 4 * (j - 1), me + 4, core)

    def down(j):
        return copy(DOWN + j, me + 4 * (j - 1), me - 4, core)

    def to_first(zz):
        return copy(FIRST + zz, col(zz), me + first, core)

    def to_second(zz, a):
        return copy(SECOND + 2 * zz + a, col(zz) + a * first, me + second, core)

    def to_twin(chip):
        return copy(TWIN + chip, chip, me, 1 - core)

    def spread(zz):
        to_first(zz).start()
        to_second(zz, 0).start()
        to_twin(col(zz)).start()

    def after_first(zz):
        to_first(zz).wait_recv()
        to_second(zz, 1).start()
        to_twin(col(zz) + first).start()

    def after_second(zz):
        for a in range(2):
            to_second(zz, a).wait_recv()
            to_twin(col(zz) + second + a * first).start()

    def off(q):
        return (q % 2) * first + (q // 2) * second

    def last_first():
        return copy(LAST_FIRST, me, me + first, core, False)

    def last_second(a):
        return copy(LAST_SECOND + a, me + a * first, me + second, core, False)

    def last_up(j, q):
        return copy(LAST_UP + 4 * (j - 1) + q, me - 4 * (j - 1) + off(q), me + 4, core, False)

    def last_down(j, q):
        return copy(LAST_DOWN + 4 * (j - 1) + q, me + 4 * (j - 1) + off(q), me - 4, core, False)

    def last_twin(chip):
        return copy(LAST_TWIN + chip, chip, me, 1 - core, False)

    def leave_plane(q):
        last_twin(me + off(q)).start()

        @pl.when(z < 3)
        def _():
            last_up(1, q).start()

        @pl.when(z > 0)
        def _():
            last_down(1, q).start()

    last_first().start()
    last_second(0).start()

    @pl.when(z < 3)
    def _():
        up(1).start()

    @pl.when(z > 0)
    def _():
        down(1).start()

    leave_plane(0)
    spread(z)

    prefix, seat = tokens.at[:, pl.ds(0, PREFIX)], held.at[:, pl.ds(0, PREFIX)]
    mine = pltpu.make_async_copy(tokens, held.at[:, pl.ds(PREFIX, tokens.shape[1])], take.at[0])
    near = pltpu.make_async_copy(prefix, seat, take.at[1])
    far = pltpu.make_async_remote_copy(
        src_ref=prefix,
        dst_ref=seat,
        send_sem=send.at[HEAD],
        recv_sem=recv.at[HEAD],
        device_id=(me, 1 - core),
        device_id_type=MESH,
    )
    mine.start()

    @pl.when(core == 0)
    def _():
        far.start()
        near.start()
        near.wait()

    @pl.when(core == 1)
    def _():
        far.wait_recv()

    mine.wait()

    def normalize(index, carry):
        tile = pl.ds(pl.multiple_of(index * PREFIX, PREFIX), PREFIX)
        unit, _ = norm_parts(held[:, tile].astype(F32))
        normed[:, tile] = (unit * params[:, 0:1] + params[:, 1:2]).astype(BF16)
        return carry

    lax.fori_loop(0, held.shape[1] // PREFIX, normalize, 0)
    def pass_last(j):
        for q in range(4):

            @pl.when(z >= j)
            def _():
                last_up(j, q).wait_recv()
                last_twin(me - 4 * j + off(q)).start()
                if j < 3:

                    @pl.when(z < 3)
                    def _():
                        last_up(j + 1, q).start()

            @pl.when(z + j <= 3)
            def _():
                last_down(j, q).wait_recv()
                last_twin(me + 4 * j + off(q)).start()
                if j < 3:

                    @pl.when(z > 0)
                    def _():
                        last_down(j + 1, q).start()

    last_first().wait_recv()
    last_second(1).start()
    leave_plane(1)
    last_second(0).wait_recv()
    leave_plane(2)
    for j in range(1, 4):

        @pl.when(z >= j)
        def _():
            up(j).wait_recv()
            if j < 3:

                @pl.when(z < 3)
                def _():
                    up(j + 1).start()

            spread(z - j)

        @pl.when(z + j <= 3)
        def _():
            down(j).wait_recv()
            if j < 3:

                @pl.when(z > 0)
                def _():
                    down(j + 1).start()

            spread(z + j)

        if j == 1:
            after_first(z)
        else:

            @pl.when(z >= j - 1)
            def _():
                after_first(z - (j - 1))

            @pl.when(z + j - 1 <= 3)
            def _():
                after_first(z + j - 1)

        if j == 1:
            last_second(1).wait_recv()
            leave_plane(3)
        else:
            pass_last(j - 1)

    @pl.when(z >= 3)
    def _():
        after_first(z - 3)

    @pl.when(z <= 0)
    def _():
        after_first(z + 3)

    pass_last(3)
    after_second(z)
    for j in range(1, 4):

        @pl.when(z >= j)
        def _():
            after_second(z - j)

        @pl.when(z + j <= 3)
        def _():
            after_second(z + j)

    for zz in range(4):
        for a in range(2):
            for b in range(2):
                chip = col(zz) + a * first + b * second
                to_twin(chip).wait_recv()
                to_twin(chip).wait_send()
                last_twin(chip).wait_recv()
                last_twin(chip).wait_send()
        to_first(zz).wait_send()
        for a in range(2):
            to_second(zz, a).wait_send()

    last_first().wait_send()
    for a in range(2):
        last_second(a).wait_send()

    @pl.when(z < 3)
    def _():
        up(1).wait_send()
        for q in range(4):
            last_up(1, q).wait_send()
        for j in range(1, 3):

            @pl.when(z >= j)
            def _():
                up(j + 1).wait_send()
                for q in range(4):
                    last_up(j + 1, q).wait_send()

    @pl.when(z > 0)
    def _():
        down(1).wait_send()
        for q in range(4):
            last_down(1, q).wait_send()
        for j in range(1, 3):

            @pl.when(z + j <= 3)
            def _():
                down(j + 1).wait_send()
                for q in range(4):
                    last_down(j + 1, q).wait_send()

    @pl.when(core == 0)
    def _():
        far.wait_send()


def gather_slots(placed, tokens, params, slots):
    anywhere, inside = pl.BlockSpec(memory_space=pl.ANY), pl.BlockSpec(memory_space=pltpu.VMEM)
    wide = (tokens.shape[0], PREFIX + tokens.shape[1])
    return pl.pallas_call(
        functools.partial(gather_kernel, slots),
        out_shape=[jax.ShapeDtypeStruct(placed.shape, placed.dtype), jax.ShapeDtypeStruct(wide, BF16)],
        in_specs=[anywhere, anywhere, inside],
        out_specs=[anywhere, inside],
        scratch_shapes=[
            pltpu.VMEM(wide, BF16),
            pltpu.SemaphoreType.DMA((GATHER_LABELS,)),
            pltpu.SemaphoreType.DMA((GATHER_LABELS,)),
            pltpu.SemaphoreType.DMA((2,)),
        ],
        input_output_aliases={0: 0},
        compiler_params=pltpu.CompilerParams(collective_id=0, has_side_effects=True),
        name="gather_slots",
    )(placed, tokens, params)


R_TWIN, R_SECOND, R_FIRST, R_LINE, R_DONE, R_PREFIX, R_FLOW, REDUCE_LABELS = 0, 16, 24, 28, 32, 33, 34, 42
RING = 3
PANELS = 5


def reduce_kernel(
    slots,
    grads,
    w_three,
    grad_three,
    tokens,
    grad_middle,
    params,
    sums,
    out,
    grad_input,
    norm_sums,
    ring,
    r_twin,
    r_second,
    r_first,
    r_line,
    total,
    weights,
    inner,
    acc,
    prefix,
    given,
    folds,
    flow,
    arrived,
    load,
    send,
    recv,
    save,
):
    me, core, z, first, second = place()
    half = slots // 2
    features, length = acc.shape
    line = [(me + 4 * ((z + r) % 4 - z), core) for r in range(1, 4)]
    greet([(me + first, core), (me + second, core), (me, 1 - core)] + line)

    def piece(chip, h):
        return grads.at[pl.ds(chip * slots + h * half, half)]

    def chip_at(zz, a, b):
        return me + 4 * (zz - z) + a * first + b * second

    def remote(src, dst, label, dp, c):
        return pltpu.make_async_remote_copy(
            src_ref=src,
            dst_ref=dst,
            send_sem=send.at[label],
            recv_sem=recv.at[label],
            device_id=(dp, c),
            device_id_type=MESH,
        )

    def twin(zz, a, b):
        chip = chip_at(zz, a, b)
        return remote(piece(chip, 1 - core), r_twin.at[chip], R_TWIN + chip, me, 1 - core)

    def to_second(zz, a):
        return remote(
            r_twin.at[chip_at(zz, a, 1)], r_second.at[2 * zz + a], R_SECOND + 2 * zz + a, me + second, core
        )

    def to_first(zz):
        return remote(r_twin.at[chip_at(zz, 1, 0)], r_first.at[zz], R_FIRST + zz, me + first, core)

    def to_line(r):
        zz = (z + r) % 4
        return remote(r_twin.at[chip_at(zz, 0, 0)], r_line.at[r - 1], R_LINE + r, chip_at(zz, 0, 0), core)

    order = [2, 1, 3, 0]
    where = [(z + r) % 4 for r in order]
    turns = []
    for index in range(3):
        turns += [(where[index], 1, 1), (where[index], 0, 1)]
    turns += [(where[0], 1, 0), (where[3], 1, 1), (where[3], 0, 1), (where[0], 0, 0), (where[1], 1, 0)]
    turns += [(where[2], 1, 0), (where[1], 0, 0), (where[3], 1, 0), (where[2], 0, 0), (where[3], 0, 0)]

    def load_piece(chip, slot):
        return pltpu.make_async_copy(piece(chip, core), ring.at[slot], load.at[slot])

    def load_own(turn):
        return load_piece(chip_at(*turns[turn]), turn % RING)

    def add_up(turn, others):
        chip = chip_at(*turns[turn])
        load_own(turn).wait()
        twin(*turns[turn]).wait_recv()

        def body(s, carry):
            value = ring[turn % RING, s].astype(F32) + r_twin[chip, s].astype(F32)
            for ref, index in others:
                value = value + ref[index, s].astype(F32)
            if turn < len(turns) - 1:
                r_twin[chip, s] = value.astype(BF16)
            else:
                total[s] = value
            return carry

        lax.fori_loop(0, half, body, 0)
        if turn + RING < len(turns):
            load_own(turn + RING).start()

    def send_second(turn):
        zz, a, _ = turns[turn]
        add_up(turn, [])
        to_second(zz, a).start()

    def send_first(turn):
        zz = turns[turn][0]
        to_second(zz, 1).wait_recv()
        add_up(turn, [(r_second, 2 * zz + 1)])
        to_first(zz).start()

    def send_line(turn, r):
        zz = turns[turn][0]
        to_second(zz, 0).wait_recv()
        to_first(zz).wait_recv()
        add_up(turn, [(r_second, 2 * zz), (r_first, zz)])
        to_line(r).start()

    for turn in range(RING):
        load_own(turn).start()
    for zz in where:
        for a in (1, 0):
            twin(zz, 1, a).start()
    for zz in where:
        for a in (1, 0):
            twin(zz, 0, a).start()
    fetches = [
        pltpu.make_async_copy(w_three, weights, save.at[0]),
        pltpu.make_async_copy(grad_three, inner, save.at[1]),
    ]
    for fetch in fetches:
        fetch.start()
    def early(turn, carry):
        def pick(values):
            return sum(jnp.where(turn == index, value, 0) for index, value in enumerate(values))

        zz, a, slot = pick([t[0] for t in turns[:6]]), 1 - turn % 2, turn % RING
        chip, after = chip_at(zz, a, 1), pick([chip_at(*t) for t in turns[RING : RING + 6]])
        load_piece(chip, slot).wait()
        twin(zz, a, 1).wait_recv()

        def body(s, inner_carry):
            r_twin[chip, s] = (ring[slot, s].astype(F32) + r_twin[chip, s].astype(F32)).astype(BF16)
            return inner_carry

        lax.fori_loop(0, half, body, 0)
        load_piece(after, slot).start()
        to_second(zz, a).start()
        return carry

    lax.fori_loop(0, 6, early, 0)
    send_first(6)
    send_second(7)
    send_second(8)
    for fetch in fetches:
        fetch.wait()

    rows = features // PANELS

    def panel(index, carry):
        mine = pl.ds(pl.multiple_of(index * rows, 16), rows)
        acc[mine, :] = sum(nn(weights[k, mine, :], inner[k]) for k in range(3))
        return carry

    lax.fori_loop(0, PANELS, panel, 0)

    swap = remote(acc.at[:, pl.ds(0, PREFIX)], prefix, R_PREFIX, me, 1 - core)
    swap.start()
    own_tokens = weights.at[0, :, pl.ds(0, length - PREFIX)]
    take = pltpu.make_async_copy(tokens, own_tokens, save.at[0])
    take.start()

    def at(index):
        return pl.ds(pl.multiple_of(index * GB, GB), GB)

    def ahead(index):
        return pl.ds(pl.multiple_of(PREFIX + index * GB, PREFIX), GB)

    def give(index, slot):
        return pltpu.make_async_copy(grad_middle.at[:, at(index)], given.at[slot], save.at[2 + slot])

    def store(index):
        return pltpu.make_async_copy(acc.at[:, ahead(index)], grad_input.at[:, at(index)], save.at[4 + index])

    give(0, 0).start()
    send_line(9, order[0])
    send_first(10)
    take.wait()
    swap.wait()
    here = (1 - core).astype(F32)
    acc[:, PREFIX : 2 * PREFIX] += (acc[:, :PREFIX] + prefix[...]) * here
    folds[...] = jnp.zeros_like(folds)
    groups = (length - PREFIX) // GB

    def back(index, carry):
        @pl.when(index + 1 < groups)
        def _():
            give(index + 1, (index + 1) % 2).start()

        give(index, index % 2).wait()
        unit, scale = norm_parts(weights[0, :, at(index)].astype(F32))
        grad = acc[:, ahead(index)]
        folds[0] += fold(grad * unit)
        folds[1] += fold(grad)
        acc[:, ahead(index)] = given[index % 2] + norm_back(unit, scale, params[:, 0:1], grad)
        store(index).start()
        return carry

    lax.fori_loop(0, groups, back, 0)
    flow[0] = sums[...] + row_sums(folds[0], 0) + row_sums(folds[1], 1)
    pairs = [(me, 1 - core), (me + first, core), (me, 1 - core), (me + first, core), (me, 1 - core)] + line
    sources = [flow.at[0], flow.at[1], flow.at[2], arrived.at[2], flow.at[3]] + [flow.at[4]] * 3

    def pass_on(k):
        return remote(sources[k], arrived.at[k], R_FLOW + k, *pairs[k])

    for k in range(2):
        pass_on(k).start()
        pass_on(k).wait_recv()
        flow[k + 1] = flow[k] + arrived[k]
    pass_on(2).start()
    pass_on(2).wait_recv()
    pass_on(3).start()
    send_first(11)
    pass_on(3).wait_recv()
    flow[3] = arrived[2] + arrived[3]
    pass_on(4).start()
    pass_on(4).wait_recv()
    plane = jnp.where(core == 0, flow[3], arrived[4])
    flow[4] = plane
    arrived[4] = plane
    for k in range(5, 8):
        pass_on(k).start()
    send_line(12, order[1])
    send_first(13)
    send_line(14, order[2])
    for k in range(5, 8):
        pass_on(k).wait_recv()
    norm_sums[...] = sum(arrived[4 + (z - zz + 4) % 4] for zz in range(4))
    to_second(z, 0).wait_recv()
    to_first(z).wait_recv()
    for r in range(1, 4):
        to_line(r).wait_recv()
    add_up(15, [(r_second, 2 * z), (r_first, z), (r_line, 0), (r_line, 1), (r_line, 2)])
    target = out.at[pl.ds(core * half, half)]
    done = remote(total, target, R_DONE, me, 1 - core)
    done.start()
    saved = pltpu.make_async_copy(total, target, save.at[0])
    saved.start()
    for zz in range(4):
        for a in range(2):
            for b in range(2):
                twin(zz, a, b).wait_send()
            to_second(zz, a).wait_send()
        to_first(zz).wait_send()
    for r in range(1, 4):
        to_line(r).wait_send()
    for k in range(len(pairs)):
        pass_on(k).wait_send()
    for index in range(groups):
        store(index).wait()
    done.wait()
    saved.wait()


def reduce_slots(grads, slots, w_three, grad_three, tokens, grad_middle, params, sums):
    _, lines, lanes = grads.shape
    half = slots // 2
    _, features, length = grad_three.shape
    pieces = lambda n: pltpu.VMEM((n, half, lines, lanes), BF16)
    anywhere, inside = pl.BlockSpec(memory_space=pl.ANY), pl.BlockSpec(memory_space=pltpu.VMEM)
    groups = (length - PREFIX) // GB
    return pl.pallas_call(
        functools.partial(reduce_kernel, slots),
        out_shape=[
            jax.ShapeDtypeStruct((slots, lines, lanes), F32),
            jax.ShapeDtypeStruct((features, length - PREFIX), F32),
            jax.ShapeDtypeStruct((8, features), F32),
        ],
        in_specs=[anywhere] * 5 + [inside] * 2,
        out_specs=[anywhere, anywhere, inside],
        scratch_shapes=[
            pieces(RING),
            pieces(16),
            pieces(8),
            pieces(4),
            pieces(3),
            pltpu.VMEM((half, lines, lanes), F32),
            pltpu.VMEM(w_three.shape, BF16),
            pltpu.VMEM(grad_three.shape, BF16),
            pltpu.VMEM((features, length), F32),
            pltpu.VMEM((features, PREFIX), F32),
            pltpu.VMEM((2, features, GB), F32),
            pltpu.VMEM((2, features, 128), F32),
            pltpu.VMEM((5, 8, features), F32),
            pltpu.VMEM((8, 8, features), F32),
            pltpu.SemaphoreType.DMA((RING,)),
            pltpu.SemaphoreType.DMA((REDUCE_LABELS,)),
            pltpu.SemaphoreType.DMA((REDUCE_LABELS,)),
            pltpu.SemaphoreType.DMA((4 + groups,)),
        ],
        compiler_params=pltpu.CompilerParams(collective_id=1, has_side_effects=True, vmem_limit_bytes=63 << 20),
        name="reduce_slots",
    )(grads, w_three, grad_three, tokens, grad_middle, params, sums)


def lay(matrix, row, col, block):
    size = block.shape[0] - RUN
    matrix[size * row : size * (row + 1), size * col : size * col + MAIN] = block[:size]
    for start, count, lane in runs(size):
        piece = block[size : size + count, lane : lane + size - MAIN]
        matrix[size * row + start : size * row + start + count, size * col + MAIN : size * (col + 1)] = piece


def block_specs(gathered, rows, cols, block_of, **mode):
    shape = (1,) + gathered.shape[1:]
    pick = lambda i, j, step, v: (v[block_of(step, i, j)], 0, 0)
    return [
        pl.BlockSpec(shape, functools.partial(pick, i, j), **mode) for i in range(rows) for j in range(cols)
    ]


def feature_parts(features):
    part = -(-features // 256) * 128
    return [slice(start, min(start + part, features)) for start in range(0, features, part)]


def fold(values):
    return sum(values[:, start : start + 128] for start in range(0, values.shape[1], 128))


def row_sums(values, row):
    ones = jnp.ones((8, values.shape[1]), F32)
    summed = lax.dot_general(
        ones, values, (((1,), (1,)), ((), ())), precision=lax.Precision.HIGHEST, preferred_element_type=F32
    )
    return jnp.where(lax.broadcasted_iota(jnp.int32, summed.shape, 0) == row, summed, 0.0)


ONCE = pl.Buffered(1)


def front_kernel(slot_of, normed, *refs):
    del slot_of
    blocks, (weights, out) = refs[:-2], refs[-2:]
    row_blocks = math.isqrt(len(blocks))
    for index, block in enumerate(blocks):
        lay(weights.at[0], index // row_blocks, index % row_blocks, block.at[0])
    out[0] = tn(weights[0], normed[...]).astype(BF16)


def front(gathered, slot_of, normed, row_blocks):
    features, length = normed.shape
    square = row_blocks * row_blocks
    blocks = block_specs(gathered, row_blocks, row_blocks, lambda s, i, j: s * square + i * row_blocks + j)
    return pl.pallas_call(
        front_kernel,
        grid_spec=pltpu.PrefetchScalarGridSpec(
            num_scalar_prefetch=1,
            grid=(3,),
            in_specs=[pl.BlockSpec((features, length), lambda s, v: (0, 0), pipeline_mode=ONCE)] + blocks,
            out_specs=[
                pl.BlockSpec((1, features, features), lambda s, v: (s, 0, 0)),
                pl.BlockSpec((1, features, length), lambda s, v: (s, 0, 0)),
            ],
        ),
        out_shape=[
            jax.ShapeDtypeStruct((3, features, features), BF16),
            jax.ShapeDtypeStruct((3, features, length), BF16),
        ],
        compiler_params=pltpu.CompilerParams(vmem_limit_bytes=60 << 20),
        name="front",
    )(slot_of, normed, *([gathered] * square))


def gelu_pair(values):
    square = values * values
    bend = jnp.tanh(values * (0.7978845608028654 + (0.7978845608028654 * 0.044715) * square))
    half = 0.5 * values
    slope = 0.7978845608028654 + (3 * 0.7978845608028654 * 0.044715) * square
    return half + half * bend, 0.5 + 0.5 * bend + half * (1.0 - bend * bend) * slope


def middle_kernel(row_blocks, slot_of, params, tokens, attended, grad_low, *refs):
    del slot_of
    square = row_blocks * row_blocks
    out_blocks, up_blocks, down_blocks = (refs[square * k : square * (k + 1)] for k in range(3))
    outs, scratch = refs[3 * square : 3 * square + 8], refs[3 * square + 8 :]
    block_out, activated, grad_pre, normed, grad_branch, grad_att, grad_middle, sums = outs
    w_out, w_up, w_down, middle, total, stats, folds, sem = scratch
    tiles, parts = grad_low.shape[1] // GB, feature_parts(normed.shape[0])
    at = lambda index: pl.ds(pl.multiple_of(index * GB, GB), GB)
    step, last = pl.program_id(0), pl.num_programs(0) - 1

    @pl.when(step == 0)
    def _():
        copies = [
            pltpu.make_async_copy(tokens, block_out, sem.at[0]),
            pltpu.make_async_copy(attended, grad_att, sem.at[1]),
        ]
        for copy in copies:
            copy.start()
        for index, block in enumerate(out_blocks):
            lay(w_out, index // row_blocks, index % row_blocks, block.at[0])
        for copy in copies:
            copy.wait()
        def enter(index, carry):
            tile = at(index)
            for part in parts:
                values = block_out[part, tile].astype(F32) + tn(w_out[:, part], grad_att[:, tile])
                middle[part, tile] = values
                total[part, tile] = values
                grad_middle[part, tile] = jnp.zeros_like(values)
            values = middle[:, tile]
            average = jnp.mean(values, axis=0, keepdims=True)
            centred = values - average
            scale = lax.rsqrt(jnp.mean(centred * centred, axis=0, keepdims=True) + 1e-05)
            stats[0:1, tile] = average
            stats[1:2, tile] = scale
            normed[:, tile] = (centred * scale * params[:, 2:3] + params[:, 3:4]).astype(BF16)
            return carry

        lax.fori_loop(0, tiles, enter, 0)
        folds[...] = jnp.zeros_like(folds)

    for index in range(square):
        lay(w_up, index // row_blocks, index % row_blocks, up_blocks[index].at[0])
        lay(w_down, index // row_blocks, index % row_blocks, down_blocks[index].at[0])

    def advance(index, carry):
        tile = pl.ds(pl.multiple_of(index * wide, wide), wide)
        for part in parts:
            value, slope = gelu_pair(tn(w_up[:, part], normed[:, tile]))
            activated[part, tile] = value.astype(BF16)
            grad_pre[part, tile] = (nn(w_down[part, :], grad_low[:, tile]) * slope).astype(BF16)
        for part in parts:
            total[part, tile] += tn(w_down[:, part], activated[:, tile])
            grad_middle[part, tile] += nn(w_up[part, :], grad_pre[:, tile])
        return carry

    wide = 2 * GB if tiles % 2 == 0 else GB
    lax.fori_loop(0, grad_low.shape[1] // wide, advance, 0)

    @pl.when(step == last)
    def _():
        def leave(index, carry):
            tile = at(index)
            block_out[:, tile] = total[:, tile].astype(BF16)
            scale = stats[1:2, tile]
            unit = (middle[:, tile] - stats[0:1, tile]) * scale
            grad = grad_middle[:, tile]
            folds[0] += fold(grad * unit)
            folds[1] += fold(grad)
            values = grad_low[:, tile].astype(F32) + norm_back(unit, scale, params[:, 2:3], grad)
            grad_middle[:, tile] = values
            grad_branch[:, tile] = values.astype(BF16)
            for part in parts:
                grad_att[part, tile] = nn(w_out[part, :], grad_branch[:, tile]).astype(BF16)
            return carry

        lax.fori_loop(0, tiles, leave, 0)
        sums[...] = row_sums(folds[0], 2) + row_sums(folds[1], 3)


def middle_part(gathered, slot_of, params, tokens, attended, grad_low, row_blocks, col_blocks):
    features, length = tokens.shape
    square = row_blocks * row_blocks
    hidden = features * col_blocks // row_blocks
    up_start, down_start = 4 * square, 4 * square + row_blocks * col_blocks
    whole = lambda *shape: pl.BlockSpec(shape, lambda s, v: (0,) * len(shape), pipeline_mode=ONCE)
    anywhere = pl.BlockSpec(memory_space=pl.ANY)
    part = pl.BlockSpec((features, length), lambda s, v: (s, 0))
    blocks = (
        block_specs(
            gathered, row_blocks, row_blocks, lambda s, i, j: 3 * square + i * row_blocks + j, pipeline_mode=ONCE
        )
        + block_specs(
            gathered, row_blocks, row_blocks, lambda s, i, j: up_start + i * col_blocks + s * row_blocks + j
        )
        + block_specs(
            gathered, row_blocks, row_blocks, lambda s, i, j: down_start + (s * row_blocks + i) * row_blocks + j
        )
    )
    shape = jax.ShapeDtypeStruct
    square_scratch = pltpu.VMEM((features, features), BF16)
    return pl.pallas_call(
        functools.partial(middle_kernel, row_blocks),
        grid_spec=pltpu.PrefetchScalarGridSpec(
            num_scalar_prefetch=1,
            grid=(col_blocks // row_blocks,),
            in_specs=[whole(*params.shape)] + [anywhere] * 2 + [whole(features, length)] + blocks,
            out_specs=[whole(features, length), part, part]
            + [whole(features, length)] * 4
            + [whole(8, features)],
            scratch_shapes=[square_scratch] * 3
            + [pltpu.VMEM((features, length), F32)] * 2
            + [
                pltpu.VMEM((8, length), F32),
                pltpu.VMEM((2, features, 128), F32),
                pltpu.SemaphoreType.DMA((2,)),
            ],
        ),
        out_shape=[
            shape((features, length), BF16),
            shape((hidden, length), BF16),
            shape((hidden, length), BF16),
            shape((features, length), BF16),
            shape((features, length), BF16),
            shape((features, length), BF16),
            shape((features, length), F32),
            shape((8, features), F32),
        ],
        compiler_params=pltpu.CompilerParams(vmem_limit_bytes=63 << 20),
        name="middle_part",
    )(slot_of, params, tokens, attended, grad_low, *([gathered] * (3 * square)))


def weight_grad_kernel(block_of, deep, size, slot_of, left, right, *refs):
    grads, stage, sem = refs[-3:]
    wide = right.shape[0] // size
    rows, cols = pl.program_id(0), pl.program_id(1)
    step = rows * pl.num_programs(1) + cols
    steps = pl.num_programs(0) * pl.num_programs(1)
    now = step % 2

    def copy(buffer, index, slot):
        return pltpu.make_async_copy(stage.at[buffer, index], grads.at[slot], sem.at[buffer, index])

    @pl.when(step >= 2)
    def _():
        for index in range(deep * wide):
            copy(now, index, 0).wait()

    other = right[...]
    for i in range(deep):
        panel = nt(left[size * i : size * (i + 1), :], other)
        for j in range(wide):
            index = i * wide + j
            block = panel[:, size * j : size * (j + 1)]
            stage[now, index, :size] = block[:, :MAIN].astype(BF16)
            stage[now, index, size:] = pack_tail(block).astype(BF16)
            copy(now, index, slot_of[block_of(rows * deep + i, cols * wide + j)]).start()

    @pl.when(step == steps - 1)
    def _():
        for index in range(deep * wide):
            copy(now, index, 0).wait()

        @pl.when(steps > 1)
        def _():
            for index in range(deep * wide):
                copy(1 - now, index, 0).wait()


def weight_grad(left, right, slot_of, grads, slot_count, size, block_of, name):
    depth = left.shape[1]
    deep = wide = 4
    grid = (left.shape[0] // (size * deep), right.shape[0] // (size * wide))
    anywhere = pl.BlockSpec(memory_space=pl.ANY)
    operands = [slot_of, left, right] + ([] if grads is None else [grads])
    return pl.pallas_call(
        functools.partial(weight_grad_kernel, block_of, deep, size),
        grid_spec=pltpu.PrefetchScalarGridSpec(
            num_scalar_prefetch=1,
            grid=grid,
            in_specs=[
                pl.BlockSpec((size * deep, depth), lambda i, j, v: (i, 0)),
                pl.BlockSpec((size * wide, depth), lambda i, j, v: (j, 0)),
            ]
            + [anywhere] * (len(operands) - 3),
            out_specs=anywhere,
            scratch_shapes=[
                pltpu.VMEM((2, deep * wide, size + RUN, MAIN), BF16),
                pltpu.SemaphoreType.DMA((2, deep * wide)),
            ],
        ),
        out_shape=jax.ShapeDtypeStruct((slot_count, size + RUN, MAIN), BF16),
        input_output_aliases={} if grads is None else {3: 0},
        cost_estimate=cost(
            2 * left.shape[0] * right.shape[0] * depth,
            2 * (left.size + right.size + left.shape[0] * right.shape[0]),
        ),
        name=name,
    )(*operands)


def weight_grads_kernel(starts, col_blocks, size, slot_of, *refs):
    activated, grad_low, normed, grad_pre, attended, grad_branch, grads, left, right, stage, get, put = refs
    out_start, up_start, down_start = starts
    side_length = left.shape[1]
    row_blocks = side_length // size
    count = row_blocks * row_blocks
    parts = activated.shape[0] // side_length
    step, steps = pl.program_id(0), pl.num_programs(0)
    now = step % 2

    def rows(index):
        return pl.ds(pl.multiple_of(index * side_length, 16), side_length)

    def fetch(index, buffer):
        def start(one, other):
            pltpu.make_async_copy(one, left.at[buffer], get.at[0, buffer]).start()
            pltpu.make_async_copy(other, right.at[buffer], get.at[1, buffer]).start()

        @pl.when(index < parts)
        def _():
            start(activated.at[rows(index)], grad_low)

        @pl.when((index >= parts) & (index < 2 * parts))
        def _():
            start(normed, grad_pre.at[rows(index - parts)])

        @pl.when(index == 2 * parts)
        def _():
            start(attended, grad_branch)

    def copy(buffer, index, slot):
        return pltpu.make_async_copy(stage.at[buffer, index], grads.at[slot], put.at[buffer, index])

    @pl.when(step == 0)
    def _():
        fetch(0, 0)

    @pl.when(step + 1 < steps)
    def _():
        fetch(step + 1, 1 - now)

    pltpu.make_async_copy(normed, left.at[now], get.at[0, now]).wait()
    pltpu.make_async_copy(normed, right.at[now], get.at[1, now]).wait()

    @pl.when(step >= 2)
    def _():
        for index in range(count):
            copy(now, index, 0).wait()

    up = (step >= parts) & (step < 2 * parts)
    start = jnp.where(up, up_start + (step - parts) * row_blocks, out_start)
    start = jnp.where(step < parts, down_start + step * count, start)
    stride = jnp.where(up, col_blocks, row_blocks)
    other = right[now]
    for i in range(row_blocks):
        panel = nt(left[now, size * i : size * (i + 1), :], other)
        for j in range(row_blocks):
            index = i * row_blocks + j
            block = panel[:, size * j : size * (j + 1)]
            stage[now, index, :size] = block[:, :MAIN].astype(BF16)
            stage[now, index, size:] = pack_tail(block).astype(BF16)
            copy(now, index, slot_of[start + i * stride + j]).start()

    @pl.when(step == steps - 1)
    def _():
        for index in range(count):
            copy(now, index, 0).wait()
            copy(1 - now, index, 0).wait()


def weight_grads(slot_of, operands, slot_count, size, starts, col_blocks):
    hidden, length = operands[0].shape
    features = operands[1].shape[0]
    count = (features // size) ** 2
    steps = 2 * (hidden // features) + 1
    anywhere = pl.BlockSpec(memory_space=pl.ANY)
    part = pltpu.VMEM((2, features, length), BF16)
    return pl.pallas_call(
        functools.partial(weight_grads_kernel, starts, col_blocks, size),
        grid_spec=pltpu.PrefetchScalarGridSpec(
            num_scalar_prefetch=1,
            grid=(steps,),
            in_specs=[anywhere] * 6,
            out_specs=anywhere,
            scratch_shapes=[
                part,
                part,
                pltpu.VMEM((2, count, size + RUN, MAIN), BF16),
                pltpu.SemaphoreType.DMA((2, 2)),
                pltpu.SemaphoreType.DMA((2, count)),
            ],
        ),
        out_shape=jax.ShapeDtypeStruct((slot_count, size + RUN, MAIN), BF16),
        cost_estimate=cost(2 * steps * features * features * length, 8 * steps * features * length),
        name="weight_grads",
    )(slot_of, *operands)


EXTRA = 8
TOGETHER = 2
FAR = -1e30


def causal():
    return lax.broadcasted_iota(jnp.int32, (HALF, HALF), 0) <= lax.broadcasted_iota(jnp.int32, (HALF, HALF), 1)


def places(groups):
    found = []
    for group in range(groups):
        base = PREFIX + GB * group
        low, high = slice(base, base + HALF), slice(base + HALF, base + GB)
        found.append((low, high, slice(base, base + GB), slice(GB * group, GB * (group + 1))))
    return found


def side(left, right):
    return jnp.concatenate([left, right], axis=1)


def attention_kernel(scale, head, qkv, extras, out, lse, queries, keys, values, keys_t):
    unit = scale * math.log2(math.e)
    heads = range(queries.shape[0])

    @pl.when(pl.program_id(0) == 0)
    def _():
        for k in heads:
            queries[k, head:] = extras[0]
            keys[k, head:] = extras[1]
            values[k, head:] = extras[2]

    for k in heads:
        rows = slice(head * k, head * (k + 1))
        queries[k, :head] = qkv[0, rows]
        keys[k, :head] = qkv[1, rows]
        values[k, :head] = qkv[2, rows]
    for k in heads:
        keys_t[k] = keys[k].T
    ahead = causal()
    spots = [(k,) + spot for k in heads for spot in places(out.shape[1] // GB)]
    scores = []
    for k, low, high, both, _ in spots:
        asked = queries[k, :, both]
        scores.append((nn(keys_t[k, :PREFIX], asked), nn(keys_t[k, low], asked), nn(keys_t[k, high], asked[:, HALF:])))

    def peak(array):
        return jnp.max(array, axis=0, keepdims=True)

    def soft(array, top):
        return jnp.exp2((array - top) * unit).astype(BF16)

    tops, weights = [], []
    for prefix, first, second in scores:
        first = side(jnp.where(ahead, first[:, :HALF], FAR), first[:, HALF:])
        second = jnp.where(ahead, second, FAR)
        top = jnp.maximum(peak(prefix), peak(first))
        top = side(top[:, :HALF], jnp.maximum(top[:, HALF:], peak(second)))
        tops.append(top)
        weights.append((soft(prefix, top), soft(first, top), soft(second, top[:, HALF:])))
    for (k, low, high, _, mine), top, (prefix, first, second) in zip(spots, tops, weights):
        sums = nn(values[k, :, :PREFIX], prefix) + nn(values[k, :, low], first)
        sums = side(sums[:, :HALF], sums[:, HALF:] + nn(values[k, :, high], second))
        total = sums[head : head + 1]
        out[head * k : head * (k + 1), mine] = (sums[:head] / total).astype(BF16)
        lse[k, :, mine] = top + jnp.log(total) * (1.0 / scale)


def thirds(values):
    high = values.astype(BF16).astype(F32)
    rest = values - high
    middle = rest.astype(BF16).astype(F32)
    return high, middle, rest - middle


def with_rows(base, start, rows):
    index = lax.broadcasted_iota(jnp.int32, base.shape, 0)
    for offset, row in enumerate(rows):
        base = jnp.where(index == start + offset, row, base)
    return base.astype(BF16)


def attention_back_kernel(
    scale, head, qkv, extras, out, lse, grad_out, grads, queries, keys, values, grad_o, keys_t, values_t
):
    own = out.shape[1]
    unit = scale * math.log2(math.e)
    heads = range(queries.shape[0])

    @pl.when(pl.program_id(0) == 0)
    def _():
        for k in heads:
            keys[k, head:] = extras[1]
            values[k, head:] = extras[2]

    for k in heads:
        rows = slice(head * k, head * (k + 1))
        queries[k, :head] = qkv[0, rows, PREFIX:]
        keys[k, :head] = qkv[1, rows]
        values[k, :head] = qkv[2, rows]
        given = grad_out[rows]
        grad_o[k, :head] = given
        queries[k, head:] = with_rows(extras[0, :, PREFIX:].astype(F32), 2, thirds(-lse[k]))
        delta = jnp.sum(given.astype(F32) * out[rows].astype(F32), axis=0, keepdims=True)
        grad_o[k, head:] = with_rows(jnp.zeros((EXTRA, own), F32), 0, thirds(-delta))
    for k in heads:
        keys_t[k] = keys[k].T
        values_t[k] = values[k].T
    ahead = causal()
    spots = [(k,) + spot for k in heads for spot in places(own // GB)]

    def weigh(k, rows, asked, given, mask):
        weights = jnp.exp2(nn(keys_t[k, rows], asked) * unit)
        if mask == 1:
            weights = side(jnp.where(ahead, weights[:, :HALF], 0.0), weights[:, HALF:])
        if mask == 2:
            weights = jnp.where(ahead, weights, 0.0)
        return weights.astype(BF16), (weights * nn(values_t[k, rows], given)).astype(BF16)

    found = []
    for k, low, high, _, mine in spots:
        asked, given = queries[k, :, mine], grad_o[k, :, mine]
        found.append(
            (
                weigh(k, slice(0, PREFIX), asked, given, 0),
                weigh(k, low, asked, given, 1),
                weigh(k, high, asked[:, HALF:], given[:, HALF:], 2),
            )
        )
    prefix_k, prefix_v = {}, {}
    for (k, low, high, both, mine), ((p0, d0), (p1, d1), (p2, d2)) in zip(spots, found):
        rows = slice(head * k, head * (k + 1))
        asked, given = queries[k, :head, mine], grad_o[k, :head, mine]
        grad_q = nn(keys[k, :head, :PREFIX], d0) + nn(keys[k, :head, low], d1)
        grad_q = side(grad_q[:, :HALF], grad_q[:, HALF:] + nn(keys[k, :head, high], d2))
        grads[0, rows, both] = (grad_q * scale).astype(BF16)
        part_k, part_v = nt(asked, d0), nt(given, p0)
        prefix_k[k] = prefix_k[k] + part_k if k in prefix_k else part_k
        prefix_v[k] = prefix_v[k] + part_v if k in prefix_v else part_v
        grads[1, rows, low] = (nt(asked, d1) * scale).astype(BF16)
        grads[2, rows, low] = nt(given, p1).astype(BF16)
        grads[1, rows, high] = (nt(asked[:, HALF:], d2) * scale).astype(BF16)
        grads[2, rows, high] = nt(given[:, HALF:], p2).astype(BF16)
    for k in heads:
        rows = slice(head * k, head * (k + 1))
        grads[0, rows, :PREFIX] = jnp.zeros((head, PREFIX), BF16)
        grads[1, rows, :PREFIX] = (prefix_k[k] * scale).astype(BF16)
        grads[2, rows, :PREFIX] = prefix_v[k].astype(BF16)


def attention_specs(qkv):
    _, features, length = qkv.shape
    head, own = features // HEADS, length - PREFIX
    three = pl.BlockSpec((3, TOGETHER * head, length), lambda h: (0, h, 0))
    extra = pl.BlockSpec((3, EXTRA, length), lambda h: (0, 0, 0))
    one = pl.BlockSpec((TOGETHER * head, own), lambda h: (h, 0))
    row = pl.BlockSpec((TOGETHER, 1, own), lambda h: (h, 0, 0))
    wide = lambda columns: pltpu.VMEM((TOGETHER, head + EXTRA, columns), BF16)
    tall = pltpu.VMEM((TOGETHER, length, head + EXTRA), BF16)
    return features, length, own, head, three, extra, one, row, wide, tall


def attention(qkv, extras):
    features, length, own, head, three, extra, one, row, wide, tall = attention_specs(qkv)
    return pl.pallas_call(
        functools.partial(attention_kernel, head ** (-0.5), head),
        grid=(HEADS // TOGETHER,),
        in_specs=[three, extra],
        out_specs=[one, row],
        out_shape=[
            jax.ShapeDtypeStruct((features, own), BF16),
            jax.ShapeDtypeStruct((HEADS, 1, own), F32),
        ],
        scratch_shapes=[wide(length), wide(length), wide(length), tall],
        cost_estimate=cost(8 * features * own * GB, 2 * qkv.size, HEADS * own * GB),
        name="attention",
    )(qkv, extras)


def attention_back(qkv, extras, out, lse, grad_out):
    features, length, own, head, three, extra, one, row, wide, tall = attention_specs(qkv)
    return pl.pallas_call(
        functools.partial(attention_back_kernel, head ** (-0.5), head),
        grid=(HEADS // TOGETHER,),
        in_specs=[three, extra, one, row, one],
        out_specs=three,
        out_shape=jax.ShapeDtypeStruct(qkv.shape, BF16),
        scratch_shapes=[wide(own), wide(length), wide(length), wide(own), tall, tall],
        cost_estimate=cost(20 * features * own * GB, 4 * qkv.size, HEADS * own * GB),
        name="attention_back",
    )(qkv, extras, out, lse, grad_out)


def score_extras(alive, prefix_alive, later):
    length = PREFIX + alive.shape[0]
    dead = jnp.where(jnp.concatenate([prefix_alive, alive]), 0.0, FAR)
    prefix = (jnp.arange(length) < PREFIX).astype(F32)
    barred = jnp.concatenate([jnp.zeros((PREFIX,)), jnp.where(jnp.repeat(later, GB), 0.0, FAR)])
    one, zero = jnp.ones((length,)), jnp.zeros((length,))
    query_rows = jnp.stack([one, barred] + [zero] * 6)
    key_rows = jnp.stack([dead, prefix] + [one] * 3 + [zero] * 3)
    value_rows = jnp.stack([one] * 3 + [zero] * 5)
    return jnp.stack([query_rows, key_rows, value_rows]).astype(BF16)


def split(values):
    high = values.astype(BF16)
    return high, (values - high.astype(F32)).astype(BF16)


def product(form, left, right):
    (left_high, left_low), (right_high, right_low) = left, right
    return form(left_high, right_high) + (form(left_high, right_low) + form(left_low, right_high))


def optimizer_kernel(scale, packed, master, average, left, right, root_left, root_right, passed, sums, norms, *outs):
    slot_grad, new_left, new_right, new_master, new_copy, new_average, passed_on, norm_grad, new_norms = outs
    size = master.shape[1]
    passed_on[...] = passed[...]

    @pl.when(pl.program_id(0) == 0)
    def _():
        count = norms.shape[0]
        scaled = sums[:count] * scale
        norm_grad[...] = scaled
        square = jnp.sum(jnp.sum(scaled * scaled, axis=1, keepdims=True), axis=0, keepdims=True)
        new_norms[...] = norms[...] - 0.1 * scaled * lax.rsqrt(square * (1.0 / norms.size) + 1e-06)

    grad = unpack(packed[0]) * scale
    slot_grad[0] = grad
    grad_parts = split(grad)
    new_left[0] = 0.5 * left[0] + (0.5 / size) * nt(grad_parts[0], grad_parts[0])
    new_right[0] = 0.5 * right[0] + (0.5 / size) * tn(grad_parts[0], grad_parts[0])
    right_part = product(nn, grad_parts, split(root_right[0]))
    step = product(nn, split(root_left[0]), split(right_part))
    moved = master[0] - 0.03 * step
    new_master[0] = moved
    new_copy[0] = moved.astype(BF16)
    new_average[0] = 0.8 * average[0] + 0.2 * moved


def optimizer(packed, scale, arrays, passed, sums, norms):
    slots, size, _ = arrays[0].shape
    block = pl.BlockSpec((1, size, size), lambda i: (i, 0, 0))
    whole = lambda array: pl.BlockSpec(array.shape, lambda i: (0, 0))
    shape = lambda dtype: jax.ShapeDtypeStruct((slots, size, size), dtype)
    width = 128 * -(-passed.shape[1] // (128 * slots))
    last = passed.shape[1] // width - 1
    strip = pl.BlockSpec((passed.shape[0], width), lambda i: (0, jnp.minimum(i, last)))
    same = lambda array: jax.ShapeDtypeStruct(array.shape, F32)
    return pl.pallas_call(
        functools.partial(optimizer_kernel, scale),
        grid=(slots,),
        in_specs=[pl.BlockSpec((1,) + packed.shape[1:], lambda i: (i, 0, 0))]
        + [block] * 6
        + [strip, whole(sums), whole(norms)],
        out_specs=[block] * 6 + [strip, whole(norms), whole(norms)],
        out_shape=[shape(F32)] * 4 + [shape(BF16), shape(F32), same(passed), same(norms), same(norms)],
        name="optimizer",
    )(packed, *arrays, passed, sums, norms)


def norm_parts(values):
    average = jnp.mean(values, axis=0, keepdims=True)
    centred = values - average
    variance = jnp.mean(centred * centred, axis=0, keepdims=True)
    scale = lax.rsqrt(variance + 1e-05)
    return centred * scale, scale


def norm_back(unit, scale, gain, grad):
    inner = grad * gain
    mean_one = jnp.mean(inner, axis=0, keepdims=True)
    mean_two = jnp.mean(inner * unit, axis=0, keepdims=True)
    return scale * (inner - mean_one - unit * mean_two)


def local(
    chips,
    cores,
    tokens,
    cotangent,
    pad_mask,
    prefix_len,
    norm_gains,
    norm_shifts,
    owner_map,
    weight_copy,
    master,
    average_weights,
    stat_left,
    stat_right,
    root_left,
    root_right,
):
    cell_count, length, features = tokens.shape
    assert cell_count == 1
    slots, size, _ = weight_copy.shape
    slot_count = owner_map.shape[0]
    row_blocks = features // size
    square = row_blocks * row_blocks
    col_blocks = (slot_count - 4 * square) // (2 * row_blocks)
    known = chips == 16 and cores == 2
    chip = lax.axis_index("dp").astype(jnp.int32)
    seq_index = lax.axis_index("seq")

    slot_of = jnp.zeros((slot_count,), jnp.int32).at[owner_map].set(jnp.arange(slot_count, dtype=jnp.int32))
    own_tokens = tokens.reshape(length, features).T
    norms = jnp.stack([norm_gains[0], norm_shifts[0], norm_gains[1], norm_shifts[1]])
    params = norms.T
    if known:
        half = slots // 2
        begin = seq_index.astype(jnp.int32) * half
        placed = pack_slots(weight_copy, jnp.stack([begin, chip * slots + begin]), half, slot_count)
        gathered, normed_in = gather_slots(placed, own_tokens, params, slots)
    else:
        packed = pack_slots(weight_copy, jnp.zeros((2,), jnp.int32), slots, slots)
        gathered = lax.all_gather(packed, "dp", axis=0, tiled=True)
        prefix_tokens = lax.all_gather(own_tokens[:, :PREFIX], "seq")[0]
        unit_all, _ = norm_parts(jnp.concatenate([prefix_tokens, own_tokens], axis=1).astype(F32))
        normed_in = (unit_all * params[:, 0:1] + params[:, 1:2]).astype(BF16)
    starts = (3 * square, 4 * square, 4 * square + row_blocks * col_blocks)

    def three_of(i, j):
        return (j // row_blocks) * square + i * row_blocks + j % row_blocks

    w_three, qkv = front(gathered, slot_of, normed_in, row_blocks)

    position = seq_index * length + jnp.arange(length, dtype=jnp.int32)
    alive = jnp.where(position < PREFIX, position < prefix_len[0], pad_mask[0] == 1)
    prefix_alive = jnp.arange(PREFIX, dtype=jnp.int32) < prefix_len[0]
    groups = length // GB
    later = seq_index * groups + jnp.arange(groups) > 0
    extras = score_extras(alive, prefix_alive, later)

    grad_low = cotangent.reshape(length, features).T
    attended, log_total = attention(qkv, extras)
    block_out, activated, grad_pre, normed_mid, grad_branch, grad_att, grad_middle, sums = middle_part(
        gathered, slot_of, params, own_tokens, attended, grad_low, row_blocks, col_blocks
    )
    operands = (activated, grad_low, normed_mid, grad_pre, attended, grad_branch)
    grads = weight_grads(slot_of, operands, slot_count, size, starts, col_blocks)
    grad_three = attention_back(qkv, extras, attended, log_total, grad_att)
    flat_three = grad_three.reshape(3 * features, PREFIX + length)
    grads = weight_grad(normed_in, flat_three, slot_of, grads, slot_count, size, three_of, "grad_three")
    grad_scale = 1.0 / math.sqrt(length * chips * cores)
    if known:
        summed, grad_input, norm_sums = reduce_slots(
            grads, slots, w_three, grad_three, own_tokens, grad_middle, params, sums
        )
    else:
        part = lax.psum_scatter(grads.astype(F32), "dp", scatter_dimension=0, tiled=True)
        summed = lax.psum(part, "seq")
        grad_all = sum(nn(w_three[k], grad_three[k]) for k in range(3))
        prefix_part = jnp.where(seq_index == 0, lax.psum(grad_all[:, :PREFIX], "seq"), 0.0)
        grad_normed = grad_all[:, PREFIX:] + jnp.pad(prefix_part, ((0, 0), (0, length - PREFIX)))
        unit_one, scale_one = norm_parts(own_tokens.astype(F32))
        grad_input = grad_middle + norm_back(unit_one, scale_one, params[:, 0:1], grad_normed)
        first_sums = [jnp.sum(grad_normed * unit_one, axis=1), jnp.sum(grad_normed, axis=1)]
        norm_sums = lax.psum(jnp.stack(first_sums + [sums[2], sums[3]]), ("dp", "seq"))
    arrays = (master, average_weights, stat_left, stat_right, root_left, root_right)
    *stepped, grad_input, norm_grad, new_norms = optimizer(summed, grad_scale, arrays, grad_input, norm_sums, norms)
    token_shape = (cell_count, length, features)
    return (
        block_out.T.reshape(token_shape),
        grad_input.T.reshape(token_shape),
        norm_grad,
        new_norms,
        *stepped,
    )


def solution(mesh):
    tokens, slots = P("dp", "seq", None), P("dp", None, None)
    in_specs = (tokens, tokens, P("dp", "seq"), P("dp"), P(), P(), P()) + (slots,) * 7
    out_specs = (tokens, tokens, P(), P()) + (slots,) * 6
    body = functools.partial(local, mesh.shape["dp"], mesh.shape["seq"])
    return jax.shard_map(body, mesh=mesh, in_specs=in_specs, out_specs=out_specs, check_vma=False)
```

```python
import functools
import math

import jax
import jax.numpy as jnp
from jax import lax
from jax.experimental import pallas as pl
from jax.experimental.pallas import tpu as pltpu
from jax.sharding import PartitionSpec as P

HEADS = 20
GB = 256
PREFIX = 128
HALF = GB // 2
MESH = pl.DeviceIdType.MESH
BF16 = jnp.bfloat16
F32 = jnp.float32

MAIN = 256
RUN = 32


def runs(size):
    rest, per_tile = size - MAIN, 128 // (size - MAIN)
    places = []
    for index in range(-(-size // RUN)):
        lane = 128 * (index // per_tile) + rest * (index % per_tile)
        places.append((RUN * index, min(RUN, size - RUN * index), lane))
    assert places[-1][2] + rest <= MAIN
    return places


def pack_tail(block):
    size = block.shape[0]
    rest = size - MAIN
    pieces, lane = [], 0
    for row, count, start in runs(size):
        if start > lane:
            pieces.append(jnp.zeros((RUN, start - lane), block.dtype))
        piece = block[row : row + count, MAIN:]
        if count < RUN:
            piece = jnp.concatenate([piece, jnp.zeros((RUN - count, rest), block.dtype)], axis=0)
        pieces.append(piece)
        lane = start + rest
    if lane < MAIN:
        pieces.append(jnp.zeros((RUN, MAIN - lane), block.dtype))
    return jnp.concatenate(pieces, axis=1)


def unpack(packed):
    size = packed.shape[0] - RUN
    rest = size - MAIN
    low = packed[size:]
    tail = [low[:count, lane : lane + rest] for _, count, lane in runs(size)]
    return jnp.concatenate([packed[:size], jnp.concatenate(tail, axis=0)], axis=1)


def tn(left, right):
    return lax.dot_general(left, right, (((0,), (0,)), ((), ())), preferred_element_type=F32)


def nn(left, right):
    return lax.dot_general(left, right, (((1,), (0,)), ((), ())), preferred_element_type=F32)


def nt(left, right):
    return lax.dot_general(left, right, (((1,), (1,)), ((), ())), preferred_element_type=F32)


def cost(flops, moved, exps=0):
    return pl.CostEstimate(flops=int(flops), bytes_accessed=int(moved), transcendentals=int(exps))


def pack_kernel(start, block, packed):
    del start
    size = block.shape[1]
    rest = size - MAIN
    packed[0, :size] = block[0, :, :MAIN]
    packed[0, size:] = jnp.zeros((RUN, MAIN), BF16)
    for row, count, lane in runs(size):
        packed[0, size : size + count, lane : lane + rest] = block[0, row : row + count, MAIN:]


def pack_slots(blocks, start, count, slot_count):
    size = blocks.shape[1]
    return pl.pallas_call(
        pack_kernel,
        grid_spec=pltpu.PrefetchScalarGridSpec(
            num_scalar_prefetch=1,
            grid=(count,),
            in_specs=[pl.BlockSpec((1, size, size), lambda i, start: (start[0] + i, 0, 0))],
            out_specs=pl.BlockSpec((1, size + RUN, MAIN), lambda i, start: (start[1] + i, 0, 0)),
        ),
        out_shape=jax.ShapeDtypeStruct((slot_count, size + RUN, MAIN), BF16),
        name="pack_slots",
    )(start, blocks)


def place():
    me, core = lax.axis_index("dp"), lax.axis_index("seq")
    x, y, z = me % 2, (me // 2) % 2, me // 4
    step_x, step_y = 1 - 2 * x, 2 * (1 - 2 * y)
    first = step_y * (1 - core) + step_x * core
    second = step_x * (1 - core) + step_y * core
    return me, core, z, first, second


def greet(partners):
    barrier = pltpu.get_barrier_semaphore()
    for chip, core in partners:
        pl.semaphore_signal(barrier, inc=1, device_id=(chip, core), device_id_type=MESH)
    pl.semaphore_wait(barrier, len(partners))


UP, DOWN, FIRST, SECOND, TWIN, HEAD = 0, 4, 8, 12, 20, 36
LAST_FIRST, LAST_SECOND, LAST_UP, LAST_DOWN, LAST_TWIN, GATHER_LABELS = 37, 38, 40, 52, 64, 80


def gather_kernel(slots, placed, tokens, params, out, normed, held, send, recv, take):
    del placed
    me, core, z, first, second = place()
    half = slots // 2
    line = [(me + 4 * ((z + r) % 4 - z), core) for r in range(1, 4)]
    greet([(me + first, core), (me + second, core), (me, 1 - core)] + line)

    def copy(label, chip, dp, c, many=True):
        start = chip * slots + core * half
        ref = out.at[pl.ds(start, half - 1)] if many else out.at[pl.ds(start + half - 1, 1)]
        return pltpu.make_async_remote_copy(
            src_ref=ref,
            dst_ref=ref,
            send_sem=send.at[label],
            recv_sem=recv.at[label],
            device_id=(dp, c),
            device_id_type=MESH,
        )

    def col(zz):
        return me + 4 * (zz - z)

    def up(j):
        return copy(UP + j, me - 4 * (j - 1), me + 4, core)

    def down(j):
        return copy(DOWN + j, me + 4 * (j - 1), me - 4, core)

    def to_first(zz):
        return copy(FIRST + zz, col(zz), me + first, core)

    def to_second(zz, a):
        return copy(SECOND + 2 * zz + a, col(zz) + a * first, me + second, core)

    def to_twin(chip):
        return copy(TWIN + chip, chip, me, 1 - core)

    def spread(zz):
        to_first(zz).start()
        to_second(zz, 0).start()
        to_twin(col(zz)).start()

    def after_first(zz):
        to_first(zz).wait_recv()
        to_second(zz, 1).start()
        to_twin(col(zz) + first).start()

    def after_second(zz):
        for a in range(2):
            to_second(zz, a).wait_recv()
            to_twin(col(zz) + second + a * first).start()

    def off(q):
        return (q % 2) * first + (q // 2) * second

    def last_first():
        return copy(LAST_FIRST, me, me + first, core, False)

    def last_second(a):
        return copy(LAST_SECOND + a, me + a * first, me + second, core, False)

    def last_up(j, q):
        return copy(LAST_UP + 4 * (j - 1) + q, me - 4 * (j - 1) + off(q), me + 4, core, False)

    def last_down(j, q):
        return copy(LAST_DOWN + 4 * (j - 1) + q, me + 4 * (j - 1) + off(q), me - 4, core, False)

    def last_twin(chip):
        return copy(LAST_TWIN + chip, chip, me, 1 - core, False)

    def leave_plane(q):
        last_twin(me + off(q)).start()

        @pl.when(z < 3)
        def _():
            last_up(1, q).start()

        @pl.when(z > 0)
        def _():
            last_down(1, q).start()

    last_first().start()
    last_second(0).start()

    @pl.when(z < 3)
    def _():
        up(1).start()

    @pl.when(z > 0)
    def _():
        down(1).start()

    leave_plane(0)
    spread(z)

    prefix, seat = tokens.at[:, pl.ds(0, PREFIX)], held.at[:, pl.ds(0, PREFIX)]
    mine = pltpu.make_async_copy(tokens, held.at[:, pl.ds(PREFIX, tokens.shape[1])], take.at[0])
    near = pltpu.make_async_copy(prefix, seat, take.at[1])
    far = pltpu.make_async_remote_copy(
        src_ref=prefix,
        dst_ref=seat,
        send_sem=send.at[HEAD],
        recv_sem=recv.at[HEAD],
        device_id=(me, 1 - core),
        device_id_type=MESH,
    )
    mine.start()

    @pl.when(core == 0)
    def _():
        far.start()
        near.start()
        near.wait()

    @pl.when(core == 1)
    def _():
        far.wait_recv()

    mine.wait()

    def normalize(index, carry):
        tile = pl.ds(pl.multiple_of(index * PREFIX, PREFIX), PREFIX)
        unit, _ = norm_parts(held[:, tile].astype(F32))
        normed[:, tile] = (unit * params[:, 0:1] + params[:, 1:2]).astype(BF16)
        return carry

    lax.fori_loop(0, held.shape[1] // PREFIX, normalize, 0)
    def pass_last(j):
        for q in range(4):

            @pl.when(z >= j)
            def _():
                last_up(j, q).wait_recv()
                last_twin(me - 4 * j + off(q)).start()
                if j < 3:

                    @pl.when(z < 3)
                    def _():
                        last_up(j + 1, q).start()

            @pl.when(z + j <= 3)
            def _():
                last_down(j, q).wait_recv()
                last_twin(me + 4 * j + off(q)).start()
                if j < 3:

                    @pl.when(z > 0)
                    def _():
                        last_down(j + 1, q).start()

    last_first().wait_recv()
    last_second(1).start()
    leave_plane(1)
    last_second(0).wait_recv()
    leave_plane(2)
    for j in range(1, 4):

        @pl.when(z >= j)
        def _():
            up(j).wait_recv()
            if j < 3:

                @pl.when(z < 3)
                def _():
                    up(j + 1).start()

            spread(z - j)

        @pl.when(z + j <= 3)
        def _():
            down(j).wait_recv()
            if j < 3:

                @pl.when(z > 0)
                def _():
                    down(j + 1).start()

            spread(z + j)

        if j == 1:
            after_first(z)
        else:

            @pl.when(z >= j - 1)
            def _():
                after_first(z - (j - 1))

            @pl.when(z + j - 1 <= 3)
            def _():
                after_first(z + j - 1)

        if j == 1:
            last_second(1).wait_recv()
            leave_plane(3)
        else:
            pass_last(j - 1)

    @pl.when(z >= 3)
    def _():
        after_first(z - 3)

    @pl.when(z <= 0)
    def _():
        after_first(z + 3)

    after_second(z)
    for j in range(1, 4):

        @pl.when(z >= j)
        def _():
            after_second(z - j)

        @pl.when(z + j <= 3)
        def _():
            after_second(z + j)

    pass_last(3)
    for zz in range(4):
        for a in range(2):
            for b in range(2):
                chip = col(zz) + a * first + b * second
                to_twin(chip).wait_recv()
                to_twin(chip).wait_send()
                last_twin(chip).wait_recv()
                last_twin(chip).wait_send()
        to_first(zz).wait_send()
        for a in range(2):
            to_second(zz, a).wait_send()

    last_first().wait_send()
    for a in range(2):
        last_second(a).wait_send()

    @pl.when(z < 3)
    def _():
        up(1).wait_send()
        for q in range(4):
            last_up(1, q).wait_send()
        for j in range(1, 3):

            @pl.when(z >= j)
            def _():
                up(j + 1).wait_send()
                for q in range(4):
                    last_up(j + 1, q).wait_send()

    @pl.when(z > 0)
    def _():
        down(1).wait_send()
        for q in range(4):
            last_down(1, q).wait_send()
        for j in range(1, 3):

            @pl.when(z + j <= 3)
            def _():
                down(j + 1).wait_send()
                for q in range(4):
                    last_down(j + 1, q).wait_send()

    @pl.when(core == 0)
    def _():
        far.wait_send()


def gather_slots(placed, tokens, params, slots):
    anywhere, inside = pl.BlockSpec(memory_space=pl.ANY), pl.BlockSpec(memory_space=pltpu.VMEM)
    wide = (tokens.shape[0], PREFIX + tokens.shape[1])
    return pl.pallas_call(
        functools.partial(gather_kernel, slots),
        out_shape=[jax.ShapeDtypeStruct(placed.shape, placed.dtype), jax.ShapeDtypeStruct(wide, BF16)],
        in_specs=[anywhere, anywhere, inside],
        out_specs=[anywhere, inside],
        scratch_shapes=[
            pltpu.VMEM(wide, BF16),
            pltpu.SemaphoreType.DMA((GATHER_LABELS,)),
            pltpu.SemaphoreType.DMA((GATHER_LABELS,)),
            pltpu.SemaphoreType.DMA((2,)),
        ],
        input_output_aliases={0: 0},
        compiler_params=pltpu.CompilerParams(collective_id=0, has_side_effects=True),
        name="gather_slots",
    )(placed, tokens, params)


R_TWIN, R_SECOND, R_FIRST, R_LINE, R_DONE, R_PREFIX, R_FLOW, REDUCE_LABELS = 0, 16, 24, 28, 32, 33, 34, 42
RING = 3
PANELS = 5


def reduce_kernel(
    slots,
    grads,
    w_three,
    grad_three,
    tokens,
    grad_middle,
    params,
    sums,
    out,
    grad_input,
    norm_sums,
    ring,
    r_twin,
    r_second,
    r_first,
    r_line,
    total,
    weights,
    inner,
    acc,
    prefix,
    given,
    folds,
    flow,
    arrived,
    load,
    send,
    recv,
    save,
):
    me, core, z, first, second = place()
    half = slots // 2
    features, length = acc.shape
    line = [(me + 4 * ((z + r) % 4 - z), core) for r in range(1, 4)]
    greet([(me + first, core), (me + second, core), (me, 1 - core)] + line)

    def piece(chip, h):
        return grads.at[pl.ds(chip * slots + h * half, half)]

    def chip_at(zz, a, b):
        return me + 4 * (zz - z) + a * first + b * second

    def remote(src, dst, label, dp, c):
        return pltpu.make_async_remote_copy(
            src_ref=src,
            dst_ref=dst,
            send_sem=send.at[label],
            recv_sem=recv.at[label],
            device_id=(dp, c),
            device_id_type=MESH,
        )

    def twin(zz, a, b):
        chip = chip_at(zz, a, b)
        return remote(piece(chip, 1 - core), r_twin.at[chip], R_TWIN + chip, me, 1 - core)

    def to_second(zz, a):
        return remote(
            r_twin.at[chip_at(zz, a, 1)], r_second.at[2 * zz + a], R_SECOND + 2 * zz + a, me + second, core
        )

    def to_first(zz):
        return remote(r_twin.at[chip_at(zz, 1, 0)], r_first.at[zz], R_FIRST + zz, me + first, core)

    def to_line(r):
        zz = (z + r) % 4
        return remote(r_twin.at[chip_at(zz, 0, 0)], r_line.at[r - 1], R_LINE + r, chip_at(zz, 0, 0), core)

    order = [2, 1, 3, 0]
    where = [(z + r) % 4 for r in order]
    turns = []
    for index in range(3):
        turns += [(where[index], 1, 1), (where[index], 0, 1)]
    turns += [(where[0], 1, 0), (where[3], 1, 1), (where[3], 0, 1), (where[0], 0, 0), (where[1], 1, 0)]
    turns += [(where[2], 1, 0), (where[1], 0, 0), (where[3], 1, 0), (where[2], 0, 0), (where[3], 0, 0)]

    def load_piece(chip, slot):
        return pltpu.make_async_copy(piece(chip, core), ring.at[slot], load.at[slot])

    def load_own(turn):
        return load_piece(chip_at(*turns[turn]), turn % RING)

    def add_up(turn, others):
        chip = chip_at(*turns[turn])
        load_own(turn).wait()
        twin(*turns[turn]).wait_recv()

        def body(s, carry):
            value = ring[turn % RING, s].astype(F32) + r_twin[chip, s].astype(F32)
            for ref, index in others:
                value = value + ref[index, s].astype(F32)
            if turn < len(turns) - 1:
                r_twin[chip, s] = value.astype(BF16)
            else:
                total[s] = value
            return carry

        lax.fori_loop(0, half, body, 0)
        if turn + RING < len(turns):
            load_own(turn + RING).start()

    def send_second(turn):
        zz, a, _ = turns[turn]
        add_up(turn, [])
        to_second(zz, a).start()

    def send_first(turn):
        zz = turns[turn][0]
        to_second(zz, 1).wait_recv()
        add_up(turn, [(r_second, 2 * zz + 1)])
        to_first(zz).start()

    def send_line(turn, r):
        zz = turns[turn][0]
        to_second(zz, 0).wait_recv()
        to_first(zz).wait_recv()
        add_up(turn, [(r_second, 2 * zz), (r_first, zz)])
        to_line(r).start()

    for turn in range(RING):
        load_own(turn).start()
    for zz in where:
        for a in (1, 0):
            twin(zz, 1, a).start()
    for zz in where:
        for a in (1, 0):
            twin(zz, 0, a).start()
    fetches = [
        pltpu.make_async_copy(w_three, weights, save.at[0]),
        pltpu.make_async_copy(grad_three, inner, save.at[1]),
    ]
    for fetch in fetches:
        fetch.start()
    def early(turn, carry):
        def pick(values):
            return sum(jnp.where(turn == index, value, 0) for index, value in enumerate(values))

        zz, a, slot = pick([t[0] for t in turns[:6]]), 1 - turn % 2, turn % RING
        chip, after = chip_at(zz, a, 1), pick([chip_at(*t) for t in turns[RING : RING + 6]])
        load_piece(chip, slot).wait()
        twin(zz, a, 1).wait_recv()

        def body(s, inner_carry):
            r_twin[chip, s] = (ring[slot, s].astype(F32) + r_twin[chip, s].astype(F32)).astype(BF16)
            return inner_carry

        lax.fori_loop(0, half, body, 0)
        load_piece(after, slot).start()
        to_second(zz, a).start()
        return carry

    lax.fori_loop(0, 6, early, 0)
    send_first(6)
    send_second(7)
    send_second(8)
    for fetch in fetches:
        fetch.wait()

    rows = features // PANELS

    def panel(index, carry):
        mine = pl.ds(pl.multiple_of(index * rows, 16), rows)
        acc[mine, :] = sum(nn(weights[k, mine, :], inner[k]) for k in range(3))
        return carry

    lax.fori_loop(0, PANELS, panel, 0)

    swap = remote(acc.at[:, pl.ds(0, PREFIX)], prefix, R_PREFIX, me, 1 - core)
    swap.start()
    own_tokens = weights.at[0, :, pl.ds(0, length - PREFIX)]
    take = pltpu.make_async_copy(tokens, own_tokens, save.at[0])
    take.start()

    def at(index):
        return pl.ds(pl.multiple_of(index * GB, GB), GB)

    def ahead(index):
        return pl.ds(pl.multiple_of(PREFIX + index * GB, PREFIX), GB)

    def give(index, slot):
        return pltpu.make_async_copy(grad_middle.at[:, at(index)], given.at[slot], save.at[2 + slot])

    def store(index):
        return pltpu.make_async_copy(acc.at[:, ahead(index)], grad_input.at[:, at(index)], save.at[4 + index])

    give(0, 0).start()
    send_line(9, order[0])
    send_first(10)
    take.wait()
    swap.wait()
    here = (1 - core).astype(F32)
    acc[:, PREFIX : 2 * PREFIX] += (acc[:, :PREFIX] + prefix[...]) * here
    folds[...] = jnp.zeros_like(folds)
    groups = (length - PREFIX) // GB

    def back(index, carry):
        @pl.when(index + 1 < groups)
        def _():
            give(index + 1, (index + 1) % 2).start()

        give(index, index % 2).wait()
        unit, scale = norm_parts(weights[0, :, at(index)].astype(F32))
        grad = acc[:, ahead(index)]
        folds[0] += fold(grad * unit)
        folds[1] += fold(grad)
        acc[:, ahead(index)] = given[index % 2] + norm_back(unit, scale, params[:, 0:1], grad)
        store(index).start()
        return carry

    lax.fori_loop(0, groups, back, 0)
    flow[0] = sums[...] + row_sums(folds[0], 0) + row_sums(folds[1], 1)
    pairs = [(me, 1 - core), (me + first, core), (me, 1 - core), (me + first, core), (me, 1 - core)] + line
    sources = [flow.at[0], flow.at[1], flow.at[2], arrived.at[2], flow.at[3]] + [flow.at[4]] * 3

    def pass_on(k):
        return remote(sources[k], arrived.at[k], R_FLOW + k, *pairs[k])

    for k in range(2):
        pass_on(k).start()
        pass_on(k).wait_recv()
        flow[k + 1] = flow[k] + arrived[k]
    pass_on(2).start()
    pass_on(2).wait_recv()
    pass_on(3).start()
    send_first(11)
    pass_on(3).wait_recv()
    flow[3] = arrived[2] + arrived[3]
    pass_on(4).start()
    pass_on(4).wait_recv()
    plane = jnp.where(core == 0, flow[3], arrived[4])
    flow[4] = plane
    arrived[4] = plane
    for k in range(5, 8):
        pass_on(k).start()
    send_line(12, order[1])
    send_first(13)
    send_line(14, order[2])
    for k in range(5, 8):
        pass_on(k).wait_recv()
    norm_sums[...] = sum(arrived[4 + (z - zz + 4) % 4] for zz in range(4))
    to_second(z, 0).wait_recv()
    to_first(z).wait_recv()
    for r in range(1, 4):
        to_line(r).wait_recv()
    add_up(15, [(r_second, 2 * z), (r_first, z), (r_line, 0), (r_line, 1), (r_line, 2)])
    target = out.at[pl.ds(core * half, half)]
    done = remote(total, target, R_DONE, me, 1 - core)
    done.start()
    saved = pltpu.make_async_copy(total, target, save.at[0])
    saved.start()
    for zz in range(4):
        for a in range(2):
            for b in range(2):
                twin(zz, a, b).wait_send()
            to_second(zz, a).wait_send()
        to_first(zz).wait_send()
    for r in range(1, 4):
        to_line(r).wait_send()
    for k in range(len(pairs)):
        pass_on(k).wait_send()
    for index in range(groups):
        store(index).wait()
    done.wait()
    saved.wait()


def reduce_slots(grads, slots, w_three, grad_three, tokens, grad_middle, params, sums):
    _, lines, lanes = grads.shape
    half = slots // 2
    _, features, length = grad_three.shape
    pieces = lambda n: pltpu.VMEM((n, half, lines, lanes), BF16)
    anywhere, inside = pl.BlockSpec(memory_space=pl.ANY), pl.BlockSpec(memory_space=pltpu.VMEM)
    groups = (length - PREFIX) // GB
    return pl.pallas_call(
        functools.partial(reduce_kernel, slots),
        out_shape=[
            jax.ShapeDtypeStruct((slots, lines, lanes), F32),
            jax.ShapeDtypeStruct((features, length - PREFIX), F32),
            jax.ShapeDtypeStruct((8, features), F32),
        ],
        in_specs=[anywhere] * 5 + [inside] * 2,
        out_specs=[anywhere, anywhere, inside],
        scratch_shapes=[
            pieces(RING),
            pieces(16),
            pieces(8),
            pieces(4),
            pieces(3),
            pltpu.VMEM((half, lines, lanes), F32),
            pltpu.VMEM(w_three.shape, BF16),
            pltpu.VMEM(grad_three.shape, BF16),
            pltpu.VMEM((features, length), F32),
            pltpu.VMEM((features, PREFIX), F32),
            pltpu.VMEM((2, features, GB), F32),
            pltpu.VMEM((2, features, 128), F32),
            pltpu.VMEM((5, 8, features), F32),
            pltpu.VMEM((8, 8, features), F32),
            pltpu.SemaphoreType.DMA((RING,)),
            pltpu.SemaphoreType.DMA((REDUCE_LABELS,)),
            pltpu.SemaphoreType.DMA((REDUCE_LABELS,)),
            pltpu.SemaphoreType.DMA((4 + groups,)),
        ],
        compiler_params=pltpu.CompilerParams(collective_id=1, has_side_effects=True, vmem_limit_bytes=63 << 20),
        name="reduce_slots",
    )(grads, w_three, grad_three, tokens, grad_middle, params, sums)


def lay(matrix, row, col, block):
    size = block.shape[0] - RUN
    matrix[size * row : size * (row + 1), size * col : size * col + MAIN] = block[:size]
    for start, count, lane in runs(size):
        piece = block[size : size + count, lane : lane + size - MAIN]
        matrix[size * row + start : size * row + start + count, size * col + MAIN : size * (col + 1)] = piece


def block_specs(gathered, rows, cols, block_of, **mode):
    shape = (1,) + gathered.shape[1:]
    pick = lambda i, j, step, v: (v[block_of(step, i, j)], 0, 0)
    return [
        pl.BlockSpec(shape, functools.partial(pick, i, j), **mode) for i in range(rows) for j in range(cols)
    ]


def feature_parts(features):
    part = -(-features // 256) * 128
    return [slice(start, min(start + part, features)) for start in range(0, features, part)]


def fold(values):
    return sum(values[:, start : start + 128] for start in range(0, values.shape[1], 128))


def row_sums(values, row):
    ones = jnp.ones((8, values.shape[1]), F32)
    summed = lax.dot_general(
        ones, values, (((1,), (1,)), ((), ())), precision=lax.Precision.HIGHEST, preferred_element_type=F32
    )
    return jnp.where(lax.broadcasted_iota(jnp.int32, summed.shape, 0) == row, summed, 0.0)


ONCE = pl.Buffered(1)


def front_kernel(slot_of, normed, *refs):
    del slot_of
    blocks, (weights, out) = refs[:-2], refs[-2:]
    row_blocks = math.isqrt(len(blocks))
    for index, block in enumerate(blocks):
        lay(weights.at[0], index // row_blocks, index % row_blocks, block.at[0])
    out[0] = tn(weights[0], normed[...]).astype(BF16)


def front(gathered, slot_of, normed, row_blocks):
    features, length = normed.shape
    square = row_blocks * row_blocks
    blocks = block_specs(gathered, row_blocks, row_blocks, lambda s, i, j: s * square + i * row_blocks + j)
    return pl.pallas_call(
        front_kernel,
        grid_spec=pltpu.PrefetchScalarGridSpec(
            num_scalar_prefetch=1,
            grid=(3,),
            in_specs=[pl.BlockSpec((features, length), lambda s, v: (0, 0), pipeline_mode=ONCE)] + blocks,
            out_specs=[
                pl.BlockSpec((1, features, features), lambda s, v: (s, 0, 0)),
                pl.BlockSpec((1, features, length), lambda s, v: (s, 0, 0)),
            ],
        ),
        out_shape=[
            jax.ShapeDtypeStruct((3, features, features), BF16),
            jax.ShapeDtypeStruct((3, features, length), BF16),
        ],
        compiler_params=pltpu.CompilerParams(vmem_limit_bytes=60 << 20),
        name="front",
    )(slot_of, normed, *([gathered] * square))


def gelu_pair(values):
    square = values * values
    bend = jnp.tanh(values * (0.7978845608028654 + (0.7978845608028654 * 0.044715) * square))
    half = 0.5 * values
    slope = 0.7978845608028654 + (3 * 0.7978845608028654 * 0.044715) * square
    return half + half * bend, 0.5 + 0.5 * bend + half * (1.0 - bend * bend) * slope


def middle_kernel(row_blocks, slot_of, params, tokens, attended, grad_low, *refs):
    del slot_of
    square = row_blocks * row_blocks
    out_blocks, up_blocks, down_blocks = (refs[square * k : square * (k + 1)] for k in range(3))
    outs, scratch = refs[3 * square : 3 * square + 8], refs[3 * square + 8 :]
    block_out, activated, grad_pre, normed, grad_branch, grad_att, grad_middle, sums = outs
    w_out, w_up, w_down, middle, total, stats, folds, sem = scratch
    tiles, parts = grad_low.shape[1] // GB, feature_parts(normed.shape[0])
    at = lambda index: pl.ds(pl.multiple_of(index * GB, GB), GB)
    step, last = pl.program_id(0), pl.num_programs(0) - 1

    @pl.when(step == 0)
    def _():
        copies = [
            pltpu.make_async_copy(tokens, block_out, sem.at[0]),
            pltpu.make_async_copy(attended, grad_att, sem.at[1]),
        ]
        for copy in copies:
            copy.start()
        for index, block in enumerate(out_blocks):
            lay(w_out, index // row_blocks, index % row_blocks, block.at[0])
        for copy in copies:
            copy.wait()
        def enter(index, carry):
            tile = at(index)
            for part in parts:
                values = block_out[part, tile].astype(F32) + tn(w_out[:, part], grad_att[:, tile])
                middle[part, tile] = values
                total[part, tile] = values
                grad_middle[part, tile] = jnp.zeros_like(values)
            values = middle[:, tile]
            average = jnp.mean(values, axis=0, keepdims=True)
            centred = values - average
            scale = lax.rsqrt(jnp.mean(centred * centred, axis=0, keepdims=True) + 1e-05)
            stats[0:1, tile] = average
            stats[1:2, tile] = scale
            normed[:, tile] = (centred * scale * params[:, 2:3] + params[:, 3:4]).astype(BF16)
            return carry

        lax.fori_loop(0, tiles, enter, 0)
        folds[...] = jnp.zeros_like(folds)

    for index in range(square):
        lay(w_up, index // row_blocks, index % row_blocks, up_blocks[index].at[0])
        lay(w_down, index // row_blocks, index % row_blocks, down_blocks[index].at[0])

    def advance(index, carry):
        tile = pl.ds(pl.multiple_of(index * wide, wide), wide)
        for part in parts:
            value, slope = gelu_pair(tn(w_up[:, part], normed[:, tile]))
            activated[part, tile] = value.astype(BF16)
            grad_pre[part, tile] = (nn(w_down[part, :], grad_low[:, tile]) * slope).astype(BF16)
        for part in parts:
            total[part, tile] += tn(w_down[:, part], activated[:, tile])
            grad_middle[part, tile] += nn(w_up[part, :], grad_pre[:, tile])
        return carry

    wide = 2 * GB if tiles % 2 == 0 else GB
    lax.fori_loop(0, grad_low.shape[1] // wide, advance, 0)

    @pl.when(step == last)
    def _():
        def leave(index, carry):
            tile = at(index)
            block_out[:, tile] = total[:, tile].astype(BF16)
            scale = stats[1:2, tile]
            unit = (middle[:, tile] - stats[0:1, tile]) * scale
            grad = grad_middle[:, tile]
            folds[0] += fold(grad * unit)
            folds[1] += fold(grad)
            values = grad_low[:, tile].astype(F32) + norm_back(unit, scale, params[:, 2:3], grad)
            grad_middle[:, tile] = values
            grad_branch[:, tile] = values.astype(BF16)
            for part in parts:
                grad_att[part, tile] = nn(w_out[part, :], grad_branch[:, tile]).astype(BF16)
            return carry

        lax.fori_loop(0, tiles, leave, 0)
        sums[...] = row_sums(folds[0], 2) + row_sums(folds[1], 3)


def middle_part(gathered, slot_of, params, tokens, attended, grad_low, row_blocks, col_blocks):
    features, length = tokens.shape
    square = row_blocks * row_blocks
    hidden = features * col_blocks // row_blocks
    up_start, down_start = 4 * square, 4 * square + row_blocks * col_blocks
    whole = lambda *shape: pl.BlockSpec(shape, lambda s, v: (0,) * len(shape), pipeline_mode=ONCE)
    anywhere = pl.BlockSpec(memory_space=pl.ANY)
    part = pl.BlockSpec((features, length), lambda s, v: (s, 0))
    blocks = (
        block_specs(
            gathered, row_blocks, row_blocks, lambda s, i, j: 3 * square + i * row_blocks + j, pipeline_mode=ONCE
        )
        + block_specs(
            gathered, row_blocks, row_blocks, lambda s, i, j: up_start + i * col_blocks + s * row_blocks + j
        )
        + block_specs(
            gathered, row_blocks, row_blocks, lambda s, i, j: down_start + (s * row_blocks + i) * row_blocks + j
        )
    )
    shape = jax.ShapeDtypeStruct
    square_scratch = pltpu.VMEM((features, features), BF16)
    return pl.pallas_call(
        functools.partial(middle_kernel, row_blocks),
        grid_spec=pltpu.PrefetchScalarGridSpec(
            num_scalar_prefetch=1,
            grid=(col_blocks // row_blocks,),
            in_specs=[whole(*params.shape)] + [anywhere] * 2 + [whole(features, length)] + blocks,
            out_specs=[whole(features, length), part, part]
            + [whole(features, length)] * 4
            + [whole(8, features)],
            scratch_shapes=[square_scratch] * 3
            + [pltpu.VMEM((features, length), F32)] * 2
            + [
                pltpu.VMEM((8, length), F32),
                pltpu.VMEM((2, features, 128), F32),
                pltpu.SemaphoreType.DMA((2,)),
            ],
        ),
        out_shape=[
            shape((features, length), BF16),
            shape((hidden, length), BF16),
            shape((hidden, length), BF16),
            shape((features, length), BF16),
            shape((features, length), BF16),
            shape((features, length), BF16),
            shape((features, length), F32),
            shape((8, features), F32),
        ],
        compiler_params=pltpu.CompilerParams(vmem_limit_bytes=63 << 20),
        name="middle_part",
    )(slot_of, params, tokens, attended, grad_low, *([gathered] * (3 * square)))


def weight_grad_kernel(block_of, deep, size, slot_of, left, right, *refs):
    grads, stage, sem = refs[-3:]
    wide = right.shape[0] // size
    rows, cols = pl.program_id(0), pl.program_id(1)
    step = rows * pl.num_programs(1) + cols
    steps = pl.num_programs(0) * pl.num_programs(1)
    now = step % 2

    def copy(buffer, index, slot):
        return pltpu.make_async_copy(stage.at[buffer, index], grads.at[slot], sem.at[buffer, index])

    @pl.when(step >= 2)
    def _():
        for index in range(deep * wide):
            copy(now, index, 0).wait()

    other = right[...]
    for i in range(deep):
        panel = nt(left[size * i : size * (i + 1), :], other)
        for j in range(wide):
            index = i * wide + j
            block = panel[:, size * j : size * (j + 1)]
            stage[now, index, :size] = block[:, :MAIN].astype(BF16)
            stage[now, index, size:] = pack_tail(block).astype(BF16)
            copy(now, index, slot_of[block_of(rows * deep + i, cols * wide + j)]).start()

    @pl.when(step == steps - 1)
    def _():
        for index in range(deep * wide):
            copy(now, index, 0).wait()

        @pl.when(steps > 1)
        def _():
            for index in range(deep * wide):
                copy(1 - now, index, 0).wait()


def weight_grad(left, right, slot_of, grads, slot_count, size, block_of, name):
    depth = left.shape[1]
    deep = wide = 4
    grid = (left.shape[0] // (size * deep), right.shape[0] // (size * wide))
    anywhere = pl.BlockSpec(memory_space=pl.ANY)
    operands = [slot_of, left, right] + ([] if grads is None else [grads])
    return pl.pallas_call(
        functools.partial(weight_grad_kernel, block_of, deep, size),
        grid_spec=pltpu.PrefetchScalarGridSpec(
            num_scalar_prefetch=1,
            grid=grid,
            in_specs=[
                pl.BlockSpec((size * deep, depth), lambda i, j, v: (i, 0)),
                pl.BlockSpec((size * wide, depth), lambda i, j, v: (j, 0)),
            ]
            + [anywhere] * (len(operands) - 3),
            out_specs=anywhere,
            scratch_shapes=[
                pltpu.VMEM((2, deep * wide, size + RUN, MAIN), BF16),
                pltpu.SemaphoreType.DMA((2, deep * wide)),
            ],
        ),
        out_shape=jax.ShapeDtypeStruct((slot_count, size + RUN, MAIN), BF16),
        input_output_aliases={} if grads is None else {3: 0},
        cost_estimate=cost(
            2 * left.shape[0] * right.shape[0] * depth,
            2 * (left.size + right.size + left.shape[0] * right.shape[0]),
        ),
        name=name,
    )(*operands)


def weight_grads_kernel(starts, col_blocks, size, slot_of, *refs):
    activated, grad_low, normed, grad_pre, attended, grad_branch, grads, left, right, stage, get, put = refs
    out_start, up_start, down_start = starts
    side_length = left.shape[1]
    row_blocks = side_length // size
    count = row_blocks * row_blocks
    parts = activated.shape[0] // side_length
    step, steps = pl.program_id(0), pl.num_programs(0)
    now = step % 2

    def rows(index):
        return pl.ds(pl.multiple_of(index * side_length, 16), side_length)

    def fetch(index, buffer):
        def start(one, other):
            pltpu.make_async_copy(one, left.at[buffer], get.at[0, buffer]).start()
            pltpu.make_async_copy(other, right.at[buffer], get.at[1, buffer]).start()

        @pl.when(index < parts)
        def _():
            start(activated.at[rows(index)], grad_low)

        @pl.when((index >= parts) & (index < 2 * parts))
        def _():
            start(normed, grad_pre.at[rows(index - parts)])

        @pl.when(index == 2 * parts)
        def _():
            start(attended, grad_branch)

    def copy(buffer, index, slot):
        return pltpu.make_async_copy(stage.at[buffer, index], grads.at[slot], put.at[buffer, index])

    @pl.when(step == 0)
    def _():
        fetch(0, 0)

    @pl.when(step + 1 < steps)
    def _():
        fetch(step + 1, 1 - now)

    pltpu.make_async_copy(normed, left.at[now], get.at[0, now]).wait()
    pltpu.make_async_copy(normed, right.at[now], get.at[1, now]).wait()

    @pl.when(step >= 2)
    def _():
        for index in range(count):
            copy(now, index, 0).wait()

    up = (step >= parts) & (step < 2 * parts)
    start = jnp.where(up, up_start + (step - parts) * row_blocks, out_start)
    start = jnp.where(step < parts, down_start + step * count, start)
    stride = jnp.where(up, col_blocks, row_blocks)
    other = right[now]
    for i in range(row_blocks):
        panel = nt(left[now, size * i : size * (i + 1), :], other)
        for j in range(row_blocks):
            index = i * row_blocks + j
            block = panel[:, size * j : size * (j + 1)]
            stage[now, index, :size] = block[:, :MAIN].astype(BF16)
            stage[now, index, size:] = pack_tail(block).astype(BF16)
            copy(now, index, slot_of[start + i * stride + j]).start()

    @pl.when(step == steps - 1)
    def _():
        for index in range(count):
            copy(now, index, 0).wait()
            copy(1 - now, index, 0).wait()


def weight_grads(slot_of, operands, slot_count, size, starts, col_blocks):
    hidden, length = operands[0].shape
    features = operands[1].shape[0]
    count = (features // size) ** 2
    steps = 2 * (hidden // features) + 1
    anywhere = pl.BlockSpec(memory_space=pl.ANY)
    part = pltpu.VMEM((2, features, length), BF16)
    return pl.pallas_call(
        functools.partial(weight_grads_kernel, starts, col_blocks, size),
        grid_spec=pltpu.PrefetchScalarGridSpec(
            num_scalar_prefetch=1,
            grid=(steps,),
            in_specs=[anywhere] * 6,
            out_specs=anywhere,
            scratch_shapes=[
                part,
                part,
                pltpu.VMEM((2, count, size + RUN, MAIN), BF16),
                pltpu.SemaphoreType.DMA((2, 2)),
                pltpu.SemaphoreType.DMA((2, count)),
            ],
        ),
        out_shape=jax.ShapeDtypeStruct((slot_count, size + RUN, MAIN), BF16),
        cost_estimate=cost(2 * steps * features * features * length, 8 * steps * features * length),
        name="weight_grads",
    )(slot_of, *operands)


EXTRA = 8
TOGETHER = 2
FAR = -1e30


def causal():
    return lax.broadcasted_iota(jnp.int32, (HALF, HALF), 0) <= lax.broadcasted_iota(jnp.int32, (HALF, HALF), 1)


def places(groups):
    found = []
    for group in range(groups):
        base = PREFIX + GB * group
        low, high = slice(base, base + HALF), slice(base + HALF, base + GB)
        found.append((low, high, slice(base, base + GB), slice(GB * group, GB * (group + 1))))
    return found


def side(left, right):
    return jnp.concatenate([left, right], axis=1)


def attention_kernel(scale, head, qkv, extras, out, lse, queries, keys, values, keys_t):
    unit = scale * math.log2(math.e)
    heads = range(queries.shape[0])

    @pl.when(pl.program_id(0) == 0)
    def _():
        for k in heads:
            queries[k, head:] = extras[0]
            keys[k, head:] = extras[1]
            values[k, head:] = extras[2]

    for k in heads:
        rows = slice(head * k, head * (k + 1))
        queries[k, :head] = qkv[0, rows]
        keys[k, :head] = qkv[1, rows]
        values[k, :head] = qkv[2, rows]
    for k in heads:
        keys_t[k] = keys[k].T
    ahead = causal()
    spots = [(k,) + spot for k in heads for spot in places(out.shape[1] // GB)]
    scores = []
    for k, low, high, both, _ in spots:
        asked = queries[k, :, both]
        scores.append((nn(keys_t[k, :PREFIX], asked), nn(keys_t[k, low], asked), nn(keys_t[k, high], asked[:, HALF:])))

    def peak(array):
        return jnp.max(array, axis=0, keepdims=True)

    def soft(array, top):
        return jnp.exp2((array - top) * unit).astype(BF16)

    tops, weights = [], []
    for prefix, first, second in scores:
        first = side(jnp.where(ahead, first[:, :HALF], FAR), first[:, HALF:])
        second = jnp.where(ahead, second, FAR)
        top = jnp.maximum(peak(prefix), peak(first))
        top = side(top[:, :HALF], jnp.maximum(top[:, HALF:], peak(second)))
        tops.append(top)
        weights.append((soft(prefix, top), soft(first, top), soft(second, top[:, HALF:])))
    for (k, low, high, _, mine), top, (prefix, first, second) in zip(spots, tops, weights):
        sums = nn(values[k, :, :PREFIX], prefix) + nn(values[k, :, low], first)
        sums = side(sums[:, :HALF], sums[:, HALF:] + nn(values[k, :, high], second))
        total = sums[head : head + 1]
        out[head * k : head * (k + 1), mine] = (sums[:head] / total).astype(BF16)
        lse[k, :, mine] = top + jnp.log(total) * (1.0 / scale)


def thirds(values):
    high = values.astype(BF16).astype(F32)
    rest = values - high
    middle = rest.astype(BF16).astype(F32)
    return high, middle, rest - middle


def with_rows(base, start, rows):
    index = lax.broadcasted_iota(jnp.int32, base.shape, 0)
    for offset, row in enumerate(rows):
        base = jnp.where(index == start + offset, row, base)
    return base.astype(BF16)


def attention_back_kernel(
    scale, head, qkv, extras, out, lse, grad_out, grads, queries, keys, values, grad_o, keys_t, values_t
):
    own = out.shape[1]
    unit = scale * math.log2(math.e)
    heads = range(queries.shape[0])

    @pl.when(pl.program_id(0) == 0)
    def _():
        for k in heads:
            keys[k, head:] = extras[1]
            values[k, head:] = extras[2]

    for k in heads:
        rows = slice(head * k, head * (k + 1))
        queries[k, :head] = qkv[0, rows, PREFIX:]
        keys[k, :head] = qkv[1, rows]
        values[k, :head] = qkv[2, rows]
        given = grad_out[rows]
        grad_o[k, :head] = given
        queries[k, head:] = with_rows(extras[0, :, PREFIX:].astype(F32), 2, thirds(-lse[k]))
        delta = jnp.sum(given.astype(F32) * out[rows].astype(F32), axis=0, keepdims=True)
        grad_o[k, head:] = with_rows(jnp.zeros((EXTRA, own), F32), 0, thirds(-delta))
    for k in heads:
        keys_t[k] = keys[k].T
        values_t[k] = values[k].T
    ahead = causal()
    spots = [(k,) + spot for k in heads for spot in places(own // GB)]

    def weigh(k, rows, asked, given, mask):
        weights = jnp.exp2(nn(keys_t[k, rows], asked) * unit)
        if mask == 1:
            weights = side(jnp.where(ahead, weights[:, :HALF], 0.0), weights[:, HALF:])
        if mask == 2:
            weights = jnp.where(ahead, weights, 0.0)
        return weights.astype(BF16), (weights * nn(values_t[k, rows], given)).astype(BF16)

    found = []
    for k, low, high, _, mine in spots:
        asked, given = queries[k, :, mine], grad_o[k, :, mine]
        found.append(
            (
                weigh(k, slice(0, PREFIX), asked, given, 0),
                weigh(k, low, asked, given, 1),
                weigh(k, high, asked[:, HALF:], given[:, HALF:], 2),
            )
        )
    prefix_k, prefix_v = {}, {}
    for (k, low, high, both, mine), ((p0, d0), (p1, d1), (p2, d2)) in zip(spots, found):
        rows = slice(head * k, head * (k + 1))
        asked, given = queries[k, :head, mine], grad_o[k, :head, mine]
        grad_q = nn(keys[k, :head, :PREFIX], d0) + nn(keys[k, :head, low], d1)
        grad_q = side(grad_q[:, :HALF], grad_q[:, HALF:] + nn(keys[k, :head, high], d2))
        grads[0, rows, both] = (grad_q * scale).astype(BF16)
        part_k, part_v = nt(asked, d0), nt(given, p0)
        prefix_k[k] = prefix_k[k] + part_k if k in prefix_k else part_k
        prefix_v[k] = prefix_v[k] + part_v if k in prefix_v else part_v
        grads[1, rows, low] = (nt(asked, d1) * scale).astype(BF16)
        grads[2, rows, low] = nt(given, p1).astype(BF16)
        grads[1, rows, high] = (nt(asked[:, HALF:], d2) * scale).astype(BF16)
        grads[2, rows, high] = nt(given[:, HALF:], p2).astype(BF16)
    for k in heads:
        rows = slice(head * k, head * (k + 1))
        grads[0, rows, :PREFIX] = jnp.zeros((head, PREFIX), BF16)
        grads[1, rows, :PREFIX] = (prefix_k[k] * scale).astype(BF16)
        grads[2, rows, :PREFIX] = prefix_v[k].astype(BF16)


def attention_specs(qkv):
    _, features, length = qkv.shape
    head, own = features // HEADS, length - PREFIX
    three = pl.BlockSpec((3, TOGETHER * head, length), lambda h: (0, h, 0))
    extra = pl.BlockSpec((3, EXTRA, length), lambda h: (0, 0, 0))
    one = pl.BlockSpec((TOGETHER * head, own), lambda h: (h, 0))
    row = pl.BlockSpec((TOGETHER, 1, own), lambda h: (h, 0, 0))
    wide = lambda columns: pltpu.VMEM((TOGETHER, head + EXTRA, columns), BF16)
    tall = pltpu.VMEM((TOGETHER, length, head + EXTRA), BF16)
    return features, length, own, head, three, extra, one, row, wide, tall


def attention(qkv, extras):
    features, length, own, head, three, extra, one, row, wide, tall = attention_specs(qkv)
    return pl.pallas_call(
        functools.partial(attention_kernel, head ** (-0.5), head),
        grid=(HEADS // TOGETHER,),
        in_specs=[three, extra],
        out_specs=[one, row],
        out_shape=[
            jax.ShapeDtypeStruct((features, own), BF16),
            jax.ShapeDtypeStruct((HEADS, 1, own), F32),
        ],
        scratch_shapes=[wide(length), wide(length), wide(length), tall],
        cost_estimate=cost(8 * features * own * GB, 2 * qkv.size, HEADS * own * GB),
        name="attention",
    )(qkv, extras)


def attention_back(qkv, extras, out, lse, grad_out):
    features, length, own, head, three, extra, one, row, wide, tall = attention_specs(qkv)
    return pl.pallas_call(
        functools.partial(attention_back_kernel, head ** (-0.5), head),
        grid=(HEADS // TOGETHER,),
        in_specs=[three, extra, one, row, one],
        out_specs=three,
        out_shape=jax.ShapeDtypeStruct(qkv.shape, BF16),
        scratch_shapes=[wide(own), wide(length), wide(length), wide(own), tall, tall],
        cost_estimate=cost(20 * features * own * GB, 4 * qkv.size, HEADS * own * GB),
        name="attention_back",
    )(qkv, extras, out, lse, grad_out)


def score_extras(alive, prefix_alive, later):
    length = PREFIX + alive.shape[0]
    dead = jnp.where(jnp.concatenate([prefix_alive, alive]), 0.0, FAR)
    prefix = (jnp.arange(length) < PREFIX).astype(F32)
    barred = jnp.concatenate([jnp.zeros((PREFIX,)), jnp.where(jnp.repeat(later, GB), 0.0, FAR)])
    one, zero = jnp.ones((length,)), jnp.zeros((length,))
    query_rows = jnp.stack([one, barred] + [zero] * 6)
    key_rows = jnp.stack([dead, prefix] + [one] * 3 + [zero] * 3)
    value_rows = jnp.stack([one] * 3 + [zero] * 5)
    return jnp.stack([query_rows, key_rows, value_rows]).astype(BF16)


def split(values):
    high = values.astype(BF16)
    return high, (values - high.astype(F32)).astype(BF16)


def product(form, left, right):
    (left_high, left_low), (right_high, right_low) = left, right
    return form(left_high, right_high) + (form(left_high, right_low) + form(left_low, right_high))


def optimizer_kernel(scale, packed, master, average, left, right, root_left, root_right, passed, sums, norms, *outs):
    slot_grad, new_left, new_right, new_master, new_copy, new_average, passed_on, norm_grad, new_norms = outs
    size = master.shape[1]
    passed_on[...] = passed[...]

    @pl.when(pl.program_id(0) == 0)
    def _():
        count = norms.shape[0]
        scaled = sums[:count] * scale
        norm_grad[...] = scaled
        square = jnp.sum(jnp.sum(scaled * scaled, axis=1, keepdims=True), axis=0, keepdims=True)
        new_norms[...] = norms[...] - 0.1 * scaled * lax.rsqrt(square * (1.0 / norms.size) + 1e-06)

    grad = unpack(packed[0]) * scale
    slot_grad[0] = grad
    grad_parts = split(grad)
    new_left[0] = 0.5 * left[0] + (0.5 / size) * nt(grad_parts[0], grad_parts[0])
    new_right[0] = 0.5 * right[0] + (0.5 / size) * tn(grad_parts[0], grad_parts[0])
    right_part = product(nn, grad_parts, split(root_right[0]))
    step = product(nn, split(root_left[0]), split(right_part))
    moved = master[0] - 0.03 * step
    new_master[0] = moved
    new_copy[0] = moved.astype(BF16)
    new_average[0] = 0.8 * average[0] + 0.2 * moved


def optimizer(packed, scale, arrays, passed, sums, norms):
    slots, size, _ = arrays[0].shape
    block = pl.BlockSpec((1, size, size), lambda i: (i, 0, 0))
    whole = lambda array: pl.BlockSpec(array.shape, lambda i: (0, 0))
    shape = lambda dtype: jax.ShapeDtypeStruct((slots, size, size), dtype)
    width = 128 * -(-passed.shape[1] // (128 * slots))
    last = passed.shape[1] // width - 1
    strip = pl.BlockSpec((passed.shape[0], width), lambda i: (0, jnp.minimum(i, last)))
    same = lambda array: jax.ShapeDtypeStruct(array.shape, F32)
    return pl.pallas_call(
        functools.partial(optimizer_kernel, scale),
        grid=(slots,),
        in_specs=[pl.BlockSpec((1,) + packed.shape[1:], lambda i: (i, 0, 0))]
        + [block] * 6
        + [strip, whole(sums), whole(norms)],
        out_specs=[block] * 6 + [strip, whole(norms), whole(norms)],
        out_shape=[shape(F32)] * 4 + [shape(BF16), shape(F32), same(passed), same(norms), same(norms)],
        name="optimizer",
    )(packed, *arrays, passed, sums, norms)


def norm_parts(values):
    average = jnp.mean(values, axis=0, keepdims=True)
    centred = values - average
    variance = jnp.mean(centred * centred, axis=0, keepdims=True)
    scale = lax.rsqrt(variance + 1e-05)
    return centred * scale, scale


def norm_back(unit, scale, gain, grad):
    inner = grad * gain
    mean_one = jnp.mean(inner, axis=0, keepdims=True)
    mean_two = jnp.mean(inner * unit, axis=0, keepdims=True)
    return scale * (inner - mean_one - unit * mean_two)


def local(
    chips,
    cores,
    tokens,
    cotangent,
    pad_mask,
    prefix_len,
    norm_gains,
    norm_shifts,
    owner_map,
    weight_copy,
    master,
    average_weights,
    stat_left,
    stat_right,
    root_left,
    root_right,
):
    cell_count, length, features = tokens.shape
    assert cell_count == 1
    slots, size, _ = weight_copy.shape
    slot_count = owner_map.shape[0]
    row_blocks = features // size
    square = row_blocks * row_blocks
    col_blocks = (slot_count - 4 * square) // (2 * row_blocks)
    known = chips == 16 and cores == 2
    chip = lax.axis_index("dp").astype(jnp.int32)
    seq_index = lax.axis_index("seq")

    slot_of = jnp.zeros((slot_count,), jnp.int32).at[owner_map].set(jnp.arange(slot_count, dtype=jnp.int32))
    own_tokens = tokens.reshape(length, features).T
    norms = jnp.stack([norm_gains[0], norm_shifts[0], norm_gains[1], norm_shifts[1]])
    params = norms.T
    if known:
        half = slots // 2
        begin = seq_index.astype(jnp.int32) * half
        placed = pack_slots(weight_copy, jnp.stack([begin, chip * slots + begin]), half, slot_count)
        gathered, normed_in = gather_slots(placed, own_tokens, params, slots)
    else:
        packed = pack_slots(weight_copy, jnp.zeros((2,), jnp.int32), slots, slots)
        gathered = lax.all_gather(packed, "dp", axis=0, tiled=True)
        prefix_tokens = lax.all_gather(own_tokens[:, :PREFIX], "seq")[0]
        unit_all, _ = norm_parts(jnp.concatenate([prefix_tokens, own_tokens], axis=1).astype(F32))
        normed_in = (unit_all * params[:, 0:1] + params[:, 1:2]).astype(BF16)
    starts = (3 * square, 4 * square, 4 * square + row_blocks * col_blocks)

    def three_of(i, j):
        return (j // row_blocks) * square + i * row_blocks + j % row_blocks

    w_three, qkv = front(gathered, slot_of, normed_in, row_blocks)

    position = seq_index * length + jnp.arange(length, dtype=jnp.int32)
    alive = jnp.where(position < PREFIX, position < prefix_len[0], pad_mask[0] == 1)
    prefix_alive = jnp.arange(PREFIX, dtype=jnp.int32) < prefix_len[0]
    groups = length // GB
    later = seq_index * groups + jnp.arange(groups) > 0
    extras = score_extras(alive, prefix_alive, later)

    grad_low = cotangent.reshape(length, features).T
    attended, log_total = attention(qkv, extras)
    block_out, activated, grad_pre, normed_mid, grad_branch, grad_att, grad_middle, sums = middle_part(
        gathered, slot_of, params, own_tokens, attended, grad_low, row_blocks, col_blocks
    )
    operands = (activated, grad_low, normed_mid, grad_pre, attended, grad_branch)
    grads = weight_grads(slot_of, operands, slot_count, size, starts, col_blocks)
    grad_three = attention_back(qkv, extras, attended, log_total, grad_att)
    flat_three = grad_three.reshape(3 * features, PREFIX + length)
    grads = weight_grad(normed_in, flat_three, slot_of, grads, slot_count, size, three_of, "grad_three")
    grad_scale = 1.0 / math.sqrt(length * chips * cores)
    if known:
        summed, grad_input, norm_sums = reduce_slots(
            grads, slots, w_three, grad_three, own_tokens, grad_middle, params, sums
        )
    else:
        part = lax.psum_scatter(grads.astype(F32), "dp", scatter_dimension=0, tiled=True)
        summed = lax.psum(part, "seq")
        grad_all = sum(nn(w_three[k], grad_three[k]) for k in range(3))
        prefix_part = jnp.where(seq_index == 0, lax.psum(grad_all[:, :PREFIX], "seq"), 0.0)
        grad_normed = grad_all[:, PREFIX:] + jnp.pad(prefix_part, ((0, 0), (0, length - PREFIX)))
        unit_one, scale_one = norm_parts(own_tokens.astype(F32))
        grad_input = grad_middle + norm_back(unit_one, scale_one, params[:, 0:1], grad_normed)
        first_sums = [jnp.sum(grad_normed * unit_one, axis=1), jnp.sum(grad_normed, axis=1)]
        norm_sums = lax.psum(jnp.stack(first_sums + [sums[2], sums[3]]), ("dp", "seq"))
    arrays = (master, average_weights, stat_left, stat_right, root_left, root_right)
    *stepped, grad_input, norm_grad, new_norms = optimizer(summed, grad_scale, arrays, grad_input, norm_sums, norms)
    token_shape = (cell_count, length, features)
    return (
        block_out.T.reshape(token_shape),
        grad_input.T.reshape(token_shape),
        norm_grad,
        new_norms,
        *stepped,
    )


def solution(mesh):
    tokens, slots = P("dp", "seq", None), P("dp", None, None)
    in_specs = (tokens, tokens, P("dp", "seq"), P("dp"), P(), P(), P()) + (slots,) * 7
    out_specs = (tokens, tokens, P(), P()) + (slots,) * 6
    body = functools.partial(local, mesh.shape["dp"], mesh.shape["seq"])
    return jax.shard_map(body, mesh=mesh, in_specs=in_specs, out_specs=out_specs, check_vma=False)
```
